32 devices in a mesh: head: 4 (over z), blk: 8 (over y, x, core).
Axes of the slice: x: 2, y: 2, z: 4, core: 2. Of those that a mesh axis runs over, the one named last changes fastest.
Arguments:
- tokens: bfloat16 [2, 2048, 1024], P(None, ('head', 'blk')), may hold values from -6 to 6
- positions: int32 [2, 2048], P(None, ('head', 'blk')), may hold values from 0 to 2047
- time_index: int32 [2], replicated, may hold values from 0 to 63
- time_table: float32 [64, 256], replicated, may hold values from -6 to 6
- w_qkv: bfloat16 [1024, 3072], P(('head', 'blk')), may hold values from -0.21875 to 0.21875
- w_out: bfloat16 [1024, 1024], P(('head', 'blk')), may hold values from -3 to 3
- w_up: bfloat16 [1024, 4096], P(('head', 'blk')), may hold values from -0.1875 to 0.1875
- w_down: bfloat16 [4096, 1024], P(('head', 'blk')), may hold values from -0.09375 to 0.09375
- scale_attn: bfloat16 [256, 1024], P(('head', 'blk')), may hold values from -0.19921875 to 0.19921875
- scale_mlp: bfloat16 [256, 1024], P(('head', 'blk')), may hold values from -0.19921875 to 0.19921875
- cotangent: bfloat16 [2, 2048, 1024], P(None, ('head', 'blk')), may hold values from -6 to 6
Outputs:
- output: bfloat16 [2, 2048, 1024], P(None, ('head', 'blk'))
- grad_tokens: float32 [2, 2048, 1024], P(None, ('head', 'blk'))
- grad_w_qkv: float32 [1024, 3072], P(('head', 'blk'))
- grad_w_out: float32 [1024, 1024], P(('head', 'blk'))
- grad_w_up: float32 [1024, 4096], P(('head', 'blk'))
- grad_w_down: float32 [4096, 1024], P(('head', 'blk'))
- grad_scale_attn: float32 [256, 1024], P(('head', 'blk'))
- grad_scale_mlp: float32 [256, 1024], P(('head', 'blk'))
The draws below stay inside these ranges and needn't reach their ends.
All inputs are finite; a program needn't handle non-finite values.
Results may differ from the reference program's by a relative error of at most 0.017.
Values may be sent and summed in bfloat16 or wider, within the bound.
A program may use at most 256 MiB of HBM per device.

```python
import jax
import jax.numpy as jnp
from jax import lax

D = 1024
HEADS = 16
HEAD_DIM = 64
FF = 4096
TE = 256
STEPS = 64
SEQS = 2
SEQ_LEN = 2048


def touch_ends(entries, rng, low, top_value):
    dims = entries.shape
    index_at = [jax.random.randint(jax.random.fold_in(rng, axis), (), 0, dims[axis]) for axis in range(len(dims))]
    entries = entries.at[tuple(index_at)].set(low)
    longest = dims.index(max(dims))
    index_at[longest] = (index_at[longest] + 1) % dims[longest]
    return entries.at[tuple(index_at)].set(top_value)


def shard_levels(stream_key, dims, shards, smallest, top_value):
    def one(axis_at, blocks):
        heights = jax.random.uniform(jax.random.fold_in(jax.random.fold_in(stream_key, 6), axis_at), (blocks,), jnp.float32, smallest / len(shards), top_value / len(shards))
        return jnp.repeat(jnp.exp(heights), dims[axis_at] // blocks).reshape((-1,) + (1,) * (len(dims) - axis_at - 1))

    factor_of = one(*shards[0])
    for cut in shards[1:]:
        factor_of = factor_of * one(*cut)
    return factor_of


def centred(rng, dims, deviation, most, pieces=(), held_as=jnp.bfloat16):
    drawn = deviation * jax.random.normal(rng, dims, jnp.float32)
    if pieces:
        drawn = drawn * shard_levels(rng, dims, pieces, -0.22, 0.18)
    return jnp.clip(drawn, -most, most).astype(held_as)


def setup_inputs(seed: int = 0) -> dict:
    keys = jax.random.split(jax.random.key(seed), 12)
    return {
        "tokens": centred(keys[0], (SEQS, SEQ_LEN, D), 1.0, 6.0, ((1, 32),)),
        "positions": touch_ends(jax.random.randint(keys[1], (SEQS, SEQ_LEN), 0, SEQ_LEN), jax.random.fold_in(keys[1], 1), 0, SEQ_LEN - 1).astype(jnp.int32),
        "time_index": jax.random.randint(keys[2], (SEQS,), 0, STEPS).astype(jnp.int32),
        "time_table": centred(keys[3], (STEPS, TE), 1.0, 6.0, (), jnp.float32),
        "w_qkv": centred(keys[4], (D, 3 * D), (3 * D // 4) ** -0.5, 0.21875, ((0, 32),)),
        "w_out": centred(keys[5], (D, D), (D // 256) ** -0.5, 3.0, ((0, 32),)),
        "w_up": centred(keys[6], (D, FF), D ** -0.5, 0.1875, ((0, 32),)),
        "w_down": centred(keys[7], (FF, D), FF ** -0.5, 0.09375, ((0, 32),)),
        "scale_attn": centred(keys[8], (TE, D), 0.03125, 0.19921875, ((0, 32),)),
        "scale_mlp": centred(keys[9], (TE, D), 0.03125, 0.19921875, ((0, 32),)),
        "cotangent": centred(keys[10], (SEQS, SEQ_LEN, D), 1.0, 6.0, ((1, 32),)),
    }


NORM_EPSILON = 1e-05
PRECISE = lax.Precision.HIGHEST

@jax.custom_vjp
def low(v):
    return lax.optimization_barrier(v.astype(jnp.bfloat16)).astype(jnp.float32)

@jax.custom_vjp
def low_back(v):
    return v

def low_keep(v):
    return (low(v), None)

def low_pass(kept, grad):
    return (grad,)

def back_keep(v):
    return (v, None)

def back_low(kept, grad):
    return (low(grad),)
low.defvjp(low_keep, low_pass)
low_back.defvjp(back_keep, back_low)

def layer_norm(value, scale):
    centered = value - lax.optimization_barrier(jnp.mean(value, axis=-1, keepdims=True))
    variance = lax.optimization_barrier(jnp.mean(centered * centered, axis=-1, keepdims=True))
    return centered * lax.rsqrt(variance + NORM_EPSILON) * scale

def rotate(value, cosine_table, sine_table):
    half_dim = value.shape[-1] // 2
    first_half = value[..., :half_dim]
    second_half = value[..., half_dim:]
    return jnp.concatenate([first_half * cosine_table - second_half * sine_table, second_half * cosine_table + first_half * sine_table], axis=-1)

def rotary_tables(positions):
    half_dim = HEAD_DIM // 2
    frequency = 10000.0 ** (-jnp.arange(half_dim, dtype=jnp.float32) / half_dim)
    turned = positions.astype(jnp.float32)[:, :, None, None] * frequency
    return (jnp.cos(turned), jnp.sin(turned))

def attend_rows(query_rows, key_all, value_all):
    scores = low_back(0.125 * jnp.einsum('qhd,khd->hqk', query_rows, key_all, precision=PRECISE))
    row_top = lax.optimization_barrier(jnp.max(scores, axis=-1, keepdims=True))
    weights = jnp.exp(scores - row_top)
    row_sum = lax.optimization_barrier(jnp.sum(weights, axis=-1))
    mixed = jnp.einsum('hqk,khd->qhd', low(weights), value_all, precision=PRECISE)
    return mixed / jnp.transpose(row_sum)[:, :, None]

def per_sequence(items):
    query_seq, key_seq, value_seq = items
    block_rows = min(512, SEQ_LEN)
    blocks = query_seq.reshape(SEQ_LEN // block_rows, block_rows, HEADS, HEAD_DIM)
    mixed = lax.map(jax.checkpoint(lambda rows_block: attend_rows(rows_block, key_seq, value_seq)), blocks)
    return mixed.reshape(SEQ_LEN, HEADS, HEAD_DIM)

def forward(token_float, weight_qkv, weight_out, weight_up, weight_down, weight_scale_attn, weight_scale_mlp, time_embed, cosine_table, sine_table):
    scale_one = 1.0 + jnp.dot(time_embed, weight_scale_attn, precision=PRECISE)
    normed = low(layer_norm(token_float, scale_one[:, None, :]))
    projected = low_back(jnp.einsum('std,de->ste', normed, weight_qkv, precision=PRECISE))
    projected = projected.reshape(SEQS, SEQ_LEN, 3, HEADS, HEAD_DIM)
    query_all = low_back(low(rotate(projected[:, :, 0], cosine_table, sine_table)))
    key_all = low_back(low(rotate(projected[:, :, 1], cosine_table, sine_table)))
    value_all = low_back(low(projected[:, :, 2]))
    mixed = lax.map(per_sequence, (query_all, key_all, value_all))
    attended = low_back(low(mixed.reshape(SEQS, SEQ_LEN, D)))
    branch = low_back(jnp.einsum('std,de->ste', attended, weight_out, precision=PRECISE))
    middle = token_float + branch
    scale_two = 1.0 + jnp.dot(time_embed, weight_scale_mlp, precision=PRECISE)
    normed_two = low(layer_norm(middle, scale_two[:, None, :]))
    hidden = low_back(jnp.einsum('std,df->stf', normed_two, weight_up, precision=PRECISE))
    active = low(jax.nn.gelu(hidden, approximate=False))
    return middle + jnp.einsum('stf,fd->std', active, weight_down, precision=PRECISE)

def reference(tokens, positions, time_index, time_table, w_qkv, w_out, w_up, w_down, scale_attn, scale_mlp, cotangent):
    picker = jax.nn.one_hot(time_index, STEPS, dtype=jnp.float32)
    time_embed = jnp.dot(picker, time_table, precision=PRECISE)
    cosine_table, sine_table = rotary_tables(positions)

    def closed(token_float, weight_qkv, weight_out, weight_up, weight_down, weight_scale_attn, weight_scale_mlp):
        return forward(token_float, weight_qkv, weight_out, weight_up, weight_down, weight_scale_attn, weight_scale_mlp, time_embed, cosine_table, sine_table)
    result, pullback = jax.vjp(closed, tokens.astype(jnp.float32), w_qkv.astype(jnp.float32), w_out.astype(jnp.float32), w_up.astype(jnp.float32), w_down.astype(jnp.float32), scale_attn.astype(jnp.float32), scale_mlp.astype(jnp.float32))
    grads = pullback(cotangent.astype(jnp.float32))
    return (result.astype(jnp.bfloat16), grads[0], grads[1], grads[2], grads[3], grads[4], grads[5], grads[6])
```

```python
import math

import jax
import jax.numpy as jnp
from jax import lax
from jax.sharding import PartitionSpec as P

HEADS = 16
HEAD_DIM = 64


NORM_EPSILON = 1e-05
PRECISE = lax.Precision.HIGHEST
START_TOP = -1e30
SCORE_SCALE = 0.125


def shifted(value, axis, steps):
    count = lax.axis_size(axis)
    pairs = [(source, (source + steps) % count) for source in range(count)]
    return lax.ppermute(value, axis, pairs)


def layer_norm(value, scale):
    centered = value - jnp.mean(value, axis=-1, keepdims=True)
    variance = jnp.mean(centered * centered, axis=-1, keepdims=True)
    return centered * lax.rsqrt(variance + NORM_EPSILON) * scale


def rotate(value, cosine_table, sine_table):
    half_dim = value.shape[-1] // 2
    first_half = value[..., :half_dim]
    second_half = value[..., half_dim:]
    return jnp.concatenate(
        [
            first_half * cosine_table - second_half * sine_table,
            second_half * cosine_table + first_half * sine_table,
        ],
        axis=-1,
    )


def rotary_tables(positions, head_dim):
    half_dim = head_dim // 2
    frequency = 10000.0 ** (-jnp.arange(half_dim, dtype=jnp.float32) / half_dim)
    turned = positions.astype(jnp.float32)[:, :, None, None] * frequency
    return (jnp.cos(turned), jnp.sin(turned))


def contract_rows(left, right):
    return lax.dot_general(
        left, right, (((0,), (0,)), ((), ())), preferred_element_type=jnp.float32
    )


def contract_cols(left, right):
    return lax.dot_general(
        left, right, (((1,), (1,)), ((), ())), preferred_element_type=jnp.float32
    )


def attend_step(running, query_block, key_block, value_block):
    row_top, row_sum, accum = running
    scores = (
        jnp.einsum("sqhd,skhd->sqhk", query_block, key_block, preferred_element_type=jnp.float32)
        * SCORE_SCALE
    )
    new_top = jnp.maximum(row_top, jnp.max(scores, axis=-1))
    shrink = jnp.exp(row_top - new_top)
    weights = jnp.exp(scores - new_top[..., None])
    row_sum = row_sum * shrink + jnp.sum(weights, axis=-1)
    accum = accum * shrink[..., None] + jnp.einsum(
        "sqhk,skhd->sqhd",
        weights.astype(jnp.bfloat16),
        value_block,
        preferred_element_type=jnp.float32,
    )
    return (new_top, row_sum, accum)


def back_step(query_block, key_block, value_block, grad_block, log_total, delta):
    scores = (
        jnp.einsum("sqhd,skhd->sqhk", query_block, key_block, preferred_element_type=jnp.float32)
        * SCORE_SCALE
    )
    probs = jnp.exp(scores - log_total[..., None])
    grad_values = jnp.einsum(
        "sqhk,sqhd->skhd",
        probs.astype(jnp.bfloat16),
        grad_block,
        preferred_element_type=jnp.float32,
    )
    grad_probs = jnp.einsum(
        "sqhd,skhd->sqhk", grad_block, value_block, preferred_element_type=jnp.float32
    )
    grad_scores = (probs * (grad_probs - delta[..., None])).astype(jnp.bfloat16)
    grad_query = jnp.einsum(
        "sqhk,skhd->sqhd", grad_scores, key_block, preferred_element_type=jnp.float32
    )
    grad_keys = jnp.einsum(
        "sqhk,sqhd->skhd", grad_scores, query_block, preferred_element_type=jnp.float32
    )
    return (grad_query, grad_keys, grad_values)


def general(
    tokens,
    positions,
    time_index,
    time_table,
    w_qkv,
    w_out,
    w_up,
    w_down,
    scale_attn,
    scale_mlp,
    cotangent,
):
    seq_count, row_count, model_width = tokens.shape
    group_count = lax.axis_size("head")
    local_heads = HEADS // group_count
    feature_width = local_heads * HEAD_DIM
    flat_rows = seq_count * row_count
    gathered = (
        lax.all_gather(w_qkv, ("head", "blk"), axis=0, tiled=True),
        lax.all_gather(w_out, ("head", "blk"), axis=0, tiled=True),
        lax.all_gather(w_up, ("head", "blk"), axis=0, tiled=True),
        lax.all_gather(w_down, ("head", "blk"), axis=0, tiled=True),
        lax.all_gather(scale_attn, ("head", "blk"), axis=0, tiled=True),
        lax.all_gather(scale_mlp, ("head", "blk"), axis=0, tiled=True),
    )
    full_qkv, full_out, full_up, full_down, full_scale_attn, full_scale_mlp = gathered
    step_count = time_table.shape[0]
    picker = (time_index[:, None] == jnp.arange(step_count, dtype=jnp.int32)[None, :]).astype(
        jnp.float32
    )
    time_embed = jnp.dot(picker, time_table, precision=PRECISE)
    scale_one = 1.0 + jnp.dot(time_embed, full_scale_attn.astype(jnp.float32), precision=PRECISE)
    scale_two = 1.0 + jnp.dot(time_embed, full_scale_mlp.astype(jnp.float32), precision=PRECISE)
    token_float = tokens.astype(jnp.float32)
    normed = (
        layer_norm(token_float, scale_one[:, None, :])
        .astype(jnp.bfloat16)
        .reshape(flat_rows, model_width)
    )
    projected = jnp.dot(normed, full_qkv, preferred_element_type=jnp.float32).reshape(
        seq_count, row_count, 3, HEADS, HEAD_DIM
    )
    cosine_table, sine_table = rotary_tables(positions, HEAD_DIM)
    query_tok = rotate(projected[:, :, 0], cosine_table, sine_table)
    keys_tok = rotate(projected[:, :, 1], cosine_table, sine_table)
    packed = (
        jnp.stack([query_tok, keys_tok, projected[:, :, 2]], axis=2)
        .reshape(seq_count, row_count, 3, model_width)
        .astype(jnp.bfloat16)
    )
    regrouped = lax.all_to_all(packed, "head", split_axis=3, concat_axis=1, tiled=True)
    block_len = regrouped.shape[1]
    local_query = regrouped[:, :, 0].reshape(seq_count, block_len, local_heads, HEAD_DIM)
    local_keys = regrouped[:, :, 1]
    local_values = regrouped[:, :, 2]
    start_state = (
        jnp.full((seq_count, block_len, local_heads), START_TOP, jnp.float32),
        jnp.zeros((seq_count, block_len, local_heads), jnp.float32),
        jnp.zeros((seq_count, block_len, local_heads, HEAD_DIM), jnp.float32),
    )
    key_piece = lax.all_gather(local_keys, "blk", axis=1, tiled=True)
    value_piece = lax.all_gather(local_values, "blk", axis=1, tiled=True)
    piece_len = key_piece.shape[1]
    step_len = math.gcd(piece_len, block_len)

    def one_block(index, state):
        key_block = lax.dynamic_slice_in_dim(key_piece, index * step_len, step_len, 1).reshape(
            seq_count, step_len, local_heads, HEAD_DIM
        )
        value_block = lax.dynamic_slice_in_dim(value_piece, index * step_len, step_len, 1).reshape(
            seq_count, step_len, local_heads, HEAD_DIM
        )
        return attend_step(state, local_query, key_block, value_block)

    row_top, row_sum, accum = lax.fori_loop(0, piece_len // step_len, one_block, start_state)
    mixed = accum / row_sum[..., None]
    log_total = row_top + jnp.log(row_sum)
    attended_heads = mixed.astype(jnp.bfloat16).reshape(seq_count, block_len, feature_width)
    attended = lax.all_to_all(
        attended_heads, "head", split_axis=1, concat_axis=2, tiled=True
    ).reshape(flat_rows, model_width)
    branch = jnp.dot(attended, full_out, preferred_element_type=jnp.float32)
    middle = token_float + branch.reshape(seq_count, row_count, model_width)
    normed_two = (
        layer_norm(middle, scale_two[:, None, :])
        .astype(jnp.bfloat16)
        .reshape(flat_rows, model_width)
    )
    hidden = jnp.dot(normed_two, full_up, preferred_element_type=jnp.float32)
    active = jax.nn.gelu(hidden, approximate=False).astype(jnp.bfloat16)
    result = middle.reshape(flat_rows, model_width) + jnp.dot(
        active, full_down, preferred_element_type=jnp.float32
    )
    output = result.astype(jnp.bfloat16).reshape(seq_count, row_count, model_width)
    back_qkv, back_out, back_up, back_down = (
        lax.all_gather(w_qkv, ("head", "blk"), axis=0, tiled=True),
        lax.all_gather(w_out, ("head", "blk"), axis=0, tiled=True),
        lax.all_gather(w_up, ("head", "blk"), axis=0, tiled=True),
        lax.all_gather(w_down, ("head", "blk"), axis=0, tiled=True),
    )
    grad_out = cotangent.reshape(flat_rows, model_width)
    grad_active = contract_cols(grad_out, back_down)
    grad_w_down = contract_rows(active, grad_out)
    gelu_value, gelu_pull = jax.vjp(lambda entry: jax.nn.gelu(entry, approximate=False), hidden)
    grad_hidden = gelu_pull(grad_active)[0].astype(jnp.bfloat16)
    grad_w_up = contract_rows(normed_two, grad_hidden)
    grad_normed_two = contract_cols(grad_hidden, back_up).reshape(seq_count, row_count, model_width)
    norm_value, norm_pull = jax.vjp(layer_norm, middle, scale_two[:, None, :])
    grad_middle_norm, grad_scale_two = norm_pull(grad_normed_two)
    grad_middle = cotangent.astype(jnp.float32) + grad_middle_norm
    grad_scale_mlp = jnp.dot(time_embed.T, grad_scale_two[:, 0, :], precision=PRECISE)
    grad_branch = grad_middle.reshape(flat_rows, model_width).astype(jnp.bfloat16)
    grad_w_out = contract_rows(attended, grad_branch)
    grad_attended = (
        contract_cols(grad_branch, back_out)
        .astype(jnp.bfloat16)
        .reshape(seq_count, row_count, model_width)
    )
    grad_heads = lax.all_to_all(
        grad_attended, "head", split_axis=2, concat_axis=1, tiled=True
    ).reshape(seq_count, block_len, local_heads, HEAD_DIM)
    delta = jnp.sum(grad_heads.astype(jnp.float32) * mixed, axis=-1)

    def turn(index, state):
        key_now, value_now, grad_keys_now, grad_values_now, grad_query_sum = state
        grad_query, grad_keys, grad_values = back_step(
            local_query,
            key_now.reshape(seq_count, block_len, local_heads, HEAD_DIM),
            value_now.reshape(seq_count, block_len, local_heads, HEAD_DIM),
            grad_heads,
            log_total,
            delta,
        )
        moved_keys, moved_values = shifted((key_now, value_now), "blk", 1)
        moved_grad_keys, moved_grad_values = (
            shifted(
                (grad_keys_now + grad_keys.reshape(seq_count, block_len, feature_width)).astype(
                    jnp.bfloat16
                ),
                "blk",
                1,
            ).astype(jnp.float32),
            shifted(
                (grad_values_now + grad_values.reshape(seq_count, block_len, feature_width)).astype(
                    jnp.bfloat16
                ),
                "blk",
                1,
            ).astype(jnp.float32),
        )
        return (
            moved_keys,
            moved_values,
            moved_grad_keys,
            moved_grad_values,
            grad_query_sum + grad_query,
        )

    zero_kv = jnp.zeros((seq_count, block_len, feature_width), jnp.float32)
    begin = (
        local_keys,
        local_values,
        zero_kv,
        zero_kv,
        jnp.zeros((seq_count, block_len, local_heads, HEAD_DIM), jnp.float32),
    )
    final_state = lax.fori_loop(0, lax.axis_size("blk"), turn, begin)
    grad_keys_own = final_state[2]
    grad_values_own = final_state[3]
    grad_query_all = final_state[4]
    stacked = jnp.stack(
        [
            grad_query_all.reshape(seq_count, block_len, feature_width) * SCORE_SCALE,
            grad_keys_own * SCORE_SCALE,
            grad_values_own,
        ],
        axis=2,
    ).astype(jnp.bfloat16)
    returned = lax.all_to_all(stacked, "head", split_axis=1, concat_axis=3, tiled=True)
    grad_query_tok = (
        returned[:, :, 0].astype(jnp.float32).reshape(seq_count, row_count, HEADS, HEAD_DIM)
    )
    grad_keys_tok = (
        returned[:, :, 1].astype(jnp.float32).reshape(seq_count, row_count, HEADS, HEAD_DIM)
    )
    grad_values_tok = (
        returned[:, :, 2].astype(jnp.float32).reshape(seq_count, row_count, HEADS, HEAD_DIM)
    )
    grad_projected = (
        jnp.stack(
            [
                rotate(grad_query_tok, cosine_table, -sine_table),
                rotate(grad_keys_tok, cosine_table, -sine_table),
                grad_values_tok,
            ],
            axis=2,
        )
        .reshape(flat_rows, 3 * model_width)
        .astype(jnp.bfloat16)
    )
    grad_w_qkv = contract_rows(normed, grad_projected)
    grad_normed = contract_cols(grad_projected, back_qkv).reshape(seq_count, row_count, model_width)
    first_value, first_pull = jax.vjp(layer_norm, token_float, scale_one[:, None, :])
    grad_token_norm, grad_scale_one = first_pull(grad_normed)
    grad_tokens = grad_middle + grad_token_norm
    grad_scale_attn = jnp.dot(time_embed.T, grad_scale_one[:, 0, :], precision=PRECISE)
    shards = (
        lax.psum_scatter(grad_w_qkv, ("head", "blk"), scatter_dimension=0, tiled=True),
        lax.psum_scatter(grad_w_out, ("head", "blk"), scatter_dimension=0, tiled=True),
        lax.psum_scatter(grad_w_up, ("head", "blk"), scatter_dimension=0, tiled=True),
        lax.psum_scatter(grad_w_down, ("head", "blk"), scatter_dimension=0, tiled=True),
        lax.psum_scatter(grad_scale_attn, ("head", "blk"), scatter_dimension=0, tiled=True),
        lax.psum_scatter(grad_scale_mlp, ("head", "blk"), scatter_dimension=0, tiled=True),
    )
    return (output, grad_tokens, shards[0], shards[1], shards[2], shards[3], shards[4], shards[5])


EPS = NORM_EPSILON
BF = jnp.bfloat16
F32 = jnp.float32


def norm_stats(value):
    centered = value - jnp.mean(value, axis=-1, keepdims=True)
    spread = lax.rsqrt(jnp.mean(centered * centered, axis=-1, keepdims=True) + EPS)
    return centered * spread, spread


def norm_back(unit, spread, grad, scale):
    scaled = grad * scale
    return spread * (
        scaled
        - jnp.mean(scaled, axis=-1, keepdims=True)
        - unit * jnp.mean(scaled * unit, axis=-1, keepdims=True)
    )


def pack_half(value):
    lead, width = value.shape[:-2], value.shape[-1]
    rows = value.shape[-2]
    axis = value.ndim - 2
    return jnp.concatenate(
        [
            lax.slice_in_dim(value, 0, rows // 2, axis=axis),
            lax.slice_in_dim(value, rows // 2, rows, axis=axis),
        ],
        axis=-1,
    )


def unpack_half(value):
    width = value.shape[-1] // 2
    return jnp.concatenate([value[..., :width], value[..., width:]], axis=-2)


def turn(value, table, sign):
    cosine = table[..., :32]
    sine = table[..., 32:64] * sign
    first, second = value[..., :32], value[..., 32:]
    return jnp.concatenate(
        [first * cosine - second * sine, second * cosine + first * sine], axis=-1
    )


def phase_one(tokens, table, wq_parts, scale_parts):
    token_all = lax.all_gather(tokens, "head", axis=0)
    table_all = lax.all_gather(table, "head", axis=0)
    scales = lax.psum(scale_parts, ("head", "blk"))
    wq = lax.all_to_all(wq_parts, "head", 0, 0, tiled=True)
    wq = jnp.swapaxes(lax.all_gather(wq, "blk", axis=0), 0, 1).reshape(1024, 768)
    unit, _ = norm_stats(token_all.astype(F32))
    scale_one = 1.0 + scales[:2]
    normed = (unit * scale_one[None, :, None, :]).astype(BF).reshape(512, 1024)
    proj = jnp.dot(normed, wq, preferred_element_type=F32).reshape(4, 2, 64, 768)
    tab = table_all.reshape(4, 2, 64, 1, 64)
    pairs = proj[..., :512].reshape(4, 2, 64, 4, 128)
    keys = turn(pairs[..., :64], tab, 1.0)
    query = turn(proj[..., 512:].reshape(4, 2, 64, 4, 64), tab, 1.0)
    kv = jnp.concatenate([keys, pairs[..., 64:]], axis=-1).astype(BF)
    kv = jnp.transpose(kv, (1, 3, 0, 2, 4))
    query = pack_half(jnp.transpose(query.astype(BF), (1, 3, 0, 2, 4)))
    tiles = jnp.concatenate([kv, query], axis=-2).reshape(8, 4, 96, 128)
    tiles = jnp.swapaxes(lax.all_to_all(tiles, "blk", 0, 0, tiled=True), 0, 1)
    return tiles, normed, wq, scales, table_all.reshape(512, 64)


def split_tiles(tiles):
    kv = tiles[:, :, :64].reshape(2048, 128)
    query = unpack_half(tiles[:, :, 64:]).reshape(2048, 64)
    return query, kv[:, :64], kv[:, 64:]


def to_all(tiles):
    return lax.all_to_all(
        tiles.reshape(32, 32, 128), ("head", "blk"), 0, 0, tiled=True
    ).reshape(4, 8, 32, 128)


def phase_two(tiles, up_parts, w_down, w_out, cotangent):
    query, keys, values = split_tiles(tiles)
    scores = SCORE_SCALE * contract_cols(keys, query)
    top = jnp.max(scores, axis=0, keepdims=True)
    weights = jnp.exp(scores - top)
    row_sum = jnp.sum(weights, axis=0, keepdims=True)
    mixed = contract_rows(values, weights.astype(BF)) / row_sum
    lse = top + jnp.log(row_sum)
    attended = pack_half(jnp.transpose(mixed).astype(BF).reshape(4, 8, 64, 64))
    received = to_all(attended)
    up = lax.all_to_all(up_parts, "head", 0, 0, tiled=True)
    up = jnp.swapaxes(lax.all_gather(up, "blk", axis=0), 0, 1).reshape(1024, 1024)
    down = lax.all_gather(w_down, "blk", axis=0, tiled=True)
    out = lax.all_gather(w_out, ("head", "blk"), axis=0, tiled=True)
    cot_all = lax.all_gather(cotangent, "head", axis=0).reshape(512, 1024)
    return mixed, lse, received, up, down, out, cot_all


def scatter_head(partial):
    parts = lax.all_to_all(
        partial.astype(BF).reshape(4, 128, 1024), "head", 0, 0, tiled=True
    )
    return jnp.sum(parts.astype(F32), axis=0)


def phase_three(received, tokens, out, up, down, cot_all, cotangent, scales):
    attended = unpack_half(received).reshape(4, 2, 4, 64, 64)
    attended = jnp.transpose(attended, (1, 3, 0, 2, 4)).reshape(128, 1024)
    middle = tokens.reshape(128, 1024).astype(F32) + jnp.dot(
        attended, out, preferred_element_type=F32
    )
    unit, spread = norm_stats(middle)
    scale_two = jnp.repeat(1.0 + scales[2:4], 64, axis=0)
    normed_two = (unit * scale_two).astype(BF)
    normed_all = lax.all_gather(normed_two, "head", axis=0, tiled=True)
    hidden = jnp.dot(normed_all, up, preferred_element_type=F32)
    cdf = 0.5 * (1.0 + lax.erf(hidden * math.sqrt(0.5)))
    active = (hidden * cdf).astype(BF)
    out_partial = jnp.dot(active, down, preferred_element_type=F32).astype(BF)
    grad_active = contract_cols(cot_all, down)
    slope = cdf + hidden * jnp.exp(-0.5 * hidden * hidden) * (1.0 / math.sqrt(2 * math.pi))
    grad_hidden = (grad_active * slope).astype(BF)
    grad_down = contract_rows(active, cot_all).astype(BF)
    grad_up = contract_rows(normed_all, grad_hidden).astype(BF)
    grad_normed = scatter_head(contract_cols(grad_hidden, up))
    grad_middle = cotangent.reshape(128, 1024).astype(F32) + norm_back(
        unit, spread, grad_normed, scale_two
    )
    sums = jnp.sum((grad_normed * unit).reshape(2, 64, 1024), axis=1)
    branch = grad_middle.astype(BF)
    grad_out = contract_rows(attended, branch).astype(BF)
    grad_att = contract_cols(branch, out).astype(BF).reshape(2, 64, 4, 4, 64)
    grad_att = pack_half(jnp.transpose(grad_att, (2, 0, 3, 1, 4)))
    grad_rx = to_all(grad_att)
    return grad_rx, grad_middle, middle, out_partial, grad_down, grad_up, grad_out, sums


def sum_parts(parts):
    return jnp.sum(parts.astype(F32), axis=0)


def phase_four(tiles, grad_rx, mixed, lse, out_partial, middle, grad_down, grad_up, grad_out):
    query, keys, values = split_tiles(tiles)
    grad = unpack_half(grad_rx).reshape(2048, 64)
    delta = jnp.sum(jnp.transpose(grad).astype(F32) * mixed, axis=0, keepdims=True)
    probs = jnp.exp(SCORE_SCALE * contract_cols(keys, query) - lse)
    grad_values = jnp.dot(probs.astype(BF), grad, preferred_element_type=F32)
    grad_scores = (probs * (contract_cols(values, grad) - delta)).astype(BF)
    grad_keys = SCORE_SCALE * jnp.dot(grad_scores, query, preferred_element_type=F32)
    grad_query = SCORE_SCALE * contract_rows(grad_scores, keys)
    kv = jnp.concatenate([grad_keys, grad_values], axis=-1).astype(BF).reshape(4, 8, 64, 128)
    packed = pack_half(grad_query.astype(BF).reshape(4, 8, 64, 64))
    back = jnp.swapaxes(jnp.concatenate([kv, packed], axis=-2), 0, 1)
    back = lax.all_to_all(back, "blk", 0, 0, tiled=True)
    output = (middle + scatter_head(out_partial)).astype(BF).reshape(2, 64, 1024)
    down = sum_parts(lax.all_to_all(grad_down.reshape(8, 128, 1024), "blk", 0, 0, tiled=True))
    up = jnp.swapaxes(grad_up.reshape(4, 8, 32, 1024), 0, 1)
    up = sum_parts(lax.all_to_all(up, "blk", 0, 0, tiled=True))
    up = lax.all_to_all(up.astype(BF), "head", 0, 0, tiled=True).astype(F32)
    up = jnp.swapaxes(up, 0, 1).reshape(32, 4096)
    out = jnp.swapaxes(grad_out.reshape(4, 8, 32, 1024), 0, 1)
    out = sum_parts(lax.all_to_all(out, "blk", 0, 0, tiled=True))
    out = sum_parts(lax.all_to_all(out.astype(BF), "head", 0, 0, tiled=True))
    return back, output, down, up, out


def phase_five(back, table_all, normed, wq, tokens, scales, grad_middle, sums):
    kv = back[:, :, :64].reshape(2, 4, 4, 64, 128)
    query = unpack_half(back[:, :, 64:]).reshape(2, 4, 4, 64, 64)
    kv = jnp.transpose(kv, (2, 0, 3, 1, 4)).astype(F32)
    query = jnp.transpose(query, (2, 0, 3, 1, 4)).astype(F32)
    tab = table_all.reshape(4, 2, 64, 1, 64)
    keys = turn(kv[..., :64], tab, -1.0)
    query = turn(query, tab, -1.0)
    kv = jnp.concatenate([keys, kv[..., 64:]], axis=-1).reshape(512, 512)
    grad_proj = jnp.concatenate([kv, query.reshape(512, 256)], axis=-1).astype(BF)
    grad_wq = contract_rows(normed, grad_proj).astype(BF)
    grad_normed = scatter_head(contract_cols(grad_proj, wq))
    unit, spread = norm_stats(tokens.reshape(128, 1024).astype(F32))
    scale_one = jnp.repeat(1.0 + scales[:2], 64, axis=0)
    grad_tokens = grad_middle + norm_back(unit, spread, grad_normed, scale_one)
    first = jnp.sum((grad_normed * unit).reshape(2, 64, 1024), axis=1)
    total = lax.psum(jnp.concatenate([first, sums], axis=0), ("head", "blk"))
    grad_wq = jnp.swapaxes(grad_wq.reshape(4, 8, 32, 768), 0, 1)
    grad_wq = sum_parts(lax.all_to_all(grad_wq, "blk", 0, 0, tiled=True))
    grad_wq = lax.all_to_all(grad_wq.astype(BF), "head", 0, 0, tiled=True).astype(F32)
    return grad_tokens.reshape(2, 64, 1024), grad_wq, total


def blocked(
    tokens,
    positions,
    time_index,
    time_table,
    w_qkv,
    w_out,
    w_up,
    w_down,
    scale_attn,
    scale_mlp,
    cotangent,
):
    place = lax.axis_index(("head", "blk"))
    embed = time_table[time_index]
    embed_own = lax.dynamic_slice_in_dim(embed, place * 8, 8, 1)
    scale_parts = jnp.concatenate(
        [
            jnp.dot(embed_own, scale_attn.astype(F32), precision=PRECISE),
            jnp.dot(embed_own, scale_mlp.astype(F32), precision=PRECISE),
        ],
        axis=0,
    )
    cosine, sine = rotary_tables(positions, HEAD_DIM)
    table = jnp.concatenate([cosine[:, :, 0], sine[:, :, 0]], axis=-1).reshape(128, 64)
    wide = w_qkv.reshape(32, 3, 4, 4, 64)
    kv_cols = jnp.stack([wide[:, 1], wide[:, 2]], axis=3).reshape(32, 4, 512)
    wq_parts = jnp.concatenate([kv_cols, wide[:, 0].reshape(32, 4, 256)], axis=-1)
    wq_parts = jnp.swapaxes(wq_parts, 0, 1)
    up_parts = jnp.swapaxes(w_up.reshape(32, 4, 1024), 0, 1)
    tiles, normed, wq, scales, table_all = phase_one(tokens, table, wq_parts, scale_parts)
    mixed, lse, received, up, down, out, cot_all = phase_two(
        tiles, up_parts, w_down, w_out, cotangent
    )
    grad_rx, grad_middle, middle, out_partial, grad_down, grad_up, grad_out, sums = phase_three(
        received, tokens, out, up, down, cot_all, cotangent, scales
    )
    back, output, down_own, up_own, out_own = phase_four(
        tiles, grad_rx, mixed, lse, out_partial, middle, grad_down, grad_up, grad_out
    )
    grad_tokens, grad_wq, total = phase_five(
        back, table_all, normed, wq, tokens, scales, grad_middle, sums
    )
    kv_cols = grad_wq[:, :, :512].reshape(4, 32, 4, 2, 64)
    wide = jnp.stack(
        [grad_wq[:, :, 512:].reshape(4, 32, 4, 64), kv_cols[:, :, :, 0], kv_cols[:, :, :, 1]],
        axis=0,
    )
    qkv_own = jnp.transpose(wide, (2, 0, 1, 3, 4)).reshape(32, 3072)
    grad_attn = contract_rows_precise(embed_own, total[:2])
    grad_mlp = contract_rows_precise(embed_own, total[2:])
    return output, grad_tokens, qkv_own, out_own, up_own, down_own, grad_attn, grad_mlp


def contract_rows_precise(left, right):
    return lax.dot_general(
        left, right, (((0,), (0,)), ((), ())), precision=PRECISE, preferred_element_type=F32
    )


def solution(mesh):
    fits = mesh.shape["head"] == 4 and mesh.shape["blk"] == 8
    placed = (
        P(None, ("head", "blk"), None),
        P(None, ("head", "blk")),
        P(),
        P(),
        P(("head", "blk"), None),
        P(("head", "blk"), None),
        P(("head", "blk"), None),
        P(("head", "blk"), None),
        P(("head", "blk"), None),
        P(("head", "blk"), None),
        P(None, ("head", "blk"), None),
    )
    return jax.shard_map(
        blocked if fits else general,
        mesh=mesh,
        in_specs=placed,
        out_specs=(
            P(None, ("head", "blk"), None),
            P(None, ("head", "blk"), None),
            P(("head", "blk"), None),
            P(("head", "blk"), None),
            P(("head", "blk"), None),
            P(("head", "blk"), None),
            P(("head", "blk"), None),
            P(("head", "blk"), None),
        ),
        check_vma=False,
    )
```

```python
import math

import jax
import jax.numpy as jnp
from jax import lax
from jax.experimental import pallas as pl
from jax.experimental.pallas import tpu as pltpu
from jax.sharding import PartitionSpec as P

HEADS = 16
HEAD_DIM = 64


NORM_EPSILON = 1e-05
PRECISE = lax.Precision.HIGHEST
START_TOP = -1e30
SCORE_SCALE = 0.125


def shifted(value, axis, steps):
    count = lax.axis_size(axis)
    pairs = [(source, (source + steps) % count) for source in range(count)]
    return lax.ppermute(value, axis, pairs)


def layer_norm(value, scale):
    centered = value - jnp.mean(value, axis=-1, keepdims=True)
    variance = jnp.mean(centered * centered, axis=-1, keepdims=True)
    return centered * lax.rsqrt(variance + NORM_EPSILON) * scale


def rotate(value, cosine_table, sine_table):
    half_dim = value.shape[-1] // 2
    first_half = value[..., :half_dim]
    second_half = value[..., half_dim:]
    return jnp.concatenate(
        [
            first_half * cosine_table - second_half * sine_table,
            second_half * cosine_table + first_half * sine_table,
        ],
        axis=-1,
    )


def rotary_tables(positions, head_dim):
    half_dim = head_dim // 2
    frequency = 10000.0 ** (-jnp.arange(half_dim, dtype=jnp.float32) / half_dim)
    turned = positions.astype(jnp.float32)[:, :, None, None] * frequency
    return (jnp.cos(turned), jnp.sin(turned))


def contract_rows(left, right):
    return lax.dot_general(
        left, right, (((0,), (0,)), ((), ())), preferred_element_type=jnp.float32
    )


def contract_cols(left, right):
    return lax.dot_general(
        left, right, (((1,), (1,)), ((), ())), preferred_element_type=jnp.float32
    )


def attend_step(running, query_block, key_block, value_block):
    row_top, row_sum, accum = running
    scores = (
        jnp.einsum("sqhd,skhd->sqhk", query_block, key_block, preferred_element_type=jnp.float32)
        * SCORE_SCALE
    )
    new_top = jnp.maximum(row_top, jnp.max(scores, axis=-1))
    shrink = jnp.exp(row_top - new_top)
    weights = jnp.exp(scores - new_top[..., None])
    row_sum = row_sum * shrink + jnp.sum(weights, axis=-1)
    accum = accum * shrink[..., None] + jnp.einsum(
        "sqhk,skhd->sqhd",
        weights.astype(jnp.bfloat16),
        value_block,
        preferred_element_type=jnp.float32,
    )
    return (new_top, row_sum, accum)


def back_step(query_block, key_block, value_block, grad_block, log_total, delta):
    scores = (
        jnp.einsum("sqhd,skhd->sqhk", query_block, key_block, preferred_element_type=jnp.float32)
        * SCORE_SCALE
    )
    probs = jnp.exp(scores - log_total[..., None])
    grad_values = jnp.einsum(
        "sqhk,sqhd->skhd",
        probs.astype(jnp.bfloat16),
        grad_block,
        preferred_element_type=jnp.float32,
    )
    grad_probs = jnp.einsum(
        "sqhd,skhd->sqhk", grad_block, value_block, preferred_element_type=jnp.float32
    )
    grad_scores = (probs * (grad_probs - delta[..., None])).astype(jnp.bfloat16)
    grad_query = jnp.einsum(
        "sqhk,skhd->sqhd", grad_scores, key_block, preferred_element_type=jnp.float32
    )
    grad_keys = jnp.einsum(
        "sqhk,sqhd->skhd", grad_scores, query_block, preferred_element_type=jnp.float32
    )
    return (grad_query, grad_keys, grad_values)


def general(
    tokens,
    positions,
    time_index,
    time_table,
    w_qkv,
    w_out,
    w_up,
    w_down,
    scale_attn,
    scale_mlp,
    cotangent,
):
    seq_count, row_count, model_width = tokens.shape
    group_count = lax.axis_size("head")
    local_heads = HEADS // group_count
    feature_width = local_heads * HEAD_DIM
    flat_rows = seq_count * row_count
    gathered = (
        lax.all_gather(w_qkv, ("head", "blk"), axis=0, tiled=True),
        lax.all_gather(w_out, ("head", "blk"), axis=0, tiled=True),
        lax.all_gather(w_up, ("head", "blk"), axis=0, tiled=True),
        lax.all_gather(w_down, ("head", "blk"), axis=0, tiled=True),
        lax.all_gather(scale_attn, ("head", "blk"), axis=0, tiled=True),
        lax.all_gather(scale_mlp, ("head", "blk"), axis=0, tiled=True),
    )
    full_qkv, full_out, full_up, full_down, full_scale_attn, full_scale_mlp = gathered
    step_count = time_table.shape[0]
    picker = (time_index[:, None] == jnp.arange(step_count, dtype=jnp.int32)[None, :]).astype(
        jnp.float32
    )
    time_embed = jnp.dot(picker, time_table, precision=PRECISE)
    scale_one = 1.0 + jnp.dot(time_embed, full_scale_attn.astype(jnp.float32), precision=PRECISE)
    scale_two = 1.0 + jnp.dot(time_embed, full_scale_mlp.astype(jnp.float32), precision=PRECISE)
    token_float = tokens.astype(jnp.float32)
    normed = (
        layer_norm(token_float, scale_one[:, None, :])
        .astype(jnp.bfloat16)
        .reshape(flat_rows, model_width)
    )
    projected = jnp.dot(normed, full_qkv, preferred_element_type=jnp.float32).reshape(
        seq_count, row_count, 3, HEADS, HEAD_DIM
    )
    cosine_table, sine_table = rotary_tables(positions, HEAD_DIM)
    query_tok = rotate(projected[:, :, 0], cosine_table, sine_table)
    keys_tok = rotate(projected[:, :, 1], cosine_table, sine_table)
    packed = (
        jnp.stack([query_tok, keys_tok, projected[:, :, 2]], axis=2)
        .reshape(seq_count, row_count, 3, model_width)
        .astype(jnp.bfloat16)
    )
    regrouped = lax.all_to_all(packed, "head", split_axis=3, concat_axis=1, tiled=True)
    block_len = regrouped.shape[1]
    local_query = regrouped[:, :, 0].reshape(seq_count, block_len, local_heads, HEAD_DIM)
    local_keys = regrouped[:, :, 1]
    local_values = regrouped[:, :, 2]
    start_state = (
        jnp.full((seq_count, block_len, local_heads), START_TOP, jnp.float32),
        jnp.zeros((seq_count, block_len, local_heads), jnp.float32),
        jnp.zeros((seq_count, block_len, local_heads, HEAD_DIM), jnp.float32),
    )
    key_piece = lax.all_gather(local_keys, "blk", axis=1, tiled=True)
    value_piece = lax.all_gather(local_values, "blk", axis=1, tiled=True)
    piece_len = key_piece.shape[1]
    step_len = math.gcd(piece_len, block_len)

    def one_block(index, state):
        key_block = lax.dynamic_slice_in_dim(key_piece, index * step_len, step_len, 1).reshape(
            seq_count, step_len, local_heads, HEAD_DIM
        )
        value_block = lax.dynamic_slice_in_dim(value_piece, index * step_len, step_len, 1).reshape(
            seq_count, step_len, local_heads, HEAD_DIM
        )
        return attend_step(state, local_query, key_block, value_block)

    row_top, row_sum, accum = lax.fori_loop(0, piece_len // step_len, one_block, start_state)
    mixed = accum / row_sum[..., None]
    log_total = row_top + jnp.log(row_sum)
    attended_heads = mixed.astype(jnp.bfloat16).reshape(seq_count, block_len, feature_width)
    attended = lax.all_to_all(
        attended_heads, "head", split_axis=1, concat_axis=2, tiled=True
    ).reshape(flat_rows, model_width)
    branch = jnp.dot(attended, full_out, preferred_element_type=jnp.float32)
    middle = token_float + branch.reshape(seq_count, row_count, model_width)
    normed_two = (
        layer_norm(middle, scale_two[:, None, :])
        .astype(jnp.bfloat16)
        .reshape(flat_rows, model_width)
    )
    hidden = jnp.dot(normed_two, full_up, preferred_element_type=jnp.float32)
    active = jax.nn.gelu(hidden, approximate=False).astype(jnp.bfloat16)
    result = middle.reshape(flat_rows, model_width) + jnp.dot(
        active, full_down, preferred_element_type=jnp.float32
    )
    output = result.astype(jnp.bfloat16).reshape(seq_count, row_count, model_width)
    back_qkv, back_out, back_up, back_down = (
        lax.all_gather(w_qkv, ("head", "blk"), axis=0, tiled=True),
        lax.all_gather(w_out, ("head", "blk"), axis=0, tiled=True),
        lax.all_gather(w_up, ("head", "blk"), axis=0, tiled=True),
        lax.all_gather(w_down, ("head", "blk"), axis=0, tiled=True),
    )
    grad_out = cotangent.reshape(flat_rows, model_width)
    grad_active = contract_cols(grad_out, back_down)
    grad_w_down = contract_rows(active, grad_out)
    gelu_value, gelu_pull = jax.vjp(lambda entry: jax.nn.gelu(entry, approximate=False), hidden)
    grad_hidden = gelu_pull(grad_active)[0].astype(jnp.bfloat16)
    grad_w_up = contract_rows(normed_two, grad_hidden)
    grad_normed_two = contract_cols(grad_hidden, back_up).reshape(seq_count, row_count, model_width)
    norm_value, norm_pull = jax.vjp(layer_norm, middle, scale_two[:, None, :])
    grad_middle_norm, grad_scale_two = norm_pull(grad_normed_two)
    grad_middle = cotangent.astype(jnp.float32) + grad_middle_norm
    grad_scale_mlp = jnp.dot(time_embed.T, grad_scale_two[:, 0, :], precision=PRECISE)
    grad_branch = grad_middle.reshape(flat_rows, model_width).astype(jnp.bfloat16)
    grad_w_out = contract_rows(attended, grad_branch)
    grad_attended = (
        contract_cols(grad_branch, back_out)
        .astype(jnp.bfloat16)
        .reshape(seq_count, row_count, model_width)
    )
    grad_heads = lax.all_to_all(
        grad_attended, "head", split_axis=2, concat_axis=1, tiled=True
    ).reshape(seq_count, block_len, local_heads, HEAD_DIM)
    delta = jnp.sum(grad_heads.astype(jnp.float32) * mixed, axis=-1)

    def turn(index, state):
        key_now, value_now, grad_keys_now, grad_values_now, grad_query_sum = state
        grad_query, grad_keys, grad_values = back_step(
            local_query,
            key_now.reshape(seq_count, block_len, local_heads, HEAD_DIM),
            value_now.reshape(seq_count, block_len, local_heads, HEAD_DIM),
            grad_heads,
            log_total,
            delta,
        )
        moved_keys, moved_values = shifted((key_now, value_now), "blk", 1)
        moved_grad_keys, moved_grad_values = (
            shifted(
                (grad_keys_now + grad_keys.reshape(seq_count, block_len, feature_width)).astype(
                    jnp.bfloat16
                ),
                "blk",
                1,
            ).astype(jnp.float32),
            shifted(
                (grad_values_now + grad_values.reshape(seq_count, block_len, feature_width)).astype(
                    jnp.bfloat16
                ),
                "blk",
                1,
            ).astype(jnp.float32),
        )
        return (
            moved_keys,
            moved_values,
            moved_grad_keys,
            moved_grad_values,
            grad_query_sum + grad_query,
        )

    zero_kv = jnp.zeros((seq_count, block_len, feature_width), jnp.float32)
    begin = (
        local_keys,
        local_values,
        zero_kv,
        zero_kv,
        jnp.zeros((seq_count, block_len, local_heads, HEAD_DIM), jnp.float32),
    )
    final_state = lax.fori_loop(0, lax.axis_size("blk"), turn, begin)
    grad_keys_own = final_state[2]
    grad_values_own = final_state[3]
    grad_query_all = final_state[4]
    stacked = jnp.stack(
        [
            grad_query_all.reshape(seq_count, block_len, feature_width) * SCORE_SCALE,
            grad_keys_own * SCORE_SCALE,
            grad_values_own,
        ],
        axis=2,
    ).astype(jnp.bfloat16)
    returned = lax.all_to_all(stacked, "head", split_axis=1, concat_axis=3, tiled=True)
    grad_query_tok = (
        returned[:, :, 0].astype(jnp.float32).reshape(seq_count, row_count, HEADS, HEAD_DIM)
    )
    grad_keys_tok = (
        returned[:, :, 1].astype(jnp.float32).reshape(seq_count, row_count, HEADS, HEAD_DIM)
    )
    grad_values_tok = (
        returned[:, :, 2].astype(jnp.float32).reshape(seq_count, row_count, HEADS, HEAD_DIM)
    )
    grad_projected = (
        jnp.stack(
            [
                rotate(grad_query_tok, cosine_table, -sine_table),
                rotate(grad_keys_tok, cosine_table, -sine_table),
                grad_values_tok,
            ],
            axis=2,
        )
        .reshape(flat_rows, 3 * model_width)
        .astype(jnp.bfloat16)
    )
    grad_w_qkv = contract_rows(normed, grad_projected)
    grad_normed = contract_cols(grad_projected, back_qkv).reshape(seq_count, row_count, model_width)
    first_value, first_pull = jax.vjp(layer_norm, token_float, scale_one[:, None, :])
    grad_token_norm, grad_scale_one = first_pull(grad_normed)
    grad_tokens = grad_middle + grad_token_norm
    grad_scale_attn = jnp.dot(time_embed.T, grad_scale_one[:, 0, :], precision=PRECISE)
    shards = (
        lax.psum_scatter(grad_w_qkv, ("head", "blk"), scatter_dimension=0, tiled=True),
        lax.psum_scatter(grad_w_out, ("head", "blk"), scatter_dimension=0, tiled=True),
        lax.psum_scatter(grad_w_up, ("head", "blk"), scatter_dimension=0, tiled=True),
        lax.psum_scatter(grad_w_down, ("head", "blk"), scatter_dimension=0, tiled=True),
        lax.psum_scatter(grad_scale_attn, ("head", "blk"), scatter_dimension=0, tiled=True),
        lax.psum_scatter(grad_scale_mlp, ("head", "blk"), scatter_dimension=0, tiled=True),
    )
    return (output, grad_tokens, shards[0], shards[1], shards[2], shards[3], shards[4], shards[5])


EPS = NORM_EPSILON
BF = jnp.bfloat16
F32 = jnp.float32


def norm_stats(value):
    centered = value - jnp.mean(value, axis=-1, keepdims=True)
    spread = lax.rsqrt(jnp.mean(centered * centered, axis=-1, keepdims=True) + EPS)
    return centered * spread, spread


def norm_back(unit, spread, grad, scale):
    scaled = grad * scale
    return spread * (
        scaled
        - jnp.mean(scaled, axis=-1, keepdims=True)
        - unit * jnp.mean(scaled * unit, axis=-1, keepdims=True)
    )


def pack_half(value):
    lead, width = value.shape[:-2], value.shape[-1]
    rows = value.shape[-2]
    axis = value.ndim - 2
    return jnp.concatenate(
        [
            lax.slice_in_dim(value, 0, rows // 2, axis=axis),
            lax.slice_in_dim(value, rows // 2, rows, axis=axis),
        ],
        axis=-1,
    )


def unpack_half(value):
    width = value.shape[-1] // 2
    return jnp.concatenate([value[..., :width], value[..., width:]], axis=-2)


def turn(value, table, sign):
    cosine = table[..., :32]
    sine = table[..., 32:64] * sign
    first, second = value[..., :32], value[..., 32:]
    return jnp.concatenate(
        [first * cosine - second * sine, second * cosine + first * sine], axis=-1
    )


def phase_one(tokens, table, wq_parts, scale_parts):
    token_all = lax.all_gather(tokens, "head", axis=0)
    table_all = lax.all_gather(table, "head", axis=0)
    scales = lax.psum(scale_parts, ("head", "blk"))
    wq = lax.all_to_all(wq_parts, "head", 0, 0, tiled=True)
    wq = jnp.swapaxes(lax.all_gather(wq, "blk", axis=0), 0, 1).reshape(1024, 768)
    unit, _ = norm_stats(token_all.astype(F32))
    scale_one = 1.0 + scales[:2]
    normed = (unit * scale_one[None, :, None, :]).astype(BF).reshape(512, 1024)
    proj = jnp.dot(normed, wq, preferred_element_type=F32).reshape(4, 2, 64, 768)
    tab = table_all.reshape(4, 2, 64, 1, 64)
    pairs = proj[..., :512].reshape(4, 2, 64, 4, 128)
    keys = turn(pairs[..., :64], tab, 1.0)
    query = turn(proj[..., 512:].reshape(4, 2, 64, 4, 64), tab, 1.0)
    kv = jnp.concatenate([keys, pairs[..., 64:]], axis=-1).astype(BF)
    kv = jnp.transpose(kv, (1, 3, 0, 2, 4))
    query = pack_half(jnp.transpose(query.astype(BF), (1, 3, 0, 2, 4)))
    tiles = jnp.concatenate([kv, query], axis=-2).reshape(8, 4, 96, 128)
    tiles = jnp.swapaxes(lax.all_to_all(tiles, "blk", 0, 0, tiled=True), 0, 1)
    return tiles, normed, wq, scales, table_all.reshape(512, 64)


def split_tiles(tiles):
    kv = tiles[:, :, :64].reshape(2048, 128)
    query = unpack_half(tiles[:, :, 64:]).reshape(2048, 64)
    return query, kv[:, :64], kv[:, 64:]


def to_all(tiles):
    return lax.all_to_all(
        tiles.reshape(32, 32, 128), ("head", "blk"), 0, 0, tiled=True
    ).reshape(4, 8, 32, 128)


def phase_two(tiles, up_parts, w_down, w_out, cotangent):
    query, keys, values = split_tiles(tiles)
    scores = SCORE_SCALE * contract_cols(keys, query)
    top = jnp.max(scores, axis=0, keepdims=True)
    weights = jnp.exp(scores - top)
    row_sum = jnp.sum(weights, axis=0, keepdims=True)
    mixed = contract_rows(values, weights.astype(BF)) / row_sum
    lse = top + jnp.log(row_sum)
    attended = pack_half(jnp.transpose(mixed).astype(BF).reshape(4, 8, 64, 64))
    received = to_all(attended)
    up = lax.all_to_all(up_parts, "blk", 0, 0, tiled=True)
    up = lax.all_gather(up, "head", axis=0)
    down = lax.all_gather(w_down, "head", axis=0)
    out = lax.all_gather(w_out, ("head", "blk"), axis=0).reshape(4, 8, 32, 1024)
    cot_all = lax.all_gather(cotangent, "blk", axis=0).reshape(8, 128, 1024)
    return mixed, lse, received, up, down, out, cot_all


def scatter_head(partial):
    parts = lax.all_to_all(
        partial.astype(BF).reshape(4, 128, 1024), "head", 0, 0, tiled=True
    )
    return jnp.sum(parts.astype(F32), axis=0)


def scatter_blk(partial):
    parts = lax.all_to_all(partial, "blk", 0, 0, tiled=True)
    return jnp.sum(parts.astype(F32), axis=0)


def phase_three(received, tokens, out, up, down, cot_all, scales):
    up = up.reshape(1024, 512)
    down = down.reshape(512, 1024)
    out = out.reshape(1024, 1024)
    attended = unpack_half(received).reshape(4, 2, 4, 64, 64)
    attended = jnp.transpose(attended, (1, 3, 0, 2, 4)).reshape(128, 1024)
    middle = tokens.reshape(128, 1024).astype(F32) + jnp.dot(
        attended, out, preferred_element_type=F32
    )
    unit, spread = norm_stats(middle)
    scale_two = jnp.repeat(scales[2:4], 64, axis=0)
    normed_two = (unit * scale_two).astype(BF)
    normed_all = lax.all_gather(normed_two, "blk", axis=0, tiled=True)
    cots = cot_all.reshape(1024, 1024)
    cotangent = cot_all[lax.axis_index("blk")]
    hidden = jnp.dot(normed_all, up, preferred_element_type=F32)
    cdf = 0.5 * (1.0 + lax.erf(hidden * math.sqrt(0.5)))
    active = (hidden * cdf).astype(BF)
    out_partial = jnp.dot(active, down, preferred_element_type=F32).astype(BF)
    grad_active = contract_cols(cots, down)
    slope = cdf + hidden * jnp.exp(-0.5 * hidden * hidden) * (1.0 / math.sqrt(2 * math.pi))
    grad_hidden = (grad_active * slope).astype(BF)
    grad_down = contract_rows(active, cots).astype(BF).reshape(4, 128, 1024)
    grad_up = contract_rows(normed_all, grad_hidden).astype(BF).reshape(4, 8, 32, 512)
    grad_normed = scatter_blk(contract_cols(grad_hidden, up).astype(BF).reshape(8, 128, 1024))
    grad_middle = cotangent.astype(F32) + norm_back(unit, spread, grad_normed, scale_two)
    sums = jnp.sum((grad_normed * unit).reshape(2, 64, 1024), axis=1)
    branch = grad_middle.astype(BF)
    grad_out = contract_rows(attended, branch).astype(BF).reshape(4, 8, 32, 1024)
    grad_att = contract_cols(branch, out).astype(BF).reshape(2, 64, 4, 4, 64)
    grad_att = pack_half(jnp.transpose(grad_att, (2, 0, 3, 1, 4)))
    grad_rx = to_all(grad_att)
    out_partial = out_partial.reshape(8, 128, 1024)
    return grad_rx, grad_middle, middle, out_partial, grad_down, grad_up, grad_out, sums


def sum_parts(parts):
    return jnp.sum(parts.astype(F32), axis=0)


def phase_four(tiles, grad_rx, mixed, lse, out_partial, middle, grad_down, grad_up, grad_out):
    query, keys, values = split_tiles(tiles)
    grad = unpack_half(grad_rx).reshape(2048, 64)
    delta = jnp.sum(jnp.transpose(grad).astype(F32) * mixed, axis=0, keepdims=True)
    probs = jnp.exp(SCORE_SCALE * contract_cols(keys, query) - lse)
    grad_values = jnp.dot(probs.astype(BF), grad, preferred_element_type=F32)
    grad_scores = (probs * (contract_cols(values, grad) - delta)).astype(BF)
    grad_keys = SCORE_SCALE * jnp.dot(grad_scores, query, preferred_element_type=F32)
    grad_query = SCORE_SCALE * contract_rows(grad_scores, keys)
    kv = jnp.concatenate([grad_keys, grad_values], axis=-1).astype(BF).reshape(4, 8, 64, 128)
    packed = pack_half(grad_query.astype(BF).reshape(4, 8, 64, 64))
    back = jnp.swapaxes(jnp.concatenate([kv, packed], axis=-2), 0, 1)
    back = lax.all_to_all(back, "blk", 0, 0, tiled=True)
    output = (middle + scatter_blk(out_partial)).astype(BF).reshape(2, 64, 1024)
    down = sum_parts(lax.all_to_all(grad_down, "head", 0, 0, tiled=True))
    up = sum_parts(lax.all_to_all(grad_up, "head", 0, 0, tiled=True))
    up = lax.all_to_all(up.astype(BF), "blk", 0, 0, tiled=True)
    out = jnp.swapaxes(grad_out, 0, 1)
    out = sum_parts(lax.all_to_all(out, "blk", 0, 0, tiled=True))
    out = sum_parts(lax.all_to_all(out.astype(BF), "head", 0, 0, tiled=True))
    return back, output, down, up, out


def phase_five(back, table_all, normed, wq, tokens, scales, grad_middle, sums):
    kv = back[:, :, :64].reshape(2, 4, 4, 64, 128)
    query = unpack_half(back[:, :, 64:]).reshape(2, 4, 4, 64, 64)
    kv = jnp.transpose(kv, (2, 0, 3, 1, 4)).astype(F32)
    query = jnp.transpose(query, (2, 0, 3, 1, 4)).astype(F32)
    tab = jnp.swapaxes(table_all.reshape(4, 64, 2, 64), 1, 2)[:, :, :, None]
    keys = turn(kv[..., :64], tab, -1.0)
    query = turn(query, tab, -1.0)
    kv = jnp.concatenate([keys, kv[..., 64:]], axis=-1).reshape(512, 512)
    grad_proj = jnp.concatenate([kv, query.reshape(512, 256)], axis=-1).astype(BF)
    normed = normed.reshape(512, 1024)
    wq = wq.reshape(1024, 768)
    grad_wq = contract_rows(normed, grad_proj).astype(BF)
    grad_normed = scatter_head(contract_cols(grad_proj, wq))
    unit, spread = norm_stats(tokens.reshape(128, 1024).astype(F32))
    scale_one = jnp.repeat(scales[:2], 64, axis=0)
    grad_tokens = grad_middle + norm_back(unit, spread, grad_normed, scale_one)
    first = jnp.sum((grad_normed * unit).reshape(2, 64, 1024), axis=1)
    total = lax.psum(jnp.concatenate([first, sums], axis=0), ("head", "blk"))
    grad_wq = jnp.swapaxes(grad_wq.reshape(4, 8, 32, 768), 0, 1)
    grad_wq = sum_parts(lax.all_to_all(grad_wq, "blk", 0, 0, tiled=True))
    grad_wq = lax.all_to_all(grad_wq.astype(BF), "head", 0, 0, tiled=True).astype(F32)
    return grad_tokens.reshape(2, 64, 1024), grad_wq, total


MESH = pl.DeviceIdType.MESH


def flip(value, bits):
    for bit in (1, 2, 4):
        if bits & bit:
            value = value + bit - 2 * bit * lax.rem(lax.div(value, bit), 2)
    return value


def greet(head, blk, heads, blks):
    barrier = pltpu.get_barrier_semaphore()
    for k in heads:
        pl.semaphore_signal(barrier, inc=1, device_id=(flip(head, k), blk), device_id_type=MESH)
    for k in blks:
        pl.semaphore_signal(barrier, inc=1, device_id=(head, flip(blk, k)), device_id_type=MESH)
    pl.semaphore_wait(barrier, len(heads) + len(blks))


def send(source, target, send_sem, recv_sem, head, blk):
    return pltpu.make_async_remote_copy(
        src_ref=source,
        dst_ref=target,
        send_sem=send_sem,
        recv_sem=recv_sem,
        device_id=(head, blk),
        device_id_type=MESH,
    )


class Swap:
    def __init__(self, head, blk, axis, source, target, sems):
        self.copies = []
        count = 4 if axis == "head" else 8
        me = head if axis == "head" else blk
        for k in range(1, count):
            peer = flip(me, k)
            where = (peer, blk) if axis == "head" else (head, peer)
            self.copies.append(
                send(source(peer), target(me), sems.at[0, k], sems.at[1, k], *where)
            )

    def start(self):
        for copy in self.copies:
            copy.start()

    def arrive(self):
        for copy in self.copies:
            copy.wait_recv()

    def drain(self):
        for copy in self.copies:
            copy.wait_send()


class Plane:
    def __init__(self, head, blk, own, slot, sems):
        sibling = flip(blk, 1)
        self.first = [send(own, slot(blk), sems.at[0, 0], sems.at[1, 0], head, sibling)]
        self.passed = []
        for i, k in enumerate((2, 4, 6)):
            peer = flip(blk, k)
            self.first.append(
                send(own, slot(blk), sems.at[0, i + 1], sems.at[1, i + 1], head, peer)
            )
            self.passed.append(
                send(slot(peer), slot(peer), sems.at[0, i + 4], sems.at[1, i + 4], head, sibling)
            )

    def start(self):
        for i in (3, 1, 2, 0):
            self.first[i].start()

    def forward(self, i):
        self.first[i + 1].wait_recv()
        self.passed[i].start()

    def arrive(self, i):
        if i < 0:
            self.first[0].wait_recv()
        else:
            self.passed[i].wait_recv()

    def finish(self):
        for i in range(3):
            self.forward(i)
        for i in range(-1, 3):
            self.arrive(i)

    def drain(self):
        for copy in self.first + self.passed:
            copy.wait_send()


def line_order(head, step):
    low = jnp.minimum(head, 3 - head)
    swap = low * ((step == 0).astype(jnp.int32) - (step == 1).astype(jnp.int32))
    at = step + swap
    return jnp.where(head < 2, at, 3 - at)


class Line:
    def __init__(self, head, blk, own, slot, sems):
        self.head, self.blk, self.own, self.slot, self.sems = head, blk, own, slot, sems

    def copy(self, source, at, up, k):
        head = self.head
        target = jnp.where(up, head + 1, head - 1)
        way = jnp.where(up, 0, 1)
        return send(
            source, self.slot(at), self.sems.at[0, way, k], self.sems.at[1, way, k], target, self.blk
        )

    def start(self):
        head = self.head

        @pl.when(head < 3)
        def _():
            self.copy(self.own, head, True, 0).start()

        @pl.when(head > 0)
        def _():
            self.copy(self.own, head, False, 0).start()

    def step(self, at):
        head = self.head
        up = at < head
        k = jnp.where(up, head - 1 - at, at - head - 1)
        self.copy(self.slot(at), at, up, k).wait_recv()

        @pl.when(jnp.where(up, head < 3, head > 0))
        def _():
            self.copy(self.slot(at), at, up, k + 1).start()

    def drain(self):
        head = self.head
        for k in range(3):

            @pl.when(jnp.logical_and(head < 3, head >= k))
            def _():
                self.copy(self.own, head, True, k).wait_send()

            @pl.when(jnp.logical_and(head > 0, head + k <= 3))
            def _():
                self.copy(self.own, head, False, k).wait_send()


def half_lane(shape):
    return lax.broadcasted_iota(jnp.int32, shape, 1) < 64


def lane_swap(value):
    lane = lax.broadcasted_iota(jnp.int32, value.shape, 1)
    return jnp.where(
        lax.rem(lane, 64) < 32, pltpu.roll(value, 96, 1), pltpu.roll(value, 32, 1)
    )


def turn_tables(table, sign):
    lane = lax.broadcasted_iota(jnp.int32, table.shape, 1)
    cosine = jnp.where(lane < 32, table, 0.0)
    cosine = cosine + pltpu.roll(cosine, 32, 1)
    sine = jnp.where(jnp.logical_and(lane >= 32, lane < 64), table, 0.0) * sign
    sine = sine - pltpu.roll(sine, 96, 1)
    both = (cosine + pltpu.roll(cosine, 64, 1), sine + pltpu.roll(sine, 64, 1))
    return both, (jnp.where(lane < 64, cosine, 1.0), sine)


def join_halves(top, bottom, right):
    left = half_lane(top.shape)
    if right:
        return jnp.where(left, pltpu.roll(top, 64, 1), bottom)
    return jnp.where(left, top, pltpu.roll(bottom, 64, 1))


def first_kernel(
    tok, tab, wqp, ttab, tix, sca, scm,
    tiles, normed, wq, scales, tabg,
    tokg, wqz, turned, part, sums, parts, out_tiles,
    zsem, lsem, tsem, wsem, asem, bsem, psem,
):
    head, blk = lax.axis_index("head"), lax.axis_index("blk")
    greet(head, blk, (1, 2, 3), range(1, 8))
    zswap = Swap(head, blk, "head", lambda i: wqp.at[i], lambda i: wqz.at[i], zsem)
    zswap.start()
    line = Line(head, blk, tok, lambda i: tokg.at[i], lsem)
    tline = Line(head, blk, tab, lambda i: tabg.at[i], tsem)
    tline.start()
    line.start()
    turned[...] = jnp.transpose(ttab[...])
    rows = turned[pl.ds(pl.multiple_of((head * 8 + blk) * 8, 8), 8), :]
    step_lane = lax.broadcasted_iota(jnp.int32, rows.shape, 1)
    terms = []
    for weight in (sca, scm):
        for seq in range(2):
            column = jnp.sum(jnp.where(step_lane == tix[seq], rows, 0.0), axis=1, keepdims=True)
            terms.append(jnp.sum(column * weight[...].astype(F32), axis=0, keepdims=True))
    part[...] = jnp.concatenate(terms + [jnp.zeros((4, 1024), F32)], axis=0)
    one = Swap(head, blk, "blk", lambda i: part, lambda i: sums.at[i], asem)
    one.start()
    sums[blk] = part[...]
    wqz[head] = wqp[head]
    tokg[head] = tok[...]
    tabg[head] = tab[...]
    zswap.arrive()
    plane = Plane(head, blk, wqz, lambda i: wq.at[:, i], wsem)
    plane.start()
    wq[:, pl.ds(blk, 1)] = wqz[...].reshape(4, 1, 32, 768)
    one.arrive()
    total = sums[0]
    for i in range(1, 8):
        total = total + sums[i]
    parts[head] = total
    two = Swap(head, blk, "head", lambda i: parts.at[head], lambda i: parts.at[i], bsem)
    two.start()
    two.arrive()
    total = 1.0 + ((parts[0] + parts[1]) + (parts[2] + parts[3]))
    scales[...] = total

    def gather(step, carry):
        at = line_order(head, step)

        @pl.when(step > 0)
        def _():
            tline.step(at)
            line.step(at)

        for seq in range(2):
            unit, _ = norm_stats(tokg[at, seq].astype(F32))
            normed[at, pl.ds(64 * seq, 64), :] = (unit * scales[seq : seq + 1, :]).astype(BF)
        return carry

    lax.fori_loop(0, 4, gather, 0)
    plane.finish()

    def project(step, carry):
        at = line_order(head, step)
        proj = jnp.dot(
            normed[at], wq[...].reshape(1024, 768), preferred_element_type=F32
        )
        for seq in range(2):
            table = tabg[at]
            if seq:
                table = pltpu.roll(table, 64, 1)
            both, keyed = turn_tables(table, 1.0)
            mine = proj[64 * seq : 64 * seq + 64]
            for j in range(4):
                kv = mine[:, 128 * j : 128 * j + 128]
                kv = kv * keyed[0] + lane_swap(kv) * keyed[1]
                out_tiles[4 * seq + j, at, 0:64, :] = kv.astype(BF)
            for i in range(2):
                query = mine[:, 512 + 128 * i : 640 + 128 * i]
                query = query * both[0] + lane_swap(query) * both[1]
                for right in range(2):
                    packed = join_halves(query[:32], query[32:], right)
                    out_tiles[4 * seq + 2 * i + right, at, 64:96, :] = packed.astype(BF)
        move(at).start()
        tiles[at, blk] = out_tiles[blk, at]
        return carry

    def move(at):
        return Swap(
            head, blk, "blk", lambda i: out_tiles.at[i, at], lambda i: tiles.at[at, i], psem.at[at]
        )

    lax.fori_loop(0, 4, project, 0)
    for at in range(4):
        move(at).arrive()
    for at in range(4):
        move(at).drain()
    for copies in (zswap, line, tline, plane, one, two):
        copies.drain()


def whole(count):
    return [pl.BlockSpec(memory_space=pltpu.VMEM)] * count


def phase_one_kernel(tokens, table, wq_parts, time_table, time_index, scale_attn, scale_mlp):
    dma = pltpu.SemaphoreType.DMA
    return pl.pallas_call(
        first_kernel,
        out_shape=(
            jax.ShapeDtypeStruct((4, 8, 96, 128), BF),
            jax.ShapeDtypeStruct((4, 128, 1024), BF),
            jax.ShapeDtypeStruct((4, 8, 32, 768), BF),
            jax.ShapeDtypeStruct((8, 1024), F32),
            jax.ShapeDtypeStruct((4, 64, 128), F32),
        ),
        in_specs=whole(4) + [pl.BlockSpec(memory_space=pltpu.SMEM)] + whole(2),
        out_specs=whole(5),
        scratch_shapes=[
            pltpu.VMEM((4, 2, 64, 1024), BF),
            pltpu.VMEM((4, 32, 768), BF),
            pltpu.VMEM((256, 64), F32),
            pltpu.VMEM((8, 1024), F32),
            pltpu.VMEM((8, 8, 1024), F32),
            pltpu.VMEM((4, 8, 1024), F32),
            pltpu.VMEM((8, 4, 96, 128), BF),
            dma((2, 4)),
            dma((2, 2, 3)),
            dma((2, 2, 3)),
            dma((2, 7)),
            dma((2, 8)),
            dma((2, 4)),
            dma((4, 2, 8)),
        ],
        compiler_params=pltpu.CompilerParams(
            collective_id=0, has_side_effects=True, vmem_limit_bytes=48 << 20
        ),
        name="first",
    )(tokens, table, wq_parts, time_table, time_index, scale_attn, scale_mlp)
def contract_rows_precise(left, right):
    return lax.dot_general(
        left, right, (((0,), (0,)), ((), ())), precision=PRECISE, preferred_element_type=F32
    )


def blocked(
    tokens,
    positions,
    time_index,
    time_table,
    w_qkv,
    w_out,
    w_up,
    w_down,
    scale_attn,
    scale_mlp,
    cotangent,
):
    place = lax.axis_index(("head", "blk"))
    embed = time_table[time_index]
    embed_own = lax.dynamic_slice_in_dim(embed, place * 8, 8, 1)
    cosine, sine = rotary_tables(positions, HEAD_DIM)
    cosine, sine = cosine[:, :, 0], sine[:, :, 0]
    table = jnp.concatenate([cosine[0], sine[0], cosine[1], sine[1]], axis=-1)
    wide = w_qkv.reshape(32, 3, 4, 4, 64)
    kv_cols = jnp.stack([wide[:, 1], wide[:, 2]], axis=3).reshape(32, 4, 512)
    wq_parts = jnp.concatenate([kv_cols, wide[:, 0].reshape(32, 4, 256)], axis=-1)
    wq_parts = jnp.swapaxes(wq_parts, 0, 1)
    up_parts = jnp.transpose(w_up.reshape(32, 4, 8, 128), (2, 0, 1, 3)).reshape(8, 32, 512)
    tiles, normed, wq, scales, table_all = phase_one_kernel(
        tokens, table, wq_parts, time_table, time_index, scale_attn, scale_mlp
    )
    mixed, lse, received, up, down, out, cot_all = phase_two(
        tiles, up_parts, w_down, w_out, cotangent
    )
    grad_rx, grad_middle, middle, out_partial, grad_down, grad_up, grad_out, sums = phase_three(
        received, tokens, out, up, down, cot_all, scales
    )
    back, output, down_own, up_own, out_own = phase_four(
        tiles, grad_rx, mixed, lse, out_partial, middle, grad_down, grad_up, grad_out
    )
    grad_tokens, grad_wq, total = phase_five(
        back, table_all, normed, wq, tokens, scales, grad_middle, sums
    )
    kv_cols = grad_wq[:, :, :512].reshape(4, 32, 4, 2, 64)
    wide = jnp.stack(
        [grad_wq[:, :, 512:].reshape(4, 32, 4, 64), kv_cols[:, :, :, 0], kv_cols[:, :, :, 1]],
        axis=0,
    )
    qkv_own = jnp.transpose(wide, (2, 0, 1, 3, 4)).reshape(32, 3072)
    up_own = jnp.transpose(up_own.reshape(8, 32, 4, 128), (1, 2, 0, 3)).reshape(32, 4096).astype(F32)
    grad_attn = contract_rows_precise(embed_own, total[:2])
    grad_mlp = contract_rows_precise(embed_own, total[2:])
    return output, grad_tokens, qkv_own, out_own, up_own, down_own, grad_attn, grad_mlp


def solution(mesh):
    fits = mesh.shape["head"] == 4 and mesh.shape["blk"] == 8
    placed = (
        P(None, ("head", "blk"), None),
        P(None, ("head", "blk")),
        P(),
        P(),
        P(("head", "blk"), None),
        P(("head", "blk"), None),
        P(("head", "blk"), None),
        P(("head", "blk"), None),
        P(("head", "blk"), None),
        P(("head", "blk"), None),
        P(None, ("head", "blk"), None),
    )
    return jax.shard_map(
        blocked if fits else general,
        mesh=mesh,
        in_specs=placed,
        out_specs=(
            P(None, ("head", "blk"), None),
            P(None, ("head", "blk"), None),
            P(("head", "blk"), None),
            P(("head", "blk"), None),
            P(("head", "blk"), None),
            P(("head", "blk"), None),
            P(("head", "blk"), None),
            P(("head", "blk"), None),
        ),
        check_vma=False,
    )
```

```python
import math

import jax
import jax.numpy as jnp
from jax import lax
from jax.experimental import pallas as pl
from jax.experimental.pallas import tpu as pltpu
from jax.sharding import PartitionSpec as P

HEADS = 16
HEAD_DIM = 64


NORM_EPSILON = 1e-05
PRECISE = lax.Precision.HIGHEST
START_TOP = -1e30
SCORE_SCALE = 0.125


def shifted(value, axis, steps):
    count = lax.axis_size(axis)
    pairs = [(source, (source + steps) % count) for source in range(count)]
    return lax.ppermute(value, axis, pairs)


def layer_norm(value, scale):
    centered = value - jnp.mean(value, axis=-1, keepdims=True)
    variance = jnp.mean(centered * centered, axis=-1, keepdims=True)
    return centered * lax.rsqrt(variance + NORM_EPSILON) * scale


def rotate(value, cosine_table, sine_table):
    half_dim = value.shape[-1] // 2
    first_half = value[..., :half_dim]
    second_half = value[..., half_dim:]
    return jnp.concatenate(
        [
            first_half * cosine_table - second_half * sine_table,
            second_half * cosine_table + first_half * sine_table,
        ],
        axis=-1,
    )


def rotary_tables(positions, head_dim):
    half_dim = head_dim // 2
    frequency = 10000.0 ** (-jnp.arange(half_dim, dtype=jnp.float32) / half_dim)
    turned = positions.astype(jnp.float32)[:, :, None, None] * frequency
    return (jnp.cos(turned), jnp.sin(turned))


def contract_rows(left, right):
    return lax.dot_general(
        left, right, (((0,), (0,)), ((), ())), preferred_element_type=jnp.float32
    )


def contract_cols(left, right):
    return lax.dot_general(
        left, right, (((1,), (1,)), ((), ())), preferred_element_type=jnp.float32
    )


def attend_step(running, query_block, key_block, value_block):
    row_top, row_sum, accum = running
    scores = (
        jnp.einsum("sqhd,skhd->sqhk", query_block, key_block, preferred_element_type=jnp.float32)
        * SCORE_SCALE
    )
    new_top = jnp.maximum(row_top, jnp.max(scores, axis=-1))
    shrink = jnp.exp(row_top - new_top)
    weights = jnp.exp(scores - new_top[..., None])
    row_sum = row_sum * shrink + jnp.sum(weights, axis=-1)
    accum = accum * shrink[..., None] + jnp.einsum(
        "sqhk,skhd->sqhd",
        weights.astype(jnp.bfloat16),
        value_block,
        preferred_element_type=jnp.float32,
    )
    return (new_top, row_sum, accum)


def back_step(query_block, key_block, value_block, grad_block, log_total, delta):
    scores = (
        jnp.einsum("sqhd,skhd->sqhk", query_block, key_block, preferred_element_type=jnp.float32)
        * SCORE_SCALE
    )
    probs = jnp.exp(scores - log_total[..., None])
    grad_values = jnp.einsum(
        "sqhk,sqhd->skhd",
        probs.astype(jnp.bfloat16),
        grad_block,
        preferred_element_type=jnp.float32,
    )
    grad_probs = jnp.einsum(
        "sqhd,skhd->sqhk", grad_block, value_block, preferred_element_type=jnp.float32
    )
    grad_scores = (probs * (grad_probs - delta[..., None])).astype(jnp.bfloat16)
    grad_query = jnp.einsum(
        "sqhk,skhd->sqhd", grad_scores, key_block, preferred_element_type=jnp.float32
    )
    grad_keys = jnp.einsum(
        "sqhk,sqhd->skhd", grad_scores, query_block, preferred_element_type=jnp.float32
    )
    return (grad_query, grad_keys, grad_values)


def general(
    tokens,
    positions,
    time_index,
    time_table,
    w_qkv,
    w_out,
    w_up,
    w_down,
    scale_attn,
    scale_mlp,
    cotangent,
):
    seq_count, row_count, model_width = tokens.shape
    group_count = lax.axis_size("head")
    local_heads = HEADS // group_count
    feature_width = local_heads * HEAD_DIM
    flat_rows = seq_count * row_count
    gathered = (
        lax.all_gather(w_qkv, ("head", "blk"), axis=0, tiled=True),
        lax.all_gather(w_out, ("head", "blk"), axis=0, tiled=True),
        lax.all_gather(w_up, ("head", "blk"), axis=0, tiled=True),
        lax.all_gather(w_down, ("head", "blk"), axis=0, tiled=True),
        lax.all_gather(scale_attn, ("head", "blk"), axis=0, tiled=True),
        lax.all_gather(scale_mlp, ("head", "blk"), axis=0, tiled=True),
    )
    full_qkv, full_out, full_up, full_down, full_scale_attn, full_scale_mlp = gathered
    step_count = time_table.shape[0]
    picker = (time_index[:, None] == jnp.arange(step_count, dtype=jnp.int32)[None, :]).astype(
        jnp.float32
    )
    time_embed = jnp.dot(picker, time_table, precision=PRECISE)
    scale_one = 1.0 + jnp.dot(time_embed, full_scale_attn.astype(jnp.float32), precision=PRECISE)
    scale_two = 1.0 + jnp.dot(time_embed, full_scale_mlp.astype(jnp.float32), precision=PRECISE)
    token_float = tokens.astype(jnp.float32)
    normed = (
        layer_norm(token_float, scale_one[:, None, :])
        .astype(jnp.bfloat16)
        .reshape(flat_rows, model_width)
    )
    projected = jnp.dot(normed, full_qkv, preferred_element_type=jnp.float32).reshape(
        seq_count, row_count, 3, HEADS, HEAD_DIM
    )
    cosine_table, sine_table = rotary_tables(positions, HEAD_DIM)
    query_tok = rotate(projected[:, :, 0], cosine_table, sine_table)
    keys_tok = rotate(projected[:, :, 1], cosine_table, sine_table)
    packed = (
        jnp.stack([query_tok, keys_tok, projected[:, :, 2]], axis=2)
        .reshape(seq_count, row_count, 3, model_width)
        .astype(jnp.bfloat16)
    )
    regrouped = lax.all_to_all(packed, "head", split_axis=3, concat_axis=1, tiled=True)
    block_len = regrouped.shape[1]
    local_query = regrouped[:, :, 0].reshape(seq_count, block_len, local_heads, HEAD_DIM)
    local_keys = regrouped[:, :, 1]
    local_values = regrouped[:, :, 2]
    start_state = (
        jnp.full((seq_count, block_len, local_heads), START_TOP, jnp.float32),
        jnp.zeros((seq_count, block_len, local_heads), jnp.float32),
        jnp.zeros((seq_count, block_len, local_heads, HEAD_DIM), jnp.float32),
    )
    key_piece = lax.all_gather(local_keys, "blk", axis=1, tiled=True)
    value_piece = lax.all_gather(local_values, "blk", axis=1, tiled=True)
    piece_len = key_piece.shape[1]
    step_len = math.gcd(piece_len, block_len)

    def one_block(index, state):
        key_block = lax.dynamic_slice_in_dim(key_piece, index * step_len, step_len, 1).reshape(
            seq_count, step_len, local_heads, HEAD_DIM
        )
        value_block = lax.dynamic_slice_in_dim(value_piece, index * step_len, step_len, 1).reshape(
            seq_count, step_len, local_heads, HEAD_DIM
        )
        return attend_step(state, local_query, key_block, value_block)

    row_top, row_sum, accum = lax.fori_loop(0, piece_len // step_len, one_block, start_state)
    mixed = accum / row_sum[..., None]
    log_total = row_top + jnp.log(row_sum)
    attended_heads = mixed.astype(jnp.bfloat16).reshape(seq_count, block_len, feature_width)
    attended = lax.all_to_all(
        attended_heads, "head", split_axis=1, concat_axis=2, tiled=True
    ).reshape(flat_rows, model_width)
    branch = jnp.dot(attended, full_out, preferred_element_type=jnp.float32)
    middle = token_float + branch.reshape(seq_count, row_count, model_width)
    normed_two = (
        layer_norm(middle, scale_two[:, None, :])
        .astype(jnp.bfloat16)
        .reshape(flat_rows, model_width)
    )
    hidden = jnp.dot(normed_two, full_up, preferred_element_type=jnp.float32)
    active = jax.nn.gelu(hidden, approximate=False).astype(jnp.bfloat16)
    result = middle.reshape(flat_rows, model_width) + jnp.dot(
        active, full_down, preferred_element_type=jnp.float32
    )
    output = result.astype(jnp.bfloat16).reshape(seq_count, row_count, model_width)
    back_qkv, back_out, back_up, back_down = (
        lax.all_gather(w_qkv, ("head", "blk"), axis=0, tiled=True),
        lax.all_gather(w_out, ("head", "blk"), axis=0, tiled=True),
        lax.all_gather(w_up, ("head", "blk"), axis=0, tiled=True),
        lax.all_gather(w_down, ("head", "blk"), axis=0, tiled=True),
    )
    grad_out = cotangent.reshape(flat_rows, model_width)
    grad_active = contract_cols(grad_out, back_down)
    grad_w_down = contract_rows(active, grad_out)
    gelu_value, gelu_pull = jax.vjp(lambda entry: jax.nn.gelu(entry, approximate=False), hidden)
    grad_hidden = gelu_pull(grad_active)[0].astype(jnp.bfloat16)
    grad_w_up = contract_rows(normed_two, grad_hidden)
    grad_normed_two = contract_cols(grad_hidden, back_up).reshape(seq_count, row_count, model_width)
    norm_value, norm_pull = jax.vjp(layer_norm, middle, scale_two[:, None, :])
    grad_middle_norm, grad_scale_two = norm_pull(grad_normed_two)
    grad_middle = cotangent.astype(jnp.float32) + grad_middle_norm
    grad_scale_mlp = jnp.dot(time_embed.T, grad_scale_two[:, 0, :], precision=PRECISE)
    grad_branch = grad_middle.reshape(flat_rows, model_width).astype(jnp.bfloat16)
    grad_w_out = contract_rows(attended, grad_branch)
    grad_attended = (
        contract_cols(grad_branch, back_out)
        .astype(jnp.bfloat16)
        .reshape(seq_count, row_count, model_width)
    )
    grad_heads = lax.all_to_all(
        grad_attended, "head", split_axis=2, concat_axis=1, tiled=True
    ).reshape(seq_count, block_len, local_heads, HEAD_DIM)
    delta = jnp.sum(grad_heads.astype(jnp.float32) * mixed, axis=-1)

    def turn(index, state):
        key_now, value_now, grad_keys_now, grad_values_now, grad_query_sum = state
        grad_query, grad_keys, grad_values = back_step(
            local_query,
            key_now.reshape(seq_count, block_len, local_heads, HEAD_DIM),
            value_now.reshape(seq_count, block_len, local_heads, HEAD_DIM),
            grad_heads,
            log_total,
            delta,
        )
        moved_keys, moved_values = shifted((key_now, value_now), "blk", 1)
        moved_grad_keys, moved_grad_values = (
            shifted(
                (grad_keys_now + grad_keys.reshape(seq_count, block_len, feature_width)).astype(
                    jnp.bfloat16
                ),
                "blk",
                1,
            ).astype(jnp.float32),
            shifted(
                (grad_values_now + grad_values.reshape(seq_count, block_len, feature_width)).astype(
                    jnp.bfloat16
                ),
                "blk",
                1,
            ).astype(jnp.float32),
        )
        return (
            moved_keys,
            moved_values,
            moved_grad_keys,
            moved_grad_values,
            grad_query_sum + grad_query,
        )

    zero_kv = jnp.zeros((seq_count, block_len, feature_width), jnp.float32)
    begin = (
        local_keys,
        local_values,
        zero_kv,
        zero_kv,
        jnp.zeros((seq_count, block_len, local_heads, HEAD_DIM), jnp.float32),
    )
    final_state = lax.fori_loop(0, lax.axis_size("blk"), turn, begin)
    grad_keys_own = final_state[2]
    grad_values_own = final_state[3]
    grad_query_all = final_state[4]
    stacked = jnp.stack(
        [
            grad_query_all.reshape(seq_count, block_len, feature_width) * SCORE_SCALE,
            grad_keys_own * SCORE_SCALE,
            grad_values_own,
        ],
        axis=2,
    ).astype(jnp.bfloat16)
    returned = lax.all_to_all(stacked, "head", split_axis=1, concat_axis=3, tiled=True)
    grad_query_tok = (
        returned[:, :, 0].astype(jnp.float32).reshape(seq_count, row_count, HEADS, HEAD_DIM)
    )
    grad_keys_tok = (
        returned[:, :, 1].astype(jnp.float32).reshape(seq_count, row_count, HEADS, HEAD_DIM)
    )
    grad_values_tok = (
        returned[:, :, 2].astype(jnp.float32).reshape(seq_count, row_count, HEADS, HEAD_DIM)
    )
    grad_projected = (
        jnp.stack(
            [
                rotate(grad_query_tok, cosine_table, -sine_table),
                rotate(grad_keys_tok, cosine_table, -sine_table),
                grad_values_tok,
            ],
            axis=2,
        )
        .reshape(flat_rows, 3 * model_width)
        .astype(jnp.bfloat16)
    )
    grad_w_qkv = contract_rows(normed, grad_projected)
    grad_normed = contract_cols(grad_projected, back_qkv).reshape(seq_count, row_count, model_width)
    first_value, first_pull = jax.vjp(layer_norm, token_float, scale_one[:, None, :])
    grad_token_norm, grad_scale_one = first_pull(grad_normed)
    grad_tokens = grad_middle + grad_token_norm
    grad_scale_attn = jnp.dot(time_embed.T, grad_scale_one[:, 0, :], precision=PRECISE)
    shards = (
        lax.psum_scatter(grad_w_qkv, ("head", "blk"), scatter_dimension=0, tiled=True),
        lax.psum_scatter(grad_w_out, ("head", "blk"), scatter_dimension=0, tiled=True),
        lax.psum_scatter(grad_w_up, ("head", "blk"), scatter_dimension=0, tiled=True),
        lax.psum_scatter(grad_w_down, ("head", "blk"), scatter_dimension=0, tiled=True),
        lax.psum_scatter(grad_scale_attn, ("head", "blk"), scatter_dimension=0, tiled=True),
        lax.psum_scatter(grad_scale_mlp, ("head", "blk"), scatter_dimension=0, tiled=True),
    )
    return (output, grad_tokens, shards[0], shards[1], shards[2], shards[3], shards[4], shards[5])


EPS = NORM_EPSILON
BF = jnp.bfloat16
F32 = jnp.float32


def norm_stats(value):
    centered = value - jnp.mean(value, axis=-1, keepdims=True)
    spread = lax.rsqrt(jnp.mean(centered * centered, axis=-1, keepdims=True) + EPS)
    return centered * spread, spread


def norm_back(unit, spread, grad, scale):
    scaled = grad * scale
    return spread * (
        scaled
        - jnp.mean(scaled, axis=-1, keepdims=True)
        - unit * jnp.mean(scaled * unit, axis=-1, keepdims=True)
    )


MESH = pl.DeviceIdType.MESH


def flip(value, bits):
    for bit in (1, 2, 4):
        if bits & bit:
            value = value + bit - 2 * bit * lax.rem(lax.div(value, bit), 2)
    return value


def greet(head, blk, heads, blks):
    barrier = pltpu.get_barrier_semaphore()
    for k in heads:
        pl.semaphore_signal(barrier, inc=1, device_id=(flip(head, k), blk), device_id_type=MESH)
    for k in blks:
        pl.semaphore_signal(barrier, inc=1, device_id=(head, flip(blk, k)), device_id_type=MESH)
    pl.semaphore_wait(barrier, len(heads) + len(blks))


def send(source, target, send_sem, recv_sem, head, blk):
    return pltpu.make_async_remote_copy(
        src_ref=source,
        dst_ref=target,
        send_sem=send_sem,
        recv_sem=recv_sem,
        device_id=(head, blk),
        device_id_type=MESH,
    )


class Swap:
    def __init__(self, head, blk, axis, source, target, sems):
        self.copies = []
        count = 4 if axis == "head" else 8
        me = head if axis == "head" else blk
        for k in range(1, count):
            peer = flip(me, k)
            where = (peer, blk) if axis == "head" else (head, peer)
            self.copies.append(
                send(source(peer), target(me), sems.at[0, k], sems.at[1, k], *where)
            )

    def start(self):
        for copy in self.copies:
            copy.start()

    def arrive(self):
        for copy in self.copies:
            copy.wait_recv()

    def drain(self):
        for copy in self.copies:
            copy.wait_send()


class Plane:
    def __init__(self, head, blk, own, slot, sems):
        sibling = flip(blk, 1)
        self.first = [send(own, slot(blk), sems.at[0, 0], sems.at[1, 0], head, sibling)]
        self.passed = []
        for i, k in enumerate((2, 4, 6)):
            peer = flip(blk, k)
            self.first.append(
                send(own, slot(blk), sems.at[0, i + 1], sems.at[1, i + 1], head, peer)
            )
            self.passed.append(
                send(slot(peer), slot(peer), sems.at[0, i + 4], sems.at[1, i + 4], head, sibling)
            )

    def start(self):
        for i in (3, 1, 2, 0):
            self.first[i].start()

    def forward(self, i):
        self.first[i + 1].wait_recv()
        self.passed[i].start()

    def arrive(self, i):
        if i < 0:
            self.first[0].wait_recv()
        else:
            self.passed[i].wait_recv()

    def finish(self):
        for i in range(3):
            self.forward(i)
        for i in range(-1, 3):
            self.arrive(i)

    def drain(self):
        for copy in self.first + self.passed:
            copy.wait_send()


def line_order(head, step):
    low = jnp.minimum(head, 3 - head)
    swap = low * ((step == 0).astype(jnp.int32) - (step == 1).astype(jnp.int32))
    at = step + swap
    return jnp.where(head < 2, at, 3 - at)


class Line:
    def __init__(self, head, blk, own, slot, sems):
        self.head, self.blk, self.own, self.slot, self.sems = head, blk, own, slot, sems

    def copy(self, source, at, up, k):
        head = self.head
        target = jnp.where(up, head + 1, head - 1)
        way = jnp.where(up, 0, 1)
        return send(
            source, self.slot(at), self.sems.at[0, way, k], self.sems.at[1, way, k], target, self.blk
        )

    def start(self):
        head = self.head

        @pl.when(head < 3)
        def _():
            self.copy(self.own, head, True, 0).start()

        @pl.when(head > 0)
        def _():
            self.copy(self.own, head, False, 0).start()

    def step(self, at):
        head = self.head
        up = at < head
        k = jnp.where(up, head - 1 - at, at - head - 1)
        self.copy(self.slot(at), at, up, k).wait_recv()

        @pl.when(jnp.where(up, head < 3, head > 0))
        def _():
            self.copy(self.slot(at), at, up, k + 1).start()

    def drain(self):
        head = self.head
        for k in range(3):

            @pl.when(jnp.logical_and(head < 3, head >= k))
            def _():
                self.copy(self.own, head, True, k).wait_send()

            @pl.when(jnp.logical_and(head > 0, head + k <= 3))
            def _():
                self.copy(self.own, head, False, k).wait_send()


def half_lane(shape):
    return lax.broadcasted_iota(jnp.int32, shape, 1) < 64


def lane_swap(value):
    lane = lax.broadcasted_iota(jnp.int32, value.shape, 1)
    return jnp.where(
        lax.rem(lane, 64) < 32, pltpu.roll(value, 96, 1), pltpu.roll(value, 32, 1)
    )


def turn_tables(table, sign):
    lane = lax.broadcasted_iota(jnp.int32, table.shape, 1)
    cosine = jnp.where(lane < 32, table, 0.0)
    cosine = cosine + pltpu.roll(cosine, 32, 1)
    sine = jnp.where(jnp.logical_and(lane >= 32, lane < 64), table, 0.0) * sign
    sine = sine - pltpu.roll(sine, 96, 1)
    both = (cosine + pltpu.roll(cosine, 64, 1), sine + pltpu.roll(sine, 64, 1))
    return both, (jnp.where(lane < 64, cosine, 1.0), sine)


def join_halves(top, bottom, right):
    left = half_lane(top.shape)
    if right:
        return jnp.where(left, pltpu.roll(top, 64, 1), bottom)
    return jnp.where(left, top, pltpu.roll(bottom, 64, 1))


def first_kernel(
    tok, tab, wqp, ttab, tix, sca, scm,
    tiles, normed, wq, scales, tabg,
    tokg, wqz, turned, part, sums, parts, out_tiles,
    zsem, lsem, tsem, wsem, asem, bsem, psem,
):
    head, blk = lax.axis_index("head"), lax.axis_index("blk")
    greet(head, blk, (1, 2, 3), range(1, 8))
    zswap = Swap(head, blk, "head", lambda i: wqp.at[i], lambda i: wqz.at[i], zsem)
    zswap.start()
    line = Line(head, blk, tok, lambda i: tokg.at[i], lsem)
    tline = Line(head, blk, tab, lambda i: tabg.at[i], tsem)
    tline.start()
    line.start()
    turned[...] = jnp.transpose(ttab[...])
    rows = turned[pl.ds(pl.multiple_of((head * 8 + blk) * 8, 8), 8), :]
    step_lane = lax.broadcasted_iota(jnp.int32, rows.shape, 1)
    terms = []
    for weight in (sca, scm):
        for seq in range(2):
            column = jnp.sum(jnp.where(step_lane == tix[seq], rows, 0.0), axis=1, keepdims=True)
            terms.append(jnp.sum(column * weight[...].astype(F32), axis=0, keepdims=True))
    part[...] = jnp.concatenate(terms + [jnp.zeros((4, 1024), F32)], axis=0)
    one = Swap(head, blk, "blk", lambda i: part, lambda i: sums.at[i], asem)
    one.start()
    sums[blk] = part[...]
    wqz[head] = wqp[head]
    tokg[head] = tok[...]
    tabg[head] = tab[...]
    zswap.arrive()
    plane = Plane(head, blk, wqz, lambda i: wq.at[:, i], wsem)
    plane.start()
    wq[:, pl.ds(blk, 1)] = wqz[...].reshape(4, 1, 32, 768)
    one.arrive()
    total = sums[0]
    for i in range(1, 8):
        total = total + sums[i]
    parts[head] = total
    two = Swap(head, blk, "head", lambda i: parts.at[head], lambda i: parts.at[i], bsem)
    two.start()
    two.arrive()
    total = 1.0 + ((parts[0] + parts[1]) + (parts[2] + parts[3]))
    scales[...] = total

    def gather(step, carry):
        at = line_order(head, step)

        @pl.when(step > 0)
        def _():
            tline.step(at)
            line.step(at)

        for seq in range(2):
            unit, _ = norm_stats(tokg[at, seq].astype(F32))
            normed[at, pl.ds(64 * seq, 64), :] = (unit * scales[seq : seq + 1, :]).astype(BF)
        return carry

    lax.fori_loop(0, 4, gather, 0)
    plane.finish()

    def project(step, carry):
        at = line_order(head, step)
        proj = jnp.dot(
            normed[at], wq[...].reshape(1024, 768), preferred_element_type=F32
        )
        for seq in range(2):
            table = tabg[at]
            if seq:
                table = pltpu.roll(table, 64, 1)
            both, keyed = turn_tables(table, 1.0)
            mine = proj[64 * seq : 64 * seq + 64]
            for j in range(4):
                kv = mine[:, 128 * j : 128 * j + 128]
                kv = kv * keyed[0] + lane_swap(kv) * keyed[1]
                out_tiles[4 * seq + j, at, 0:64, :] = kv.astype(BF)
            for i in range(2):
                query = mine[:, 512 + 128 * i : 640 + 128 * i]
                query = query * both[0] + lane_swap(query) * both[1]
                for right in range(2):
                    packed = join_halves(query[:32], query[32:], right)
                    out_tiles[4 * seq + 2 * i + right, at, 64:96, :] = packed.astype(BF)
        move(at).start()
        tiles[at, blk] = out_tiles[blk, at]
        return carry

    def move(at):
        return Swap(
            head, blk, "blk", lambda i: out_tiles.at[i, at], lambda i: tiles.at[at, i], psem.at[at]
        )

    lax.fori_loop(0, 4, project, 0)
    for at in range(4):
        move(at).arrive()
    for at in range(4):
        move(at).drain()
    for copies in (zswap, line, tline, plane, one, two):
        copies.drain()


def whole(count):
    return [pl.BlockSpec(memory_space=pltpu.VMEM)] * count


def phase_one_kernel(tokens, table, wq_parts, time_table, time_index, scale_attn, scale_mlp):
    dma = pltpu.SemaphoreType.DMA
    return pl.pallas_call(
        first_kernel,
        out_shape=(
            jax.ShapeDtypeStruct((4, 8, 96, 128), BF),
            jax.ShapeDtypeStruct((4, 128, 1024), BF),
            jax.ShapeDtypeStruct((4, 8, 32, 768), BF),
            jax.ShapeDtypeStruct((8, 1024), F32),
            jax.ShapeDtypeStruct((4, 64, 128), F32),
        ),
        in_specs=whole(4) + [pl.BlockSpec(memory_space=pltpu.SMEM)] + whole(2),
        out_specs=whole(5),
        scratch_shapes=[
            pltpu.VMEM((4, 2, 64, 1024), BF),
            pltpu.VMEM((4, 32, 768), BF),
            pltpu.VMEM((256, 64), F32),
            pltpu.VMEM((8, 1024), F32),
            pltpu.VMEM((8, 8, 1024), F32),
            pltpu.VMEM((4, 8, 1024), F32),
            pltpu.VMEM((8, 4, 96, 128), BF),
            dma((2, 4)),
            dma((2, 2, 3)),
            dma((2, 2, 3)),
            dma((2, 7)),
            dma((2, 8)),
            dma((2, 4)),
            dma((4, 2, 8)),
        ],
        compiler_params=pltpu.CompilerParams(
            collective_id=0, has_side_effects=True, vmem_limit_bytes=48 << 20
        ),
        name="first",
    )(tokens, table, wq_parts, time_table, time_index, scale_attn, scale_mlp)
EXP_SCALE = SCORE_SCALE * math.log2(math.e)
KEYS = 256


class Everyone:
    def __init__(self, head, blk, source, target, sems):
        self.head, self.blk, self.source, self.target, self.sems = head, blk, source, target, sems

    def copy(self, kz, k):
        z, b = flip(self.head, kz), flip(self.blk, k)
        return send(
            self.source(z, b),
            self.target(self.head, self.blk),
            self.sems.at[0, kz, k],
            self.sems.at[1, kz, k],
            z,
            b,
        )

    def start(self, kz):
        for k in range(1 if kz == 0 else 0, 8):
            self.copy(kz, k).start()

    def arrive(self):
        for kz in range(4):
            for k in range(1 if kz == 0 else 0, 8):
                self.copy(kz, k).wait_recv()

    def drain(self):
        for kz in range(4):
            for k in range(1 if kz == 0 else 0, 8):
                self.copy(kz, k).wait_send()


def greet_all(head, blk):
    barrier = pltpu.get_barrier_semaphore()
    for kz in range(4):
        for k in range(8):
            if kz or k:
                pl.semaphore_signal(
                    barrier, inc=1, device_id=(flip(head, kz), flip(blk, k)), device_id_type=MESH
                )
    pl.semaphore_wait(barrier, 31)


def group_rows(value):
    return jnp.sum(value.reshape(value.shape[0] // 8, 8, value.shape[1]), axis=0)


def second_kernel(
    tiles, upp, down_own, out_own, cot_own,
    mixed, lse, received, up, down, out, cots,
    upz, outz, kvt, scores, att,
    usem, lsem, dsem, osem, psem, csem, esem,
):
    head, blk = lax.axis_index("head"), lax.axis_index("blk")
    greet_all(head, blk)
    uswap = Swap(head, blk, "blk", lambda i: upp.at[i], lambda i: upz.at[i], usem)
    uswap.start()
    oline = Line(head, blk, out_own, lambda i: outz.at[i], osem)
    oline.start()
    dline = Line(head, blk, down_own, lambda i: down.at[i], dsem)
    dline.start()
    cplane = Plane(head, blk, cot_own, lambda i: cots.at[i], csem)
    cplane.start()
    upz[blk] = upp[blk]
    outz[head] = out_own[...]
    down[head] = down_own[...]
    cots[blk] = cot_own[...]
    uswap.arrive()
    up[head] = upz[...]
    uline = Line(head, blk, upz, lambda i: up.at[i], lsem)
    uline.start()
    oplane = Plane(head, blk, outz, lambda i: out.at[:, i], psem)
    everyone = Everyone(head, blk, lambda z, b: att.at[z, b], lambda z, b: received.at[z, b], esem)
    kvt[...] = jnp.transpose(tiles[:, :, 0:64, :].reshape(2048, 128))

    def attend(z, carry):
        packed = tiles[z, :, 64:96, :].reshape(256, 128)
        left = half_lane((256, 128))
        flat = packed.astype(F32)
        results = []
        for side in range(2):
            query = flat if side == 0 else pltpu.roll(flat, 64, 1)
            query = jnp.where(left, query, 0.0).astype(BF)
            top = None
            for c in range(2048 // KEYS):
                keys = tiles[c // 2, 4 * (c % 2) : 4 * (c % 2) + 4, 0:64, :].reshape(KEYS, 128)
                part = contract_cols(keys, query)
                scores[side, c] = part
                peak = jnp.max(part.reshape(KEYS // 8, 8, 256), axis=0)
                top = peak if top is None else jnp.maximum(top, peak)
            top = jnp.max(top, axis=0, keepdims=True)
            total = jnp.zeros((8, 256), F32)
            mix = jnp.zeros((64, 256), F32)
            for c in range(2048 // KEYS):
                weights = jnp.exp2((scores[side, c] - top) * EXP_SCALE)
                total = total + group_rows(weights)
                mix = mix + jnp.dot(
                    kvt[64:128, KEYS * c : KEYS * c + KEYS],
                    weights.astype(BF),
                    preferred_element_type=F32,
                )
            total = jnp.sum(total, axis=0, keepdims=True)
            mix = mix / total
            mixed[z, 64 * side : 64 * side + 64, :] = mix
            lse[z, side : side + 1, :] = top * SCORE_SCALE + jnp.log(total)
            results.append(mix)
        both = jnp.transpose(jnp.concatenate(results, axis=0))
        att[z] = both.astype(BF).reshape(8, 32, 128)

        @pl.when(z > 0)
        def _():
            at = line_order(head, z)
            oline.step(at)
            dline.step(at)

        return carry

    lse[...] = jnp.zeros_like(lse)
    lax.fori_loop(0, 4, attend, 0)
    for kz in range(4):
        everyone.start(kz)
    received[head, blk] = att[head, blk]
    oplane.start()
    out[:, pl.ds(blk, 1)] = outz[...].reshape(4, 1, 32, 1024)
    for step in range(1, 4):
        uline.step(line_order(head, jnp.int32(step)))
    cplane.finish()
    oplane.finish()
    everyone.arrive()
    for copies in (uswap, oline, dline, uline, cplane, oplane, everyone):
        copies.drain()


def phase_two_kernel(tiles, up_parts, w_down, w_out, cotangent):
    dma = pltpu.SemaphoreType.DMA
    return pl.pallas_call(
        second_kernel,
        out_shape=(
            jax.ShapeDtypeStruct((4, 128, 256), F32),
            jax.ShapeDtypeStruct((4, 8, 256), F32),
            jax.ShapeDtypeStruct((4, 8, 32, 128), BF),
            jax.ShapeDtypeStruct((4, 8, 32, 512), BF),
            jax.ShapeDtypeStruct((4, 128, 1024), BF),
            jax.ShapeDtypeStruct((4, 8, 32, 1024), BF),
            jax.ShapeDtypeStruct((8, 128, 1024), BF),
        ),
        in_specs=whole(5),
        out_specs=whole(7),
        scratch_shapes=[
            pltpu.VMEM((8, 32, 512), BF),
            pltpu.VMEM((4, 32, 1024), BF),
            pltpu.VMEM((128, 2048), BF),
            pltpu.VMEM((2, 2048 // KEYS, KEYS, 256), F32),
            pltpu.VMEM((4, 8, 32, 128), BF),
            dma((2, 8)),
            dma((2, 2, 3)),
            dma((2, 2, 3)),
            dma((2, 2, 3)),
            dma((2, 7)),
            dma((2, 7)),
            dma((2, 4, 8)),
        ],
        compiler_params=pltpu.CompilerParams(
            collective_id=1, has_side_effects=True, vmem_limit_bytes=56 << 20
        ),
        name="second",
    )(tiles, up_parts, w_down, w_out, cotangent)
def third_kernel(
    received, tok, out, up, down, cots, scales,
    grad_rx, grad_middle, middle, outq, grad_down, grad_up, grad_out, sums,
    attended, n2g, act, gh, pairs, prx, gsend, gin, tsend, branch,
    nsem, ssem, gsem, esem,
):
    head, blk = lax.axis_index("head"), lax.axis_index("blk")
    core = lax.rem(blk, 2)
    greet_all(head, blk)
    for seq in range(2):
        for group in range(4):
            for i in range(2):
                first = received[group, 4 * seq + 2 * i].astype(F32)
                second = received[group, 4 * seq + 2 * i + 1].astype(F32)
                lanes = slice(256 * group + 128 * i, 256 * group + 128 * i + 128)
                attended[64 * seq : 64 * seq + 32, lanes] = join_halves(first, second, 0).astype(BF)
                attended[64 * seq + 32 : 64 * seq + 64, lanes] = join_halves(
                    first, second, 1
                ).astype(BF)
    middle[...] = tok[...].astype(F32) + jnp.dot(
        attended[...], out[...].reshape(1024, 1024), preferred_element_type=F32
    )
    for seq in range(2):
        rows = slice(64 * seq, 64 * seq + 64)
        unit, _ = norm_stats(middle[rows, :])
        n2g[blk, rows, :] = (unit * scales[2 + seq : 3 + seq, :]).astype(BF)
    plane = Plane(head, blk, n2g.at[blk], lambda i: n2g.at[i], nsem)
    plane.start()
    sibling = flip(blk, 1)

    def halves(i):
        return [
            send(pairs.at[w, i, 1 - core], prx.at[w, i], ssem.at[0, w, i], ssem.at[1, w, i], head, sibling)
            for w in range(2)
        ]

    def onward(i):
        peer = flip(blk, 2 * i)
        return send(gsend.at[i], gin.at[i], gsem.at[0, i], gsem.at[1, i], head, peer)

    def reduce(i):
        chip = lax.div(flip(blk, 2 * i), 2)
        for copy in halves(i):
            copy.wait_recv()
        gsend[i] = (pairs[0, i, core].astype(F32) + prx[0, i].astype(F32)).astype(BF)
        if i:
            onward(i).start()
        outq[chip] = (pairs[1, i, core].astype(F32) + prx[1, i].astype(F32)).astype(BF)

    for i in range(4):
        chip = lax.div(flip(blk, 2 * i), 2)
        if i == 0:
            plane.arrive(-1)
        else:
            plane.forward(i - 1)
            if i > 1:
                reduce(i - 1)
            plane.arrive(i - 1)
        at = pl.ds(2 * chip, 2)
        rows = n2g[at].reshape(256, 1024)
        hidden = jnp.dot(rows, up[...].reshape(1024, 512), preferred_element_type=F32)
        grad_active = contract_cols(cots[at].reshape(256, 1024), down[...].reshape(512, 1024))
        cdf = 0.5 * (1.0 + lax.erf(hidden * math.sqrt(0.5)))
        active = (hidden * cdf).astype(BF)
        slope = cdf + hidden * jnp.exp(-0.5 * hidden * hidden) * (1.0 / math.sqrt(2 * math.pi))
        grad_hidden = (grad_active * slope).astype(BF)
        act[at] = active.reshape(2, 128, 512)
        gh[at] = grad_hidden.reshape(2, 128, 512)
        pairs[0, i] = (
            contract_cols(grad_hidden, up[...].reshape(1024, 512)).astype(BF).reshape(2, 128, 1024)
        )
        pairs[1, i] = (
            jnp.dot(active, down[...].reshape(512, 1024), preferred_element_type=F32)
            .astype(BF)
            .reshape(2, 128, 1024)
        )
        for copy in halves(i):
            copy.start()
    reduce(3)
    reduce(0)
    for group in range(4):
        lanes = slice(128 * group, 128 * group + 128)
        grad_down[group] = contract_rows(
            act[:, :, lanes].reshape(1024, 128), cots[...].reshape(1024, 1024)
        ).astype(BF)
    for group in range(4):
        lanes = slice(256 * group, 256 * group + 256)
        part = contract_rows(n2g[:, :, lanes].reshape(1024, 256), gh[...].reshape(1024, 512))
        grad_up[group] = part.astype(BF).reshape(8, 32, 512)
    for i in range(1, 4):
        onward(i).wait_recv()
    sums[...] = jnp.zeros_like(sums)
    for seq in range(2):
        rows = slice(64 * seq, 64 * seq + 64)
        grad = gsend[0, rows, :].astype(F32)
        for i in range(1, 4):
            grad = grad + gin[i, rows, :].astype(F32)
        unit, spread = norm_stats(middle[rows, :])
        whole_grad = cots[blk, rows, :].astype(F32) + norm_back(
            unit, spread, grad, scales[2 + seq : 3 + seq, :]
        )
        grad_middle[rows, :] = whole_grad
        branch[rows, :] = whole_grad.astype(BF)
        sums[seq : seq + 1, :] = jnp.sum(grad * unit, axis=0, keepdims=True)
    grad_att = contract_cols(branch[...], out[...].reshape(1024, 1024))
    for seq in range(2):
        for group in range(4):
            for i in range(2):
                lanes = slice(256 * group + 128 * i, 256 * group + 128 * i + 128)
                top = grad_att[64 * seq : 64 * seq + 32, lanes]
                bottom = grad_att[64 * seq + 32 : 64 * seq + 64, lanes]
                for right in range(2):
                    tsend[group, 4 * seq + 2 * i + right] = join_halves(top, bottom, right).astype(BF)
    everyone = Everyone(head, blk, lambda z, b: tsend.at[z, b], lambda z, b: grad_rx.at[z, b], esem)
    for kz in range(4):
        everyone.start(kz)
    grad_rx[head, blk] = tsend[head, blk]
    for group in range(4):
        lanes = slice(256 * group, 256 * group + 256)
        part = contract_rows(attended[:, lanes], branch[...])
        grad_out[group] = part.astype(BF).reshape(8, 32, 1024)
    everyone.arrive()
    plane.drain()
    for i in range(4):
        for copy in halves(i):
            copy.wait_send()
        if i:
            onward(i).wait_send()
    everyone.drain()


def phase_three_kernel(received, tokens, out, up, down, cots, scales):
    dma = pltpu.SemaphoreType.DMA
    return pl.pallas_call(
        third_kernel,
        out_shape=(
            jax.ShapeDtypeStruct((4, 8, 32, 128), BF),
            jax.ShapeDtypeStruct((128, 1024), F32),
            jax.ShapeDtypeStruct((128, 1024), F32),
            jax.ShapeDtypeStruct((4, 128, 1024), BF),
            jax.ShapeDtypeStruct((4, 128, 1024), BF),
            jax.ShapeDtypeStruct((4, 8, 32, 512), BF),
            jax.ShapeDtypeStruct((4, 8, 32, 1024), BF),
            jax.ShapeDtypeStruct((8, 1024), F32),
        ),
        in_specs=whole(7),
        out_specs=whole(8),
        scratch_shapes=[
            pltpu.VMEM((128, 1024), BF),
            pltpu.VMEM((8, 128, 1024), BF),
            pltpu.VMEM((8, 128, 512), BF),
            pltpu.VMEM((8, 128, 512), BF),
            pltpu.VMEM((2, 4, 2, 128, 1024), BF),
            pltpu.VMEM((2, 4, 128, 1024), BF),
            pltpu.VMEM((4, 128, 1024), BF),
            pltpu.VMEM((4, 128, 1024), BF),
            pltpu.VMEM((4, 8, 32, 128), BF),
            pltpu.VMEM((128, 1024), BF),
            dma((2, 7)),
            dma((2, 2, 4)),
            dma((2, 4)),
            dma((2, 4, 8)),
        ],
        compiler_params=pltpu.CompilerParams(
            collective_id=2, has_side_effects=True, vmem_limit_bytes=58 << 20
        ),
        name="third",
    )(received, tokens, out, up, down, cots, scales)
class Scatter:
    def __init__(self, head, blk, terms, near, joined, far, sems):
        self.head, self.blk, self.core = head, blk, lax.rem(blk, 2)
        self.terms, self.near, self.joined, self.far, self.sems = terms, near, joined, far, sems

    def halves(self):
        return send(
            self.terms.at[:, :, 1 - self.core],
            self.near,
            self.sems.at[0, 0],
            self.sems.at[1, 0],
            self.head,
            flip(self.blk, 1),
        )

    def chips(self, i):
        peer = flip(self.blk, 2 * i)
        return send(
            self.joined.at[lax.div(peer, 2)],
            self.far.at[i],
            self.sems.at[0, i],
            self.sems.at[1, i],
            self.head,
            peer,
        )

    def start(self):
        self.halves().start()

    def join(self):
        self.halves().wait_recv()
        for chip in range(4):
            mine = self.terms[:, chip, pl.ds(self.core, 1)].astype(F32)
            mine = mine.reshape(mine.shape[0], *mine.shape[2:])
            self.joined[chip] = (mine + self.near[:, chip].astype(F32)).astype(BF)
        for i in (3, 1, 2):
            self.chips(i).start()

    def total(self):
        value = self.joined[lax.div(self.blk, 2)].astype(F32)
        for i in range(1, 4):
            self.chips(i).wait_recv()
            value = value + self.far[i].astype(F32)
        return value

    def drain(self):
        self.halves().wait_send()
        for i in range(1, 4):
            self.chips(i).wait_send()


def sum_four(parts):
    return (parts[0].astype(F32) + parts[1].astype(F32)) + (
        parts[2].astype(F32) + parts[3].astype(F32)
    )


def fourth_kernel(
    tiles, grad_rx, mixed, lse, outq, middle, grad_down, grad_up, grad_out,
    back, output, down_own, up_own, out_own,
    queries, grads, stats, keyt, dkv, dqt, bsend, oin, din, uin, usum, near, joined, far, osum, zin,
    qsem, dsem, usem, vsem, osem, xsem, bsem,
):
    head, blk = lax.axis_index("head"), lax.axis_index("blk")
    greet(head, blk, (1, 2, 3), range(1, 8))
    dswap = Swap(head, blk, "head", lambda i: grad_down.at[i], lambda i: din.at[i], dsem)
    dswap.start()
    scatter = Scatter(head, blk, grad_out, near, joined, far, osem)
    scatter.start()
    uswap = Swap(head, blk, "head", lambda i: grad_up.at[i], lambda i: uin.at[i], usem)
    uswap.start()
    outs = []
    for i in range(1, 4):
        peer = flip(blk, 2 * i)
        outs.append(
            send(outq.at[lax.div(peer, 2)], oin.at[i], qsem.at[0, i], qsem.at[1, i], head, peer)
        )
        outs[-1].start()
    vswap = Swap(head, blk, "blk", lambda i: usum.at[i], lambda i: up_own.at[i], vsem)
    xswap = Swap(head, blk, "head", lambda i: osum.at[i], lambda i: zin.at[i], xsem)
    left = half_lane((256, 128))
    keyt[...] = jnp.transpose(tiles[:, :, 0:64, :].reshape(2048, 128))[:64]

    def prepare(z, carry):
        flat = tiles[z, :, 64:96, :].reshape(256, 128).astype(F32)
        grad = grad_rx[z].reshape(256, 128).astype(F32)
        product = jnp.transpose(grad) * mixed[z]
        queries[2 * z] = jnp.where(left, flat, 0.0).astype(BF)
        queries[2 * z + 1] = jnp.where(left, pltpu.roll(flat, 64, 1), 0.0).astype(BF)
        grads[2 * z] = jnp.where(left, 0.0, pltpu.roll(grad, 64, 1)).astype(BF)
        grads[2 * z + 1] = jnp.where(left, 0.0, grad).astype(BF)
        for side in range(2):
            delta = jnp.sum(product[64 * side : 64 * side + 64], axis=0, keepdims=True)
            shift = lse[z, side : side + 1, :] * math.log2(math.e)
            stats[2 * z + side] = jnp.concatenate([shift, delta, jnp.zeros((6, 256), F32)], axis=0)
        return carry

    lax.fori_loop(0, 4, prepare, 0)
    dqt[...] = jnp.zeros_like(dqt)

    def kv_move(z):
        return Swap(
            head,
            blk,
            "blk",
            lambda i: bsend.at[i, z, pl.ds(0, 64)],
            lambda i: back.at[i, z, pl.ds(0, 64)],
            bsem.at[z],
        )

    def keys_step(z, carry):
        dkv[...] = jnp.zeros_like(dkv)

        def query_step(q, inner):
            query, grad = queries[q], grads[q]
            shift, delta = stats[q, 0:1, :], stats[q, 1:2, :]
            dq = dqt[q]
            for c in range(2):
                keys = tiles[z, 4 * c : 4 * c + 4, 0:64, :].reshape(256, 128)
                probs = jnp.exp2(contract_cols(keys, query) * EXP_SCALE - shift)
                slopes = (probs * (contract_cols(keys, grad) - delta)).astype(BF)
                dkv[c] += jnp.dot(slopes, query, preferred_element_type=F32) + jnp.dot(
                    probs.astype(BF), grad, preferred_element_type=F32
                )
                at = pl.ds(pl.multiple_of(512 * z + 256 * c, 256), 256)
                dq = dq + jnp.dot(keyt[:, at], slopes, preferred_element_type=F32)
            dqt[q] = dq
            return inner

        lax.fori_loop(0, 8, query_step, 0)
        scale = jnp.where(left, SCORE_SCALE, 1.0)
        for c in range(2):
            bsend[4 * c : 4 * c + 4, pl.ds(z, 1), 0:64, :] = (
                (dkv[c] * scale).astype(BF).reshape(4, 1, 64, 128)
            )
        kv_move(z).start()

        @pl.when(z == 0)
        def _():
            scatter.join()

        @pl.when(z == 2)
        def _():
            total = middle[...] + outq[lax.div(blk, 2)].astype(F32)
            for i in range(1, 4):
                outs[i - 1].wait_recv()
                total = total + oin[i].astype(F32)
            output[...] = total.astype(BF)
            osum[...] = scatter.total().astype(BF)
            xswap.start()
            zin[head] = osum[head]

        return carry

    lax.fori_loop(0, 4, keys_step, 0)
    for z in range(4):
        both = jnp.concatenate([dqt[2 * z], dqt[2 * z + 1]], axis=0)
        both = (jnp.transpose(both) * SCORE_SCALE).astype(BF)
        bsend[:, z, 64:96, :] = both.reshape(8, 32, 128)
    qmove = Swap(
        head,
        blk,
        "blk",
        lambda i: bsend.at[i, :, pl.ds(64, 32)],
        lambda i: back.at[i, :, pl.ds(64, 32)],
        bsem.at[4],
    )
    qmove.start()
    back[blk] = bsend[blk]
    uswap.arrive()
    uin[head] = grad_up[head]
    usum[...] = sum_four(uin).astype(BF)
    vswap.start()
    up_own[blk] = usum[blk]
    dswap.arrive()
    din[head] = grad_down[head]
    down_own[...] = sum_four(din)
    xswap.arrive()
    out_own[...] = sum_four(zin)
    vswap.arrive()
    for z in range(4):
        kv_move(z).arrive()
    qmove.arrive()
    for z in range(4):
        kv_move(z).drain()
    for copy in outs:
        copy.wait_send()
    for copies in (dswap, scatter, uswap, vswap, xswap, qmove):
        copies.drain()


def phase_four_kernel(tiles, grad_rx, mixed, lse, outq, middle, grad_down, grad_up, grad_out):
    dma = pltpu.SemaphoreType.DMA
    return pl.pallas_call(
        fourth_kernel,
        out_shape=(
            jax.ShapeDtypeStruct((8, 4, 96, 128), BF),
            jax.ShapeDtypeStruct((128, 1024), BF),
            jax.ShapeDtypeStruct((128, 1024), F32),
            jax.ShapeDtypeStruct((8, 32, 512), BF),
            jax.ShapeDtypeStruct((32, 1024), F32),
        ),
        in_specs=whole(9),
        out_specs=whole(5),
        scratch_shapes=[
            pltpu.VMEM((8, 256, 128), BF),
            pltpu.VMEM((8, 256, 128), BF),
            pltpu.VMEM((8, 8, 256), F32),
            pltpu.VMEM((64, 2048), BF),
            pltpu.VMEM((2, 256, 128), F32),
            pltpu.VMEM((8, 64, 256), F32),
            pltpu.VMEM((8, 4, 96, 128), BF),
            pltpu.VMEM((4, 128, 1024), BF),
            pltpu.VMEM((4, 128, 1024), BF),
            pltpu.VMEM((4, 8, 32, 512), BF),
            pltpu.VMEM((8, 32, 512), BF),
            pltpu.VMEM((4, 4, 32, 1024), BF),
            pltpu.VMEM((4, 4, 32, 1024), BF),
            pltpu.VMEM((4, 4, 32, 1024), BF),
            pltpu.VMEM((4, 32, 1024), BF),
            pltpu.VMEM((4, 32, 1024), BF),
            dma((2, 4)),
            dma((2, 4)),
            dma((2, 4)),
            dma((2, 8)),
            dma((2, 4)),
            dma((2, 4)),
            dma((5, 2, 8)),
        ],
        compiler_params=pltpu.CompilerParams(
            collective_id=3, has_side_effects=True, vmem_limit_bytes=56 << 20
        ),
        name="fourth",
    )(tiles, grad_rx, mixed, lse, outq, middle, grad_down, grad_up, grad_out)
def fifth_kernel(
    back, tabg, normed, wq, tok, scales, grad_middle, sums, ttab, tix,
    grad_tokens, gq, grad_attn, grad_mlp,
    gp, gnp, gin, terms, near, joined, far, osum, turned, part, sums_in, parts,
    gsem, osem, xsem, asem, bsem,
):
    head, blk = lax.axis_index("head"), lax.axis_index("blk")
    greet(head, blk, (1, 2, 3), range(1, 8))
    gswap = Swap(head, blk, "head", lambda i: gnp.at[i], lambda i: gin.at[i], gsem)

    def unturn(step, carry):
        at = flip(head, step)
        for seq in range(2):
            table = tabg[at]
            if seq:
                table = pltpu.roll(table, 64, 1)
            both, keyed = turn_tables(table, -1.0)
            rows = slice(64 * seq, 64 * seq + 64)
            for j in range(4):
                kv = back[4 * seq + j, at, 0:64, :].astype(F32)
                kv = kv * keyed[0] + lane_swap(kv) * keyed[1]
                gp[at, rows, 128 * j : 128 * j + 128] = kv.astype(BF)
            for i in range(2):
                first = back[4 * seq + 2 * i, at, 64:96, :].astype(F32)
                second = back[4 * seq + 2 * i + 1, at, 64:96, :].astype(F32)
                query = jnp.concatenate(
                    [join_halves(first, second, 0), join_halves(first, second, 1)], axis=0
                )
                query = query * both[0] + lane_swap(query) * both[1]
                gp[at, rows, 512 + 128 * i : 640 + 128 * i] = query.astype(BF)
        gnp[at] = contract_cols(gp[at], wq[...].reshape(1024, 768)).astype(BF)
        return carry

    for step in (3, 2, 1, 0):
        unturn(step, 0)
        if step:
            gswap.copies[step - 1].start()
    for group in range(4):
        lanes = slice(256 * group, 256 * group + 256)
        value = contract_rows(normed[:, :, lanes].reshape(512, 256), gp[...].reshape(512, 768))
        terms[group] = value.astype(BF).reshape(4, 2, 32, 768)
    scatter = Scatter(head, blk, terms, near, joined, far, osem)
    scatter.start()
    turned[...] = jnp.transpose(ttab[...])
    picked = turned[pl.ds(pl.multiple_of((head * 8 + blk) * 8, 8), 8), :]
    step_lane = lax.broadcasted_iota(jnp.int32, picked.shape, 1)
    columns = [
        jnp.sum(jnp.where(step_lane == tix[seq], picked, 0.0), axis=1, keepdims=True)
        for seq in range(2)
    ]
    scatter.join()
    osum[...] = scatter.total().astype(BF)
    xswap = Swap(head, blk, "head", lambda i: osum.at[i], lambda i: gq.at[i], xsem)
    xswap.start()
    gq[head] = osum[head]
    gswap.arrive()
    gin[head] = gnp[head]
    firsts = []
    for seq in range(2):
        rows = slice(64 * seq, 64 * seq + 64)
        grad = sum_four([gin[i, rows, :] for i in range(4)])
        unit, spread = norm_stats(tok[rows, :].astype(F32))
        grad_tokens[rows, :] = grad_middle[rows, :] + norm_back(
            unit, spread, grad, scales[seq : seq + 1, :]
        )
        firsts.append(jnp.sum(grad * unit, axis=0, keepdims=True))
    part[...] = jnp.concatenate(firsts + [sums[0:2, :], jnp.zeros((4, 1024), F32)], axis=0)
    one = Swap(head, blk, "blk", lambda i: part, lambda i: sums_in.at[i], asem)
    one.start()
    sums_in[blk] = part[...]
    one.arrive()
    total = sums_in[0]
    for i in range(1, 8):
        total = total + sums_in[i]
    parts[head] = total
    two = Swap(head, blk, "head", lambda i: parts.at[head], lambda i: parts.at[i], bsem)
    two.start()
    two.arrive()
    total = (parts[0] + parts[1]) + (parts[2] + parts[3])
    grad_attn[...] = columns[0] * total[0:1] + columns[1] * total[1:2]
    grad_mlp[...] = columns[0] * total[2:3] + columns[1] * total[3:4]
    xswap.arrive()
    for copies in (gswap, scatter, xswap, one, two):
        copies.drain()


def phase_five_kernel(back, tabg, normed, wq, tok, scales, grad_middle, sums, ttab, tix):
    dma = pltpu.SemaphoreType.DMA
    return pl.pallas_call(
        fifth_kernel,
        out_shape=(
            jax.ShapeDtypeStruct((128, 1024), F32),
            jax.ShapeDtypeStruct((4, 32, 768), BF),
            jax.ShapeDtypeStruct((8, 1024), F32),
            jax.ShapeDtypeStruct((8, 1024), F32),
        ),
        in_specs=whole(9) + [pl.BlockSpec(memory_space=pltpu.SMEM)],
        out_specs=whole(4),
        scratch_shapes=[
            pltpu.VMEM((4, 128, 768), BF),
            pltpu.VMEM((4, 128, 1024), BF),
            pltpu.VMEM((4, 128, 1024), BF),
            pltpu.VMEM((4, 4, 2, 32, 768), BF),
            pltpu.VMEM((4, 4, 32, 768), BF),
            pltpu.VMEM((4, 4, 32, 768), BF),
            pltpu.VMEM((4, 4, 32, 768), BF),
            pltpu.VMEM((4, 32, 768), BF),
            pltpu.VMEM((256, 64), F32),
            pltpu.VMEM((8, 1024), F32),
            pltpu.VMEM((8, 8, 1024), F32),
            pltpu.VMEM((4, 8, 1024), F32),
            dma((2, 4)),
            dma((2, 4)),
            dma((2, 4)),
            dma((2, 8)),
            dma((2, 4)),
        ],
        compiler_params=pltpu.CompilerParams(
            collective_id=4, has_side_effects=True, vmem_limit_bytes=48 << 20
        ),
        name="fifth",
    )(back, tabg, normed, wq, tok, scales, grad_middle, sums, ttab, tix)
def blocked(
    tokens,
    positions,
    time_index,
    time_table,
    w_qkv,
    w_out,
    w_up,
    w_down,
    scale_attn,
    scale_mlp,
    cotangent,
):
    cosine, sine = rotary_tables(positions, HEAD_DIM)
    cosine, sine = cosine[:, :, 0], sine[:, :, 0]
    table = jnp.concatenate([cosine[0], sine[0], cosine[1], sine[1]], axis=-1)
    wide = w_qkv.reshape(32, 3, 4, 4, 64)
    kv_cols = jnp.stack([wide[:, 1], wide[:, 2]], axis=3).reshape(32, 4, 512)
    wq_parts = jnp.concatenate([kv_cols, wide[:, 0].reshape(32, 4, 256)], axis=-1)
    wq_parts = jnp.swapaxes(wq_parts, 0, 1)
    up_parts = jnp.transpose(w_up.reshape(32, 4, 8, 128), (2, 0, 1, 3)).reshape(8, 32, 512)
    flat_tokens = tokens.reshape(128, 1024)
    tiles, normed, wq, scales, table_all = phase_one_kernel(
        tokens, table, wq_parts, time_table, time_index, scale_attn, scale_mlp
    )
    mixed, lse, received, up, down, out, cot_all = phase_two_kernel(
        tiles, up_parts, w_down, w_out, cotangent.reshape(128, 1024)
    )
    grad_rx, grad_middle, middle, outq, grad_down, grad_up, grad_out, sums = phase_three_kernel(
        received, flat_tokens, out, up, down, cot_all, scales
    )
    back, output, down_own, up_own, out_own = phase_four_kernel(
        tiles,
        grad_rx,
        mixed,
        lse,
        outq,
        middle,
        grad_down,
        grad_up,
        grad_out.reshape(4, 4, 2, 32, 1024),
    )
    grad_tokens, grad_wq, grad_attn, grad_mlp = phase_five_kernel(
        back,
        table_all,
        normed,
        wq,
        flat_tokens,
        scales,
        grad_middle,
        sums,
        time_table,
        time_index,
    )
    kv_cols = grad_wq[:, :, :512].reshape(4, 32, 4, 2, 64)
    wide = jnp.stack(
        [grad_wq[:, :, 512:].reshape(4, 32, 4, 64), kv_cols[:, :, :, 0], kv_cols[:, :, :, 1]],
        axis=0,
    )
    qkv_own = jnp.transpose(wide, (2, 0, 1, 3, 4)).reshape(32, 3072).astype(F32)
    up_own = jnp.transpose(up_own.reshape(8, 32, 4, 128), (1, 2, 0, 3)).reshape(32, 4096)
    return (
        output.reshape(2, 64, 1024),
        grad_tokens.reshape(2, 64, 1024),
        qkv_own,
        out_own,
        up_own.astype(F32),
        down_own,
        grad_attn,
        grad_mlp,
    )


def solution(mesh):
    fits = mesh.shape["head"] == 4 and mesh.shape["blk"] == 8
    placed = (
        P(None, ("head", "blk"), None),
        P(None, ("head", "blk")),
        P(),
        P(),
        P(("head", "blk"), None),
        P(("head", "blk"), None),
        P(("head", "blk"), None),
        P(("head", "blk"), None),
        P(("head", "blk"), None),
        P(("head", "blk"), None),
        P(None, ("head", "blk"), None),
    )
    return jax.shard_map(
        blocked if fits else general,
        mesh=mesh,
        in_specs=placed,
        out_specs=(
            P(None, ("head", "blk"), None),
            P(None, ("head", "blk"), None),
            P(("head", "blk"), None),
            P(("head", "blk"), None),
            P(("head", "blk"), None),
            P(("head", "blk"), None),
            P(("head", "blk"), None),
            P(("head", "blk"), None),
        ),
        check_vma=False,
    )
```

```python
import math

import jax
import jax.numpy as jnp
from jax import lax
from jax.experimental import pallas as pl
from jax.experimental.pallas import tpu as pltpu
from jax.sharding import PartitionSpec as P

HEADS = 16
HEAD_DIM = 64


NORM_EPSILON = 1e-05
PRECISE = lax.Precision.HIGHEST
START_TOP = -1e30
SCORE_SCALE = 0.125


def shifted(value, axis, steps):
    count = lax.axis_size(axis)
    pairs = [(source, (source + steps) % count) for source in range(count)]
    return lax.ppermute(value, axis, pairs)


def layer_norm(value, scale):
    centered = value - jnp.mean(value, axis=-1, keepdims=True)
    variance = jnp.mean(centered * centered, axis=-1, keepdims=True)
    return centered * lax.rsqrt(variance + NORM_EPSILON) * scale


def rotate(value, cosine_table, sine_table):
    half_dim = value.shape[-1] // 2
    first_half = value[..., :half_dim]
    second_half = value[..., half_dim:]
    return jnp.concatenate(
        [
            first_half * cosine_table - second_half * sine_table,
            second_half * cosine_table + first_half * sine_table,
        ],
        axis=-1,
    )


def rotary_tables(positions, head_dim):
    half_dim = head_dim // 2
    frequency = 10000.0 ** (-jnp.arange(half_dim, dtype=jnp.float32) / half_dim)
    turned = positions.astype(jnp.float32)[:, :, None, None] * frequency
    return (jnp.cos(turned), jnp.sin(turned))


def contract_rows(left, right):
    return lax.dot_general(
        left, right, (((0,), (0,)), ((), ())), preferred_element_type=jnp.float32
    )


def contract_cols(left, right):
    return lax.dot_general(
        left, right, (((1,), (1,)), ((), ())), preferred_element_type=jnp.float32
    )


def attend_step(running, query_block, key_block, value_block):
    row_top, row_sum, accum = running
    scores = (
        jnp.einsum("sqhd,skhd->sqhk", query_block, key_block, preferred_element_type=jnp.float32)
        * SCORE_SCALE
    )
    new_top = jnp.maximum(row_top, jnp.max(scores, axis=-1))
    shrink = jnp.exp(row_top - new_top)
    weights = jnp.exp(scores - new_top[..., None])
    row_sum = row_sum * shrink + jnp.sum(weights, axis=-1)
    accum = accum * shrink[..., None] + jnp.einsum(
        "sqhk,skhd->sqhd",
        weights.astype(jnp.bfloat16),
        value_block,
        preferred_element_type=jnp.float32,
    )
    return (new_top, row_sum, accum)


def back_step(query_block, key_block, value_block, grad_block, log_total, delta):
    scores = (
        jnp.einsum("sqhd,skhd->sqhk", query_block, key_block, preferred_element_type=jnp.float32)
        * SCORE_SCALE
    )
    probs = jnp.exp(scores - log_total[..., None])
    grad_values = jnp.einsum(
        "sqhk,sqhd->skhd",
        probs.astype(jnp.bfloat16),
        grad_block,
        preferred_element_type=jnp.float32,
    )
    grad_probs = jnp.einsum(
        "sqhd,skhd->sqhk", grad_block, value_block, preferred_element_type=jnp.float32
    )
    grad_scores = (probs * (grad_probs - delta[..., None])).astype(jnp.bfloat16)
    grad_query = jnp.einsum(
        "sqhk,skhd->sqhd", grad_scores, key_block, preferred_element_type=jnp.float32
    )
    grad_keys = jnp.einsum(
        "sqhk,sqhd->skhd", grad_scores, query_block, preferred_element_type=jnp.float32
    )
    return (grad_query, grad_keys, grad_values)


def general(
    tokens,
    positions,
    time_index,
    time_table,
    w_qkv,
    w_out,
    w_up,
    w_down,
    scale_attn,
    scale_mlp,
    cotangent,
):
    seq_count, row_count, model_width = tokens.shape
    group_count = lax.axis_size("head")
    local_heads = HEADS // group_count
    feature_width = local_heads * HEAD_DIM
    flat_rows = seq_count * row_count
    gathered = (
        lax.all_gather(w_qkv, ("head", "blk"), axis=0, tiled=True),
        lax.all_gather(w_out, ("head", "blk"), axis=0, tiled=True),
        lax.all_gather(w_up, ("head", "blk"), axis=0, tiled=True),
        lax.all_gather(w_down, ("head", "blk"), axis=0, tiled=True),
        lax.all_gather(scale_attn, ("head", "blk"), axis=0, tiled=True),
        lax.all_gather(scale_mlp, ("head", "blk"), axis=0, tiled=True),
    )
    full_qkv, full_out, full_up, full_down, full_scale_attn, full_scale_mlp = gathered
    step_count = time_table.shape[0]
    picker = (time_index[:, None] == jnp.arange(step_count, dtype=jnp.int32)[None, :]).astype(
        jnp.float32
    )
    time_embed = jnp.dot(picker, time_table, precision=PRECISE)
    scale_one = 1.0 + jnp.dot(time_embed, full_scale_attn.astype(jnp.float32), precision=PRECISE)
    scale_two = 1.0 + jnp.dot(time_embed, full_scale_mlp.astype(jnp.float32), precision=PRECISE)
    token_float = tokens.astype(jnp.float32)
    normed = (
        layer_norm(token_float, scale_one[:, None, :])
        .astype(jnp.bfloat16)
        .reshape(flat_rows, model_width)
    )
    projected = jnp.dot(normed, full_qkv, preferred_element_type=jnp.float32).reshape(
        seq_count, row_count, 3, HEADS, HEAD_DIM
    )
    cosine_table, sine_table = rotary_tables(positions, HEAD_DIM)
    query_tok = rotate(projected[:, :, 0], cosine_table, sine_table)
    keys_tok = rotate(projected[:, :, 1], cosine_table, sine_table)
    packed = (
        jnp.stack([query_tok, keys_tok, projected[:, :, 2]], axis=2)
        .reshape(seq_count, row_count, 3, model_width)
        .astype(jnp.bfloat16)
    )
    regrouped = lax.all_to_all(packed, "head", split_axis=3, concat_axis=1, tiled=True)
    block_len = regrouped.shape[1]
    local_query = regrouped[:, :, 0].reshape(seq_count, block_len, local_heads, HEAD_DIM)
    local_keys = regrouped[:, :, 1]
    local_values = regrouped[:, :, 2]
    start_state = (
        jnp.full((seq_count, block_len, local_heads), START_TOP, jnp.float32),
        jnp.zeros((seq_count, block_len, local_heads), jnp.float32),
        jnp.zeros((seq_count, block_len, local_heads, HEAD_DIM), jnp.float32),
    )
    key_piece = lax.all_gather(local_keys, "blk", axis=1, tiled=True)
    value_piece = lax.all_gather(local_values, "blk", axis=1, tiled=True)
    piece_len = key_piece.shape[1]
    step_len = math.gcd(piece_len, block_len)

    def one_block(index, state):
        key_block = lax.dynamic_slice_in_dim(key_piece, index * step_len, step_len, 1).reshape(
            seq_count, step_len, local_heads, HEAD_DIM
        )
        value_block = lax.dynamic_slice_in_dim(value_piece, index * step_len, step_len, 1).reshape(
            seq_count, step_len, local_heads, HEAD_DIM
        )
        return attend_step(state, local_query, key_block, value_block)

    row_top, row_sum, accum = lax.fori_loop(0, piece_len // step_len, one_block, start_state)
    mixed = accum / row_sum[..., None]
    log_total = row_top + jnp.log(row_sum)
    attended_heads = mixed.astype(jnp.bfloat16).reshape(seq_count, block_len, feature_width)
    attended = lax.all_to_all(
        attended_heads, "head", split_axis=1, concat_axis=2, tiled=True
    ).reshape(flat_rows, model_width)
    branch = jnp.dot(attended, full_out, preferred_element_type=jnp.float32)
    middle = token_float + branch.reshape(seq_count, row_count, model_width)
    normed_two = (
        layer_norm(middle, scale_two[:, None, :])
        .astype(jnp.bfloat16)
        .reshape(flat_rows, model_width)
    )
    hidden = jnp.dot(normed_two, full_up, preferred_element_type=jnp.float32)
    active = jax.nn.gelu(hidden, approximate=False).astype(jnp.bfloat16)
    result = middle.reshape(flat_rows, model_width) + jnp.dot(
        active, full_down, preferred_element_type=jnp.float32
    )
    output = result.astype(jnp.bfloat16).reshape(seq_count, row_count, model_width)
    back_qkv, back_out, back_up, back_down = (
        lax.all_gather(w_qkv, ("head", "blk"), axis=0, tiled=True),
        lax.all_gather(w_out, ("head", "blk"), axis=0, tiled=True),
        lax.all_gather(w_up, ("head", "blk"), axis=0, tiled=True),
        lax.all_gather(w_down, ("head", "blk"), axis=0, tiled=True),
    )
    grad_out = cotangent.reshape(flat_rows, model_width)
    grad_active = contract_cols(grad_out, back_down)
    grad_w_down = contract_rows(active, grad_out)
    gelu_value, gelu_pull = jax.vjp(lambda entry: jax.nn.gelu(entry, approximate=False), hidden)
    grad_hidden = gelu_pull(grad_active)[0].astype(jnp.bfloat16)
    grad_w_up = contract_rows(normed_two, grad_hidden)
    grad_normed_two = contract_cols(grad_hidden, back_up).reshape(seq_count, row_count, model_width)
    norm_value, norm_pull = jax.vjp(layer_norm, middle, scale_two[:, None, :])
    grad_middle_norm, grad_scale_two = norm_pull(grad_normed_two)
    grad_middle = cotangent.astype(jnp.float32) + grad_middle_norm
    grad_scale_mlp = jnp.dot(time_embed.T, grad_scale_two[:, 0, :], precision=PRECISE)
    grad_branch = grad_middle.reshape(flat_rows, model_width).astype(jnp.bfloat16)
    grad_w_out = contract_rows(attended, grad_branch)
    grad_attended = (
        contract_cols(grad_branch, back_out)
        .astype(jnp.bfloat16)
        .reshape(seq_count, row_count, model_width)
    )
    grad_heads = lax.all_to_all(
        grad_attended, "head", split_axis=2, concat_axis=1, tiled=True
    ).reshape(seq_count, block_len, local_heads, HEAD_DIM)
    delta = jnp.sum(grad_heads.astype(jnp.float32) * mixed, axis=-1)

    def turn(index, state):
        key_now, value_now, grad_keys_now, grad_values_now, grad_query_sum = state
        grad_query, grad_keys, grad_values = back_step(
            local_query,
            key_now.reshape(seq_count, block_len, local_heads, HEAD_DIM),
            value_now.reshape(seq_count, block_len, local_heads, HEAD_DIM),
            grad_heads,
            log_total,
            delta,
        )
        moved_keys, moved_values = shifted((key_now, value_now), "blk", 1)
        moved_grad_keys, moved_grad_values = (
            shifted(
                (grad_keys_now + grad_keys.reshape(seq_count, block_len, feature_width)).astype(
                    jnp.bfloat16
                ),
                "blk",
                1,
            ).astype(jnp.float32),
            shifted(
                (grad_values_now + grad_values.reshape(seq_count, block_len, feature_width)).astype(
                    jnp.bfloat16
                ),
                "blk",
                1,
            ).astype(jnp.float32),
        )
        return (
            moved_keys,
            moved_values,
            moved_grad_keys,
            moved_grad_values,
            grad_query_sum + grad_query,
        )

    zero_kv = jnp.zeros((seq_count, block_len, feature_width), jnp.float32)
    begin = (
        local_keys,
        local_values,
        zero_kv,
        zero_kv,
        jnp.zeros((seq_count, block_len, local_heads, HEAD_DIM), jnp.float32),
    )
    final_state = lax.fori_loop(0, lax.axis_size("blk"), turn, begin)
    grad_keys_own = final_state[2]
    grad_values_own = final_state[3]
    grad_query_all = final_state[4]
    stacked = jnp.stack(
        [
            grad_query_all.reshape(seq_count, block_len, feature_width) * SCORE_SCALE,
            grad_keys_own * SCORE_SCALE,
            grad_values_own,
        ],
        axis=2,
    ).astype(jnp.bfloat16)
    returned = lax.all_to_all(stacked, "head", split_axis=1, concat_axis=3, tiled=True)
    grad_query_tok = (
        returned[:, :, 0].astype(jnp.float32).reshape(seq_count, row_count, HEADS, HEAD_DIM)
    )
    grad_keys_tok = (
        returned[:, :, 1].astype(jnp.float32).reshape(seq_count, row_count, HEADS, HEAD_DIM)
    )
    grad_values_tok = (
        returned[:, :, 2].astype(jnp.float32).reshape(seq_count, row_count, HEADS, HEAD_DIM)
    )
    grad_projected = (
        jnp.stack(
            [
                rotate(grad_query_tok, cosine_table, -sine_table),
                rotate(grad_keys_tok, cosine_table, -sine_table),
                grad_values_tok,
            ],
            axis=2,
        )
        .reshape(flat_rows, 3 * model_width)
        .astype(jnp.bfloat16)
    )
    grad_w_qkv = contract_rows(normed, grad_projected)
    grad_normed = contract_cols(grad_projected, back_qkv).reshape(seq_count, row_count, model_width)
    first_value, first_pull = jax.vjp(layer_norm, token_float, scale_one[:, None, :])
    grad_token_norm, grad_scale_one = first_pull(grad_normed)
    grad_tokens = grad_middle + grad_token_norm
    grad_scale_attn = jnp.dot(time_embed.T, grad_scale_one[:, 0, :], precision=PRECISE)
    shards = (
        lax.psum_scatter(grad_w_qkv, ("head", "blk"), scatter_dimension=0, tiled=True),
        lax.psum_scatter(grad_w_out, ("head", "blk"), scatter_dimension=0, tiled=True),
        lax.psum_scatter(grad_w_up, ("head", "blk"), scatter_dimension=0, tiled=True),
        lax.psum_scatter(grad_w_down, ("head", "blk"), scatter_dimension=0, tiled=True),
        lax.psum_scatter(grad_scale_attn, ("head", "blk"), scatter_dimension=0, tiled=True),
        lax.psum_scatter(grad_scale_mlp, ("head", "blk"), scatter_dimension=0, tiled=True),
    )
    return (output, grad_tokens, shards[0], shards[1], shards[2], shards[3], shards[4], shards[5])


EPS = NORM_EPSILON
BF = jnp.bfloat16
F32 = jnp.float32


def norm_stats(value):
    centered = value - jnp.mean(value, axis=-1, keepdims=True)
    spread = lax.rsqrt(jnp.mean(centered * centered, axis=-1, keepdims=True) + EPS)
    return centered * spread, spread


def norm_back(unit, spread, grad, scale):
    scaled = grad * scale
    return spread * (
        scaled
        - jnp.mean(scaled, axis=-1, keepdims=True)
        - unit * jnp.mean(scaled * unit, axis=-1, keepdims=True)
    )


MESH = pl.DeviceIdType.MESH


def flip(value, bits):
    for bit in (1, 2, 4):
        if bits & bit:
            value = value + bit - 2 * bit * lax.rem(lax.div(value, bit), 2)
    return value


def greet(head, blk, heads, blks):
    barrier = pltpu.get_barrier_semaphore()
    for k in heads:
        pl.semaphore_signal(barrier, inc=1, device_id=(flip(head, k), blk), device_id_type=MESH)
    for k in blks:
        pl.semaphore_signal(barrier, inc=1, device_id=(head, flip(blk, k)), device_id_type=MESH)
    pl.semaphore_wait(barrier, len(heads) + len(blks))


def send(source, target, send_sem, recv_sem, head, blk):
    return pltpu.make_async_remote_copy(
        src_ref=source,
        dst_ref=target,
        send_sem=send_sem,
        recv_sem=recv_sem,
        device_id=(head, blk),
        device_id_type=MESH,
    )


class Swap:
    def __init__(self, head, blk, axis, source, target, sems):
        self.copies = []
        count = 4 if axis == "head" else 8
        me = head if axis == "head" else blk
        for k in range(1, count):
            peer = flip(me, k)
            where = (peer, blk) if axis == "head" else (head, peer)
            self.copies.append(
                send(source(peer), target(me), sems.at[0, k], sems.at[1, k], *where)
            )

    def start(self):
        for copy in self.copies:
            copy.start()

    def arrive(self):
        for copy in self.copies:
            copy.wait_recv()

    def drain(self):
        for copy in self.copies:
            copy.wait_send()


class Plane:
    def __init__(self, head, blk, own, slot, sems):
        sibling = flip(blk, 1)
        self.first = [send(own, slot(blk), sems.at[0, 0], sems.at[1, 0], head, sibling)]
        self.passed = []
        for i, k in enumerate((2, 4, 6)):
            peer = flip(blk, k)
            self.first.append(
                send(own, slot(blk), sems.at[0, i + 1], sems.at[1, i + 1], head, peer)
            )
            self.passed.append(
                send(slot(peer), slot(peer), sems.at[0, i + 4], sems.at[1, i + 4], head, sibling)
            )

    def start(self):
        for i in (3, 1, 2, 0):
            self.first[i].start()

    def forward(self, i):
        self.first[i + 1].wait_recv()
        self.passed[i].start()

    def arrive(self, i):
        if i < 0:
            self.first[0].wait_recv()
        else:
            self.passed[i].wait_recv()

    def finish(self):
        for i in range(3):
            self.forward(i)
        for i in range(-1, 3):
            self.arrive(i)

    def drain(self):
        for copy in self.first + self.passed:
            copy.wait_send()


def line_order(head, step):
    low = jnp.minimum(head, 3 - head)
    swap = low * ((step == 0).astype(jnp.int32) - (step == 1).astype(jnp.int32))
    at = step + swap
    return jnp.where(head < 2, at, 3 - at)


class Line:
    def __init__(self, head, blk, own, slot, sems):
        self.head, self.blk, self.own, self.slot, self.sems = head, blk, own, slot, sems

    def copy(self, source, at, up, k):
        head = self.head
        target = jnp.where(up, head + 1, head - 1)
        way = jnp.where(up, 0, 1)
        return send(
            source, self.slot(at), self.sems.at[0, way, k], self.sems.at[1, way, k], target, self.blk
        )

    def start(self):
        head = self.head

        @pl.when(head < 3)
        def _():
            self.copy(self.own, head, True, 0).start()

        @pl.when(head > 0)
        def _():
            self.copy(self.own, head, False, 0).start()

    def step(self, at):
        head = self.head
        up = at < head
        k = jnp.where(up, head - 1 - at, at - head - 1)
        self.copy(self.slot(at), at, up, k).wait_recv()

        @pl.when(jnp.where(up, head < 3, head > 0))
        def _():
            self.copy(self.slot(at), at, up, k + 1).start()

    def drain(self):
        head = self.head
        for k in range(3):

            @pl.when(jnp.logical_and(head < 3, head >= k))
            def _():
                self.copy(self.own, head, True, k).wait_send()

            @pl.when(jnp.logical_and(head > 0, head + k <= 3))
            def _():
                self.copy(self.own, head, False, k).wait_send()


class Reach:
    def __init__(self, head, blk, own, slot, sems):
        self.head, self.blk, self.own, self.slot, self.sems = head, blk, own, slot, sems
        self.middle = jnp.logical_and(head > 0, head < 3)

    def copy(self, k):
        peer = flip(self.head, k)
        return send(
            self.own, self.slot(self.head), self.sems.at[0, k], self.sems.at[1, k], peer, self.blk
        )

    def passed(self):
        at = self.slot(flip(self.head, 2))
        return send(at, at, self.sems.at[0, 0], self.sems.at[1, 3], flip(self.head, 1), self.blk)

    def start(self):
        self.copy(2).start()
        self.copy(1).start()

        @pl.when(self.middle)
        def _():
            self.copy(3).start()

    def forward(self):
        self.copy(2).wait_recv()

        @pl.when(self.middle)
        def _():
            self.passed().start()

    def arrive(self):
        self.copy(1).wait_recv()
        self.copy(3).wait_recv()

    def drain(self):
        self.copy(1).wait_send()
        self.copy(2).wait_send()

        @pl.when(self.middle)
        def _():
            self.copy(3).wait_send()
            self.passed().wait_send()


class Fold:
    def __init__(self, head, blk, terms, via, joined, into, sems):
        self.head, self.blk, self.sems = head, blk, sems
        self.terms, self.via, self.joined, self.into = terms, via, joined, into
        self.middle = jnp.logical_and(head > 0, head < 3)

    def copy(self, k):
        peer = flip(self.head, k)
        return send(
            self.terms.at[peer],
            self.into.at[k],
            self.sems.at[0, k],
            self.sems.at[1, k],
            peer,
            self.blk,
        )

    def handed(self):
        return send(
            self.terms.at[flip(self.head, 3)],
            self.via,
            self.sems.at[0, 0],
            self.sems.at[1, 0],
            flip(self.head, 1),
            self.blk,
        )

    def relayed(self):
        return send(
            self.joined,
            self.into.at[2],
            self.sems.at[0, 2],
            self.sems.at[1, 2],
            flip(self.head, 2),
            self.blk,
        )

    def start_far(self):
        @pl.when(jnp.logical_not(self.middle))
        def _():
            self.handed().start()

    def start_one(self, k):
        if k == 1:
            self.copy(1).start()
        elif k == 2:

            @pl.when(jnp.logical_not(self.middle))
            def _():
                self.copy(2).start()

        else:

            @pl.when(self.middle)
            def _():
                self.copy(3).start()

    def start(self):
        self.start_far()
        for k in (2, 3, 1):
            self.start_one(k)

    def relay(self):
        @pl.when(self.middle)
        def _():
            self.handed().wait_recv()
            mine = self.terms[flip(self.head, 2)].astype(F32)
            self.joined[...] = (mine + self.via[...].astype(F32)).astype(BF)
            self.relayed().start()

    def arrive(self):
        self.copy(1).wait_recv()
        self.copy(2).wait_recv()

        @pl.when(self.middle)
        def _():
            self.copy(3).wait_recv()

        @pl.when(jnp.logical_not(self.middle))
        def _():
            self.into[3] = jnp.zeros_like(self.into[3])

        self.into[0] = self.terms[self.head]

    def drain(self):
        self.copy(1).wait_send()

        @pl.when(self.middle)
        def _():
            self.copy(3).wait_send()
            self.relayed().wait_send()

        @pl.when(jnp.logical_not(self.middle))
        def _():
            self.copy(2).wait_send()
            self.handed().wait_send()


def half_lane(shape):
    return lax.broadcasted_iota(jnp.int32, shape, 1) < 64


def lane_swap(value):
    lane = lax.broadcasted_iota(jnp.int32, value.shape, 1)
    return jnp.where(
        lax.rem(lane, 64) < 32, pltpu.roll(value, 96, 1), pltpu.roll(value, 32, 1)
    )


def turn_tables(table, sign):
    lane = lax.broadcasted_iota(jnp.int32, table.shape, 1)
    cosine = jnp.where(lane < 32, table, 0.0)
    cosine = cosine + pltpu.roll(cosine, 32, 1)
    sine = jnp.where(jnp.logical_and(lane >= 32, lane < 64), table, 0.0) * sign
    sine = sine - pltpu.roll(sine, 96, 1)
    both = (cosine + pltpu.roll(cosine, 64, 1), sine + pltpu.roll(sine, 64, 1))
    return both, (jnp.where(lane < 64, cosine, 1.0), sine)


def join_halves(top, bottom, right):
    left = half_lane(top.shape)
    if right:
        return jnp.where(left, pltpu.roll(top, 64, 1), bottom)
    return jnp.where(left, top, pltpu.roll(bottom, 64, 1))


def first_kernel(
    tok, tab, wqp, ttab, sca, scm, upp, out_own, tix,
    tiles, normed, wq, scales, tabg, upz, outz, tokg,
    wqz, turned, part, sums, parts, out_tiles,
    zsem, lsem, tsem, wsem, asem, bsem, psem, usem, osem,
):
    head, blk = lax.axis_index("head"), lax.axis_index("blk")
    greet(head, blk, (1, 2, 3), range(1, 8))
    zswap = Swap(head, blk, "head", lambda i: wqp.at[i], lambda i: wqz.at[i], zsem)
    zswap.start()
    line = Line(head, blk, tok, lambda i: tokg.at[i], lsem)
    tline = Line(head, blk, tab, lambda i: tabg.at[i], tsem)
    tline.start()
    line.start()
    uswap = Swap(head, blk, "blk", lambda i: upp.at[i], lambda i: upz.at[i], usem)
    oline = Reach(head, blk, out_own, lambda i: outz.at[i], osem)
    turned[...] = jnp.transpose(ttab[...])
    rows = turned[pl.ds(pl.multiple_of((head * 8 + blk) * 8, 8), 8), :]
    step_lane = lax.broadcasted_iota(jnp.int32, rows.shape, 1)
    terms = []
    for weight in (sca, scm):
        for seq in range(2):
            column = jnp.sum(jnp.where(step_lane == tix[seq], rows, 0.0), axis=1, keepdims=True)
            terms.append(jnp.sum(column * weight[...].astype(F32), axis=0, keepdims=True))
    part[...] = jnp.concatenate(terms + [jnp.zeros((4, 1024), F32)], axis=0)
    one = Swap(head, blk, "blk", lambda i: part, lambda i: sums.at[i], asem)
    one.start()
    uswap.start()
    sums[blk] = part[...]
    wqz[head] = wqp[head]
    tokg[head] = tok[...]
    tabg[head] = tab[...]
    upz[blk] = upp[blk]
    outz[head] = out_own[...]
    one.arrive()
    total = sums[0]
    for i in range(1, 8):
        total = total + sums[i]
    parts[head] = total
    two = Swap(head, blk, "head", lambda i: parts.at[head], lambda i: parts.at[i], bsem)
    two.start()
    zswap.arrive()
    plane = Plane(head, blk, wqz, lambda i: wq.at[:, i], wsem)
    plane.start()
    wq[:, pl.ds(blk, 1)] = wqz[...].reshape(4, 1, 32, 768)
    two.arrive()
    total = 1.0 + ((parts[0] + parts[1]) + (parts[2] + parts[3]))
    scales[...] = total

    def gather(step, carry):
        at = line_order(head, step)

        @pl.when(step > 0)
        def _():
            tline.step(at)
            line.step(at)

        for seq in range(2):
            unit, _ = norm_stats(tokg[at, seq].astype(F32))
            normed[at, pl.ds(64 * seq, 64), :] = (unit * scales[seq : seq + 1, :]).astype(BF)
        return carry

    def project(step, carry):
        at = line_order(head, step)
        proj = jnp.dot(
            normed[at], wq[...].reshape(1024, 768), preferred_element_type=F32
        )
        for seq in range(2):
            table = tabg[at]
            if seq:
                table = pltpu.roll(table, 64, 1)
            both, keyed = turn_tables(table, 1.0)
            mine = proj[64 * seq : 64 * seq + 64]
            for j in range(4):
                kv = mine[:, 128 * j : 128 * j + 128]
                kv = kv * keyed[0] + lane_swap(kv) * keyed[1]
                out_tiles[4 * seq + j, at, 0:64, :] = kv.astype(BF)
            for i in range(2):
                query = mine[:, 512 + 128 * i : 640 + 128 * i]
                query = query * both[0] + lane_swap(query) * both[1]
                for right in range(2):
                    packed = join_halves(query[:32], query[32:], right)
                    out_tiles[4 * seq + 2 * i + right, at, 64:96, :] = packed.astype(BF)
        move(at).start()
        tiles[at, blk] = out_tiles[blk, at]
        return carry

    def move(at):
        return Swap(
            head, blk, "blk", lambda i: out_tiles.at[i, at], lambda i: tiles.at[at, i], psem.at[at]
        )

    lax.fori_loop(0, 3, gather, 0)
    oline.start()
    plane.finish()
    lax.fori_loop(0, 3, project, 0)

    def last(step, carry):
        gather(step, carry)
        return project(step, carry)

    lax.fori_loop(3, 4, last, 0)
    oline.forward()
    uswap.arrive()
    oline.arrive()
    for at in range(4):
        move(at).arrive()
    for at in range(4):
        move(at).drain()
    for copies in (zswap, line, tline, plane, one, two, uswap, oline):
        copies.drain()


def whole(count):
    return [pl.BlockSpec(memory_space=pltpu.VMEM)] * count


def phase_one_kernel(
    tokens, table, wq_parts, time_table, time_index, scale_attn, scale_mlp, up_parts, w_out
):
    dma = pltpu.SemaphoreType.DMA
    return pl.pallas_call(
        first_kernel,
        out_shape=(
            jax.ShapeDtypeStruct((4, 8, 96, 128), BF),
            jax.ShapeDtypeStruct((4, 128, 1024), BF),
            jax.ShapeDtypeStruct((4, 8, 32, 768), BF),
            jax.ShapeDtypeStruct((8, 1024), F32),
            jax.ShapeDtypeStruct((4, 64, 128), F32),
            jax.ShapeDtypeStruct((8, 32, 512), BF),
            jax.ShapeDtypeStruct((4, 32, 1024), BF),
            jax.ShapeDtypeStruct((4, 2, 64, 1024), BF),
        ),
        in_specs=whole(8) + [pl.BlockSpec(memory_space=pltpu.SMEM)],
        out_specs=whole(8),
        scratch_shapes=[
            pltpu.VMEM((4, 32, 768), BF),
            pltpu.VMEM((256, 64), F32),
            pltpu.VMEM((8, 1024), F32),
            pltpu.VMEM((8, 8, 1024), F32),
            pltpu.VMEM((4, 8, 1024), F32),
            pltpu.VMEM((8, 4, 96, 128), BF),
            dma((2, 4)),
            dma((2, 2, 3)),
            dma((2, 2, 3)),
            dma((2, 7)),
            dma((2, 8)),
            dma((2, 4)),
            dma((4, 2, 8)),
            dma((2, 8)),
            dma((2, 4)),
        ],
        compiler_params=pltpu.CompilerParams(
            collective_id=0, has_side_effects=True, vmem_limit_bytes=48 << 20
        ),
        name="first",
    )(tokens, table, wq_parts, time_table, scale_attn, scale_mlp, up_parts, w_out, time_index)


EXP_SCALE = SCORE_SCALE * math.log2(math.e)
KEYS = 256


class Everyone:
    def __init__(self, head, blk, source, target, sems):
        self.head, self.blk, self.source, self.target, self.sems = head, blk, source, target, sems

    def copy(self, kz, k):
        z, b = flip(self.head, kz), flip(self.blk, k)
        return send(
            self.source(z, b),
            self.target(self.head, self.blk),
            self.sems.at[0, kz, k],
            self.sems.at[1, kz, k],
            z,
            b,
        )

    def start(self, kz):
        for k in range(1 if kz == 0 else 0, 8):
            self.copy(kz, k).start()

    def arrive(self):
        for kz in range(4):
            for k in range(1 if kz == 0 else 0, 8):
                self.copy(kz, k).wait_recv()

    def drain(self):
        for kz in range(4):
            for k in range(1 if kz == 0 else 0, 8):
                self.copy(kz, k).wait_send()


def greet_all(head, blk):
    barrier = pltpu.get_barrier_semaphore()
    for kz in range(4):
        for k in range(8):
            if kz or k:
                pl.semaphore_signal(
                    barrier, inc=1, device_id=(flip(head, kz), flip(blk, k)), device_id_type=MESH
                )
    pl.semaphore_wait(barrier, 31)


def group_rows(value):
    return jnp.sum(value.reshape(value.shape[0] // 8, 8, value.shape[1]), axis=0)


def second_kernel(
    tiles, upz, down_own, outz, cot_own,
    mixed, lse, received, up, down, out, cots,
    kvt, scores, att,
    lsem, dsem, psem, csem, esem,
):
    head, blk = lax.axis_index("head"), lax.axis_index("blk")
    greet_all(head, blk)
    uline = Reach(head, blk, upz, lambda i: up.at[i], lsem)
    uline.start()
    dline = Reach(head, blk, down_own, lambda i: down.at[i], dsem)
    dline.start()
    oplane = Plane(head, blk, outz, lambda i: out.at[:, i], psem)
    oplane.start()
    cplane = Plane(head, blk, cot_own, lambda i: cots.at[i], csem)
    cplane.start()
    up[head] = upz[...]
    down[head] = down_own[...]
    cots[blk] = cot_own[...]
    out[:, pl.ds(blk, 1)] = outz[...].reshape(4, 1, 32, 1024)
    everyone = Everyone(head, blk, lambda z, b: att.at[z, b], lambda z, b: received.at[z, b], esem)
    kvt[...] = jnp.transpose(tiles[:, :, 0:64, :].reshape(2048, 128))

    def attend(z, carry):
        packed = tiles[z, :, 64:96, :].reshape(256, 128)
        left = half_lane((256, 128))
        flat = packed.astype(F32)
        results = []
        for side in range(2):
            query = flat if side == 0 else pltpu.roll(flat, 64, 1)
            query = jnp.where(left, query, 0.0).astype(BF)
            top = None
            for c in range(2048 // KEYS):
                keys = tiles[c // 2, 4 * (c % 2) : 4 * (c % 2) + 4, 0:64, :].reshape(KEYS, 128)
                part = contract_cols(keys, query)
                scores[side, c] = part
                peak = jnp.max(part.reshape(KEYS // 8, 8, 256), axis=0)
                top = peak if top is None else jnp.maximum(top, peak)
            top = jnp.max(top, axis=0, keepdims=True)
            total = jnp.zeros((8, 256), F32)
            mix = jnp.zeros((64, 256), F32)
            for c in range(2048 // KEYS):
                weights = jnp.exp2((scores[side, c] - top) * EXP_SCALE)
                total = total + group_rows(weights)
                mix = mix + jnp.dot(
                    kvt[64:128, KEYS * c : KEYS * c + KEYS],
                    weights.astype(BF),
                    preferred_element_type=F32,
                )
            total = jnp.sum(total, axis=0, keepdims=True)
            mix = mix / total
            mixed[z, 64 * side : 64 * side + 64, :] = mix
            lse[z, side : side + 1, :] = top * SCORE_SCALE + jnp.log(total)
            results.append(mix)
        both = jnp.transpose(jnp.concatenate(results, axis=0))
        att[z] = both.astype(BF).reshape(8, 32, 128)

        return carry

    lse[...] = jnp.zeros_like(lse)
    lax.fori_loop(0, 4, attend, 0)
    for kz in range(4):
        everyone.start(kz)
    received[head, blk] = att[head, blk]
    for i in range(3):
        oplane.forward(i)
    for i in range(3):
        cplane.forward(i)
    uline.forward()
    dline.forward()
    for i in range(-1, 3):
        oplane.arrive(i)
        cplane.arrive(i)
    everyone.arrive()
    uline.arrive()
    dline.arrive()
    for copies in (dline, uline, cplane, oplane, everyone):
        copies.drain()


def phase_two_kernel(tiles, upz, w_down, outz, cotangent):
    dma = pltpu.SemaphoreType.DMA
    return pl.pallas_call(
        second_kernel,
        out_shape=(
            jax.ShapeDtypeStruct((4, 128, 256), F32),
            jax.ShapeDtypeStruct((4, 8, 256), F32),
            jax.ShapeDtypeStruct((4, 8, 32, 128), BF),
            jax.ShapeDtypeStruct((4, 8, 32, 512), BF),
            jax.ShapeDtypeStruct((4, 128, 1024), BF),
            jax.ShapeDtypeStruct((4, 8, 32, 1024), BF),
            jax.ShapeDtypeStruct((8, 128, 1024), BF),
        ),
        in_specs=whole(5),
        out_specs=whole(7),
        scratch_shapes=[
            pltpu.VMEM((128, 2048), BF),
            pltpu.VMEM((2, 2048 // KEYS, KEYS, 256), F32),
            pltpu.VMEM((4, 8, 32, 128), BF),
            dma((2, 4)),
            dma((2, 4)),
            dma((2, 7)),
            dma((2, 7)),
            dma((2, 4, 8)),
        ],
        compiler_params=pltpu.CompilerParams(
            collective_id=1, has_side_effects=True, vmem_limit_bytes=56 << 20
        ),
        name="second",
    )(tiles, upz, w_down, outz, cotangent)
def third_kernel(
    received, tok, out, up, down, cots, scales,
    grad_rx, grad_middle, middle, outq, down_own, grad_up, grad_out, sums,
    grad_down, dvia, djoin, din, attended, n2g, act, gh, pairs, prx, gsend, gin, tsend, branch,
    nsem, ssem, gsem, esem, dsem,
):
    head, blk = lax.axis_index("head"), lax.axis_index("blk")
    core = lax.rem(blk, 2)
    greet_all(head, blk)
    for seq in range(2):
        for group in range(4):
            for i in range(2):
                first = received[group, 4 * seq + 2 * i].astype(F32)
                second = received[group, 4 * seq + 2 * i + 1].astype(F32)
                lanes = slice(256 * group + 128 * i, 256 * group + 128 * i + 128)
                attended[64 * seq : 64 * seq + 32, lanes] = join_halves(first, second, 0).astype(BF)
                attended[64 * seq + 32 : 64 * seq + 64, lanes] = join_halves(
                    first, second, 1
                ).astype(BF)
    middle[...] = tok[...].astype(F32) + jnp.dot(
        attended[...], out[...].reshape(1024, 1024), preferred_element_type=F32
    )
    for seq in range(2):
        rows = slice(64 * seq, 64 * seq + 64)
        unit, _ = norm_stats(middle[rows, :])
        n2g[blk, rows, :] = (unit * scales[2 + seq : 3 + seq, :]).astype(BF)
    plane = Plane(head, blk, n2g.at[blk], lambda i: n2g.at[i], nsem)
    for i in (1, 2, 0):
        plane.first[i].start()
    dfold = Fold(head, blk, grad_down, dvia, djoin, din, dsem)
    sibling = flip(blk, 1)

    def halves(i):
        return [
            send(pairs.at[w, i, 1 - core], prx.at[w, i], ssem.at[0, w, i], ssem.at[1, w, i], head, sibling)
            for w in range(2)
        ]

    def onward(i):
        peer = flip(blk, 2 * i)
        return send(gsend.at[i], gin.at[i], gsem.at[0, i], gsem.at[1, i], head, peer)

    def reduce(i):
        chip = lax.div(flip(blk, 2 * i), 2)
        for copy in halves(i):
            copy.wait_recv()
        gsend[i] = (pairs[0, i, core].astype(F32) + prx[0, i].astype(F32)).astype(BF)
        if i:
            onward(i).start()
        outq[chip] = (pairs[1, i, core].astype(F32) + prx[1, i].astype(F32)).astype(BF)

    for i in range(4):
        chip = lax.div(flip(blk, 2 * i), 2)
        if i == 0:
            plane.arrive(-1)
        else:
            plane.forward(i - 1)
            if i > 1:
                reduce(i - 1)
            plane.arrive(i - 1)
        at = pl.ds(2 * chip, 2)
        rows = n2g[at].reshape(256, 1024)
        hidden = jnp.dot(rows, up[...].reshape(1024, 512), preferred_element_type=F32)
        grad_active = contract_cols(cots[at].reshape(256, 1024), down[...].reshape(512, 1024))
        cdf = 0.5 * (1.0 + lax.erf(hidden * math.sqrt(0.5)))
        active = (hidden * cdf).astype(BF)
        slope = cdf + hidden * jnp.exp(-0.5 * hidden * hidden) * (1.0 / math.sqrt(2 * math.pi))
        grad_hidden = (grad_active * slope).astype(BF)
        act[at] = active.reshape(2, 128, 512)
        gh[at] = grad_hidden.reshape(2, 128, 512)
        pairs[0, i] = (
            contract_cols(grad_hidden, up[...].reshape(1024, 512)).astype(BF).reshape(2, 128, 1024)
        )
        pairs[1, i] = (
            jnp.dot(active, down[...].reshape(512, 1024), preferred_element_type=F32)
            .astype(BF)
            .reshape(2, 128, 1024)
        )
        for copy in halves(i):
            copy.start()
        if i == 0:
            plane.first[3].start()
    reduce(3)
    reduce(0)
    for group in range(4):
        lanes = slice(128 * group, 128 * group + 128)
        grad_down[group] = contract_rows(
            act[:, :, lanes].reshape(1024, 128), cots[...].reshape(1024, 1024)
        ).astype(BF)
    dfold.start()
    for group in range(4):
        lanes = slice(256 * group, 256 * group + 256)
        part = contract_rows(n2g[:, :, lanes].reshape(1024, 256), gh[...].reshape(1024, 512))
        grad_up[group] = part.astype(BF).reshape(8, 32, 512)
    dfold.relay()
    for i in range(1, 4):
        onward(i).wait_recv()
    sums[...] = jnp.zeros_like(sums)
    for seq in range(2):
        rows = slice(64 * seq, 64 * seq + 64)
        grad = gsend[0, rows, :].astype(F32)
        for i in range(1, 4):
            grad = grad + gin[i, rows, :].astype(F32)
        unit, spread = norm_stats(middle[rows, :])
        whole_grad = cots[blk, rows, :].astype(F32) + norm_back(
            unit, spread, grad, scales[2 + seq : 3 + seq, :]
        )
        grad_middle[rows, :] = whole_grad
        branch[rows, :] = whole_grad.astype(BF)
        sums[seq : seq + 1, :] = jnp.sum(grad * unit, axis=0, keepdims=True)
    grad_att = contract_cols(branch[...], out[...].reshape(1024, 1024))
    for seq in range(2):
        for group in range(4):
            for i in range(2):
                lanes = slice(256 * group + 128 * i, 256 * group + 128 * i + 128)
                top = grad_att[64 * seq : 64 * seq + 32, lanes]
                bottom = grad_att[64 * seq + 32 : 64 * seq + 64, lanes]
                for right in range(2):
                    tsend[group, 4 * seq + 2 * i + right] = join_halves(top, bottom, right).astype(BF)
    everyone = Everyone(head, blk, lambda z, b: tsend.at[z, b], lambda z, b: grad_rx.at[z, b], esem)
    for kz in range(4):
        everyone.start(kz)
    grad_rx[head, blk] = tsend[head, blk]
    for group in range(4):
        lanes = slice(256 * group, 256 * group + 256)
        part = contract_rows(attended[:, lanes], branch[...])
        grad_out[group] = part.astype(BF).reshape(8, 32, 1024)
    dfold.arrive()
    down_own[...] = sum_four(din)
    everyone.arrive()
    plane.drain()
    dfold.drain()
    for i in range(4):
        for copy in halves(i):
            copy.wait_send()
        if i:
            onward(i).wait_send()
    everyone.drain()


def phase_three_kernel(received, tokens, out, up, down, cots, scales):
    dma = pltpu.SemaphoreType.DMA
    return pl.pallas_call(
        third_kernel,
        out_shape=(
            jax.ShapeDtypeStruct((4, 8, 32, 128), BF),
            jax.ShapeDtypeStruct((128, 1024), F32),
            jax.ShapeDtypeStruct((128, 1024), F32),
            jax.ShapeDtypeStruct((4, 128, 1024), BF),
            jax.ShapeDtypeStruct((128, 1024), F32),
            jax.ShapeDtypeStruct((4, 8, 32, 512), BF),
            jax.ShapeDtypeStruct((4, 8, 32, 1024), BF),
            jax.ShapeDtypeStruct((8, 1024), F32),
        ),
        in_specs=whole(7),
        out_specs=whole(8),
        scratch_shapes=[
            pltpu.VMEM((4, 128, 1024), BF),
            pltpu.VMEM((128, 1024), BF),
            pltpu.VMEM((128, 1024), BF),
            pltpu.VMEM((4, 128, 1024), BF),
            pltpu.VMEM((128, 1024), BF),
            pltpu.VMEM((8, 128, 1024), BF),
            pltpu.VMEM((8, 128, 512), BF),
            pltpu.VMEM((8, 128, 512), BF),
            pltpu.VMEM((2, 4, 2, 128, 1024), BF),
            pltpu.VMEM((2, 4, 128, 1024), BF),
            pltpu.VMEM((4, 128, 1024), BF),
            pltpu.VMEM((4, 128, 1024), BF),
            pltpu.VMEM((4, 8, 32, 128), BF),
            pltpu.VMEM((128, 1024), BF),
            dma((2, 7)),
            dma((2, 2, 4)),
            dma((2, 4)),
            dma((2, 4, 8)),
            dma((2, 4)),
        ],
        compiler_params=pltpu.CompilerParams(
            collective_id=2, has_side_effects=True, vmem_limit_bytes=58 << 20
        ),
        name="third",
    )(received, tokens, out, up, down, cots, scales)
class Scatter:
    def __init__(self, head, blk, terms, near, joined, far, sems):
        self.head, self.blk, self.core = head, blk, lax.rem(blk, 2)
        self.terms, self.near, self.joined, self.far, self.sems = terms, near, joined, far, sems

    def halves(self):
        return send(
            self.terms.at[:, :, 1 - self.core],
            self.near,
            self.sems.at[0, 0],
            self.sems.at[1, 0],
            self.head,
            flip(self.blk, 1),
        )

    def chips(self, i):
        peer = flip(self.blk, 2 * i)
        return send(
            self.joined.at[lax.div(peer, 2)],
            self.far.at[i],
            self.sems.at[0, i],
            self.sems.at[1, i],
            self.head,
            peer,
        )

    def start(self):
        self.halves().start()

    def join(self):
        self.halves().wait_recv()
        for chip in range(4):
            mine = self.terms[:, chip, pl.ds(self.core, 1)].astype(F32)
            mine = mine.reshape(mine.shape[0], *mine.shape[2:])
            self.joined[chip] = (mine + self.near[:, chip].astype(F32)).astype(BF)
        for i in (3, 1, 2):
            self.chips(i).start()

    def total(self):
        value = self.joined[lax.div(self.blk, 2)].astype(F32)
        for i in range(1, 4):
            self.chips(i).wait_recv()
            value = value + self.far[i].astype(F32)
        return value

    def drain(self):
        self.halves().wait_send()
        for i in range(1, 4):
            self.chips(i).wait_send()


def sum_four(parts):
    return (parts[0].astype(F32) + parts[1].astype(F32)) + (
        parts[2].astype(F32) + parts[3].astype(F32)
    )


def fourth_kernel(
    tiles, grad_rx, mixed, lse, outq, middle, grad_up, grad_out,
    back, output, up_own, out_own,
    queries, grads, stats, keyt, dkv, dqt, bsend, oin, uin, usum, near, joined, far, osum, zin,
    uvia, ujoin,
    qsem, usem, vsem, osem, xsem, bsem,
):
    head, blk = lax.axis_index("head"), lax.axis_index("blk")
    greet(head, blk, (1, 2, 3), range(1, 8))
    scatter = Scatter(head, blk, grad_out, near, joined, far, osem)
    scatter.start()
    uswap = Fold(head, blk, grad_up, uvia, ujoin, uin, usem)
    uswap.start()
    outs = []
    for i in range(1, 4):
        peer = flip(blk, 2 * i)
        outs.append(
            send(outq.at[lax.div(peer, 2)], oin.at[i], qsem.at[0, i], qsem.at[1, i], head, peer)
        )
        outs[-1].start()
    vswap = Swap(head, blk, "blk", lambda i: usum.at[i], lambda i: up_own.at[i], vsem)
    xswap = Swap(head, blk, "head", lambda i: osum.at[i], lambda i: zin.at[i], xsem)
    left = half_lane((256, 128))
    keyt[...] = jnp.transpose(tiles[:, :, 0:64, :].reshape(2048, 128))[:64]

    def prepare(z, carry):
        flat = tiles[z, :, 64:96, :].reshape(256, 128).astype(F32)
        grad = grad_rx[z].reshape(256, 128).astype(F32)
        product = jnp.transpose(grad) * mixed[z]
        queries[2 * z] = jnp.where(left, flat, 0.0).astype(BF)
        queries[2 * z + 1] = jnp.where(left, pltpu.roll(flat, 64, 1), 0.0).astype(BF)
        grads[2 * z] = jnp.where(left, 0.0, pltpu.roll(grad, 64, 1)).astype(BF)
        grads[2 * z + 1] = jnp.where(left, 0.0, grad).astype(BF)
        for side in range(2):
            delta = jnp.sum(product[64 * side : 64 * side + 64], axis=0, keepdims=True)
            shift = lse[z, side : side + 1, :] * math.log2(math.e)
            stats[2 * z + side] = jnp.concatenate([shift, delta, jnp.zeros((6, 256), F32)], axis=0)
        return carry

    lax.fori_loop(0, 4, prepare, 0)
    dqt[...] = jnp.zeros_like(dqt)

    def kv_move(z):
        return Swap(
            head,
            blk,
            "blk",
            lambda i: bsend.at[i, z, pl.ds(0, 64)],
            lambda i: back.at[i, z, pl.ds(0, 64)],
            bsem.at[z],
        )

    def keys_step(z, carry):
        dkv[...] = jnp.zeros_like(dkv)

        def query_step(q, inner):
            query, grad = queries[q], grads[q]
            shift, delta = stats[q, 0:1, :], stats[q, 1:2, :]
            dq = dqt[q]
            for c in range(2):
                keys = tiles[z, 4 * c : 4 * c + 4, 0:64, :].reshape(256, 128)
                probs = jnp.exp2(contract_cols(keys, query) * EXP_SCALE - shift)
                slopes = (probs * (contract_cols(keys, grad) - delta)).astype(BF)
                dkv[c] += jnp.dot(slopes, query, preferred_element_type=F32) + jnp.dot(
                    probs.astype(BF), grad, preferred_element_type=F32
                )
                at = pl.ds(pl.multiple_of(512 * z + 256 * c, 256), 256)
                dq = dq + jnp.dot(keyt[:, at], slopes, preferred_element_type=F32)
            dqt[q] = dq
            return inner

        lax.fori_loop(0, 8, query_step, 0)
        scale = jnp.where(left, SCORE_SCALE, 1.0)
        for c in range(2):
            bsend[4 * c : 4 * c + 4, pl.ds(z, 1), 0:64, :] = (
                (dkv[c] * scale).astype(BF).reshape(4, 1, 64, 128)
            )
        kv_move(z).start()

        @pl.when(z == 0)
        def _():
            scatter.join()

        @pl.when(z == 1)
        def _():
            uswap.relay()

        @pl.when(z == 2)
        def _():
            total = middle[...] + outq[lax.div(blk, 2)].astype(F32)
            for i in range(1, 4):
                outs[i - 1].wait_recv()
                total = total + oin[i].astype(F32)
            output[...] = total.astype(BF)
            osum[...] = scatter.total().astype(BF)
            xswap.start()
            zin[head] = osum[head]

        return carry

    lax.fori_loop(0, 4, keys_step, 0)
    for z in range(4):
        both = jnp.concatenate([dqt[2 * z], dqt[2 * z + 1]], axis=0)
        both = (jnp.transpose(both) * SCORE_SCALE).astype(BF)
        bsend[:, z, 64:96, :] = both.reshape(8, 32, 128)
    qmove = Swap(
        head,
        blk,
        "blk",
        lambda i: bsend.at[i, :, pl.ds(64, 32)],
        lambda i: back.at[i, :, pl.ds(64, 32)],
        bsem.at[4],
    )
    qmove.start()
    back[blk] = bsend[blk]
    uswap.arrive()
    usum[...] = sum_four(uin).astype(BF)
    vswap.start()
    up_own[blk] = usum[blk]
    xswap.arrive()
    out_own[...] = sum_four(zin)
    vswap.arrive()
    for z in range(4):
        kv_move(z).arrive()
    qmove.arrive()
    for z in range(4):
        kv_move(z).drain()
    for copy in outs:
        copy.wait_send()
    for copies in (scatter, uswap, vswap, xswap, qmove):
        copies.drain()


def phase_four_kernel(tiles, grad_rx, mixed, lse, outq, middle, grad_up, grad_out):
    dma = pltpu.SemaphoreType.DMA
    return pl.pallas_call(
        fourth_kernel,
        out_shape=(
            jax.ShapeDtypeStruct((8, 4, 96, 128), BF),
            jax.ShapeDtypeStruct((128, 1024), BF),
            jax.ShapeDtypeStruct((8, 32, 512), BF),
            jax.ShapeDtypeStruct((32, 1024), F32),
        ),
        in_specs=whole(8),
        out_specs=whole(4),
        scratch_shapes=[
            pltpu.VMEM((8, 256, 128), BF),
            pltpu.VMEM((8, 256, 128), BF),
            pltpu.VMEM((8, 8, 256), F32),
            pltpu.VMEM((64, 2048), BF),
            pltpu.VMEM((2, 256, 128), F32),
            pltpu.VMEM((8, 64, 256), F32),
            pltpu.VMEM((8, 4, 96, 128), BF),
            pltpu.VMEM((4, 128, 1024), BF),
            pltpu.VMEM((4, 8, 32, 512), BF),
            pltpu.VMEM((8, 32, 512), BF),
            pltpu.VMEM((4, 4, 32, 1024), BF),
            pltpu.VMEM((4, 4, 32, 1024), BF),
            pltpu.VMEM((4, 4, 32, 1024), BF),
            pltpu.VMEM((4, 32, 1024), BF),
            pltpu.VMEM((4, 32, 1024), BF),
            pltpu.VMEM((8, 32, 512), BF),
            pltpu.VMEM((8, 32, 512), BF),
            dma((2, 4)),
            dma((2, 4)),
            dma((2, 8)),
            dma((2, 4)),
            dma((2, 4)),
            dma((5, 2, 8)),
        ],
        compiler_params=pltpu.CompilerParams(
            collective_id=3, has_side_effects=True, vmem_limit_bytes=56 << 20
        ),
        name="fourth",
    )(tiles, grad_rx, mixed, lse, outq, middle, grad_up, grad_out)
def fifth_kernel(
    back, tabg, normed, wq, tokg, scales, grad_middle, sums, ttab, tix,
    grad_tokens, gq, grad_attn, grad_mlp,
    gp, gnf, gnp, gvia, gjoin, gin, terms, near, joined, far, osum, turned, part, sums_in, parts,
    gsem, osem, xsem, asem, bsem,
):
    head, blk = lax.axis_index("head"), lax.axis_index("blk")
    greet(head, blk, (1, 2, 3), range(1, 8))
    gswap = Fold(head, blk, gnp, gvia, gjoin, gin, gsem)

    def unturn(step, carry):
        at = flip(head, step)
        for seq in range(2):
            table = tabg[at]
            if seq:
                table = pltpu.roll(table, 64, 1)
            both, keyed = turn_tables(table, -1.0)
            rows = slice(64 * seq, 64 * seq + 64)
            for j in range(4):
                kv = back[4 * seq + j, at, 0:64, :].astype(F32)
                kv = kv * keyed[0] + lane_swap(kv) * keyed[1]
                gp[at, rows, 128 * j : 128 * j + 128] = kv.astype(BF)
            for i in range(2):
                first = back[4 * seq + 2 * i, at, 64:96, :].astype(F32)
                second = back[4 * seq + 2 * i + 1, at, 64:96, :].astype(F32)
                query = jnp.concatenate(
                    [join_halves(first, second, 0), join_halves(first, second, 1)], axis=0
                )
                query = query * both[0] + lane_swap(query) * both[1]
                gp[at, rows, 512 + 128 * i : 640 + 128 * i] = query.astype(BF)
        gnf[at] = contract_cols(gp[at], wq[...].reshape(1024, 768))
        gnp[at] = gnf[at].astype(BF)
        return carry

    for step in (3, 2, 1, 0):
        unturn(step, 0)
        if step == 3:
            gswap.start_far()
        if step:
            gswap.start_one(step)
    for group in range(4):
        lanes = slice(256 * group, 256 * group + 256)
        value = contract_rows(normed[:, :, lanes].reshape(512, 256), gp[...].reshape(512, 768))
        terms[group] = value.astype(BF).reshape(4, 2, 32, 768)
    scatter = Scatter(head, blk, terms, near, joined, far, osem)
    scatter.start()
    turned[...] = jnp.transpose(ttab[...])
    picked = turned[pl.ds(pl.multiple_of((head * 8 + blk) * 8, 8), 8), :]
    step_lane = lax.broadcasted_iota(jnp.int32, picked.shape, 1)
    columns = [
        jnp.sum(jnp.where(step_lane == tix[seq], picked, 0.0), axis=1, keepdims=True)
        for seq in range(2)
    ]
    gswap.relay()
    part[...] = jnp.concatenate(
        [jnp.zeros((2, 1024), F32), sums[0:2, :], jnp.zeros((4, 1024), F32)], axis=0
    )

    def gather(at, carry):
        for seq in range(2):
            unit, _ = norm_stats(tokg[at, seq].astype(F32))
            part[seq : seq + 1, :] += jnp.sum(
                gnf[at, pl.ds(64 * seq, 64), :] * unit, axis=0, keepdims=True
            )
        return carry

    lax.fori_loop(0, 4, gather, 0)
    one = Swap(head, blk, "blk", lambda i: part, lambda i: sums_in.at[i], asem)
    one.start()
    sums_in[blk] = part[...]
    scatter.join()
    one.arrive()
    total = sums_in[0]
    for i in range(1, 8):
        total = total + sums_in[i]
    parts[head] = total
    two = Swap(head, blk, "head", lambda i: parts.at[head], lambda i: parts.at[i], bsem)
    two.start()
    osum[...] = scatter.total().astype(BF)
    xswap = Swap(head, blk, "head", lambda i: osum.at[i], lambda i: gq.at[i], xsem)
    xswap.start()
    gq[head] = osum[head]
    two.arrive()
    total = (parts[0] + parts[1]) + (parts[2] + parts[3])
    grad_attn[...] = columns[0] * total[0:1] + columns[1] * total[1:2]
    grad_mlp[...] = columns[0] * total[2:3] + columns[1] * total[3:4]
    gswap.arrive()
    for seq in range(2):
        rows = slice(64 * seq, 64 * seq + 64)
        grad = sum_four([gin[i, rows, :] for i in range(4)])
        unit, spread = norm_stats(tokg[head, seq].astype(F32))
        grad_tokens[rows, :] = grad_middle[rows, :] + norm_back(
            unit, spread, grad, scales[seq : seq + 1, :]
        )
    xswap.arrive()
    for copies in (gswap, scatter, xswap, one, two):
        copies.drain()


def phase_five_kernel(back, tabg, normed, wq, tokg, scales, grad_middle, sums, ttab, tix):
    dma = pltpu.SemaphoreType.DMA
    return pl.pallas_call(
        fifth_kernel,
        out_shape=(
            jax.ShapeDtypeStruct((128, 1024), F32),
            jax.ShapeDtypeStruct((4, 32, 768), BF),
            jax.ShapeDtypeStruct((8, 1024), F32),
            jax.ShapeDtypeStruct((8, 1024), F32),
        ),
        in_specs=whole(9) + [pl.BlockSpec(memory_space=pltpu.SMEM)],
        out_specs=whole(4),
        scratch_shapes=[
            pltpu.VMEM((4, 128, 768), BF),
            pltpu.VMEM((4, 128, 1024), F32),
            pltpu.VMEM((4, 128, 1024), BF),
            pltpu.VMEM((128, 1024), BF),
            pltpu.VMEM((128, 1024), BF),
            pltpu.VMEM((4, 128, 1024), BF),
            pltpu.VMEM((4, 4, 2, 32, 768), BF),
            pltpu.VMEM((4, 4, 32, 768), BF),
            pltpu.VMEM((4, 4, 32, 768), BF),
            pltpu.VMEM((4, 4, 32, 768), BF),
            pltpu.VMEM((4, 32, 768), BF),
            pltpu.VMEM((256, 64), F32),
            pltpu.VMEM((8, 1024), F32),
            pltpu.VMEM((8, 8, 1024), F32),
            pltpu.VMEM((4, 8, 1024), F32),
            dma((2, 4)),
            dma((2, 4)),
            dma((2, 4)),
            dma((2, 8)),
            dma((2, 4)),
        ],
        compiler_params=pltpu.CompilerParams(
            collective_id=4, has_side_effects=True, vmem_limit_bytes=48 << 20
        ),
        name="fifth",
    )(back, tabg, normed, wq, tokg, scales, grad_middle, sums, ttab, tix)
def blocked(
    tokens,
    positions,
    time_index,
    time_table,
    w_qkv,
    w_out,
    w_up,
    w_down,
    scale_attn,
    scale_mlp,
    cotangent,
):
    cosine, sine = rotary_tables(positions, HEAD_DIM)
    cosine, sine = cosine[:, :, 0], sine[:, :, 0]
    table = jnp.concatenate([cosine[0], sine[0], cosine[1], sine[1]], axis=-1)
    wide = w_qkv.reshape(32, 3, 4, 4, 64)
    kv_cols = jnp.stack([wide[:, 1], wide[:, 2]], axis=3).reshape(32, 4, 512)
    wq_parts = jnp.concatenate([kv_cols, wide[:, 0].reshape(32, 4, 256)], axis=-1)
    wq_parts = jnp.swapaxes(wq_parts, 0, 1)
    up_parts = jnp.transpose(w_up.reshape(32, 4, 8, 128), (2, 0, 1, 3)).reshape(8, 32, 512)
    flat_tokens = tokens.reshape(128, 1024)
    tiles, normed, wq, scales, table_all, upz, outz, tokens_all = phase_one_kernel(
        tokens, table, wq_parts, time_table, time_index, scale_attn, scale_mlp, up_parts, w_out
    )
    mixed, lse, received, up, down, out, cot_all = phase_two_kernel(
        tiles, upz, w_down, outz, cotangent.reshape(128, 1024)
    )
    grad_rx, grad_middle, middle, outq, down_own, grad_up, grad_out, sums = phase_three_kernel(
        received, flat_tokens, out, up, down, cot_all, scales
    )
    back, output, up_own, out_own = phase_four_kernel(
        tiles,
        grad_rx,
        mixed,
        lse,
        outq,
        middle,
        grad_up,
        grad_out.reshape(4, 4, 2, 32, 1024),
    )
    grad_tokens, grad_wq, grad_attn, grad_mlp = phase_five_kernel(
        back,
        table_all,
        normed,
        wq,
        tokens_all,
        scales,
        grad_middle,
        sums,
        time_table,
        time_index,
    )
    kv_cols = grad_wq[:, :, :512].reshape(4, 32, 4, 2, 64)
    wide = jnp.stack(
        [grad_wq[:, :, 512:].reshape(4, 32, 4, 64), kv_cols[:, :, :, 0], kv_cols[:, :, :, 1]],
        axis=0,
    )
    qkv_own = jnp.transpose(wide, (2, 0, 1, 3, 4)).reshape(32, 3072).astype(F32)
    up_own = jnp.transpose(up_own.reshape(8, 32, 4, 128), (1, 2, 0, 3)).reshape(32, 4096)
    return (
        output.reshape(2, 64, 1024),
        grad_tokens.reshape(2, 64, 1024),
        qkv_own,
        out_own,
        up_own.astype(F32),
        down_own,
        grad_attn,
        grad_mlp,
    )


def solution(mesh):
    fits = mesh.shape["head"] == 4 and mesh.shape["blk"] == 8
    placed = (
        P(None, ("head", "blk"), None),
        P(None, ("head", "blk")),
        P(),
        P(),
        P(("head", "blk"), None),
        P(("head", "blk"), None),
        P(("head", "blk"), None),
        P(("head", "blk"), None),
        P(("head", "blk"), None),
        P(("head", "blk"), None),
        P(None, ("head", "blk"), None),
    )
    return jax.shard_map(
        blocked if fits else general,
        mesh=mesh,
        in_specs=placed,
        out_specs=(
            P(None, ("head", "blk"), None),
            P(None, ("head", "blk"), None),
            P(("head", "blk"), None),
            P(("head", "blk"), None),
            P(("head", "blk"), None),
            P(("head", "blk"), None),
            P(("head", "blk"), None),
            P(("head", "blk"), None),
        ),
        check_vma=False,
    )
```

```python
import math

import jax
import jax.numpy as jnp
from jax import lax
from jax.experimental import pallas as pl
from jax.experimental.pallas import tpu as pltpu
from jax.sharding import PartitionSpec as P

HEADS = 16
HEAD_DIM = 64


NORM_EPSILON = 1e-05
PRECISE = lax.Precision.HIGHEST
START_TOP = -1e30
SCORE_SCALE = 0.125


def shifted(value, axis, steps):
    count = lax.axis_size(axis)
    pairs = [(source, (source + steps) % count) for source in range(count)]
    return lax.ppermute(value, axis, pairs)


def layer_norm(value, scale):
    centered = value - jnp.mean(value, axis=-1, keepdims=True)
    variance = jnp.mean(centered * centered, axis=-1, keepdims=True)
    return centered * lax.rsqrt(variance + NORM_EPSILON) * scale


def rotate(value, cosine_table, sine_table):
    half_dim = value.shape[-1] // 2
    first_half = value[..., :half_dim]
    second_half = value[..., half_dim:]
    return jnp.concatenate(
        [
            first_half * cosine_table - second_half * sine_table,
            second_half * cosine_table + first_half * sine_table,
        ],
        axis=-1,
    )


def rotary_tables(positions, head_dim):
    half_dim = head_dim // 2
    frequency = 10000.0 ** (-jnp.arange(half_dim, dtype=jnp.float32) / half_dim)
    turned = positions.astype(jnp.float32)[:, :, None, None] * frequency
    return (jnp.cos(turned), jnp.sin(turned))


def contract_rows(left, right):
    return lax.dot_general(
        left, right, (((0,), (0,)), ((), ())), preferred_element_type=jnp.float32
    )


def contract_cols(left, right):
    return lax.dot_general(
        left, right, (((1,), (1,)), ((), ())), preferred_element_type=jnp.float32
    )


def attend_step(running, query_block, key_block, value_block):
    row_top, row_sum, accum = running
    scores = (
        jnp.einsum("sqhd,skhd->sqhk", query_block, key_block, preferred_element_type=jnp.float32)
        * SCORE_SCALE
    )
    new_top = jnp.maximum(row_top, jnp.max(scores, axis=-1))
    shrink = jnp.exp(row_top - new_top)
    weights = jnp.exp(scores - new_top[..., None])
    row_sum = row_sum * shrink + jnp.sum(weights, axis=-1)
    accum = accum * shrink[..., None] + jnp.einsum(
        "sqhk,skhd->sqhd",
        weights.astype(jnp.bfloat16),
        value_block,
        preferred_element_type=jnp.float32,
    )
    return (new_top, row_sum, accum)


def back_step(query_block, key_block, value_block, grad_block, log_total, delta):
    scores = (
        jnp.einsum("sqhd,skhd->sqhk", query_block, key_block, preferred_element_type=jnp.float32)
        * SCORE_SCALE
    )
    probs = jnp.exp(scores - log_total[..., None])
    grad_values = jnp.einsum(
        "sqhk,sqhd->skhd",
        probs.astype(jnp.bfloat16),
        grad_block,
        preferred_element_type=jnp.float32,
    )
    grad_probs = jnp.einsum(
        "sqhd,skhd->sqhk", grad_block, value_block, preferred_element_type=jnp.float32
    )
    grad_scores = (probs * (grad_probs - delta[..., None])).astype(jnp.bfloat16)
    grad_query = jnp.einsum(
        "sqhk,skhd->sqhd", grad_scores, key_block, preferred_element_type=jnp.float32
    )
    grad_keys = jnp.einsum(
        "sqhk,sqhd->skhd", grad_scores, query_block, preferred_element_type=jnp.float32
    )
    return (grad_query, grad_keys, grad_values)


def general(
    tokens,
    positions,
    time_index,
    time_table,
    w_qkv,
    w_out,
    w_up,
    w_down,
    scale_attn,
    scale_mlp,
    cotangent,
):
    seq_count, row_count, model_width = tokens.shape
    group_count = lax.axis_size("head")
    local_heads = HEADS // group_count
    feature_width = local_heads * HEAD_DIM
    flat_rows = seq_count * row_count
    gathered = (
        lax.all_gather(w_qkv, ("head", "blk"), axis=0, tiled=True),
        lax.all_gather(w_out, ("head", "blk"), axis=0, tiled=True),
        lax.all_gather(w_up, ("head", "blk"), axis=0, tiled=True),
        lax.all_gather(w_down, ("head", "blk"), axis=0, tiled=True),
        lax.all_gather(scale_attn, ("head", "blk"), axis=0, tiled=True),
        lax.all_gather(scale_mlp, ("head", "blk"), axis=0, tiled=True),
    )
    full_qkv, full_out, full_up, full_down, full_scale_attn, full_scale_mlp = gathered
    step_count = time_table.shape[0]
    picker = (time_index[:, None] == jnp.arange(step_count, dtype=jnp.int32)[None, :]).astype(
        jnp.float32
    )
    time_embed = jnp.dot(picker, time_table, precision=PRECISE)
    scale_one = 1.0 + jnp.dot(time_embed, full_scale_attn.astype(jnp.float32), precision=PRECISE)
    scale_two = 1.0 + jnp.dot(time_embed, full_scale_mlp.astype(jnp.float32), precision=PRECISE)
    token_float = tokens.astype(jnp.float32)
    normed = (
        layer_norm(token_float, scale_one[:, None, :])
        .astype(jnp.bfloat16)
        .reshape(flat_rows, model_width)
    )
    projected = jnp.dot(normed, full_qkv, preferred_element_type=jnp.float32).reshape(
        seq_count, row_count, 3, HEADS, HEAD_DIM
    )
    cosine_table, sine_table = rotary_tables(positions, HEAD_DIM)
    query_tok = rotate(projected[:, :, 0], cosine_table, sine_table)
    keys_tok = rotate(projected[:, :, 1], cosine_table, sine_table)
    packed = (
        jnp.stack([query_tok, keys_tok, projected[:, :, 2]], axis=2)
        .reshape(seq_count, row_count, 3, model_width)
        .astype(jnp.bfloat16)
    )
    regrouped = lax.all_to_all(packed, "head", split_axis=3, concat_axis=1, tiled=True)
    block_len = regrouped.shape[1]
    local_query = regrouped[:, :, 0].reshape(seq_count, block_len, local_heads, HEAD_DIM)
    local_keys = regrouped[:, :, 1]
    local_values = regrouped[:, :, 2]
    start_state = (
        jnp.full((seq_count, block_len, local_heads), START_TOP, jnp.float32),
        jnp.zeros((seq_count, block_len, local_heads), jnp.float32),
        jnp.zeros((seq_count, block_len, local_heads, HEAD_DIM), jnp.float32),
    )
    key_piece = lax.all_gather(local_keys, "blk", axis=1, tiled=True)
    value_piece = lax.all_gather(local_values, "blk", axis=1, tiled=True)
    piece_len = key_piece.shape[1]
    step_len = math.gcd(piece_len, block_len)

    def one_block(index, state):
        key_block = lax.dynamic_slice_in_dim(key_piece, index * step_len, step_len, 1).reshape(
            seq_count, step_len, local_heads, HEAD_DIM
        )
        value_block = lax.dynamic_slice_in_dim(value_piece, index * step_len, step_len, 1).reshape(
            seq_count, step_len, local_heads, HEAD_DIM
        )
        return attend_step(state, local_query, key_block, value_block)

    row_top, row_sum, accum = lax.fori_loop(0, piece_len // step_len, one_block, start_state)
    mixed = accum / row_sum[..., None]
    log_total = row_top + jnp.log(row_sum)
    attended_heads = mixed.astype(jnp.bfloat16).reshape(seq_count, block_len, feature_width)
    attended = lax.all_to_all(
        attended_heads, "head", split_axis=1, concat_axis=2, tiled=True
    ).reshape(flat_rows, model_width)
    branch = jnp.dot(attended, full_out, preferred_element_type=jnp.float32)
    middle = token_float + branch.reshape(seq_count, row_count, model_width)
    normed_two = (
        layer_norm(middle, scale_two[:, None, :])
        .astype(jnp.bfloat16)
        .reshape(flat_rows, model_width)
    )
    hidden = jnp.dot(normed_two, full_up, preferred_element_type=jnp.float32)
    active = jax.nn.gelu(hidden, approximate=False).astype(jnp.bfloat16)
    result = middle.reshape(flat_rows, model_width) + jnp.dot(
        active, full_down, preferred_element_type=jnp.float32
    )
    output = result.astype(jnp.bfloat16).reshape(seq_count, row_count, model_width)
    back_qkv, back_out, back_up, back_down = (
        lax.all_gather(w_qkv, ("head", "blk"), axis=0, tiled=True),
        lax.all_gather(w_out, ("head", "blk"), axis=0, tiled=True),
        lax.all_gather(w_up, ("head", "blk"), axis=0, tiled=True),
        lax.all_gather(w_down, ("head", "blk"), axis=0, tiled=True),
    )
    grad_out = cotangent.reshape(flat_rows, model_width)
    grad_active = contract_cols(grad_out, back_down)
    grad_w_down = contract_rows(active, grad_out)
    gelu_value, gelu_pull = jax.vjp(lambda entry: jax.nn.gelu(entry, approximate=False), hidden)
    grad_hidden = gelu_pull(grad_active)[0].astype(jnp.bfloat16)
    grad_w_up = contract_rows(normed_two, grad_hidden)
    grad_normed_two = contract_cols(grad_hidden, back_up).reshape(seq_count, row_count, model_width)
    norm_value, norm_pull = jax.vjp(layer_norm, middle, scale_two[:, None, :])
    grad_middle_norm, grad_scale_two = norm_pull(grad_normed_two)
    grad_middle = cotangent.astype(jnp.float32) + grad_middle_norm
    grad_scale_mlp = jnp.dot(time_embed.T, grad_scale_two[:, 0, :], precision=PRECISE)
    grad_branch = grad_middle.reshape(flat_rows, model_width).astype(jnp.bfloat16)
    grad_w_out = contract_rows(attended, grad_branch)
    grad_attended = (
        contract_cols(grad_branch, back_out)
        .astype(jnp.bfloat16)
        .reshape(seq_count, row_count, model_width)
    )
    grad_heads = lax.all_to_all(
        grad_attended, "head", split_axis=2, concat_axis=1, tiled=True
    ).reshape(seq_count, block_len, local_heads, HEAD_DIM)
    delta = jnp.sum(grad_heads.astype(jnp.float32) * mixed, axis=-1)

    def turn(index, state):
        key_now, value_now, grad_keys_now, grad_values_now, grad_query_sum = state
        grad_query, grad_keys, grad_values = back_step(
            local_query,
            key_now.reshape(seq_count, block_len, local_heads, HEAD_DIM),
            value_now.reshape(seq_count, block_len, local_heads, HEAD_DIM),
            grad_heads,
            log_total,
            delta,
        )
        moved_keys, moved_values = shifted((key_now, value_now), "blk", 1)
        moved_grad_keys, moved_grad_values = (
            shifted(
                (grad_keys_now + grad_keys.reshape(seq_count, block_len, feature_width)).astype(
                    jnp.bfloat16
                ),
                "blk",
                1,
            ).astype(jnp.float32),
            shifted(
                (grad_values_now + grad_values.reshape(seq_count, block_len, feature_width)).astype(
                    jnp.bfloat16
                ),
                "blk",
                1,
            ).astype(jnp.float32),
        )
        return (
            moved_keys,
            moved_values,
            moved_grad_keys,
            moved_grad_values,
            grad_query_sum + grad_query,
        )

    zero_kv = jnp.zeros((seq_count, block_len, feature_width), jnp.float32)
    begin = (
        local_keys,
        local_values,
        zero_kv,
        zero_kv,
        jnp.zeros((seq_count, block_len, local_heads, HEAD_DIM), jnp.float32),
    )
    final_state = lax.fori_loop(0, lax.axis_size("blk"), turn, begin)
    grad_keys_own = final_state[2]
    grad_values_own = final_state[3]
    grad_query_all = final_state[4]
    stacked = jnp.stack(
        [
            grad_query_all.reshape(seq_count, block_len, feature_width) * SCORE_SCALE,
            grad_keys_own * SCORE_SCALE,
            grad_values_own,
        ],
        axis=2,
    ).astype(jnp.bfloat16)
    returned = lax.all_to_all(stacked, "head", split_axis=1, concat_axis=3, tiled=True)
    grad_query_tok = (
        returned[:, :, 0].astype(jnp.float32).reshape(seq_count, row_count, HEADS, HEAD_DIM)
    )
    grad_keys_tok = (
        returned[:, :, 1].astype(jnp.float32).reshape(seq_count, row_count, HEADS, HEAD_DIM)
    )
    grad_values_tok = (
        returned[:, :, 2].astype(jnp.float32).reshape(seq_count, row_count, HEADS, HEAD_DIM)
    )
    grad_projected = (
        jnp.stack(
            [
                rotate(grad_query_tok, cosine_table, -sine_table),
                rotate(grad_keys_tok, cosine_table, -sine_table),
                grad_values_tok,
            ],
            axis=2,
        )
        .reshape(flat_rows, 3 * model_width)
        .astype(jnp.bfloat16)
    )
    grad_w_qkv = contract_rows(normed, grad_projected)
    grad_normed = contract_cols(grad_projected, back_qkv).reshape(seq_count, row_count, model_width)
    first_value, first_pull = jax.vjp(layer_norm, token_float, scale_one[:, None, :])
    grad_token_norm, grad_scale_one = first_pull(grad_normed)
    grad_tokens = grad_middle + grad_token_norm
    grad_scale_attn = jnp.dot(time_embed.T, grad_scale_one[:, 0, :], precision=PRECISE)
    shards = (
        lax.psum_scatter(grad_w_qkv, ("head", "blk"), scatter_dimension=0, tiled=True),
        lax.psum_scatter(grad_w_out, ("head", "blk"), scatter_dimension=0, tiled=True),
        lax.psum_scatter(grad_w_up, ("head", "blk"), scatter_dimension=0, tiled=True),
        lax.psum_scatter(grad_w_down, ("head", "blk"), scatter_dimension=0, tiled=True),
        lax.psum_scatter(grad_scale_attn, ("head", "blk"), scatter_dimension=0, tiled=True),
        lax.psum_scatter(grad_scale_mlp, ("head", "blk"), scatter_dimension=0, tiled=True),
    )
    return (output, grad_tokens, shards[0], shards[1], shards[2], shards[3], shards[4], shards[5])


EPS = NORM_EPSILON
BF = jnp.bfloat16
F32 = jnp.float32


def norm_stats(value):
    centered = value - jnp.mean(value, axis=-1, keepdims=True)
    spread = lax.rsqrt(jnp.mean(centered * centered, axis=-1, keepdims=True) + EPS)
    return centered * spread, spread


def norm_back(unit, spread, grad, scale):
    scaled = grad * scale
    return spread * (
        scaled
        - jnp.mean(scaled, axis=-1, keepdims=True)
        - unit * jnp.mean(scaled * unit, axis=-1, keepdims=True)
    )


MESH = pl.DeviceIdType.MESH


def flip(value, bits):
    for bit in (1, 2, 4):
        if bits & bit:
            value = value + bit - 2 * bit * lax.rem(lax.div(value, bit), 2)
    return value


def greet(head, blk, heads, blks):
    barrier = pltpu.get_barrier_semaphore()
    for k in heads:
        pl.semaphore_signal(barrier, inc=1, device_id=(flip(head, k), blk), device_id_type=MESH)
    for k in blks:
        pl.semaphore_signal(barrier, inc=1, device_id=(head, flip(blk, k)), device_id_type=MESH)
    pl.semaphore_wait(barrier, len(heads) + len(blks))


def send(source, target, send_sem, recv_sem, head, blk):
    return pltpu.make_async_remote_copy(
        src_ref=source,
        dst_ref=target,
        send_sem=send_sem,
        recv_sem=recv_sem,
        device_id=(head, blk),
        device_id_type=MESH,
    )


class Swap:
    def __init__(self, head, blk, axis, source, target, sems):
        self.copies = []
        count = 4 if axis == "head" else 8
        me = head if axis == "head" else blk
        for k in range(1, count):
            peer = flip(me, k)
            where = (peer, blk) if axis == "head" else (head, peer)
            self.copies.append(
                send(source(peer), target(me), sems.at[0, k], sems.at[1, k], *where)
            )

    def start(self):
        for copy in self.copies:
            copy.start()

    def arrive(self):
        for copy in self.copies:
            copy.wait_recv()

    def drain(self):
        for copy in self.copies:
            copy.wait_send()


class Plane:
    def __init__(self, head, blk, own, slot, sems):
        sibling = flip(blk, 1)
        self.first = [send(own, slot(blk), sems.at[0, 0], sems.at[1, 0], head, sibling)]
        self.passed = []
        for i, k in enumerate((2, 4, 6)):
            peer = flip(blk, k)
            self.first.append(
                send(own, slot(blk), sems.at[0, i + 1], sems.at[1, i + 1], head, peer)
            )
            self.passed.append(
                send(slot(peer), slot(peer), sems.at[0, i + 4], sems.at[1, i + 4], head, sibling)
            )

    def start(self):
        for i in (3, 1, 2, 0):
            self.first[i].start()

    def forward(self, i):
        self.first[i + 1].wait_recv()
        self.passed[i].start()

    def arrive(self, i):
        if i < 0:
            self.first[0].wait_recv()
        else:
            self.passed[i].wait_recv()

    def finish(self):
        for i in range(3):
            self.forward(i)
        for i in range(-1, 3):
            self.arrive(i)

    def drain(self):
        for copy in self.first + self.passed:
            copy.wait_send()


def line_order(head, step):
    low = jnp.minimum(head, 3 - head)
    swap = low * ((step == 0).astype(jnp.int32) - (step == 1).astype(jnp.int32))
    at = step + swap
    return jnp.where(head < 2, at, 3 - at)


class Line:
    def __init__(self, head, blk, own, slot, sems):
        self.head, self.blk, self.own, self.slot, self.sems = head, blk, own, slot, sems

    def copy(self, source, at, up, k):
        head = self.head
        target = jnp.where(up, head + 1, head - 1)
        way = jnp.where(up, 0, 1)
        return send(
            source, self.slot(at), self.sems.at[0, way, k], self.sems.at[1, way, k], target, self.blk
        )

    def start(self):
        head = self.head

        @pl.when(head < 3)
        def _():
            self.copy(self.own, head, True, 0).start()

        @pl.when(head > 0)
        def _():
            self.copy(self.own, head, False, 0).start()

    def step(self, at):
        head = self.head
        up = at < head
        k = jnp.where(up, head - 1 - at, at - head - 1)
        self.copy(self.slot(at), at, up, k).wait_recv()

        @pl.when(jnp.where(up, head < 3, head > 0))
        def _():
            self.copy(self.slot(at), at, up, k + 1).start()

    def drain(self):
        head = self.head
        for k in range(3):

            @pl.when(jnp.logical_and(head < 3, head >= k))
            def _():
                self.copy(self.own, head, True, k).wait_send()

            @pl.when(jnp.logical_and(head > 0, head + k <= 3))
            def _():
                self.copy(self.own, head, False, k).wait_send()


class Reach:
    def __init__(self, head, blk, own, slot, sems):
        self.head, self.blk, self.own, self.slot, self.sems = head, blk, own, slot, sems
        self.middle = jnp.logical_and(head > 0, head < 3)

    def copy(self, k):
        peer = flip(self.head, k)
        return send(
            self.own, self.slot(self.head), self.sems.at[0, k], self.sems.at[1, k], peer, self.blk
        )

    def passed(self):
        at = self.slot(flip(self.head, 2))
        return send(at, at, self.sems.at[0, 0], self.sems.at[1, 3], flip(self.head, 1), self.blk)

    def start(self):
        self.copy(2).start()
        self.copy(1).start()

        @pl.when(self.middle)
        def _():
            self.copy(3).start()

    def forward(self):
        self.copy(2).wait_recv()

        @pl.when(self.middle)
        def _():
            self.passed().start()

    def arrive(self):
        self.copy(1).wait_recv()
        self.copy(3).wait_recv()

    def drain(self):
        self.copy(1).wait_send()
        self.copy(2).wait_send()

        @pl.when(self.middle)
        def _():
            self.copy(3).wait_send()
            self.passed().wait_send()


class Fold:
    def __init__(self, head, blk, terms, via, joined, into, sems):
        self.head, self.blk, self.sems = head, blk, sems
        self.terms, self.via, self.joined, self.into = terms, via, joined, into
        self.middle = jnp.logical_and(head > 0, head < 3)

    def copy(self, k):
        peer = flip(self.head, k)
        return send(
            self.terms.at[peer],
            self.into.at[k],
            self.sems.at[0, k],
            self.sems.at[1, k],
            peer,
            self.blk,
        )

    def handed(self):
        return send(
            self.terms.at[flip(self.head, 3)],
            self.via,
            self.sems.at[0, 0],
            self.sems.at[1, 0],
            flip(self.head, 1),
            self.blk,
        )

    def relayed(self):
        return send(
            self.joined,
            self.into.at[2],
            self.sems.at[0, 2],
            self.sems.at[1, 2],
            flip(self.head, 2),
            self.blk,
        )

    def start_far(self):
        @pl.when(jnp.logical_not(self.middle))
        def _():
            self.handed().start()

    def start_one(self, k):
        if k == 1:
            self.copy(1).start()
        elif k == 2:

            @pl.when(jnp.logical_not(self.middle))
            def _():
                self.copy(2).start()

        else:

            @pl.when(self.middle)
            def _():
                self.copy(3).start()

    def start(self):
        self.start_far()
        for k in (2, 3, 1):
            self.start_one(k)

    def relay(self):
        @pl.when(self.middle)
        def _():
            self.handed().wait_recv()
            mine = self.terms[flip(self.head, 2)].astype(F32)
            self.joined[...] = (mine + self.via[...].astype(F32)).astype(BF)
            self.relayed().start()

    def arrive(self):
        self.copy(1).wait_recv()
        self.copy(2).wait_recv()

        @pl.when(self.middle)
        def _():
            self.copy(3).wait_recv()

        @pl.when(jnp.logical_not(self.middle))
        def _():
            self.into[3] = jnp.zeros_like(self.into[3])

        self.into[0] = self.terms[self.head]

    def drain(self):
        self.copy(1).wait_send()

        @pl.when(self.middle)
        def _():
            self.copy(3).wait_send()
            self.relayed().wait_send()

        @pl.when(jnp.logical_not(self.middle))
        def _():
            self.copy(2).wait_send()
            self.handed().wait_send()


def half_lane(shape):
    return lax.broadcasted_iota(jnp.int32, shape, 1) < 64


def lane_swap(value):
    lane = lax.broadcasted_iota(jnp.int32, value.shape, 1)
    return jnp.where(
        lax.rem(lane, 64) < 32, pltpu.roll(value, 96, 1), pltpu.roll(value, 32, 1)
    )


def turn_tables(table, sign):
    lane = lax.broadcasted_iota(jnp.int32, table.shape, 1)
    cosine = jnp.where(lane < 32, table, 0.0)
    cosine = cosine + pltpu.roll(cosine, 32, 1)
    sine = jnp.where(jnp.logical_and(lane >= 32, lane < 64), table, 0.0) * sign
    sine = sine - pltpu.roll(sine, 96, 1)
    both = (cosine + pltpu.roll(cosine, 64, 1), sine + pltpu.roll(sine, 64, 1))
    return both, (jnp.where(lane < 64, cosine, 1.0), sine)


def join_halves(top, bottom, right):
    left = half_lane(top.shape)
    if right:
        return jnp.where(left, pltpu.roll(top, 64, 1), bottom)
    return jnp.where(left, top, pltpu.roll(bottom, 64, 1))


EXP_SCALE = SCORE_SCALE * math.log2(math.e)
KEYS = 256


def flip_by(head, k):
    low, high = lax.rem(k, 2), lax.div(k, 2)
    value = head + low - 2 * low * lax.rem(head, 2)
    return value + 2 * high - 4 * high * lax.div(head, 2)


class Everyone:
    def __init__(self, head, blk, source, target, sems):
        self.head, self.blk, self.source, self.target, self.sems = head, blk, source, target, sems

    def copy(self, kz, k):
        z, b = flip_by(self.head, jnp.int32(kz)), flip(self.blk, k)
        return send(
            self.source(z, b),
            self.target(self.head, self.blk),
            self.sems.at[0, kz, k],
            self.sems.at[1, kz, k],
            z,
            b,
        )

    def start(self, kz):
        if isinstance(kz, int):
            first = kz > 0
        else:

            @pl.when(kz > 0)
            def _():
                self.copy(kz, 0).start()

            first = False
        for k in range(0 if first else 1, 8):
            self.copy(kz, k).start()

    def arrive(self):
        for kz in range(4):
            for k in range(1 if kz == 0 else 0, 8):
                self.copy(kz, k).wait_recv()

    def drain(self):
        for kz in range(4):
            for k in range(1 if kz == 0 else 0, 8):
                self.copy(kz, k).wait_send()


def greet_all(head, blk):
    barrier = pltpu.get_barrier_semaphore()
    for kz in range(4):
        for k in range(8):
            if kz or k:
                pl.semaphore_signal(
                    barrier, inc=1, device_id=(flip(head, kz), flip(blk, k)), device_id_type=MESH
                )
    pl.semaphore_wait(barrier, 31)


def group_rows(value):
    return jnp.sum(value.reshape(value.shape[0] // 8, 8, value.shape[1]), axis=0)


def front_kernel(
    tok, tab, wqp, ttab, sca, scm, upp, out_own, down_own, cot_own, tix,
    tiles, normed, wq, scales, tabg, tokg, mixed, lse,
    grad_rx, grad_middle, middle, outq, grad_down, grad_up, grad_out, sums,
    wqz, turned, part, sums_in, parts, out_tiles, upz, outz, up, down, out, cots,
    kvt, scores, att, received, attended, n2g, act, gh, pairs, prx, gsend, gin, tsend, branch,
    zsem, lsem, tsem, wsem, asem, bsem, psem, usem, osem,
    usem2, dsem, qsem, csem, esem, nsem, ssem, gsem, fsem,
):
    head, blk = lax.axis_index("head"), lax.axis_index("blk")
    core = lax.rem(blk, 2)
    greet_all(head, blk)
    zswap = Swap(head, blk, "head", lambda i: wqp.at[i], lambda i: wqz.at[i], zsem)
    zswap.start()
    line = Line(head, blk, tok, lambda i: tokg.at[i], lsem)
    tline = Line(head, blk, tab, lambda i: tabg.at[i], tsem)
    tline.start()
    line.start()
    uswap = Swap(head, blk, "blk", lambda i: upp.at[i], lambda i: upz.at[i], usem)
    oline = Reach(head, blk, out_own, lambda i: outz.at[i], osem)
    uline = Line(head, blk, upz, lambda i: up.at[i], usem2)
    dline = Line(head, blk, down_own, lambda i: down.at[i], dsem)
    oplane = Plane(head, blk, outz, lambda i: out.at[:, i], qsem)
    cplane = Plane(head, blk, cot_own, lambda i: cots.at[i], csem)
    everyone = Everyone(head, blk, lambda z, b: att.at[z, b], lambda z, b: received.at[z, b], esem)
    backward = Everyone(head, blk, lambda z, b: tsend.at[z, b], lambda z, b: grad_rx.at[z, b], fsem)
    turned[...] = jnp.transpose(ttab[...])
    rows = turned[pl.ds(pl.multiple_of((head * 8 + blk) * 8, 8), 8), :]
    step_lane = lax.broadcasted_iota(jnp.int32, rows.shape, 1)
    terms = []
    for weight in (sca, scm):
        for seq in range(2):
            column = jnp.sum(jnp.where(step_lane == tix[seq], rows, 0.0), axis=1, keepdims=True)
            terms.append(jnp.sum(column * weight[...].astype(F32), axis=0, keepdims=True))
    part[...] = jnp.concatenate(terms + [jnp.zeros((4, 1024), F32)], axis=0)
    one = Swap(head, blk, "blk", lambda i: part, lambda i: sums_in.at[i], asem)
    one.start()
    uswap.start()
    sums_in[blk] = part[...]
    wqz[head] = wqp[head]
    tokg[head] = tok[...]
    tabg[head] = tab[...]
    upz[blk] = upp[blk]
    outz[head] = out_own[...]
    down[head] = down_own[...]
    cots[blk] = cot_own[...]
    one.arrive()
    total = sums_in[0]
    for i in range(1, 8):
        total = total + sums_in[i]
    parts[head] = total
    two = Swap(head, blk, "head", lambda i: parts.at[head], lambda i: parts.at[i], bsem)
    two.start()
    zswap.arrive()
    plane = Plane(head, blk, wqz, lambda i: wq.at[:, i], wsem)
    plane.start()
    wq[:, pl.ds(blk, 1)] = wqz[...].reshape(4, 1, 32, 768)
    two.arrive()
    total = 1.0 + ((parts[0] + parts[1]) + (parts[2] + parts[3]))
    scales[...] = total

    def gather(step, carry):
        at = line_order(head, step)

        @pl.when(step > 0)
        def _():
            tline.step(at)
            line.step(at)

        for seq in range(2):
            unit, _ = norm_stats(tokg[at, seq].astype(F32))
            normed[at, pl.ds(64 * seq, 64), :] = (unit * scales[seq : seq + 1, :]).astype(BF)
        return carry

    def project(step, carry):
        at = line_order(head, step)
        proj = jnp.dot(
            normed[at], wq[...].reshape(1024, 768), preferred_element_type=F32
        )
        for seq in range(2):
            table = tabg[at]
            if seq:
                table = pltpu.roll(table, 64, 1)
            both, keyed = turn_tables(table, 1.0)
            mine = proj[64 * seq : 64 * seq + 64]
            for j in range(4):
                kv = mine[:, 128 * j : 128 * j + 128]
                kv = kv * keyed[0] + lane_swap(kv) * keyed[1]
                out_tiles[4 * seq + j, at, 0:64, :] = kv.astype(BF)
            for i in range(2):
                query = mine[:, 512 + 128 * i : 640 + 128 * i]
                query = query * both[0] + lane_swap(query) * both[1]
                for right in range(2):
                    packed = join_halves(query[:32], query[32:], right)
                    out_tiles[4 * seq + 2 * i + right, at, 64:96, :] = packed.astype(BF)
        move(at).start()
        tiles[at, blk] = out_tiles[blk, at]
        return carry

    def move(at):
        return Swap(
            head, blk, "blk", lambda i: out_tiles.at[i, at], lambda i: tiles.at[at, i], psem.at[at]
        )

    lax.fori_loop(0, 3, gather, 0)
    oline.start()
    plane.finish()
    lax.fori_loop(0, 3, project, 0)

    def last(step, carry):
        gather(step, carry)
        return project(step, carry)

    lax.fori_loop(3, 4, last, 0)
    uswap.arrive()
    up[head] = upz[...]
    uline.start()
    oline.forward()
    oline.arrive()
    out[:, pl.ds(blk, 1)] = outz[...].reshape(4, 1, 32, 1024)
    for at in range(4):
        move(at).arrive()
    oplane.start()
    kvt[...] = jnp.transpose(tiles[:, :, 0:64, :].reshape(2048, 128))

    def attend(step, carry):
        z = flip_by(head, 3 - step)
        flat = jnp.transpose(tiles[z, :, 64:96, :].reshape(256, 128).astype(F32))
        blank = jnp.zeros((64, 256), F32)
        results = []
        for side in range(2):
            query = jnp.concatenate([flat[64 * side : 64 * side + 64], blank], axis=0).astype(BF)
            top = None
            for c in range(2048 // KEYS):
                keys = tiles[c // 2, 4 * (c % 2) : 4 * (c % 2) + 4, 0:64, :].reshape(KEYS, 128)
                part = jnp.dot(keys, query, preferred_element_type=F32)
                scores[side, c] = part
                peak = jnp.max(part.reshape(KEYS // 8, 8, 256), axis=0)
                top = peak if top is None else jnp.maximum(top, peak)
            top = jnp.max(top, axis=0, keepdims=True)
            total = jnp.zeros((8, 256), F32)
            mix = jnp.zeros((64, 256), F32)
            for c in range(2048 // KEYS):
                weights = jnp.exp2((scores[side, c] - top) * EXP_SCALE)
                total = total + group_rows(weights)
                mix = mix + jnp.dot(
                    kvt[64:128, KEYS * c : KEYS * c + KEYS],
                    weights.astype(BF),
                    preferred_element_type=F32,
                )
            total = jnp.sum(total, axis=0, keepdims=True)
            mix = mix / total
            mixed[z, 64 * side : 64 * side + 64, :] = mix
            lse[z, side : side + 1, :] = top * SCORE_SCALE + jnp.log(total)
            results.append(mix)
        both = jnp.transpose(jnp.concatenate(results, axis=0))
        att[z] = both.astype(BF).reshape(8, 32, 128)
        everyone.start(3 - step)

        @pl.when(step == 0)
        def _():
            uline.step(line_order(head, jnp.int32(1)))

        @pl.when(step == 1)
        def _():
            uline.step(line_order(head, jnp.int32(2)))

        @pl.when(step == 2)
        def _():
            uline.step(line_order(head, jnp.int32(3)))
            dline.start()
            for i in range(3):
                oplane.forward(i)
            cplane.start()

        return carry

    lse[...] = jnp.zeros_like(lse)
    lax.fori_loop(0, 4, attend, 0)
    received[head, blk] = att[head, blk]
    dline.step(line_order(head, jnp.int32(1)))
    for i in range(-1, 3):
        oplane.arrive(i)
    everyone.arrive()
    for seq in range(2):
        for group in range(4):
            for i in range(2):
                first = received[group, 4 * seq + 2 * i].astype(F32)
                second = received[group, 4 * seq + 2 * i + 1].astype(F32)
                lanes = slice(256 * group + 128 * i, 256 * group + 128 * i + 128)
                attended[64 * seq : 64 * seq + 32, lanes] = join_halves(first, second, 0).astype(BF)
                attended[64 * seq + 32 : 64 * seq + 64, lanes] = join_halves(
                    first, second, 1
                ).astype(BF)
    middle[...] = tok[...].astype(F32).reshape(128, 1024) + jnp.dot(
        attended[...], out[...].reshape(1024, 1024), preferred_element_type=F32
    )
    for seq in range(2):
        rows = slice(64 * seq, 64 * seq + 64)
        unit, _ = norm_stats(middle[rows, :])
        n2g[blk, rows, :] = (unit * scales[2 + seq : 3 + seq, :]).astype(BF)
    nplane = Plane(head, blk, n2g.at[blk], lambda i: n2g.at[i], nsem)
    for i in (1, 2, 0):
        nplane.first[i].start()
    dline.step(line_order(head, jnp.int32(2)))
    nplane.first[3].start()
    cplane.finish()
    dline.step(line_order(head, jnp.int32(3)))
    sibling = flip(blk, 1)

    def halves(i):
        return [
            send(pairs.at[w, i, 1 - core], prx.at[w, i], ssem.at[0, w, i], ssem.at[1, w, i], head, sibling)
            for w in range(2)
        ]

    def onward(i):
        peer = flip(blk, 2 * i)
        return send(gsend.at[i], gin.at[i], gsem.at[0, i], gsem.at[1, i], head, peer)

    def reduce(i):
        chip = lax.div(flip(blk, 2 * i), 2)
        for copy in halves(i):
            copy.wait_recv()
        gsend[i] = (pairs[0, i, core].astype(F32) + prx[0, i].astype(F32)).astype(BF)
        if i:
            onward(i).start()
        outq[chip] = (pairs[1, i, core].astype(F32) + prx[1, i].astype(F32)).astype(BF)

    for i in range(4):
        chip = lax.div(flip(blk, 2 * i), 2)
        if i == 0:
            nplane.arrive(-1)
        else:
            nplane.forward(i - 1)
            if i > 1:
                reduce(i - 1)
            nplane.arrive(i - 1)
        at = pl.ds(2 * chip, 2)
        rows = n2g[at].reshape(256, 1024)
        hidden = jnp.dot(rows, up[...].reshape(1024, 512), preferred_element_type=F32)
        grad_active = contract_cols(cots[at].reshape(256, 1024), down[...].reshape(512, 1024))
        cdf = 0.5 * (1.0 + lax.erf(hidden * math.sqrt(0.5)))
        active = (hidden * cdf).astype(BF)
        slope = cdf + hidden * jnp.exp(-0.5 * hidden * hidden) * (1.0 / math.sqrt(2 * math.pi))
        grad_hidden = (grad_active * slope).astype(BF)
        act[at] = active.reshape(2, 128, 512)
        gh[at] = grad_hidden.reshape(2, 128, 512)
        pairs[0, i] = (
            contract_cols(grad_hidden, up[...].reshape(1024, 512)).astype(BF).reshape(2, 128, 1024)
        )
        pairs[1, i] = (
            jnp.dot(active, down[...].reshape(512, 1024), preferred_element_type=F32)
            .astype(BF)
            .reshape(2, 128, 1024)
        )
        for copy in halves(i):
            copy.start()
    reduce(3)
    reduce(0)
    for group in range(4):
        lanes = slice(128 * group, 128 * group + 128)
        grad_down[group] = contract_rows(
            act[:, :, lanes].reshape(1024, 128), cots[...].reshape(1024, 1024)
        ).astype(BF)
    for group in range(4):
        lanes = slice(256 * group, 256 * group + 256)
        part = contract_rows(n2g[:, :, lanes].reshape(1024, 256), gh[...].reshape(1024, 512))
        grad_up[group] = part.astype(BF).reshape(8, 32, 512)
    for i in range(1, 4):
        onward(i).wait_recv()
    sums[...] = jnp.zeros_like(sums)
    for seq in range(2):
        rows = slice(64 * seq, 64 * seq + 64)
        grad = gsend[0, rows, :].astype(F32)
        for i in range(1, 4):
            grad = grad + gin[i, rows, :].astype(F32)
        unit, spread = norm_stats(middle[rows, :])
        whole_grad = cots[blk, rows, :].astype(F32) + norm_back(
            unit, spread, grad, scales[2 + seq : 3 + seq, :]
        )
        grad_middle[rows, :] = whole_grad
        branch[rows, :] = whole_grad.astype(BF)
        sums[seq : seq + 1, :] = jnp.sum(grad * unit, axis=0, keepdims=True)

    def give(step, carry):
        group = flip_by(head, 3 - step)
        part = contract_cols(branch[...], out[group].reshape(256, 1024))
        for seq in range(2):
            for i in range(2):
                lanes = slice(128 * i, 128 * i + 128)
                top = part[64 * seq : 64 * seq + 32, lanes]
                bottom = part[64 * seq + 32 : 64 * seq + 64, lanes]
                for right in range(2):
                    tsend[group, 4 * seq + 2 * i + right] = join_halves(top, bottom, right).astype(BF)
        backward.start(3 - step)
        return carry

    lax.fori_loop(0, 4, give, 0)
    grad_rx[head, blk] = tsend[head, blk]
    for group in range(4):
        lanes = slice(256 * group, 256 * group + 256)
        part = contract_rows(attended[:, lanes], branch[...])
        grad_out[group] = part.astype(BF).reshape(8, 32, 1024)
    backward.arrive()
    for at in range(4):
        move(at).drain()
    for i in range(4):
        for copy in halves(i):
            copy.wait_send()
        if i:
            onward(i).wait_send()
    for copies in (
        zswap, line, tline, plane, one, two, uswap, oline,
        uline, dline, oplane, cplane, everyone, nplane, backward,
    ):
        copies.drain()


def whole(count):
    return [pl.BlockSpec(memory_space=pltpu.VMEM)] * count


def front(tokens, table, wq_parts, time_table, scales_in, up_parts, w_out, w_down, cot, time_index):
    dma = pltpu.SemaphoreType.DMA
    shape = jax.ShapeDtypeStruct
    return pl.pallas_call(
        front_kernel,
        out_shape=(
            shape((4, 8, 96, 128), BF),
            shape((4, 128, 1024), BF),
            shape((4, 8, 32, 768), BF),
            shape((8, 1024), F32),
            shape((4, 64, 128), F32),
            shape((4, 2, 64, 1024), BF),
            shape((4, 128, 256), F32),
            shape((4, 8, 256), F32),
            shape((4, 8, 32, 128), BF),
            shape((128, 1024), F32),
            shape((128, 1024), F32),
            shape((4, 128, 1024), BF),
            shape((4, 128, 1024), BF),
            shape((4, 8, 32, 512), BF),
            shape((4, 8, 32, 1024), BF),
            shape((8, 1024), F32),
        ),
        in_specs=whole(10) + [pl.BlockSpec(memory_space=pltpu.SMEM)],
        out_specs=whole(16),
        scratch_shapes=[
            pltpu.VMEM((4, 32, 768), BF),
            pltpu.VMEM((256, 64), F32),
            pltpu.VMEM((8, 1024), F32),
            pltpu.VMEM((8, 8, 1024), F32),
            pltpu.VMEM((4, 8, 1024), F32),
            pltpu.VMEM((8, 4, 96, 128), BF),
            pltpu.VMEM((8, 32, 512), BF),
            pltpu.VMEM((4, 32, 1024), BF),
            pltpu.VMEM((4, 8, 32, 512), BF),
            pltpu.VMEM((4, 128, 1024), BF),
            pltpu.VMEM((4, 8, 32, 1024), BF),
            pltpu.VMEM((8, 128, 1024), BF),
            pltpu.VMEM((128, 2048), BF),
            pltpu.VMEM((2, 2048 // KEYS, KEYS, 256), F32),
            pltpu.VMEM((4, 8, 32, 128), BF),
            pltpu.VMEM((4, 8, 32, 128), BF),
            pltpu.VMEM((128, 1024), BF),
            pltpu.VMEM((8, 128, 1024), BF),
            pltpu.VMEM((8, 128, 512), BF),
            pltpu.VMEM((8, 128, 512), BF),
            pltpu.VMEM((2, 4, 2, 128, 1024), BF),
            pltpu.VMEM((2, 4, 128, 1024), BF),
            pltpu.VMEM((4, 128, 1024), BF),
            pltpu.VMEM((4, 128, 1024), BF),
            pltpu.VMEM((4, 8, 32, 128), BF),
            pltpu.VMEM((128, 1024), BF),
            dma((2, 4)),
            dma((2, 2, 3)),
            dma((2, 2, 3)),
            dma((2, 7)),
            dma((2, 8)),
            dma((2, 4)),
            dma((4, 2, 8)),
            dma((2, 8)),
            dma((2, 4)),
            dma((2, 2, 3)),
            dma((2, 2, 3)),
            dma((2, 7)),
            dma((2, 7)),
            dma((2, 4, 8)),
            dma((2, 7)),
            dma((2, 2, 4)),
            dma((2, 4)),
            dma((2, 4, 8)),
        ],
        compiler_params=pltpu.CompilerParams(
            collective_id=0, has_side_effects=True, vmem_limit_bytes=56 << 20
        ),
        name="front",
    )(tokens, table, wq_parts, time_table, *scales_in, up_parts, w_out, w_down, cot, time_index)


class Scatter:
    def __init__(self, head, blk, terms, near, joined, far, sems):
        self.head, self.blk, self.core = head, blk, lax.rem(blk, 2)
        self.terms, self.near, self.joined, self.far, self.sems = terms, near, joined, far, sems

    def halves(self):
        return send(
            self.terms.at[:, :, 1 - self.core],
            self.near,
            self.sems.at[0, 0],
            self.sems.at[1, 0],
            self.head,
            flip(self.blk, 1),
        )

    def chips(self, i):
        peer = flip(self.blk, 2 * i)
        return send(
            self.joined.at[lax.div(peer, 2)],
            self.far.at[i],
            self.sems.at[0, i],
            self.sems.at[1, i],
            self.head,
            peer,
        )

    def start(self):
        self.halves().start()

    def join(self):
        self.halves().wait_recv()
        for chip in range(4):
            mine = self.terms[:, chip, pl.ds(self.core, 1)].astype(F32)
            mine = mine.reshape(mine.shape[0], *mine.shape[2:])
            self.joined[chip] = (mine + self.near[:, chip].astype(F32)).astype(BF)
        for i in (3, 1, 2):
            self.chips(i).start()

    def total(self):
        value = self.joined[lax.div(self.blk, 2)].astype(F32)
        for i in range(1, 4):
            self.chips(i).wait_recv()
            value = value + self.far[i].astype(F32)
        return value

    def drain(self):
        self.halves().wait_send()
        for i in range(1, 4):
            self.chips(i).wait_send()


def sum_four(parts):
    return (parts[0].astype(F32) + parts[1].astype(F32)) + (
        parts[2].astype(F32) + parts[3].astype(F32)
    )


def fourth_kernel(
    tiles, grad_rx, mixed, lse, outq, middle, grad_down, grad_up, grad_out,
    back, output, down_own, up_own, out_own,
    queries, grads, queries_t, grads_t, stats, keyt, dkv, dqt, bsend, oin, din, uin, usum, near, joined, far, osum, zin,
    dvia, djoin, uvia, ujoin,
    qsem, dsem, usem, vsem, osem, xsem, bsem,
):
    head, blk = lax.axis_index("head"), lax.axis_index("blk")
    greet(head, blk, (1, 2, 3), range(1, 8))
    scatter = Scatter(head, blk, grad_out, near, joined, far, osem)
    scatter.start()
    dswap = Fold(head, blk, grad_down, dvia, djoin, din, dsem)
    uswap = Fold(head, blk, grad_up, uvia, ujoin, uin, usem)
    uswap.start()
    dswap.start()
    outs = []
    for i in range(1, 4):
        peer = flip(blk, 2 * i)
        outs.append(
            send(outq.at[lax.div(peer, 2)], oin.at[i], qsem.at[0, i], qsem.at[1, i], head, peer)
        )
        outs[-1].start()
    vswap = Swap(head, blk, "blk", lambda i: usum.at[i], lambda i: up_own.at[i], vsem)
    xswap = Swap(head, blk, "head", lambda i: osum.at[i], lambda i: zin.at[i], xsem)
    left = half_lane((256, 128))
    keyt[...] = jnp.transpose(tiles[:, :, 0:64, :].reshape(2048, 128))[:64]

    def prepare(z, carry):
        flat = tiles[z, :, 64:96, :].reshape(256, 128).astype(F32)
        grad = grad_rx[z].reshape(256, 128).astype(F32)
        product = jnp.transpose(grad) * mixed[z]
        queries[2 * z] = jnp.where(left, flat, 0.0).astype(BF)
        queries[2 * z + 1] = jnp.where(left, pltpu.roll(flat, 64, 1), 0.0).astype(BF)
        turned = jnp.transpose(flat)
        slopes = jnp.transpose(grad)
        blank = jnp.zeros((64, 256), F32)
        for side in range(2):
            rows = slice(64 * side, 64 * side + 64)
            queries_t[2 * z + side] = jnp.concatenate([turned[rows], blank], axis=0).astype(BF)
            grads_t[2 * z + side] = jnp.concatenate([blank, slopes[rows]], axis=0).astype(BF)
        grads[2 * z] = jnp.where(left, 0.0, pltpu.roll(grad, 64, 1)).astype(BF)
        grads[2 * z + 1] = jnp.where(left, 0.0, grad).astype(BF)
        for side in range(2):
            delta = jnp.sum(product[64 * side : 64 * side + 64], axis=0, keepdims=True)
            shift = lse[z, side : side + 1, :] * math.log2(math.e)
            stats[2 * z + side] = jnp.concatenate([shift, delta, jnp.zeros((6, 256), F32)], axis=0)
        return carry

    lax.fori_loop(0, 4, prepare, 0)
    dqt[...] = jnp.zeros_like(dqt)

    def kv_move(z):
        return Swap(
            head,
            blk,
            "blk",
            lambda i: bsend.at[i, z, pl.ds(0, 64)],
            lambda i: back.at[i, z, pl.ds(0, 64)],
            bsem.at[z],
        )

    def keys_step(z, carry):
        dkv[...] = jnp.zeros_like(dkv)

        def query_step(q, inner):
            query, grad = queries[q], grads[q]
            query_t, grad_t = queries_t[q], grads_t[q]
            shift, delta = stats[q, 0:1, :], stats[q, 1:2, :]
            dq = dqt[q]
            for c in range(2):
                keys = tiles[z, 4 * c : 4 * c + 4, 0:64, :].reshape(256, 128)
                probs = jnp.dot(keys, query_t, preferred_element_type=F32)
                probs = jnp.exp2(probs * EXP_SCALE - shift)
                slopes = jnp.dot(keys, grad_t, preferred_element_type=F32)
                slopes = (probs * (slopes - delta)).astype(BF)
                dkv[c] += jnp.dot(slopes, query, preferred_element_type=F32) + jnp.dot(
                    probs.astype(BF), grad, preferred_element_type=F32
                )
                at = pl.ds(pl.multiple_of(512 * z + 256 * c, 256), 256)
                dq = dq + jnp.dot(keyt[:, at], slopes, preferred_element_type=F32)
            dqt[q] = dq
            return inner

        lax.fori_loop(0, 8, query_step, 0)
        scale = jnp.where(left, SCORE_SCALE, 1.0)
        for c in range(2):
            bsend[4 * c : 4 * c + 4, pl.ds(z, 1), 0:64, :] = (
                (dkv[c] * scale).astype(BF).reshape(4, 1, 64, 128)
            )
        kv_move(z).start()

        @pl.when(z == 0)
        def _():
            scatter.join()

        @pl.when(z == 1)
        def _():
            uswap.relay()
            dswap.relay()

        @pl.when(z == 2)
        def _():
            total = middle[...] + outq[lax.div(blk, 2)].astype(F32)
            for i in range(1, 4):
                outs[i - 1].wait_recv()
                total = total + oin[i].astype(F32)
            output[...] = total.astype(BF)
            osum[...] = scatter.total().astype(BF)
            xswap.start()
            zin[head] = osum[head]

        return carry

    lax.fori_loop(0, 4, keys_step, 0)
    for z in range(4):
        both = jnp.concatenate([dqt[2 * z], dqt[2 * z + 1]], axis=0)
        both = (jnp.transpose(both) * SCORE_SCALE).astype(BF)
        bsend[:, z, 64:96, :] = both.reshape(8, 32, 128)
    qmove = Swap(
        head,
        blk,
        "blk",
        lambda i: bsend.at[i, :, pl.ds(64, 32)],
        lambda i: back.at[i, :, pl.ds(64, 32)],
        bsem.at[4],
    )
    qmove.start()
    back[blk] = bsend[blk]
    uswap.arrive()
    usum[...] = sum_four(uin).astype(BF)
    vswap.start()
    up_own[blk] = usum[blk]
    dswap.arrive()
    down_own[...] = sum_four(din)
    xswap.arrive()
    out_own[...] = sum_four(zin)
    vswap.arrive()
    for z in range(4):
        kv_move(z).arrive()
    qmove.arrive()
    for z in range(4):
        kv_move(z).drain()
    for copy in outs:
        copy.wait_send()
    for copies in (dswap, scatter, uswap, vswap, xswap, qmove):
        copies.drain()


def phase_four_kernel(tiles, grad_rx, mixed, lse, outq, middle, grad_down, grad_up, grad_out):
    dma = pltpu.SemaphoreType.DMA
    return pl.pallas_call(
        fourth_kernel,
        out_shape=(
            jax.ShapeDtypeStruct((8, 4, 96, 128), BF),
            jax.ShapeDtypeStruct((128, 1024), BF),
            jax.ShapeDtypeStruct((128, 1024), F32),
            jax.ShapeDtypeStruct((8, 32, 512), BF),
            jax.ShapeDtypeStruct((32, 1024), F32),
        ),
        in_specs=whole(9),
        out_specs=whole(5),
        scratch_shapes=[
            pltpu.VMEM((8, 256, 128), BF),
            pltpu.VMEM((8, 256, 128), BF),
            pltpu.VMEM((8, 128, 256), BF),
            pltpu.VMEM((8, 128, 256), BF),
            pltpu.VMEM((8, 8, 256), F32),
            pltpu.VMEM((64, 2048), BF),
            pltpu.VMEM((2, 256, 128), F32),
            pltpu.VMEM((8, 64, 256), F32),
            pltpu.VMEM((8, 4, 96, 128), BF),
            pltpu.VMEM((4, 128, 1024), BF),
            pltpu.VMEM((4, 128, 1024), BF),
            pltpu.VMEM((4, 8, 32, 512), BF),
            pltpu.VMEM((8, 32, 512), BF),
            pltpu.VMEM((4, 4, 32, 1024), BF),
            pltpu.VMEM((4, 4, 32, 1024), BF),
            pltpu.VMEM((4, 4, 32, 1024), BF),
            pltpu.VMEM((4, 32, 1024), BF),
            pltpu.VMEM((4, 32, 1024), BF),
            pltpu.VMEM((128, 1024), BF),
            pltpu.VMEM((128, 1024), BF),
            pltpu.VMEM((8, 32, 512), BF),
            pltpu.VMEM((8, 32, 512), BF),
            dma((2, 4)),
            dma((2, 4)),
            dma((2, 4)),
            dma((2, 8)),
            dma((2, 4)),
            dma((2, 4)),
            dma((5, 2, 8)),
        ],
        compiler_params=pltpu.CompilerParams(
            collective_id=3, has_side_effects=True, vmem_limit_bytes=56 << 20
        ),
        name="fourth",
    )(tiles, grad_rx, mixed, lse, outq, middle, grad_down, grad_up, grad_out)
def fifth_kernel(
    back, tabg, normed, wq, tokg, scales, grad_middle, sums, ttab, tix,
    grad_tokens, gq, grad_attn, grad_mlp,
    gp, gnf, gnp, gvia, gjoin, gin, terms, near, joined, far, osum, turned, part, sums_in, parts,
    gsem, osem, xsem, asem, bsem,
):
    head, blk = lax.axis_index("head"), lax.axis_index("blk")
    greet(head, blk, (1, 2, 3), range(1, 8))
    gswap = Fold(head, blk, gnp, gvia, gjoin, gin, gsem)

    def unturn(step, carry):
        at = flip(head, step)
        for seq in range(2):
            table = tabg[at]
            if seq:
                table = pltpu.roll(table, 64, 1)
            both, keyed = turn_tables(table, -1.0)
            rows = slice(64 * seq, 64 * seq + 64)
            for j in range(4):
                kv = back[4 * seq + j, at, 0:64, :].astype(F32)
                kv = kv * keyed[0] + lane_swap(kv) * keyed[1]
                gp[at, rows, 128 * j : 128 * j + 128] = kv.astype(BF)
            for i in range(2):
                first = back[4 * seq + 2 * i, at, 64:96, :].astype(F32)
                second = back[4 * seq + 2 * i + 1, at, 64:96, :].astype(F32)
                query = jnp.concatenate(
                    [join_halves(first, second, 0), join_halves(first, second, 1)], axis=0
                )
                query = query * both[0] + lane_swap(query) * both[1]
                gp[at, rows, 512 + 128 * i : 640 + 128 * i] = query.astype(BF)
        gnf[at] = contract_cols(gp[at], wq[...].reshape(1024, 768))
        gnp[at] = gnf[at].astype(BF)
        return carry

    for step in (3, 2, 1, 0):
        unturn(step, 0)
        if step == 3:
            gswap.start_far()
        if step:
            gswap.start_one(step)
    for group in range(4):
        lanes = slice(256 * group, 256 * group + 256)
        value = contract_rows(normed[:, :, lanes].reshape(512, 256), gp[...].reshape(512, 768))
        terms[group] = value.astype(BF).reshape(4, 2, 32, 768)
    scatter = Scatter(head, blk, terms, near, joined, far, osem)
    scatter.start()
    turned[...] = jnp.transpose(ttab[...])
    picked = turned[pl.ds(pl.multiple_of((head * 8 + blk) * 8, 8), 8), :]
    step_lane = lax.broadcasted_iota(jnp.int32, picked.shape, 1)
    columns = [
        jnp.sum(jnp.where(step_lane == tix[seq], picked, 0.0), axis=1, keepdims=True)
        for seq in range(2)
    ]
    gswap.relay()
    part[...] = jnp.concatenate(
        [jnp.zeros((2, 1024), F32), sums[0:2, :], jnp.zeros((4, 1024), F32)], axis=0
    )

    def gather(at, carry):
        for seq in range(2):
            unit, _ = norm_stats(tokg[at, seq].astype(F32))
            part[seq : seq + 1, :] += jnp.sum(
                gnf[at, pl.ds(64 * seq, 64), :] * unit, axis=0, keepdims=True
            )
        return carry

    lax.fori_loop(0, 4, gather, 0)
    one = Swap(head, blk, "blk", lambda i: part, lambda i: sums_in.at[i], asem)
    one.start()
    sums_in[blk] = part[...]
    scatter.join()
    one.arrive()
    total = sums_in[0]
    for i in range(1, 8):
        total = total + sums_in[i]
    parts[head] = total
    two = Swap(head, blk, "head", lambda i: parts.at[head], lambda i: parts.at[i], bsem)
    two.start()
    osum[...] = scatter.total().astype(BF)
    xswap = Swap(head, blk, "head", lambda i: osum.at[i], lambda i: gq.at[i], xsem)
    xswap.start()
    gq[head] = osum[head]
    two.arrive()
    total = (parts[0] + parts[1]) + (parts[2] + parts[3])
    grad_attn[...] = columns[0] * total[0:1] + columns[1] * total[1:2]
    grad_mlp[...] = columns[0] * total[2:3] + columns[1] * total[3:4]
    gswap.arrive()
    for seq in range(2):
        rows = slice(64 * seq, 64 * seq + 64)
        grad = sum_four([gin[i, rows, :] for i in range(4)])
        unit, spread = norm_stats(tokg[head, seq].astype(F32))
        grad_tokens[rows, :] = grad_middle[rows, :] + norm_back(
            unit, spread, grad, scales[seq : seq + 1, :]
        )
    xswap.arrive()
    for copies in (gswap, scatter, xswap, one, two):
        copies.drain()


def phase_five_kernel(back, tabg, normed, wq, tokg, scales, grad_middle, sums, ttab, tix):
    dma = pltpu.SemaphoreType.DMA
    return pl.pallas_call(
        fifth_kernel,
        out_shape=(
            jax.ShapeDtypeStruct((128, 1024), F32),
            jax.ShapeDtypeStruct((4, 32, 768), BF),
            jax.ShapeDtypeStruct((8, 1024), F32),
            jax.ShapeDtypeStruct((8, 1024), F32),
        ),
        in_specs=whole(9) + [pl.BlockSpec(memory_space=pltpu.SMEM)],
        out_specs=whole(4),
        scratch_shapes=[
            pltpu.VMEM((4, 128, 768), BF),
            pltpu.VMEM((4, 128, 1024), F32),
            pltpu.VMEM((4, 128, 1024), BF),
            pltpu.VMEM((128, 1024), BF),
            pltpu.VMEM((128, 1024), BF),
            pltpu.VMEM((4, 128, 1024), BF),
            pltpu.VMEM((4, 4, 2, 32, 768), BF),
            pltpu.VMEM((4, 4, 32, 768), BF),
            pltpu.VMEM((4, 4, 32, 768), BF),
            pltpu.VMEM((4, 4, 32, 768), BF),
            pltpu.VMEM((4, 32, 768), BF),
            pltpu.VMEM((256, 64), F32),
            pltpu.VMEM((8, 1024), F32),
            pltpu.VMEM((8, 8, 1024), F32),
            pltpu.VMEM((4, 8, 1024), F32),
            dma((2, 4)),
            dma((2, 4)),
            dma((2, 4)),
            dma((2, 8)),
            dma((2, 4)),
        ],
        compiler_params=pltpu.CompilerParams(
            collective_id=4, has_side_effects=True, vmem_limit_bytes=48 << 20
        ),
        name="fifth",
    )(back, tabg, normed, wq, tokg, scales, grad_middle, sums, ttab, tix)
def blocked(
    tokens,
    positions,
    time_index,
    time_table,
    w_qkv,
    w_out,
    w_up,
    w_down,
    scale_attn,
    scale_mlp,
    cotangent,
):
    cosine, sine = rotary_tables(positions, HEAD_DIM)
    cosine, sine = cosine[:, :, 0], sine[:, :, 0]
    table = jnp.concatenate([cosine[0], sine[0], cosine[1], sine[1]], axis=-1)
    wide = w_qkv.reshape(32, 3, 4, 4, 64)
    kv_cols = jnp.stack([wide[:, 1], wide[:, 2]], axis=3).reshape(32, 4, 512)
    wq_parts = jnp.concatenate([kv_cols, wide[:, 0].reshape(32, 4, 256)], axis=-1)
    wq_parts = jnp.swapaxes(wq_parts, 0, 1)
    up_parts = jnp.transpose(w_up.reshape(32, 4, 8, 128), (2, 0, 1, 3)).reshape(8, 32, 512)
    (
        tiles, normed, wq, scales, table_all, tokens_all, mixed, lse,
        grad_rx, grad_middle, middle, outq, grad_down, grad_up, grad_out, sums,
    ) = front(
        tokens, table, wq_parts, time_table, (scale_attn, scale_mlp), up_parts, w_out,
        w_down, cotangent.reshape(128, 1024), time_index,
    )
    back, output, down_own, up_own, out_own = phase_four_kernel(
        tiles,
        grad_rx,
        mixed,
        lse,
        outq,
        middle,
        grad_down,
        grad_up,
        grad_out.reshape(4, 4, 2, 32, 1024),
    )
    grad_tokens, grad_wq, grad_attn, grad_mlp = phase_five_kernel(
        back,
        table_all,
        normed,
        wq,
        tokens_all,
        scales,
        grad_middle,
        sums,
        time_table,
        time_index,
    )
    kv_cols = grad_wq[:, :, :512].reshape(4, 32, 4, 2, 64)
    wide = jnp.stack(
        [grad_wq[:, :, 512:].reshape(4, 32, 4, 64), kv_cols[:, :, :, 0], kv_cols[:, :, :, 1]],
        axis=0,
    )
    qkv_own = jnp.transpose(wide, (2, 0, 1, 3, 4)).reshape(32, 3072).astype(F32)
    up_own = jnp.transpose(up_own.reshape(8, 32, 4, 128), (1, 2, 0, 3)).reshape(32, 4096)
    return (
        output.reshape(2, 64, 1024),
        grad_tokens.reshape(2, 64, 1024),
        qkv_own,
        out_own,
        up_own.astype(F32),
        down_own,
        grad_attn,
        grad_mlp,
    )


def solution(mesh):
    fits = mesh.shape["head"] == 4 and mesh.shape["blk"] == 8
    placed = (
        P(None, ("head", "blk"), None),
        P(None, ("head", "blk")),
        P(),
        P(),
        P(("head", "blk"), None),
        P(("head", "blk"), None),
        P(("head", "blk"), None),
        P(("head", "blk"), None),
        P(("head", "blk"), None),
        P(("head", "blk"), None),
        P(None, ("head", "blk"), None),
    )
    return jax.shard_map(
        blocked if fits else general,
        mesh=mesh,
        in_specs=placed,
        out_specs=(
            P(None, ("head", "blk"), None),
            P(None, ("head", "blk"), None),
            P(("head", "blk"), None),
            P(("head", "blk"), None),
            P(("head", "blk"), None),
            P(("head", "blk"), None),
            P(("head", "blk"), None),
            P(("head", "blk"), None),
        ),
        check_vma=False,
    )
```

```python
import math

import jax
import jax.numpy as jnp
from jax import lax
from jax.experimental import pallas as pl
from jax.experimental.pallas import tpu as pltpu
from jax.sharding import PartitionSpec as P

HEADS = 16
HEAD_DIM = 64


NORM_EPSILON = 1e-05
PRECISE = lax.Precision.HIGHEST
START_TOP = -1e30
SCORE_SCALE = 0.125


def shifted(value, axis, steps):
    count = lax.axis_size(axis)
    pairs = [(source, (source + steps) % count) for source in range(count)]
    return lax.ppermute(value, axis, pairs)


def layer_norm(value, scale):
    centered = value - jnp.mean(value, axis=-1, keepdims=True)
    variance = jnp.mean(centered * centered, axis=-1, keepdims=True)
    return centered * lax.rsqrt(variance + NORM_EPSILON) * scale


def rotate(value, cosine_table, sine_table):
    half_dim = value.shape[-1] // 2
    first_half = value[..., :half_dim]
    second_half = value[..., half_dim:]
    return jnp.concatenate(
        [
            first_half * cosine_table - second_half * sine_table,
            second_half * cosine_table + first_half * sine_table,
        ],
        axis=-1,
    )


def rotary_tables(positions, head_dim):
    half_dim = head_dim // 2
    frequency = 10000.0 ** (-jnp.arange(half_dim, dtype=jnp.float32) / half_dim)
    turned = positions.astype(jnp.float32)[:, :, None, None] * frequency
    return (jnp.cos(turned), jnp.sin(turned))


def contract_rows(left, right):
    return lax.dot_general(
        left, right, (((0,), (0,)), ((), ())), preferred_element_type=jnp.float32
    )


def contract_cols(left, right):
    return lax.dot_general(
        left, right, (((1,), (1,)), ((), ())), preferred_element_type=jnp.float32
    )


def attend_step(running, query_block, key_block, value_block):
    row_top, row_sum, accum = running
    scores = (
        jnp.einsum("sqhd,skhd->sqhk", query_block, key_block, preferred_element_type=jnp.float32)
        * SCORE_SCALE
    )
    new_top = jnp.maximum(row_top, jnp.max(scores, axis=-1))
    shrink = jnp.exp(row_top - new_top)
    weights = jnp.exp(scores - new_top[..., None])
    row_sum = row_sum * shrink + jnp.sum(weights, axis=-1)
    accum = accum * shrink[..., None] + jnp.einsum(
        "sqhk,skhd->sqhd",
        weights.astype(jnp.bfloat16),
        value_block,
        preferred_element_type=jnp.float32,
    )
    return (new_top, row_sum, accum)


def back_step(query_block, key_block, value_block, grad_block, log_total, delta):
    scores = (
        jnp.einsum("sqhd,skhd->sqhk", query_block, key_block, preferred_element_type=jnp.float32)
        * SCORE_SCALE
    )
    probs = jnp.exp(scores - log_total[..., None])
    grad_values = jnp.einsum(
        "sqhk,sqhd->skhd",
        probs.astype(jnp.bfloat16),
        grad_block,
        preferred_element_type=jnp.float32,
    )
    grad_probs = jnp.einsum(
        "sqhd,skhd->sqhk", grad_block, value_block, preferred_element_type=jnp.float32
    )
    grad_scores = (probs * (grad_probs - delta[..., None])).astype(jnp.bfloat16)
    grad_query = jnp.einsum(
        "sqhk,skhd->sqhd", grad_scores, key_block, preferred_element_type=jnp.float32
    )
    grad_keys = jnp.einsum(
        "sqhk,sqhd->skhd", grad_scores, query_block, preferred_element_type=jnp.float32
    )
    return (grad_query, grad_keys, grad_values)


def general(
    tokens,
    positions,
    time_index,
    time_table,
    w_qkv,
    w_out,
    w_up,
    w_down,
    scale_attn,
    scale_mlp,
    cotangent,
):
    seq_count, row_count, model_width = tokens.shape
    group_count = lax.axis_size("head")
    local_heads = HEADS // group_count
    feature_width = local_heads * HEAD_DIM
    flat_rows = seq_count * row_count
    gathered = (
        lax.all_gather(w_qkv, ("head", "blk"), axis=0, tiled=True),
        lax.all_gather(w_out, ("head", "blk"), axis=0, tiled=True),
        lax.all_gather(w_up, ("head", "blk"), axis=0, tiled=True),
        lax.all_gather(w_down, ("head", "blk"), axis=0, tiled=True),
        lax.all_gather(scale_attn, ("head", "blk"), axis=0, tiled=True),
        lax.all_gather(scale_mlp, ("head", "blk"), axis=0, tiled=True),
    )
    full_qkv, full_out, full_up, full_down, full_scale_attn, full_scale_mlp = gathered
    step_count = time_table.shape[0]
    picker = (time_index[:, None] == jnp.arange(step_count, dtype=jnp.int32)[None, :]).astype(
        jnp.float32
    )
    time_embed = jnp.dot(picker, time_table, precision=PRECISE)
    scale_one = 1.0 + jnp.dot(time_embed, full_scale_attn.astype(jnp.float32), precision=PRECISE)
    scale_two = 1.0 + jnp.dot(time_embed, full_scale_mlp.astype(jnp.float32), precision=PRECISE)
    token_float = tokens.astype(jnp.float32)
    normed = (
        layer_norm(token_float, scale_one[:, None, :])
        .astype(jnp.bfloat16)
        .reshape(flat_rows, model_width)
    )
    projected = jnp.dot(normed, full_qkv, preferred_element_type=jnp.float32).reshape(
        seq_count, row_count, 3, HEADS, HEAD_DIM
    )
    cosine_table, sine_table = rotary_tables(positions, HEAD_DIM)
    query_tok = rotate(projected[:, :, 0], cosine_table, sine_table)
    keys_tok = rotate(projected[:, :, 1], cosine_table, sine_table)
    packed = (
        jnp.stack([query_tok, keys_tok, projected[:, :, 2]], axis=2)
        .reshape(seq_count, row_count, 3, model_width)
        .astype(jnp.bfloat16)
    )
    regrouped = lax.all_to_all(packed, "head", split_axis=3, concat_axis=1, tiled=True)
    block_len = regrouped.shape[1]
    local_query = regrouped[:, :, 0].reshape(seq_count, block_len, local_heads, HEAD_DIM)
    local_keys = regrouped[:, :, 1]
    local_values = regrouped[:, :, 2]
    start_state = (
        jnp.full((seq_count, block_len, local_heads), START_TOP, jnp.float32),
        jnp.zeros((seq_count, block_len, local_heads), jnp.float32),
        jnp.zeros((seq_count, block_len, local_heads, HEAD_DIM), jnp.float32),
    )
    key_piece = lax.all_gather(local_keys, "blk", axis=1, tiled=True)
    value_piece = lax.all_gather(local_values, "blk", axis=1, tiled=True)
    piece_len = key_piece.shape[1]
    step_len = math.gcd(piece_len, block_len)

    def one_block(index, state):
        key_block = lax.dynamic_slice_in_dim(key_piece, index * step_len, step_len, 1).reshape(
            seq_count, step_len, local_heads, HEAD_DIM
        )
        value_block = lax.dynamic_slice_in_dim(value_piece, index * step_len, step_len, 1).reshape(
            seq_count, step_len, local_heads, HEAD_DIM
        )
        return attend_step(state, local_query, key_block, value_block)

    row_top, row_sum, accum = lax.fori_loop(0, piece_len // step_len, one_block, start_state)
    mixed = accum / row_sum[..., None]
    log_total = row_top + jnp.log(row_sum)
    attended_heads = mixed.astype(jnp.bfloat16).reshape(seq_count, block_len, feature_width)
    attended = lax.all_to_all(
        attended_heads, "head", split_axis=1, concat_axis=2, tiled=True
    ).reshape(flat_rows, model_width)
    branch = jnp.dot(attended, full_out, preferred_element_type=jnp.float32)
    middle = token_float + branch.reshape(seq_count, row_count, model_width)
    normed_two = (
        layer_norm(middle, scale_two[:, None, :])
        .astype(jnp.bfloat16)
        .reshape(flat_rows, model_width)
    )
    hidden = jnp.dot(normed_two, full_up, preferred_element_type=jnp.float32)
    active = jax.nn.gelu(hidden, approximate=False).astype(jnp.bfloat16)
    result = middle.reshape(flat_rows, model_width) + jnp.dot(
        active, full_down, preferred_element_type=jnp.float32
    )
    output = result.astype(jnp.bfloat16).reshape(seq_count, row_count, model_width)
    back_qkv, back_out, back_up, back_down = (
        lax.all_gather(w_qkv, ("head", "blk"), axis=0, tiled=True),
        lax.all_gather(w_out, ("head", "blk"), axis=0, tiled=True),
        lax.all_gather(w_up, ("head", "blk"), axis=0, tiled=True),
        lax.all_gather(w_down, ("head", "blk"), axis=0, tiled=True),
    )
    grad_out = cotangent.reshape(flat_rows, model_width)
    grad_active = contract_cols(grad_out, back_down)
    grad_w_down = contract_rows(active, grad_out)
    gelu_value, gelu_pull = jax.vjp(lambda entry: jax.nn.gelu(entry, approximate=False), hidden)
    grad_hidden = gelu_pull(grad_active)[0].astype(jnp.bfloat16)
    grad_w_up = contract_rows(normed_two, grad_hidden)
    grad_normed_two = contract_cols(grad_hidden, back_up).reshape(seq_count, row_count, model_width)
    norm_value, norm_pull = jax.vjp(layer_norm, middle, scale_two[:, None, :])
    grad_middle_norm, grad_scale_two = norm_pull(grad_normed_two)
    grad_middle = cotangent.astype(jnp.float32) + grad_middle_norm
    grad_scale_mlp = jnp.dot(time_embed.T, grad_scale_two[:, 0, :], precision=PRECISE)
    grad_branch = grad_middle.reshape(flat_rows, model_width).astype(jnp.bfloat16)
    grad_w_out = contract_rows(attended, grad_branch)
    grad_attended = (
        contract_cols(grad_branch, back_out)
        .astype(jnp.bfloat16)
        .reshape(seq_count, row_count, model_width)
    )
    grad_heads = lax.all_to_all(
        grad_attended, "head", split_axis=2, concat_axis=1, tiled=True
    ).reshape(seq_count, block_len, local_heads, HEAD_DIM)
    delta = jnp.sum(grad_heads.astype(jnp.float32) * mixed, axis=-1)

    def turn(index, state):
        key_now, value_now, grad_keys_now, grad_values_now, grad_query_sum = state
        grad_query, grad_keys, grad_values = back_step(
            local_query,
            key_now.reshape(seq_count, block_len, local_heads, HEAD_DIM),
            value_now.reshape(seq_count, block_len, local_heads, HEAD_DIM),
            grad_heads,
            log_total,
            delta,
        )
        moved_keys, moved_values = shifted((key_now, value_now), "blk", 1)
        moved_grad_keys, moved_grad_values = (
            shifted(
                (grad_keys_now + grad_keys.reshape(seq_count, block_len, feature_width)).astype(
                    jnp.bfloat16
                ),
                "blk",
                1,
            ).astype(jnp.float32),
            shifted(
                (grad_values_now + grad_values.reshape(seq_count, block_len, feature_width)).astype(
                    jnp.bfloat16
                ),
                "blk",
                1,
            ).astype(jnp.float32),
        )
        return (
            moved_keys,
            moved_values,
            moved_grad_keys,
            moved_grad_values,
            grad_query_sum + grad_query,
        )

    zero_kv = jnp.zeros((seq_count, block_len, feature_width), jnp.float32)
    begin = (
        local_keys,
        local_values,
        zero_kv,
        zero_kv,
        jnp.zeros((seq_count, block_len, local_heads, HEAD_DIM), jnp.float32),
    )
    final_state = lax.fori_loop(0, lax.axis_size("blk"), turn, begin)
    grad_keys_own = final_state[2]
    grad_values_own = final_state[3]
    grad_query_all = final_state[4]
    stacked = jnp.stack(
        [
            grad_query_all.reshape(seq_count, block_len, feature_width) * SCORE_SCALE,
            grad_keys_own * SCORE_SCALE,
            grad_values_own,
        ],
        axis=2,
    ).astype(jnp.bfloat16)
    returned = lax.all_to_all(stacked, "head", split_axis=1, concat_axis=3, tiled=True)
    grad_query_tok = (
        returned[:, :, 0].astype(jnp.float32).reshape(seq_count, row_count, HEADS, HEAD_DIM)
    )
    grad_keys_tok = (
        returned[:, :, 1].astype(jnp.float32).reshape(seq_count, row_count, HEADS, HEAD_DIM)
    )
    grad_values_tok = (
        returned[:, :, 2].astype(jnp.float32).reshape(seq_count, row_count, HEADS, HEAD_DIM)
    )
    grad_projected = (
        jnp.stack(
            [
                rotate(grad_query_tok, cosine_table, -sine_table),
                rotate(grad_keys_tok, cosine_table, -sine_table),
                grad_values_tok,
            ],
            axis=2,
        )
        .reshape(flat_rows, 3 * model_width)
        .astype(jnp.bfloat16)
    )
    grad_w_qkv = contract_rows(normed, grad_projected)
    grad_normed = contract_cols(grad_projected, back_qkv).reshape(seq_count, row_count, model_width)
    first_value, first_pull = jax.vjp(layer_norm, token_float, scale_one[:, None, :])
    grad_token_norm, grad_scale_one = first_pull(grad_normed)
    grad_tokens = grad_middle + grad_token_norm
    grad_scale_attn = jnp.dot(time_embed.T, grad_scale_one[:, 0, :], precision=PRECISE)
    shards = (
        lax.psum_scatter(grad_w_qkv, ("head", "blk"), scatter_dimension=0, tiled=True),
        lax.psum_scatter(grad_w_out, ("head", "blk"), scatter_dimension=0, tiled=True),
        lax.psum_scatter(grad_w_up, ("head", "blk"), scatter_dimension=0, tiled=True),
        lax.psum_scatter(grad_w_down, ("head", "blk"), scatter_dimension=0, tiled=True),
        lax.psum_scatter(grad_scale_attn, ("head", "blk"), scatter_dimension=0, tiled=True),
        lax.psum_scatter(grad_scale_mlp, ("head", "blk"), scatter_dimension=0, tiled=True),
    )
    return (output, grad_tokens, shards[0], shards[1], shards[2], shards[3], shards[4], shards[5])


EPS = NORM_EPSILON
BF = jnp.bfloat16
F32 = jnp.float32


def norm_stats(value):
    centered = value - jnp.mean(value, axis=-1, keepdims=True)
    spread = lax.rsqrt(jnp.mean(centered * centered, axis=-1, keepdims=True) + EPS)
    return centered * spread, spread


def norm_back(unit, spread, grad, scale):
    scaled = grad * scale
    return spread * (
        scaled
        - jnp.mean(scaled, axis=-1, keepdims=True)
        - unit * jnp.mean(scaled * unit, axis=-1, keepdims=True)
    )


MESH = pl.DeviceIdType.MESH


def flip(value, bits):
    for bit in (1, 2, 4):
        if bits & bit:
            value = value + bit - 2 * bit * lax.rem(lax.div(value, bit), 2)
    return value


def greet(head, blk, heads, blks):
    barrier = pltpu.get_barrier_semaphore()
    for k in heads:
        pl.semaphore_signal(barrier, inc=1, device_id=(flip(head, k), blk), device_id_type=MESH)
    for k in blks:
        pl.semaphore_signal(barrier, inc=1, device_id=(head, flip(blk, k)), device_id_type=MESH)
    pl.semaphore_wait(barrier, len(heads) + len(blks))


def send(source, target, send_sem, recv_sem, head, blk):
    return pltpu.make_async_remote_copy(
        src_ref=source,
        dst_ref=target,
        send_sem=send_sem,
        recv_sem=recv_sem,
        device_id=(head, blk),
        device_id_type=MESH,
    )


class Swap:
    def __init__(self, head, blk, axis, source, target, sems):
        self.copies = []
        count = 4 if axis == "head" else 8
        me = head if axis == "head" else blk
        for k in range(1, count):
            peer = flip(me, k)
            where = (peer, blk) if axis == "head" else (head, peer)
            self.copies.append(
                send(source(peer), target(me), sems.at[0, k], sems.at[1, k], *where)
            )

    def start(self):
        for copy in self.copies:
            copy.start()

    def arrive(self):
        for copy in self.copies:
            copy.wait_recv()

    def drain(self):
        for copy in self.copies:
            copy.wait_send()


class Plane:
    def __init__(self, head, blk, own, slot, sems):
        sibling = flip(blk, 1)
        self.first = [send(own, slot(blk), sems.at[0, 0], sems.at[1, 0], head, sibling)]
        self.passed = []
        for i, k in enumerate((2, 4, 6)):
            peer = flip(blk, k)
            self.first.append(
                send(own, slot(blk), sems.at[0, i + 1], sems.at[1, i + 1], head, peer)
            )
            self.passed.append(
                send(slot(peer), slot(peer), sems.at[0, i + 4], sems.at[1, i + 4], head, sibling)
            )

    def start(self):
        for i in (3, 1, 2, 0):
            self.first[i].start()

    def forward(self, i):
        self.first[i + 1].wait_recv()
        self.passed[i].start()

    def arrive(self, i):
        if i < 0:
            self.first[0].wait_recv()
        else:
            self.passed[i].wait_recv()

    def finish(self):
        for i in range(3):
            self.forward(i)
        for i in range(-1, 3):
            self.arrive(i)

    def drain(self):
        for copy in self.first + self.passed:
            copy.wait_send()


def line_order(head, step):
    low = jnp.minimum(head, 3 - head)
    swap = low * ((step == 0).astype(jnp.int32) - (step == 1).astype(jnp.int32))
    at = step + swap
    return jnp.where(head < 2, at, 3 - at)


class Line:
    def __init__(self, head, blk, own, slot, sems):
        self.head, self.blk, self.own, self.slot, self.sems = head, blk, own, slot, sems

    def copy(self, source, at, up, k):
        head = self.head
        target = jnp.where(up, head + 1, head - 1)
        way = jnp.where(up, 0, 1)
        return send(
            source, self.slot(at), self.sems.at[0, way, k], self.sems.at[1, way, k], target, self.blk
        )

    def start(self):
        head = self.head

        @pl.when(head < 3)
        def _():
            self.copy(self.own, head, True, 0).start()

        @pl.when(head > 0)
        def _():
            self.copy(self.own, head, False, 0).start()

    def step(self, at):
        head = self.head
        up = at < head
        k = jnp.where(up, head - 1 - at, at - head - 1)
        self.copy(self.slot(at), at, up, k).wait_recv()

        @pl.when(jnp.where(up, head < 3, head > 0))
        def _():
            self.copy(self.slot(at), at, up, k + 1).start()

    def drain(self):
        head = self.head
        for k in range(3):

            @pl.when(jnp.logical_and(head < 3, head >= k))
            def _():
                self.copy(self.own, head, True, k).wait_send()

            @pl.when(jnp.logical_and(head > 0, head + k <= 3))
            def _():
                self.copy(self.own, head, False, k).wait_send()


class Reach:
    def __init__(self, head, blk, own, slot, sems):
        self.head, self.blk, self.own, self.slot, self.sems = head, blk, own, slot, sems
        self.middle = jnp.logical_and(head > 0, head < 3)

    def copy(self, k):
        peer = flip(self.head, k)
        return send(
            self.own, self.slot(self.head), self.sems.at[0, k], self.sems.at[1, k], peer, self.blk
        )

    def passed(self):
        at = self.slot(flip(self.head, 2))
        return send(at, at, self.sems.at[0, 0], self.sems.at[1, 3], flip(self.head, 1), self.blk)

    def start(self):
        self.copy(2).start()
        self.copy(1).start()

        @pl.when(self.middle)
        def _():
            self.copy(3).start()

    def forward(self):
        self.copy(2).wait_recv()

        @pl.when(self.middle)
        def _():
            self.passed().start()

    def arrive(self):
        self.copy(1).wait_recv()
        self.copy(3).wait_recv()

    def drain(self):
        self.copy(1).wait_send()
        self.copy(2).wait_send()

        @pl.when(self.middle)
        def _():
            self.copy(3).wait_send()
            self.passed().wait_send()


class Fold:
    def __init__(self, head, blk, terms, via, joined, into, sems):
        self.head, self.blk, self.sems = head, blk, sems
        self.terms, self.via, self.joined, self.into = terms, via, joined, into
        self.middle = jnp.logical_and(head > 0, head < 3)

    def copy(self, k):
        peer = flip(self.head, k)
        return send(
            self.terms.at[peer],
            self.into.at[k],
            self.sems.at[0, k],
            self.sems.at[1, k],
            peer,
            self.blk,
        )

    def handed(self):
        return send(
            self.terms.at[flip(self.head, 3)],
            self.via,
            self.sems.at[0, 0],
            self.sems.at[1, 0],
            flip(self.head, 1),
            self.blk,
        )

    def relayed(self):
        return send(
            self.joined,
            self.into.at[2],
            self.sems.at[0, 2],
            self.sems.at[1, 2],
            flip(self.head, 2),
            self.blk,
        )

    def start_far(self):
        @pl.when(jnp.logical_not(self.middle))
        def _():
            self.handed().start()

    def start_one(self, k):
        if k == 1:
            self.copy(1).start()
        elif k == 2:

            @pl.when(jnp.logical_not(self.middle))
            def _():
                self.copy(2).start()

        else:

            @pl.when(self.middle)
            def _():
                self.copy(3).start()

    def start(self):
        self.start_far()
        for k in (2, 3, 1):
            self.start_one(k)

    def relay(self):
        @pl.when(self.middle)
        def _():
            self.handed().wait_recv()
            mine = self.terms[flip(self.head, 2)].astype(F32)
            self.joined[...] = (mine + self.via[...].astype(F32)).astype(BF)
            self.relayed().start()

    def arrive(self):
        self.copy(1).wait_recv()
        self.copy(2).wait_recv()

        @pl.when(self.middle)
        def _():
            self.copy(3).wait_recv()

        @pl.when(jnp.logical_not(self.middle))
        def _():
            self.into[3] = jnp.zeros_like(self.into[3])

        self.into[0] = self.terms[self.head]

    def drain(self):
        self.copy(1).wait_send()

        @pl.when(self.middle)
        def _():
            self.copy(3).wait_send()
            self.relayed().wait_send()

        @pl.when(jnp.logical_not(self.middle))
        def _():
            self.copy(2).wait_send()
            self.handed().wait_send()


def half_lane(shape):
    return lax.broadcasted_iota(jnp.int32, shape, 1) < 64


def lane_swap(value):
    lane = lax.broadcasted_iota(jnp.int32, value.shape, 1)
    return jnp.where(
        lax.rem(lane, 64) < 32, pltpu.roll(value, 96, 1), pltpu.roll(value, 32, 1)
    )


def turn_tables(table, sign):
    lane = lax.broadcasted_iota(jnp.int32, table.shape, 1)
    cosine = jnp.where(lane < 32, table, 0.0)
    cosine = cosine + pltpu.roll(cosine, 32, 1)
    sine = jnp.where(jnp.logical_and(lane >= 32, lane < 64), table, 0.0) * sign
    sine = sine - pltpu.roll(sine, 96, 1)
    both = (cosine + pltpu.roll(cosine, 64, 1), sine + pltpu.roll(sine, 64, 1))
    return both, (jnp.where(lane < 64, cosine, 1.0), sine)


def join_halves(top, bottom, right):
    left = half_lane(top.shape)
    if right:
        return jnp.where(left, pltpu.roll(top, 64, 1), bottom)
    return jnp.where(left, top, pltpu.roll(bottom, 64, 1))


EXP_SCALE = SCORE_SCALE * math.log2(math.e)
KEYS = 256


def flip_by(head, k):
    low, high = lax.rem(k, 2), lax.div(k, 2)
    value = head + low - 2 * low * lax.rem(head, 2)
    return value + 2 * high - 4 * high * lax.div(head, 2)


class Everyone:
    def __init__(self, head, blk, source, target, sems):
        self.head, self.blk, self.source, self.target, self.sems = head, blk, source, target, sems
        self.peers = [flip(blk, k) for k in range(8)]

    def copy(self, kz, k):
        z = flip_by(self.head, jnp.int32(kz))
        return self.copy_to(z, kz, k)

    def copy_to(self, z, kz, k):
        b = self.peers[k]
        return send(
            self.source(z, b),
            self.target(self.head, self.blk),
            self.sems.at[0, kz, k],
            self.sems.at[1, kz, k],
            z,
            b,
        )

    def start(self, kz):
        z = flip_by(self.head, jnp.int32(kz))

        @pl.when(kz > 0)
        def _():
            self.copy_to(z, kz, 0).start()

        for k in range(1, 8):
            self.copy_to(z, kz, k).start()

    def arrive(self, kz):
        z = flip_by(self.head, jnp.int32(kz))

        @pl.when(kz > 0)
        def _():
            self.copy_to(z, kz, 0).wait_recv()

        for k in range(1, 8):
            self.copy_to(z, kz, k).wait_recv()

    def drain(self):
        for kz in range(4):
            for k in range(1 if kz == 0 else 0, 8):
                self.copy(kz, k).wait_send()


def greet_all(head, blk):
    barrier = pltpu.get_barrier_semaphore()
    for kz in range(4):
        for k in range(8):
            if kz or k:
                pl.semaphore_signal(
                    barrier, inc=1, device_id=(flip(head, kz), flip(blk, k)), device_id_type=MESH
                )
    pl.semaphore_wait(barrier, 31)


def group_rows(value):
    return jnp.sum(value.reshape(value.shape[0] // 8, 8, value.shape[1]), axis=0)


VMEM_LIMIT = 61 << 20


class Scatter:
    def __init__(self, head, blk, terms, near, joined, far, sems):
        self.head, self.blk, self.core = head, blk, lax.rem(blk, 2)
        self.terms, self.near, self.joined, self.far, self.sems = terms, near, joined, far, sems

    def halves(self):
        return send(
            self.terms.at[:, :, 1 - self.core],
            self.near,
            self.sems.at[0, 0],
            self.sems.at[1, 0],
            self.head,
            flip(self.blk, 1),
        )

    def chips(self, i):
        peer = flip(self.blk, 2 * i)
        return send(
            self.joined.at[lax.div(peer, 2)],
            self.far.at[i],
            self.sems.at[0, i],
            self.sems.at[1, i],
            self.head,
            peer,
        )

    def start(self):
        self.halves().start()

    def join(self):
        self.halves().wait_recv()
        for chip in range(4):
            mine = self.terms[:, chip, pl.ds(self.core, 1)].astype(F32)
            mine = mine.reshape(mine.shape[0], *mine.shape[2:])
            self.joined[chip] = (mine + self.near[:, chip].astype(F32)).astype(BF)
        for i in (3, 1, 2):
            self.chips(i).start()

    def total(self):
        value = self.joined[lax.div(self.blk, 2)].astype(F32)
        for i in range(1, 4):
            self.chips(i).wait_recv()
            value = value + self.far[i].astype(F32)
        return value

    def drain(self):
        self.halves().wait_send()
        for i in range(1, 4):
            self.chips(i).wait_send()


def sum_four(parts):
    return (parts[0].astype(F32) + parts[1].astype(F32)) + (
        parts[2].astype(F32) + parts[3].astype(F32)
    )


def layer_kernel(
    tok, tab, wqp, ttab, sca, scm, upp, out_own, down_own, cot_own, tix,
    output, g_down, g_up, g_out, grad_tokens, gq, grad_attn, grad_mlp,
    tiles, normed, wq, scales, tabg, tokg, mixed, lse, grad_rx, grad_middle, middle, outq, grad_down,
    grad_up, grad_out, sums, wqz, turned, part, sums_in, parts, out_tiles, upz, outz, up, down, out, cots,
    kvt, scores, att, received, attended, n2g, act, gh, pairs, prx, gsend, gin, tsend, branch, queries,
    grads, queries_t, grads_t, stats, keyt, dkv, dqt, bsend, back, oin, din, dvia, djoin, uin, uvia, ujoin,
    usum, near, joined, far, osum, zin, gp, gnp, gvia, gjoin, gin_r, terms, near_q, joined_q, far_q, osum_q,
    part_r, sums_in_r, parts_r, zsem, lsem, tsem, wsem, asem, bsem, psem, usem, osem, usem2, dsem, qsem,
    csem, esem, nsem, ssem, gsem, fsem, qsem_r, dsem_r, usem_r, vsem, osem_r, xsem, bsem_r, gsem_r, osem_q,
    xsem_q, asem_r, csem_r,
):
    head, blk = lax.axis_index("head"), lax.axis_index("blk")
    core = lax.rem(blk, 2)
    greet_all(head, blk)
    zswap = Swap(head, blk, "head", lambda i: wqp.at[i], lambda i: wqz.at[i], zsem)
    zswap.start()
    line = Line(head, blk, tok, lambda i: tokg.at[i], lsem)
    tline = Line(head, blk, tab, lambda i: tabg.at[i], tsem)
    tline.start()
    line.start()
    uswap = Swap(head, blk, "blk", lambda i: upp.at[i], lambda i: upz.at[i], usem)
    oline = Reach(head, blk, out_own, lambda i: outz.at[i], osem)
    uline = Line(head, blk, upz, lambda i: up.at[i], usem2)
    dline = Line(head, blk, down_own, lambda i: down.at[i], dsem)
    oplane = Plane(head, blk, outz, lambda i: out.at[:, i], qsem)
    cplane = Plane(head, blk, cot_own, lambda i: cots.at[i], csem)
    everyone = Everyone(head, blk, lambda z, b: att.at[z, b], lambda z, b: received.at[z, b], esem)
    backward = Everyone(head, blk, lambda z, b: tsend.at[z, b], lambda z, b: grad_rx.at[z, b], fsem)
    turned[...] = jnp.transpose(ttab[...])
    rows = turned[pl.ds(pl.multiple_of((head * 8 + blk) * 8, 8), 8), :]
    step_lane = lax.broadcasted_iota(jnp.int32, rows.shape, 1)
    pieces = []
    for weight in (sca, scm):
        for seq in range(2):
            column = jnp.sum(jnp.where(step_lane == tix[seq], rows, 0.0), axis=1, keepdims=True)
            pieces.append(jnp.sum(column * weight[...].astype(F32), axis=0, keepdims=True))
    part[...] = jnp.concatenate(pieces + [jnp.zeros((4, 1024), F32)], axis=0)
    one = Swap(head, blk, "blk", lambda i: part, lambda i: sums_in.at[i], asem)
    one.start()
    uswap.start()
    sums_in[blk] = part[...]
    wqz[head] = wqp[head]
    tokg[head] = tok[...]
    tabg[head] = tab[...]
    upz[blk] = upp[blk]
    outz[head] = out_own[...]
    down[head] = down_own[...]
    cots[blk] = cot_own[...]
    one.arrive()
    total = sums_in[0]
    for i in range(1, 8):
        total = total + sums_in[i]
    parts[head] = total
    two = Swap(head, blk, "head", lambda i: parts.at[head], lambda i: parts.at[i], bsem)
    two.start()
    zswap.arrive()
    plane = Plane(head, blk, wqz, lambda i: wq.at[:, i], wsem)
    plane.start()
    wq[:, pl.ds(blk, 1)] = wqz[...].reshape(4, 1, 32, 768)
    two.arrive()
    total = 1.0 + ((parts[0] + parts[1]) + (parts[2] + parts[3]))
    scales[...] = total

    def gather(step, carry):
        at = line_order(head, step)

        @pl.when(step > 0)
        def _():
            tline.step(at)
            line.step(at)

        for seq in range(2):
            unit, _ = norm_stats(tokg[at, seq].astype(F32))
            normed[at, pl.ds(64 * seq, 64), :] = (unit * scales[seq : seq + 1, :]).astype(BF)
        return carry

    def project(step, carry):
        at = line_order(head, step)
        proj = jnp.dot(
            normed[at], wq[...].reshape(1024, 768), preferred_element_type=F32
        )
        for seq in range(2):
            table = tabg[at]
            if seq:
                table = pltpu.roll(table, 64, 1)
            both, keyed = turn_tables(table, 1.0)
            mine = proj[64 * seq : 64 * seq + 64]
            for j in range(4):
                kv = mine[:, 128 * j : 128 * j + 128]
                kv = kv * keyed[0] + lane_swap(kv) * keyed[1]
                out_tiles[4 * seq + j, at, 0:64, :] = kv.astype(BF)
            for i in range(2):
                query = mine[:, 512 + 128 * i : 640 + 128 * i]
                query = query * both[0] + lane_swap(query) * both[1]
                for right in range(2):
                    packed = join_halves(query[:32], query[32:], right)
                    out_tiles[4 * seq + 2 * i + right, at, 64:96, :] = packed.astype(BF)
        move(at).start()
        tiles[at, blk] = out_tiles[blk, at]
        return carry

    def move(at):
        return Swap(
            head, blk, "blk", lambda i: out_tiles.at[i, at], lambda i: tiles.at[at, i], psem.at[at]
        )

    lax.fori_loop(0, 3, gather, 0)
    oline.start()
    plane.finish()
    lax.fori_loop(0, 3, project, 0)

    def last(step, carry):
        gather(step, carry)
        return project(step, carry)

    lax.fori_loop(3, 4, last, 0)
    uswap.arrive()
    up[head] = upz[...]
    uline.start()
    oline.forward()
    oline.arrive()
    out[:, pl.ds(blk, 1)] = outz[...].reshape(4, 1, 32, 1024)
    for at in range(4):
        move(at).arrive()
    oplane.start()
    kvt[...] = jnp.transpose(tiles[:, :, 0:64, :].reshape(2048, 128))

    def attend(step, carry):
        z = flip_by(head, 3 - step)
        flat = jnp.transpose(tiles[z, :, 64:96, :].reshape(256, 128).astype(F32))
        blank = jnp.zeros((64, 256), F32)
        results = []
        for side in range(2):
            query = jnp.concatenate([flat[64 * side : 64 * side + 64], blank], axis=0).astype(BF)
            top = None
            for c in range(2048 // KEYS):
                keys = tiles[c // 2, 4 * (c % 2) : 4 * (c % 2) + 4, 0:64, :].reshape(KEYS, 128)
                part = jnp.dot(keys, query, preferred_element_type=F32)
                scores[side, c] = part
                peak = jnp.max(part.reshape(KEYS // 8, 8, 256), axis=0)
                top = peak if top is None else jnp.maximum(top, peak)
            top = jnp.max(top, axis=0, keepdims=True)
            total = jnp.zeros((8, 256), F32)
            mix = jnp.zeros((64, 256), F32)
            for c in range(2048 // KEYS):
                weights = jnp.exp2((scores[side, c] - top) * EXP_SCALE)
                total = total + group_rows(weights)
                mix = mix + jnp.dot(
                    kvt[64:128, KEYS * c : KEYS * c + KEYS],
                    weights.astype(BF),
                    preferred_element_type=F32,
                )
            total = jnp.sum(total, axis=0, keepdims=True)
            mix = mix / total
            mixed[z, 64 * side : 64 * side + 64, :] = mix
            lse[z, side : side + 1, :] = top * SCORE_SCALE + jnp.log(total)
            results.append(mix)
        both = jnp.transpose(jnp.concatenate(results, axis=0))
        att[z] = both.astype(BF).reshape(8, 32, 128)
        everyone.start(3 - step)

        @pl.when(step == 0)
        def _():
            uline.step(line_order(head, jnp.int32(1)))

        @pl.when(step == 1)
        def _():
            uline.step(line_order(head, jnp.int32(2)))

        @pl.when(step == 2)
        def _():
            uline.step(line_order(head, jnp.int32(3)))
            dline.start()
            for i in range(3):
                oplane.forward(i)
            cplane.start()

        return carry

    lse[...] = jnp.zeros_like(lse)
    lax.fori_loop(0, 4, attend, 0)
    received[head, blk] = att[head, blk]
    dline.step(line_order(head, jnp.int32(1)))
    for i in range(-1, 3):
        oplane.arrive(i)
    middle[...] = tok[...].astype(F32).reshape(128, 1024)
    for kz in range(4):
        group = flip(head, kz)
        everyone.arrive(kz)
        for seq in range(2):
            for i in range(2):
                first = received[group, 4 * seq + 2 * i].astype(F32)
                second = received[group, 4 * seq + 2 * i + 1].astype(F32)
                lanes = slice(128 * i, 128 * i + 128)
                for right in range(2):
                    at = slice(64 * seq + 32 * right, 64 * seq + 32 * right + 32)
                    attended[group, at, lanes] = join_halves(first, second, right).astype(BF)
        middle[...] += jnp.dot(
            attended[group], out[group].reshape(256, 1024), preferred_element_type=F32
        )
    for seq in range(2):
        rows = slice(64 * seq, 64 * seq + 64)
        unit, _ = norm_stats(middle[rows, :])
        n2g[blk, rows, :] = (unit * scales[2 + seq : 3 + seq, :]).astype(BF)
    nplane = Plane(head, blk, n2g.at[blk], lambda i: n2g.at[i], nsem)
    for i in (1, 2, 0):
        nplane.first[i].start()
    dline.step(line_order(head, jnp.int32(2)))
    nplane.first[3].start()
    cplane.finish()
    dline.step(line_order(head, jnp.int32(3)))
    sibling = flip(blk, 1)

    def halves(i):
        return [
            send(pairs.at[w, i, 1 - core], prx.at[w, i], ssem.at[0, w, i], ssem.at[1, w, i], head, sibling)
            for w in range(2)
        ]

    def onward(i):
        peer = flip(blk, 2 * i)
        return send(gsend.at[i], gin.at[i], gsem.at[0, i], gsem.at[1, i], head, peer)

    def reduce(i):
        chip = lax.div(flip(blk, 2 * i), 2)
        for copy in halves(i):
            copy.wait_recv()
        gsend[i] = (pairs[0, i, core].astype(F32) + prx[0, i].astype(F32)).astype(BF)
        if i:
            onward(i).start()
        outq[chip] = (pairs[1, i, core].astype(F32) + prx[1, i].astype(F32)).astype(BF)

    for i in range(4):
        chip = lax.div(flip(blk, 2 * i), 2)
        if i == 0:
            nplane.arrive(-1)
        else:
            nplane.forward(i - 1)
            if i > 1:
                reduce(i - 1)
            nplane.arrive(i - 1)
        at = pl.ds(2 * chip, 2)
        rows = n2g[at].reshape(256, 1024)
        hidden = jnp.dot(rows, up[...].reshape(1024, 512), preferred_element_type=F32)
        grad_active = contract_cols(cots[at].reshape(256, 1024), down[...].reshape(512, 1024))
        cdf = 0.5 * (1.0 + lax.erf(hidden * math.sqrt(0.5)))
        active = (hidden * cdf).astype(BF)
        slope = cdf + hidden * jnp.exp(-0.5 * hidden * hidden) * (1.0 / math.sqrt(2 * math.pi))
        grad_hidden = (grad_active * slope).astype(BF)
        act[at] = active.reshape(2, 128, 512)
        gh[at] = grad_hidden.reshape(2, 128, 512)
        pairs[0, i] = (
            contract_cols(grad_hidden, up[...].reshape(1024, 512)).astype(BF).reshape(2, 128, 1024)
        )
        pairs[1, i] = (
            jnp.dot(active, down[...].reshape(512, 1024), preferred_element_type=F32)
            .astype(BF)
            .reshape(2, 128, 1024)
        )
        for copy in halves(i):
            copy.start()
    reduce(3)
    reduce(0)
    for group in range(4):
        lanes = slice(128 * group, 128 * group + 128)
        grad_down[group] = contract_rows(
            act[:, :, lanes].reshape(1024, 128), cots[...].reshape(1024, 1024)
        ).astype(BF)
    for group in range(4):
        lanes = slice(256 * group, 256 * group + 256)
        value = contract_rows(n2g[:, :, lanes].reshape(1024, 256), gh[...].reshape(1024, 512))
        grad_up[group] = value.astype(BF).reshape(8, 32, 512)
    uswap_r = Fold(head, blk, grad_up, uvia, ujoin, uin, usem_r)
    dfold = Fold(head, blk, grad_down, dvia, djoin, din, dsem_r)
    folds = (uswap_r, dfold)
    for fold in folds:
        fold.start_far()
        fold.start_one(3)

        @pl.when(fold.middle)
        def _():
            fold.copy(1).start()

    for i in range(1, 4):
        onward(i).wait_recv()
    sums[...] = jnp.zeros_like(sums)
    for seq in range(2):
        rows = slice(64 * seq, 64 * seq + 64)
        grad = gsend[0, rows, :].astype(F32)
        for i in range(1, 4):
            grad = grad + gin[i, rows, :].astype(F32)
        unit, spread = norm_stats(middle[rows, :])
        whole_grad = cots[blk, rows, :].astype(F32) + norm_back(
            unit, spread, grad, scales[2 + seq : 3 + seq, :]
        )
        grad_middle[rows, :] = whole_grad
        branch[rows, :] = whole_grad.astype(BF)
        sums[seq : seq + 1, :] = jnp.sum(grad * unit, axis=0, keepdims=True)

    def give(step, carry):
        group = flip_by(head, 3 - step)
        value = contract_cols(branch[...], out[group].reshape(256, 1024))
        for seq in range(2):
            for i in range(2):
                lanes = slice(128 * i, 128 * i + 128)
                top = value[64 * seq : 64 * seq + 32, lanes]
                bottom = value[64 * seq + 32 : 64 * seq + 64, lanes]
                for right in range(2):
                    tsend[group, 4 * seq + 2 * i + right] = join_halves(top, bottom, right).astype(BF)
        backward.start(3 - step)
        return carry

    lax.fori_loop(0, 4, give, 0)
    grad_rx[head, blk] = tsend[head, blk]
    for group in range(4):
        value = contract_rows(attended[group], branch[...])
        grad_out[group] = value.astype(BF).reshape(4, 2, 32, 1024)
    scatter = Scatter(head, blk, grad_out, near, joined, far, osem_r)
    scatter.start()
    outs = []
    for i in range(1, 4):
        peer = flip(blk, 2 * i)
        outs.append(
            send(outq.at[lax.div(peer, 2)], oin.at[i], qsem_r.at[0, i], qsem_r.at[1, i], head, peer)
        )
    vswap = Swap(head, blk, "blk", lambda i: usum.at[i], lambda i: g_up.at[i], vsem)
    xswap = Swap(head, blk, "head", lambda i: osum.at[i], lambda i: zin.at[i], xsem)
    left = half_lane((256, 128))
    keyt[...] = jnp.transpose(tiles[:, :, 0:64, :].reshape(2048, 128))[:64]

    def prepare(z, carry):
        flat = tiles[z, :, 64:96, :].reshape(256, 128).astype(F32)
        grad = grad_rx[z].reshape(256, 128).astype(F32)
        product = jnp.transpose(grad) * mixed[z]
        queries[2 * z] = jnp.where(left, flat, 0.0).astype(BF)
        queries[2 * z + 1] = jnp.where(left, pltpu.roll(flat, 64, 1), 0.0).astype(BF)
        turned = jnp.transpose(flat)
        slopes = jnp.transpose(grad)
        blank = jnp.zeros((64, 256), F32)
        for side in range(2):
            rows = slice(64 * side, 64 * side + 64)
            queries_t[2 * z + side] = jnp.concatenate([turned[rows], blank], axis=0).astype(BF)
            grads_t[2 * z + side] = jnp.concatenate([blank, slopes[rows]], axis=0).astype(BF)
        grads[2 * z] = jnp.where(left, 0.0, pltpu.roll(grad, 64, 1)).astype(BF)
        grads[2 * z + 1] = jnp.where(left, 0.0, grad).astype(BF)
        for side in range(2):
            delta = jnp.sum(product[64 * side : 64 * side + 64], axis=0, keepdims=True)
            shift = lse[z, side : side + 1, :] * math.log2(math.e)
            stats[2 * z + side] = jnp.concatenate([shift, delta, jnp.zeros((6, 256), F32)], axis=0)
        return carry

    def ready(kz, carry):
        backward.arrive(kz)
        return prepare(flip_by(head, kz), carry)

    scatter.join()
    lax.fori_loop(0, 4, ready, 0)
    dqt[...] = jnp.zeros_like(dqt)

    def kv_move(z):
        return Swap(
            head,
            blk,
            "blk",
            lambda i: bsend.at[i, z, pl.ds(0, 64)],
            lambda i: back.at[i, z, pl.ds(0, 64)],
            bsem_r.at[z],
        )

    def keys_step(z, carry):
        dkv[...] = jnp.zeros_like(dkv)

        def query_step(q, inner):
            query, grad = queries[q], grads[q]
            query_t, grad_t = queries_t[q], grads_t[q]
            shift, delta = stats[q, 0:1, :], stats[q, 1:2, :]
            dq = dqt[q]
            for c in range(2):
                keys = tiles[z, 4 * c : 4 * c + 4, 0:64, :].reshape(256, 128)
                probs = jnp.dot(keys, query_t, preferred_element_type=F32)
                probs = jnp.exp2(probs * EXP_SCALE - shift)
                slopes = jnp.dot(keys, grad_t, preferred_element_type=F32)
                slopes = (probs * (slopes - delta)).astype(BF)
                dkv[c] += jnp.dot(slopes, query, preferred_element_type=F32) + jnp.dot(
                    probs.astype(BF), grad, preferred_element_type=F32
                )
                at = pl.ds(pl.multiple_of(512 * z + 256 * c, 256), 256)
                dq = dq + jnp.dot(keyt[:, at], slopes, preferred_element_type=F32)
            dqt[q] = dq
            return inner

        lax.fori_loop(0, 8, query_step, 0)
        scale = jnp.where(left, SCORE_SCALE, 1.0)
        for c in range(2):
            bsend[4 * c : 4 * c + 4, pl.ds(z, 1), 0:64, :] = (
                (dkv[c] * scale).astype(BF).reshape(4, 1, 64, 128)
            )
        kv_move(z).start()

        @pl.when(z == 0)
        def _():
            for fold in folds:
                fold.start_one(2)

        @pl.when(z == 1)
        def _():
            for fold in folds:
                fold.relay()
            for copy in outs:
                copy.start()

        @pl.when(z == 2)
        def _():
            for fold in folds:

                @pl.when(jnp.logical_not(fold.middle))
                def _():
                    fold.copy(1).start()

            osum[...] = scatter.total().astype(BF)
            xswap.start()
            zin[head] = osum[head]

        return carry

    lax.fori_loop(0, 4, keys_step, 0)
    for z in range(4):
        both = jnp.concatenate([dqt[2 * z], dqt[2 * z + 1]], axis=0)
        both = (jnp.transpose(both) * SCORE_SCALE).astype(BF)
        bsend[:, z, 64:96, :] = both.reshape(8, 32, 128)
    qmove = Swap(
        head,
        blk,
        "blk",
        lambda i: bsend.at[i, :, pl.ds(64, 32)],
        lambda i: back.at[i, :, pl.ds(64, 32)],
        bsem_r.at[4],
    )
    qmove.start()
    back[blk] = bsend[blk]
    picked = turned[pl.ds(pl.multiple_of((head * 8 + blk) * 8, 8), 8), :]
    step_lane = lax.broadcasted_iota(jnp.int32, picked.shape, 1)
    columns = [
        jnp.sum(jnp.where(step_lane == tix[seq], picked, 0.0), axis=1, keepdims=True)
        for seq in range(2)
    ]
    for z in range(4):
        kv_move(z).arrive()
    qmove.arrive()
    gswap = Fold(head, blk, gnp, gvia, gjoin, gin_r, gsem_r)

    def unturn(step, carry):
        at = flip(head, step)
        for seq in range(2):
            table = tabg[at]
            if seq:
                table = pltpu.roll(table, 64, 1)
            both, keyed = turn_tables(table, -1.0)
            rows = slice(64 * seq, 64 * seq + 64)
            for j in range(4):
                kv = back[4 * seq + j, at, 0:64, :].astype(F32)
                kv = kv * keyed[0] + lane_swap(kv) * keyed[1]
                gp[at, rows, 128 * j : 128 * j + 128] = kv.astype(BF)
            for i in range(2):
                first = back[4 * seq + 2 * i, at, 64:96, :].astype(F32)
                second = back[4 * seq + 2 * i + 1, at, 64:96, :].astype(F32)
                query = jnp.concatenate(
                    [join_halves(first, second, 0), join_halves(first, second, 1)], axis=0
                )
                query = query * both[0] + lane_swap(query) * both[1]
                gp[at, rows, 512 + 128 * i : 640 + 128 * i] = query.astype(BF)
        gnp[at] = contract_cols(gp[at], wq[...].reshape(1024, 768)).astype(BF)
        return carry

    for step in (3, 2, 1, 0):
        unturn(step, 0)
        if step == 3:
            gswap.start_far()
            gswap.start_one(3)
    for group in range(4):
        lanes = slice(256 * group, 256 * group + 256)
        value = contract_rows(normed[:, :, lanes].reshape(512, 256), gp[...].reshape(512, 768))
        terms[group] = value.astype(BF).reshape(4, 2, 32, 768)
    scatter_q = Scatter(head, blk, terms, near_q, joined_q, far_q, osem_q)
    scatter_q.start()
    part_r[...] = jnp.concatenate(
        [jnp.zeros((2, 1024), F32), sums[0:2, :], jnp.zeros((4, 1024), F32)], axis=0
    )

    def gather_r(at, carry):
        for seq in range(2):
            unit, _ = norm_stats(tokg[at, seq].astype(F32))
            part_r[seq : seq + 1, :] += jnp.sum(
                gnp[at, pl.ds(64 * seq, 64), :].astype(F32) * unit, axis=0, keepdims=True
            )
        return carry

    lax.fori_loop(0, 4, gather_r, 0)
    one_r = Swap(head, blk, "blk", lambda i: part_r, lambda i: sums_in_r.at[i], asem_r)
    one_r.start()
    sums_in_r[blk] = part_r[...]
    gswap.start_one(2)
    gswap.relay()
    gswap.start_one(1)
    scatter_q.join()
    uswap_r.arrive()
    usum[...] = sum_four(uin).astype(BF)
    vswap.start()
    g_up[blk] = usum[blk]
    one_r.arrive()
    total = sums_in_r[0]
    for i in range(1, 8):
        total = total + sums_in_r[i]
    parts_r[head] = total
    two_r = Swap(head, blk, "head", lambda i: parts_r.at[head], lambda i: parts_r.at[i], csem_r)
    two_r.start()
    total = middle[...] + outq[lax.div(blk, 2)].astype(F32)
    for i in range(1, 4):
        outs[i - 1].wait_recv()
        total = total + oin[i].astype(F32)
    output[...] = total.astype(BF)
    dfold.arrive()
    g_down[...] = sum_four(din)
    osum_q[...] = scatter_q.total().astype(BF)
    xswap_q = Swap(head, blk, "head", lambda i: osum_q.at[i], lambda i: gq.at[i], xsem_q)
    xswap_q.start()
    gq[head] = osum_q[head]
    xswap.arrive()
    g_out[...] = sum_four(zin)
    two_r.arrive()
    total = (parts_r[0] + parts_r[1]) + (parts_r[2] + parts_r[3])
    grad_attn[...] = columns[0] * total[0:1] + columns[1] * total[1:2]
    grad_mlp[...] = columns[0] * total[2:3] + columns[1] * total[3:4]
    gswap.arrive()
    for seq in range(2):
        rows = slice(64 * seq, 64 * seq + 64)
        grad = sum_four([gin_r[i, rows, :] for i in range(4)])
        unit, spread = norm_stats(tokg[head, seq].astype(F32))
        grad_tokens[rows, :] = grad_middle[rows, :] + norm_back(
            unit, spread, grad, scales[seq : seq + 1, :]
        )
    vswap.arrive()
    xswap_q.arrive()
    for z in range(4):
        kv_move(z).drain()
    for copy in outs:
        copy.wait_send()
    for copies in (
        scatter, uswap_r, dfold, vswap, xswap, qmove, gswap, scatter_q, xswap_q, one_r, two_r
    ):
        copies.drain()
    for at in range(4):
        move(at).drain()
    for i in range(4):
        for copy in halves(i):
            copy.wait_send()
        if i:
            onward(i).wait_send()
    for copies in (
        zswap, line, tline, plane, one, two, uswap, oline,
        uline, dline, oplane, cplane, everyone, nplane, backward,
    ):
        copies.drain()


def whole(count):
    return [pl.BlockSpec(memory_space=pltpu.VMEM)] * count


def layer(*operands):
    dma = pltpu.SemaphoreType.DMA
    shape = jax.ShapeDtypeStruct
    return pl.pallas_call(
        layer_kernel,
        out_shape=(
            shape((128, 1024), BF),
            shape((128, 1024), F32),
            shape((8, 32, 512), BF),
            shape((32, 1024), F32),
            shape((128, 1024), F32),
            shape((4, 32, 768), BF),
            shape((8, 1024), F32),
            shape((8, 1024), F32),
        ),
        in_specs=whole(10) + [pl.BlockSpec(memory_space=pltpu.SMEM)],
        out_specs=whole(8),
        scratch_shapes=[
            pltpu.VMEM((4, 8, 96, 128), BF),
            pltpu.VMEM((4, 128, 1024), BF),
            pltpu.VMEM((4, 8, 32, 768), BF),
            pltpu.VMEM((8, 1024), F32),
            pltpu.VMEM((4, 64, 128), F32),
            pltpu.VMEM((4, 2, 64, 1024), BF),
            pltpu.VMEM((4, 128, 256), F32),
            pltpu.VMEM((4, 8, 256), F32),
            pltpu.VMEM((4, 8, 32, 128), BF),
            pltpu.VMEM((128, 1024), F32),
            pltpu.VMEM((128, 1024), F32),
            pltpu.VMEM((4, 128, 1024), BF),
            pltpu.VMEM((4, 128, 1024), BF),
            pltpu.VMEM((4, 8, 32, 512), BF),
            pltpu.VMEM((4, 4, 2, 32, 1024), BF),
            pltpu.VMEM((8, 1024), F32),
            pltpu.VMEM((4, 32, 768), BF),
            pltpu.VMEM((256, 64), F32),
            pltpu.VMEM((8, 1024), F32),
            pltpu.VMEM((8, 8, 1024), F32),
            pltpu.VMEM((4, 8, 1024), F32),
            pltpu.VMEM((8, 4, 96, 128), BF),
            pltpu.VMEM((8, 32, 512), BF),
            pltpu.VMEM((4, 32, 1024), BF),
            pltpu.VMEM((4, 8, 32, 512), BF),
            pltpu.VMEM((4, 128, 1024), BF),
            pltpu.VMEM((4, 8, 32, 1024), BF),
            pltpu.VMEM((8, 128, 1024), BF),
            pltpu.VMEM((128, 2048), BF),
            pltpu.VMEM((2, 2048 // KEYS, KEYS, 256), F32),
            pltpu.VMEM((4, 8, 32, 128), BF),
            pltpu.VMEM((4, 8, 32, 128), BF),
            pltpu.VMEM((4, 128, 256), BF),
            pltpu.VMEM((8, 128, 1024), BF),
            pltpu.VMEM((8, 128, 512), BF),
            pltpu.VMEM((8, 128, 512), BF),
            pltpu.VMEM((2, 4, 2, 128, 1024), BF),
            pltpu.VMEM((2, 4, 128, 1024), BF),
            pltpu.VMEM((4, 128, 1024), BF),
            pltpu.VMEM((4, 128, 1024), BF),
            pltpu.VMEM((4, 8, 32, 128), BF),
            pltpu.VMEM((128, 1024), BF),
            pltpu.VMEM((8, 256, 128), BF),
            pltpu.VMEM((8, 256, 128), BF),
            pltpu.VMEM((8, 128, 256), BF),
            pltpu.VMEM((8, 128, 256), BF),
            pltpu.VMEM((8, 8, 256), F32),
            pltpu.VMEM((64, 2048), BF),
            pltpu.VMEM((2, 256, 128), F32),
            pltpu.VMEM((8, 64, 256), F32),
            pltpu.VMEM((8, 4, 96, 128), BF),
            pltpu.VMEM((8, 4, 96, 128), BF),
            pltpu.VMEM((4, 128, 1024), BF),
            pltpu.VMEM((4, 128, 1024), BF),
            pltpu.VMEM((128, 1024), BF),
            pltpu.VMEM((128, 1024), BF),
            pltpu.VMEM((4, 8, 32, 512), BF),
            pltpu.VMEM((8, 32, 512), BF),
            pltpu.VMEM((8, 32, 512), BF),
            pltpu.VMEM((8, 32, 512), BF),
            pltpu.VMEM((4, 4, 32, 1024), BF),
            pltpu.VMEM((4, 4, 32, 1024), BF),
            pltpu.VMEM((4, 4, 32, 1024), BF),
            pltpu.VMEM((4, 32, 1024), BF),
            pltpu.VMEM((4, 32, 1024), BF),
            pltpu.VMEM((4, 128, 768), BF),
            pltpu.VMEM((4, 128, 1024), BF),
            pltpu.VMEM((128, 1024), BF),
            pltpu.VMEM((128, 1024), BF),
            pltpu.VMEM((4, 128, 1024), BF),
            pltpu.VMEM((4, 4, 2, 32, 768), BF),
            pltpu.VMEM((4, 4, 32, 768), BF),
            pltpu.VMEM((4, 4, 32, 768), BF),
            pltpu.VMEM((4, 4, 32, 768), BF),
            pltpu.VMEM((4, 32, 768), BF),
            pltpu.VMEM((8, 1024), F32),
            pltpu.VMEM((8, 8, 1024), F32),
            pltpu.VMEM((4, 8, 1024), F32),
            dma((2, 4)),
            dma((2, 2, 3)),
            dma((2, 2, 3)),
            dma((2, 7)),
            dma((2, 8)),
            dma((2, 4)),
            dma((4, 2, 8)),
            dma((2, 8)),
            dma((2, 4)),
            dma((2, 2, 3)),
            dma((2, 2, 3)),
            dma((2, 7)),
            dma((2, 7)),
            dma((2, 4, 8)),
            dma((2, 7)),
            dma((2, 2, 4)),
            dma((2, 4)),
            dma((2, 4, 8)),
            dma((2, 4)),
            dma((2, 4)),
            dma((2, 4)),
            dma((2, 8)),
            dma((2, 4)),
            dma((2, 4)),
            dma((5, 2, 8)),
            dma((2, 4)),
            dma((2, 4)),
            dma((2, 4)),
            dma((2, 8)),
            dma((2, 4)),
        ],
        compiler_params=pltpu.CompilerParams(
            collective_id=0, has_side_effects=True, vmem_limit_bytes=VMEM_LIMIT
        ),
        name="layer",
    )(*operands)


def blocked(
    tokens,
    positions,
    time_index,
    time_table,
    w_qkv,
    w_out,
    w_up,
    w_down,
    scale_attn,
    scale_mlp,
    cotangent,
):
    cosine, sine = rotary_tables(positions, HEAD_DIM)
    cosine, sine = cosine[:, :, 0], sine[:, :, 0]
    table = jnp.concatenate([cosine[0], sine[0], cosine[1], sine[1]], axis=-1)
    wide = w_qkv.reshape(32, 3, 4, 4, 64)
    kv_cols = jnp.stack([wide[:, 1], wide[:, 2]], axis=3).reshape(32, 4, 512)
    wq_parts = jnp.concatenate([kv_cols, wide[:, 0].reshape(32, 4, 256)], axis=-1)
    wq_parts = jnp.swapaxes(wq_parts, 0, 1)
    up_parts = jnp.transpose(w_up.reshape(32, 4, 8, 128), (2, 0, 1, 3)).reshape(8, 32, 512)
    output, down_own, up_own, out_own, grad_tokens, grad_wq, grad_attn, grad_mlp = layer(
        tokens, table, wq_parts, time_table, scale_attn, scale_mlp, up_parts, w_out,
        w_down, cotangent.reshape(128, 1024), time_index,
    )
    kv_cols = grad_wq[:, :, :512].reshape(4, 32, 4, 2, 64)
    wide = jnp.stack(
        [grad_wq[:, :, 512:].reshape(4, 32, 4, 64), kv_cols[:, :, :, 0], kv_cols[:, :, :, 1]],
        axis=0,
    )
    qkv_own = jnp.transpose(wide, (2, 0, 1, 3, 4)).reshape(32, 3072).astype(F32)
    up_own = jnp.transpose(up_own.reshape(8, 32, 4, 128), (1, 2, 0, 3)).reshape(32, 4096)
    return (
        output.reshape(2, 64, 1024),
        grad_tokens.reshape(2, 64, 1024),
        qkv_own,
        out_own,
        up_own.astype(F32),
        down_own,
        grad_attn,
        grad_mlp,
    )


def solution(mesh):
    fits = mesh.shape["head"] == 4 and mesh.shape["blk"] == 8
    placed = (
        P(None, ("head", "blk"), None),
        P(None, ("head", "blk")),
        P(),
        P(),
        P(("head", "blk"), None),
        P(("head", "blk"), None),
        P(("head", "blk"), None),
        P(("head", "blk"), None),
        P(("head", "blk"), None),
        P(("head", "blk"), None),
        P(None, ("head", "blk"), None),
    )
    return jax.shard_map(
        blocked if fits else general,
        mesh=mesh,
        in_specs=placed,
        out_specs=(
            P(None, ("head", "blk"), None),
            P(None, ("head", "blk"), None),
            P(("head", "blk"), None),
            P(("head", "blk"), None),
            P(("head", "blk"), None),
            P(("head", "blk"), None),
            P(("head", "blk"), None),
            P(("head", "blk"), None),
        ),
        check_vma=False,
    )
```

```python
import math

import jax
import jax.numpy as jnp
from jax import lax
from jax.experimental import pallas as pl
from jax.experimental.pallas import tpu as pltpu
from jax.sharding import PartitionSpec as P

HEADS = 16
HEAD_DIM = 64


NORM_EPSILON = 1e-05
PRECISE = lax.Precision.HIGHEST
START_TOP = -1e30
SCORE_SCALE = 0.125


def shifted(value, axis, steps):
    count = lax.axis_size(axis)
    pairs = [(source, (source + steps) % count) for source in range(count)]
    return lax.ppermute(value, axis, pairs)


def layer_norm(value, scale):
    centered = value - jnp.mean(value, axis=-1, keepdims=True)
    variance = jnp.mean(centered * centered, axis=-1, keepdims=True)
    return centered * lax.rsqrt(variance + NORM_EPSILON) * scale


def rotate(value, cosine_table, sine_table):
    half_dim = value.shape[-1] // 2
    first_half = value[..., :half_dim]
    second_half = value[..., half_dim:]
    return jnp.concatenate(
        [
            first_half * cosine_table - second_half * sine_table,
            second_half * cosine_table + first_half * sine_table,
        ],
        axis=-1,
    )


def rotary_tables(positions, head_dim):
    half_dim = head_dim // 2
    frequency = 10000.0 ** (-jnp.arange(half_dim, dtype=jnp.float32) / half_dim)
    turned = positions.astype(jnp.float32)[:, :, None, None] * frequency
    return (jnp.cos(turned), jnp.sin(turned))


def contract_rows(left, right):
    return lax.dot_general(
        left, right, (((0,), (0,)), ((), ())), preferred_element_type=jnp.float32
    )


def contract_cols(left, right):
    return lax.dot_general(
        left, right, (((1,), (1,)), ((), ())), preferred_element_type=jnp.float32
    )


def attend_step(running, query_block, key_block, value_block):
    row_top, row_sum, accum = running
    scores = (
        jnp.einsum("sqhd,skhd->sqhk", query_block, key_block, preferred_element_type=jnp.float32)
        * SCORE_SCALE
    )
    new_top = jnp.maximum(row_top, jnp.max(scores, axis=-1))
    shrink = jnp.exp(row_top - new_top)
    weights = jnp.exp(scores - new_top[..., None])
    row_sum = row_sum * shrink + jnp.sum(weights, axis=-1)
    accum = accum * shrink[..., None] + jnp.einsum(
        "sqhk,skhd->sqhd",
        weights.astype(jnp.bfloat16),
        value_block,
        preferred_element_type=jnp.float32,
    )
    return (new_top, row_sum, accum)


def back_step(query_block, key_block, value_block, grad_block, log_total, delta):
    scores = (
        jnp.einsum("sqhd,skhd->sqhk", query_block, key_block, preferred_element_type=jnp.float32)
        * SCORE_SCALE
    )
    probs = jnp.exp(scores - log_total[..., None])
    grad_values = jnp.einsum(
        "sqhk,sqhd->skhd",
        probs.astype(jnp.bfloat16),
        grad_block,
        preferred_element_type=jnp.float32,
    )
    grad_probs = jnp.einsum(
        "sqhd,skhd->sqhk", grad_block, value_block, preferred_element_type=jnp.float32
    )
    grad_scores = (probs * (grad_probs - delta[..., None])).astype(jnp.bfloat16)
    grad_query = jnp.einsum(
        "sqhk,skhd->sqhd", grad_scores, key_block, preferred_element_type=jnp.float32
    )
    grad_keys = jnp.einsum(
        "sqhk,sqhd->skhd", grad_scores, query_block, preferred_element_type=jnp.float32
    )
    return (grad_query, grad_keys, grad_values)


def general(
    tokens,
    positions,
    time_index,
    time_table,
    w_qkv,
    w_out,
    w_up,
    w_down,
    scale_attn,
    scale_mlp,
    cotangent,
):
    seq_count, row_count, model_width = tokens.shape
    group_count = lax.axis_size("head")
    local_heads = HEADS // group_count
    feature_width = local_heads * HEAD_DIM
    flat_rows = seq_count * row_count
    gathered = (
        lax.all_gather(w_qkv, ("head", "blk"), axis=0, tiled=True),
        lax.all_gather(w_out, ("head", "blk"), axis=0, tiled=True),
        lax.all_gather(w_up, ("head", "blk"), axis=0, tiled=True),
        lax.all_gather(w_down, ("head", "blk"), axis=0, tiled=True),
        lax.all_gather(scale_attn, ("head", "blk"), axis=0, tiled=True),
        lax.all_gather(scale_mlp, ("head", "blk"), axis=0, tiled=True),
    )
    full_qkv, full_out, full_up, full_down, full_scale_attn, full_scale_mlp = gathered
    step_count = time_table.shape[0]
    picker = (time_index[:, None] == jnp.arange(step_count, dtype=jnp.int32)[None, :]).astype(
        jnp.float32
    )
    time_embed = jnp.dot(picker, time_table, precision=PRECISE)
    scale_one = 1.0 + jnp.dot(time_embed, full_scale_attn.astype(jnp.float32), precision=PRECISE)
    scale_two = 1.0 + jnp.dot(time_embed, full_scale_mlp.astype(jnp.float32), precision=PRECISE)
    token_float = tokens.astype(jnp.float32)
    normed = (
        layer_norm(token_float, scale_one[:, None, :])
        .astype(jnp.bfloat16)
        .reshape(flat_rows, model_width)
    )
    projected = jnp.dot(normed, full_qkv, preferred_element_type=jnp.float32).reshape(
        seq_count, row_count, 3, HEADS, HEAD_DIM
    )
    cosine_table, sine_table = rotary_tables(positions, HEAD_DIM)
    query_tok = rotate(projected[:, :, 0], cosine_table, sine_table)
    keys_tok = rotate(projected[:, :, 1], cosine_table, sine_table)
    packed = (
        jnp.stack([query_tok, keys_tok, projected[:, :, 2]], axis=2)
        .reshape(seq_count, row_count, 3, model_width)
        .astype(jnp.bfloat16)
    )
    regrouped = lax.all_to_all(packed, "head", split_axis=3, concat_axis=1, tiled=True)
    block_len = regrouped.shape[1]
    local_query = regrouped[:, :, 0].reshape(seq_count, block_len, local_heads, HEAD_DIM)
    local_keys = regrouped[:, :, 1]
    local_values = regrouped[:, :, 2]
    start_state = (
        jnp.full((seq_count, block_len, local_heads), START_TOP, jnp.float32),
        jnp.zeros((seq_count, block_len, local_heads), jnp.float32),
        jnp.zeros((seq_count, block_len, local_heads, HEAD_DIM), jnp.float32),
    )
    key_piece = lax.all_gather(local_keys, "blk", axis=1, tiled=True)
    value_piece = lax.all_gather(local_values, "blk", axis=1, tiled=True)
    piece_len = key_piece.shape[1]
    step_len = math.gcd(piece_len, block_len)

    def one_block(index, state):
        key_block = lax.dynamic_slice_in_dim(key_piece, index * step_len, step_len, 1).reshape(
            seq_count, step_len, local_heads, HEAD_DIM
        )
        value_block = lax.dynamic_slice_in_dim(value_piece, index * step_len, step_len, 1).reshape(
            seq_count, step_len, local_heads, HEAD_DIM
        )
        return attend_step(state, local_query, key_block, value_block)

    row_top, row_sum, accum = lax.fori_loop(0, piece_len // step_len, one_block, start_state)
    mixed = accum / row_sum[..., None]
    log_total = row_top + jnp.log(row_sum)
    attended_heads = mixed.astype(jnp.bfloat16).reshape(seq_count, block_len, feature_width)
    attended = lax.all_to_all(
        attended_heads, "head", split_axis=1, concat_axis=2, tiled=True
    ).reshape(flat_rows, model_width)
    branch = jnp.dot(attended, full_out, preferred_element_type=jnp.float32)
    middle = token_float + branch.reshape(seq_count, row_count, model_width)
    normed_two = (
        layer_norm(middle, scale_two[:, None, :])
        .astype(jnp.bfloat16)
        .reshape(flat_rows, model_width)
    )
    hidden = jnp.dot(normed_two, full_up, preferred_element_type=jnp.float32)
    active = jax.nn.gelu(hidden, approximate=False).astype(jnp.bfloat16)
    result = middle.reshape(flat_rows, model_width) + jnp.dot(
        active, full_down, preferred_element_type=jnp.float32
    )
    output = result.astype(jnp.bfloat16).reshape(seq_count, row_count, model_width)
    back_qkv, back_out, back_up, back_down = (
        lax.all_gather(w_qkv, ("head", "blk"), axis=0, tiled=True),
        lax.all_gather(w_out, ("head", "blk"), axis=0, tiled=True),
        lax.all_gather(w_up, ("head", "blk"), axis=0, tiled=True),
        lax.all_gather(w_down, ("head", "blk"), axis=0, tiled=True),
    )
    grad_out = cotangent.reshape(flat_rows, model_width)
    grad_active = contract_cols(grad_out, back_down)
    grad_w_down = contract_rows(active, grad_out)
    gelu_value, gelu_pull = jax.vjp(lambda entry: jax.nn.gelu(entry, approximate=False), hidden)
    grad_hidden = gelu_pull(grad_active)[0].astype(jnp.bfloat16)
    grad_w_up = contract_rows(normed_two, grad_hidden)
    grad_normed_two = contract_cols(grad_hidden, back_up).reshape(seq_count, row_count, model_width)
    norm_value, norm_pull = jax.vjp(layer_norm, middle, scale_two[:, None, :])
    grad_middle_norm, grad_scale_two = norm_pull(grad_normed_two)
    grad_middle = cotangent.astype(jnp.float32) + grad_middle_norm
    grad_scale_mlp = jnp.dot(time_embed.T, grad_scale_two[:, 0, :], precision=PRECISE)
    grad_branch = grad_middle.reshape(flat_rows, model_width).astype(jnp.bfloat16)
    grad_w_out = contract_rows(attended, grad_branch)
    grad_attended = (
        contract_cols(grad_branch, back_out)
        .astype(jnp.bfloat16)
        .reshape(seq_count, row_count, model_width)
    )
    grad_heads = lax.all_to_all(
        grad_attended, "head", split_axis=2, concat_axis=1, tiled=True
    ).reshape(seq_count, block_len, local_heads, HEAD_DIM)
    delta = jnp.sum(grad_heads.astype(jnp.float32) * mixed, axis=-1)

    def turn(index, state):
        key_now, value_now, grad_keys_now, grad_values_now, grad_query_sum = state
        grad_query, grad_keys, grad_values = back_step(
            local_query,
            key_now.reshape(seq_count, block_len, local_heads, HEAD_DIM),
            value_now.reshape(seq_count, block_len, local_heads, HEAD_DIM),
            grad_heads,
            log_total,
            delta,
        )
        moved_keys, moved_values = shifted((key_now, value_now), "blk", 1)
        moved_grad_keys, moved_grad_values = (
            shifted(
                (grad_keys_now + grad_keys.reshape(seq_count, block_len, feature_width)).astype(
                    jnp.bfloat16
                ),
                "blk",
                1,
            ).astype(jnp.float32),
            shifted(
                (grad_values_now + grad_values.reshape(seq_count, block_len, feature_width)).astype(
                    jnp.bfloat16
                ),
                "blk",
                1,
            ).astype(jnp.float32),
        )
        return (
            moved_keys,
            moved_values,
            moved_grad_keys,
            moved_grad_values,
            grad_query_sum + grad_query,
        )

    zero_kv = jnp.zeros((seq_count, block_len, feature_width), jnp.float32)
    begin = (
        local_keys,
        local_values,
        zero_kv,
        zero_kv,
        jnp.zeros((seq_count, block_len, local_heads, HEAD_DIM), jnp.float32),
    )
    final_state = lax.fori_loop(0, lax.axis_size("blk"), turn, begin)
    grad_keys_own = final_state[2]
    grad_values_own = final_state[3]
    grad_query_all = final_state[4]
    stacked = jnp.stack(
        [
            grad_query_all.reshape(seq_count, block_len, feature_width) * SCORE_SCALE,
            grad_keys_own * SCORE_SCALE,
            grad_values_own,
        ],
        axis=2,
    ).astype(jnp.bfloat16)
    returned = lax.all_to_all(stacked, "head", split_axis=1, concat_axis=3, tiled=True)
    grad_query_tok = (
        returned[:, :, 0].astype(jnp.float32).reshape(seq_count, row_count, HEADS, HEAD_DIM)
    )
    grad_keys_tok = (
        returned[:, :, 1].astype(jnp.float32).reshape(seq_count, row_count, HEADS, HEAD_DIM)
    )
    grad_values_tok = (
        returned[:, :, 2].astype(jnp.float32).reshape(seq_count, row_count, HEADS, HEAD_DIM)
    )
    grad_projected = (
        jnp.stack(
            [
                rotate(grad_query_tok, cosine_table, -sine_table),
                rotate(grad_keys_tok, cosine_table, -sine_table),
                grad_values_tok,
            ],
            axis=2,
        )
        .reshape(flat_rows, 3 * model_width)
        .astype(jnp.bfloat16)
    )
    grad_w_qkv = contract_rows(normed, grad_projected)
    grad_normed = contract_cols(grad_projected, back_qkv).reshape(seq_count, row_count, model_width)
    first_value, first_pull = jax.vjp(layer_norm, token_float, scale_one[:, None, :])
    grad_token_norm, grad_scale_one = first_pull(grad_normed)
    grad_tokens = grad_middle + grad_token_norm
    grad_scale_attn = jnp.dot(time_embed.T, grad_scale_one[:, 0, :], precision=PRECISE)
    shards = (
        lax.psum_scatter(grad_w_qkv, ("head", "blk"), scatter_dimension=0, tiled=True),
        lax.psum_scatter(grad_w_out, ("head", "blk"), scatter_dimension=0, tiled=True),
        lax.psum_scatter(grad_w_up, ("head", "blk"), scatter_dimension=0, tiled=True),
        lax.psum_scatter(grad_w_down, ("head", "blk"), scatter_dimension=0, tiled=True),
        lax.psum_scatter(grad_scale_attn, ("head", "blk"), scatter_dimension=0, tiled=True),
        lax.psum_scatter(grad_scale_mlp, ("head", "blk"), scatter_dimension=0, tiled=True),
    )
    return (output, grad_tokens, shards[0], shards[1], shards[2], shards[3], shards[4], shards[5])


EPS = NORM_EPSILON
BF = jnp.bfloat16
F32 = jnp.float32


def norm_stats(value):
    centered = value - jnp.mean(value, axis=-1, keepdims=True)
    spread = lax.rsqrt(jnp.mean(centered * centered, axis=-1, keepdims=True) + EPS)
    return centered * spread, spread


def norm_back(unit, spread, grad, scale):
    scaled = grad * scale
    return spread * (
        scaled
        - jnp.mean(scaled, axis=-1, keepdims=True)
        - unit * jnp.mean(scaled * unit, axis=-1, keepdims=True)
    )


MESH = pl.DeviceIdType.MESH


def flip(value, bits):
    for bit in (1, 2, 4):
        if bits & bit:
            value = value + bit - 2 * bit * lax.rem(lax.div(value, bit), 2)
    return value


def greet(head, blk, heads, blks):
    barrier = pltpu.get_barrier_semaphore()
    for k in heads:
        pl.semaphore_signal(barrier, inc=1, device_id=(flip(head, k), blk), device_id_type=MESH)
    for k in blks:
        pl.semaphore_signal(barrier, inc=1, device_id=(head, flip(blk, k)), device_id_type=MESH)
    pl.semaphore_wait(barrier, len(heads) + len(blks))


def send(source, target, send_sem, recv_sem, head, blk):
    return pltpu.make_async_remote_copy(
        src_ref=source,
        dst_ref=target,
        send_sem=send_sem,
        recv_sem=recv_sem,
        device_id=(head, blk),
        device_id_type=MESH,
    )


class Swap:
    def __init__(self, head, blk, axis, source, target, sems):
        self.copies = []
        count = 4 if axis == "head" else 8
        me = head if axis == "head" else blk
        for k in range(1, count):
            peer = flip(me, k)
            where = (peer, blk) if axis == "head" else (head, peer)
            self.copies.append(
                send(source(peer), target(me), sems.at[0, k], sems.at[1, k], *where)
            )

    def start(self):
        for copy in self.copies:
            copy.start()

    def arrive(self):
        for copy in self.copies:
            copy.wait_recv()

    def drain(self):
        for copy in self.copies:
            copy.wait_send()


class Plane:
    def __init__(self, head, blk, own, slot, sems):
        sibling = flip(blk, 1)
        self.first = [send(own, slot(blk), sems.at[0, 0], sems.at[1, 0], head, sibling)]
        self.passed = []
        for i, k in enumerate((2, 4, 6)):
            peer = flip(blk, k)
            self.first.append(
                send(own, slot(blk), sems.at[0, i + 1], sems.at[1, i + 1], head, peer)
            )
            self.passed.append(
                send(slot(peer), slot(peer), sems.at[0, i + 4], sems.at[1, i + 4], head, sibling)
            )

    def start(self):
        for i in (3, 1, 2, 0):
            self.first[i].start()

    def forward(self, i):
        self.first[i + 1].wait_recv()
        self.passed[i].start()

    def arrive(self, i):
        if i < 0:
            self.first[0].wait_recv()
        else:
            self.passed[i].wait_recv()

    def finish(self):
        for i in range(3):
            self.forward(i)
        for i in range(-1, 3):
            self.arrive(i)

    def drain(self):
        for copy in self.first + self.passed:
            copy.wait_send()


def line_order(head, step):
    low = jnp.minimum(head, 3 - head)
    swap = low * ((step == 0).astype(jnp.int32) - (step == 1).astype(jnp.int32))
    at = step + swap
    return jnp.where(head < 2, at, 3 - at)


class Line:
    def __init__(self, head, blk, own, slot, sems):
        self.head, self.blk, self.own, self.slot, self.sems = head, blk, own, slot, sems

    def copy(self, source, at, up, k):
        head = self.head
        target = jnp.where(up, head + 1, head - 1)
        way = jnp.where(up, 0, 1)
        return send(
            source, self.slot(at), self.sems.at[0, way, k], self.sems.at[1, way, k], target, self.blk
        )

    def start(self):
        head = self.head

        @pl.when(head < 3)
        def _():
            self.copy(self.own, head, True, 0).start()

        @pl.when(head > 0)
        def _():
            self.copy(self.own, head, False, 0).start()

    def step(self, at):
        head = self.head
        up = at < head
        k = jnp.where(up, head - 1 - at, at - head - 1)
        self.copy(self.slot(at), at, up, k).wait_recv()

        @pl.when(jnp.where(up, head < 3, head > 0))
        def _():
            self.copy(self.slot(at), at, up, k + 1).start()

    def hop(self, k):
        head = self.head

        @pl.when(head >= k)
        def _():
            self.step(head - k)

        @pl.when(head + k <= 3)
        def _():
            self.step(head + k)

    def drain(self):
        head = self.head
        for k in range(3):

            @pl.when(jnp.logical_and(head < 3, head >= k))
            def _():
                self.copy(self.own, head, True, k).wait_send()

            @pl.when(jnp.logical_and(head > 0, head + k <= 3))
            def _():
                self.copy(self.own, head, False, k).wait_send()


class Reach:
    def __init__(self, head, blk, own, slot, sems):
        self.head, self.blk, self.own, self.slot, self.sems = head, blk, own, slot, sems
        self.middle = jnp.logical_and(head > 0, head < 3)

    def copy(self, k):
        peer = flip(self.head, k)
        return send(
            self.own, self.slot(self.head), self.sems.at[0, k], self.sems.at[1, k], peer, self.blk
        )

    def passed(self):
        at = self.slot(flip(self.head, 2))
        return send(at, at, self.sems.at[0, 0], self.sems.at[1, 3], flip(self.head, 1), self.blk)

    def start(self):
        self.copy(2).start()
        self.copy(1).start()

        @pl.when(self.middle)
        def _():
            self.copy(3).start()

    def forward(self):
        self.copy(2).wait_recv()

        @pl.when(self.middle)
        def _():
            self.passed().start()

    def arrive(self):
        self.copy(1).wait_recv()
        self.copy(3).wait_recv()

    def drain(self):
        self.copy(1).wait_send()
        self.copy(2).wait_send()

        @pl.when(self.middle)
        def _():
            self.copy(3).wait_send()
            self.passed().wait_send()


class Fold:
    def __init__(self, head, blk, terms, via, joined, into, sems):
        self.head, self.blk, self.sems = head, blk, sems
        self.terms, self.via, self.joined, self.into = terms, via, joined, into
        self.middle = jnp.logical_and(head > 0, head < 3)

    def copy(self, k):
        peer = flip(self.head, k)
        return send(
            self.terms.at[peer],
            self.into.at[k],
            self.sems.at[0, k],
            self.sems.at[1, k],
            peer,
            self.blk,
        )

    def handed(self):
        return send(
            self.terms.at[flip(self.head, 3)],
            self.via,
            self.sems.at[0, 0],
            self.sems.at[1, 0],
            flip(self.head, 1),
            self.blk,
        )

    def relayed(self):
        return send(
            self.joined,
            self.into.at[2],
            self.sems.at[0, 2],
            self.sems.at[1, 2],
            flip(self.head, 2),
            self.blk,
        )

    def start_far(self):
        @pl.when(jnp.logical_not(self.middle))
        def _():
            self.handed().start()

    def start_one(self, k):
        if k == 1:
            self.copy(1).start()
        elif k == 2:

            @pl.when(jnp.logical_not(self.middle))
            def _():
                self.copy(2).start()

        else:

            @pl.when(self.middle)
            def _():
                self.copy(3).start()

    def start(self):
        self.start_far()
        for k in (2, 3, 1):
            self.start_one(k)

    def relay(self):
        @pl.when(self.middle)
        def _():
            self.handed().wait_recv()
            mine = self.terms[flip(self.head, 2)].astype(F32)
            self.joined[...] = (mine + self.via[...].astype(F32)).astype(BF)
            self.relayed().start()

    def arrive(self):
        self.copy(1).wait_recv()
        self.copy(2).wait_recv()

        @pl.when(self.middle)
        def _():
            self.copy(3).wait_recv()

        @pl.when(jnp.logical_not(self.middle))
        def _():
            self.into[3] = jnp.zeros_like(self.into[3])

        self.into[0] = self.terms[self.head]

    def drain(self):
        self.copy(1).wait_send()

        @pl.when(self.middle)
        def _():
            self.copy(3).wait_send()
            self.relayed().wait_send()

        @pl.when(jnp.logical_not(self.middle))
        def _():
            self.copy(2).wait_send()
            self.handed().wait_send()


def half_lane(shape):
    return lax.broadcasted_iota(jnp.int32, shape, 1) < 64


def lane_swap(value):
    lane = lax.broadcasted_iota(jnp.int32, value.shape, 1)
    return jnp.where(
        lax.rem(lane, 64) < 32, pltpu.roll(value, 96, 1), pltpu.roll(value, 32, 1)
    )


def turn_tables(table, sign):
    lane = lax.broadcasted_iota(jnp.int32, table.shape, 1)
    cosine = jnp.where(lane < 32, table, 0.0)
    cosine = cosine + pltpu.roll(cosine, 32, 1)
    sine = jnp.where(jnp.logical_and(lane >= 32, lane < 64), table, 0.0) * sign
    sine = sine - pltpu.roll(sine, 96, 1)
    both = (cosine + pltpu.roll(cosine, 64, 1), sine + pltpu.roll(sine, 64, 1))
    return both, (jnp.where(lane < 64, cosine, 1.0), sine)


def join_halves(top, bottom, right):
    left = half_lane(top.shape)
    if right:
        return jnp.where(left, pltpu.roll(top, 64, 1), bottom)
    return jnp.where(left, top, pltpu.roll(bottom, 64, 1))


EXP_SCALE = SCORE_SCALE * math.log2(math.e)
KEYS = 256


def flip_by(head, k):
    low, high = lax.rem(k, 2), lax.div(k, 2)
    value = head + low - 2 * low * lax.rem(head, 2)
    return value + 2 * high - 4 * high * lax.div(head, 2)


class Everyone:
    def __init__(self, head, blk, source, target, sems):
        self.head, self.blk, self.source, self.target, self.sems = head, blk, source, target, sems
        self.peers = [flip(blk, k) for k in range(8)]

    def copy(self, kz, k):
        z = flip_by(self.head, jnp.int32(kz))
        return self.copy_to(z, kz, k)

    def copy_to(self, z, kz, k):
        b = self.peers[k]
        return send(
            self.source(z, b),
            self.target(self.head, self.blk),
            self.sems.at[0, kz, k],
            self.sems.at[1, kz, k],
            z,
            b,
        )

    def start(self, kz):
        z = flip_by(self.head, jnp.int32(kz))

        @pl.when(kz > 0)
        def _():
            self.copy_to(z, kz, 0).start()

        for k in range(1, 8):
            self.copy_to(z, kz, k).start()

    def arrive(self, kz):
        z = flip_by(self.head, jnp.int32(kz))

        @pl.when(kz > 0)
        def _():
            self.copy_to(z, kz, 0).wait_recv()

        for k in range(1, 8):
            self.copy_to(z, kz, k).wait_recv()

    def drain(self):
        for kz in range(4):
            for k in range(1 if kz == 0 else 0, 8):
                self.copy(kz, k).wait_send()


def greet_all(head, blk):
    barrier = pltpu.get_barrier_semaphore()
    for kz in range(4):
        for k in range(8):
            if kz or k:
                pl.semaphore_signal(
                    barrier, inc=1, device_id=(flip(head, kz), flip(blk, k)), device_id_type=MESH
                )
    pl.semaphore_wait(barrier, 31)


def group_rows(value):
    return jnp.sum(value.reshape(value.shape[0] // 8, 8, value.shape[1]), axis=0)


VMEM_LIMIT = 61 << 20


class Scatter:
    def __init__(self, head, blk, terms, near, joined, far, sems):
        self.head, self.blk, self.core = head, blk, lax.rem(blk, 2)
        self.terms, self.near, self.joined, self.far, self.sems = terms, near, joined, far, sems

    def halves(self):
        return send(
            self.terms.at[:, :, 1 - self.core],
            self.near,
            self.sems.at[0, 0],
            self.sems.at[1, 0],
            self.head,
            flip(self.blk, 1),
        )

    def chips(self, i):
        peer = flip(self.blk, 2 * i)
        return send(
            self.joined.at[lax.div(peer, 2)],
            self.far.at[i],
            self.sems.at[0, i],
            self.sems.at[1, i],
            self.head,
            peer,
        )

    def start(self):
        self.halves().start()

    def join(self):
        self.halves().wait_recv()
        for chip in range(4):
            mine = self.terms[:, chip, pl.ds(self.core, 1)].astype(F32)
            mine = mine.reshape(mine.shape[0], *mine.shape[2:])
            self.joined[chip] = (mine + self.near[:, chip].astype(F32)).astype(BF)
        for i in (3, 1, 2):
            self.chips(i).start()

    def total(self):
        value = self.joined[lax.div(self.blk, 2)].astype(F32)
        for i in range(1, 4):
            self.chips(i).wait_recv()
            value = value + self.far[i].astype(F32)
        return value

    def drain(self):
        self.halves().wait_send()
        for i in range(1, 4):
            self.chips(i).wait_send()


def sum_four(parts):
    return (parts[0].astype(F32) + parts[1].astype(F32)) + (
        parts[2].astype(F32) + parts[3].astype(F32)
    )


def layer_kernel(
    tok, pos, freq, w_qkv, ttab, sca, scm, w_up, out_own, down_own, cot_own, tix,
    output, grad_tokens, g_qkv, g_out, g_up, g_down, grad_attn, grad_mlp,
    tab, wqp, upp, gq, up_own,
    tiles, normed, wq, scales, tabg, tokg, mixed, lse, grad_rx, grad_middle, middle, outq, grad_down,
    grad_up, grad_out, sums, wqz, turned, part, sums_in, parts, out_tiles, upz, outz, up, down, out, cots,
    kvt, scores, att, received, attended, n2g, act, gh, pairs, prx, gsend, gin, tsend, branch, queries,
    grads, queries_t, grads_t, stats, keyt, dkv, dqt, bsend, back, oin, din, dvia, djoin, uin, uvia, ujoin,
    usum, near, joined, far, osum, zin, gp, gnp, gvia, gjoin, gin_r, terms, near_q, joined_q, far_q, osum_q,
    part_r, sums_in_r, parts_r, zsem, lsem, tsem, wsem, asem, bsem, psem, usem, osem, usem2, dsem, qsem,
    csem, esem, nsem, ssem, gsem, fsem, qsem_r, dsem_r, usem_r, vsem, osem_r, xsem, bsem_r, gsem_r, osem_q,
    xsem_q, asem_r, csem_r,
):
    head, blk = lax.axis_index("head"), lax.axis_index("blk")
    core = lax.rem(blk, 2)
    for group in range(4):
        for i in range(2):
            at = 256 * group + 128 * i
            keys = w_qkv[:, 1024 + at : 1152 + at].astype(F32)
            values = w_qkv[:, 2048 + at : 2176 + at].astype(F32)
            for right in range(2):
                lanes = slice(256 * i + 128 * right, 256 * i + 128 * right + 128)
                wqp[group, :, lanes] = join_halves(keys, values, right).astype(BF)
        wqp[group, :, 512:768] = w_qkv[:, 256 * group : 256 * group + 256]
    angles = [freq[:, 0:64] * pos[seq : seq + 1, :].astype(F32) for seq in range(2)]
    tab[...] = jnp.transpose(
        jnp.concatenate([turn(angle) for angle in angles for turn in (jnp.cos, jnp.sin)], axis=0)
    )
    for i in range(8):
        for group in range(4):
            at = 128 * (8 * group + i)
            upp[i, :, 128 * group : 128 * group + 128] = w_up[:, at : at + 128]
    greet_all(head, blk)
    zswap = Swap(head, blk, "head", lambda i: wqp.at[i], lambda i: wqz.at[i], zsem)
    zswap.start()
    line = Line(head, blk, tok, lambda i: tokg.at[i], lsem)
    tline = Line(head, blk, tab, lambda i: tabg.at[i], tsem)
    tline.start()
    line.start()
    uswap = Swap(head, blk, "blk", lambda i: upp.at[i], lambda i: upz.at[i], usem)
    oline = Reach(head, blk, out_own, lambda i: outz.at[i], osem)
    uline = Line(head, blk, upz, lambda i: up.at[i], usem2)
    dline = Line(head, blk, down_own, lambda i: down.at[i], dsem)
    oplane = Plane(head, blk, outz, lambda i: out.at[:, i], qsem)
    cplane = Plane(head, blk, cot_own, lambda i: cots.at[i], csem)
    everyone = Everyone(head, blk, lambda z, b: att.at[z, b], lambda z, b: received.at[z, b], esem)
    backward = Everyone(head, blk, lambda z, b: tsend.at[z, b], lambda z, b: grad_rx.at[z, b], fsem)
    turned[...] = jnp.transpose(ttab[...])
    rows = turned[pl.ds(pl.multiple_of((head * 8 + blk) * 8, 8), 8), :]
    step_lane = lax.broadcasted_iota(jnp.int32, rows.shape, 1)
    pieces = []
    for weight in (sca, scm):
        for seq in range(2):
            column = jnp.sum(jnp.where(step_lane == tix[seq], rows, 0.0), axis=1, keepdims=True)
            pieces.append(jnp.sum(column * weight[...].astype(F32), axis=0, keepdims=True))
    part[...] = jnp.concatenate(pieces + [jnp.zeros((4, 1024), F32)], axis=0)
    one = Swap(head, blk, "blk", lambda i: part, lambda i: sums_in.at[i], asem)
    one.start()
    uswap.start()
    sums_in[blk] = part[...]
    wqz[head] = wqp[head]
    tokg[head] = tok[...]
    tabg[head] = tab[...]
    upz[blk] = upp[blk]
    outz[head] = out_own[...]
    down[head] = down_own[...]
    cots[blk] = cot_own[...]
    one.arrive()
    total = sums_in[0]
    for i in range(1, 8):
        total = total + sums_in[i]
    parts[head] = total
    two = Swap(head, blk, "head", lambda i: parts.at[head], lambda i: parts.at[i], bsem)
    two.start()
    zswap.arrive()
    plane = Plane(head, blk, wqz, lambda i: wq.at[:, i], wsem)
    plane.start()
    wq[:, pl.ds(blk, 1)] = wqz[...].reshape(4, 1, 32, 768)
    two.arrive()
    total = 1.0 + ((parts[0] + parts[1]) + (parts[2] + parts[3]))
    scales[...] = total

    def gather(step, carry):
        at = line_order(head, step)

        @pl.when(step > 0)
        def _():
            tline.step(at)
            line.step(at)

        for seq in range(2):
            unit, _ = norm_stats(tokg[at, seq].astype(F32))
            normed[at, pl.ds(64 * seq, 64), :] = (unit * scales[seq : seq + 1, :]).astype(BF)
        return carry

    def project(step, carry):
        at = line_order(head, step)
        proj = jnp.dot(
            normed[at], wq[...].reshape(1024, 768), preferred_element_type=F32
        )
        for seq in range(2):
            table = tabg[at]
            if seq:
                table = pltpu.roll(table, 64, 1)
            both, keyed = turn_tables(table, 1.0)
            mine = proj[64 * seq : 64 * seq + 64]
            for j in range(4):
                kv = mine[:, 128 * j : 128 * j + 128]
                kv = kv * keyed[0] + lane_swap(kv) * keyed[1]
                out_tiles[4 * seq + j, at, 0:64, :] = kv.astype(BF)
            for i in range(2):
                query = mine[:, 512 + 128 * i : 640 + 128 * i]
                query = query * both[0] + lane_swap(query) * both[1]
                for right in range(2):
                    packed = join_halves(query[:32], query[32:], right)
                    out_tiles[4 * seq + 2 * i + right, at, 64:96, :] = packed.astype(BF)
        move(at).start()
        tiles[at, blk] = out_tiles[blk, at]
        return carry

    def move(at):
        return Swap(
            head, blk, "blk", lambda i: out_tiles.at[i, at], lambda i: tiles.at[at, i], psem.at[at]
        )

    lax.fori_loop(0, 3, gather, 0)
    oline.start()
    plane.finish()
    lax.fori_loop(0, 3, project, 0)

    def last(step, carry):
        gather(step, carry)
        return project(step, carry)

    lax.fori_loop(3, 4, last, 0)
    uswap.arrive()
    up[head] = upz[...]
    uline.start()
    oline.forward()
    oline.arrive()
    out[:, pl.ds(blk, 1)] = outz[...].reshape(4, 1, 32, 1024)
    for at in range(4):
        move(at).arrive()
    oplane.start()
    uline.hop(1)
    dline.start()
    kvt[...] = jnp.transpose(tiles[:, :, 0:64, :].reshape(2048, 128))

    def attend(step, carry):
        z = flip_by(head, 3 - step)
        flat = jnp.transpose(tiles[z, :, 64:96, :].reshape(256, 128).astype(F32))
        blank = jnp.zeros((64, 256), F32)
        results = []
        for side in range(2):
            query = jnp.concatenate([flat[64 * side : 64 * side + 64], blank], axis=0).astype(BF)
            top = None
            for c in range(2048 // KEYS):
                keys = tiles[c // 2, 4 * (c % 2) : 4 * (c % 2) + 4, 0:64, :].reshape(KEYS, 128)
                part = jnp.dot(keys, query, preferred_element_type=F32)
                scores[c] = part
                peak = jnp.max(part.reshape(KEYS // 8, 8, 256), axis=0)
                top = peak if top is None else jnp.maximum(top, peak)
            top = jnp.max(top, axis=0, keepdims=True)
            total = jnp.zeros((8, 256), F32)
            mix = jnp.zeros((64, 256), F32)
            for c in range(2048 // KEYS):
                weights = jnp.exp2((scores[c] - top) * EXP_SCALE)
                total = total + group_rows(weights)
                mix = mix + jnp.dot(
                    kvt[64:128, KEYS * c : KEYS * c + KEYS],
                    weights.astype(BF),
                    preferred_element_type=F32,
                )
            total = jnp.sum(total, axis=0, keepdims=True)
            mix = mix / total
            mixed[z, 64 * side : 64 * side + 64, :] = mix
            lse[z, side : side + 1, :] = top * SCORE_SCALE + jnp.log(total)
            results.append(mix)
        both = jnp.transpose(jnp.concatenate(results, axis=0))
        att[z] = both.astype(BF).reshape(8, 32, 128)
        everyone.start(3 - step)

        @pl.when(step == 2)
        def _():
            uline.hop(2)
            dline.hop(1)
            for i in range(3):
                oplane.forward(i)
            cplane.start()

        return carry

    lse[...] = jnp.zeros_like(lse)
    lax.fori_loop(0, 4, attend, 0)
    received[head, blk] = att[head, blk]
    for i in range(-1, 3):
        oplane.arrive(i)
    middle[...] = tok[...].astype(F32).reshape(128, 1024)
    for kz in range(4):
        group = flip(head, kz)
        everyone.arrive(kz)
        for seq in range(2):
            for i in range(2):
                first = received[group, 4 * seq + 2 * i].astype(F32)
                second = received[group, 4 * seq + 2 * i + 1].astype(F32)
                lanes = slice(128 * i, 128 * i + 128)
                for right in range(2):
                    at = slice(64 * seq + 32 * right, 64 * seq + 32 * right + 32)
                    attended[group, at, lanes] = join_halves(first, second, right).astype(BF)
        middle[...] += jnp.dot(
            attended[group], out[group].reshape(256, 1024), preferred_element_type=F32
        )
    for seq in range(2):
        rows = slice(64 * seq, 64 * seq + 64)
        unit, _ = norm_stats(middle[rows, :])
        n2g[blk, rows, :] = (unit * scales[2 + seq : 3 + seq, :]).astype(BF)
    nplane = Plane(head, blk, n2g.at[blk], lambda i: n2g.at[i], nsem)
    for i in (1, 2, 0):
        nplane.first[i].start()
    uline.hop(3)
    dline.hop(2)
    nplane.first[3].start()
    cplane.finish()
    dline.hop(3)
    sibling = flip(blk, 1)

    def halves(i):
        return [
            send(pairs.at[w, i, 1 - core], prx.at[w, i], ssem.at[0, w, i], ssem.at[1, w, i], head, sibling)
            for w in range(2)
        ]

    def onward(i):
        peer = flip(blk, 2 * i)
        return send(gsend.at[i], gin.at[i], gsem.at[0, i], gsem.at[1, i], head, peer)

    def reduce(i):
        chip = lax.div(flip(blk, 2 * i), 2)
        for copy in halves(i):
            copy.wait_recv()
        gsend[i] = (pairs[0, i, core].astype(F32) + prx[0, i].astype(F32)).astype(BF)
        if i:
            onward(i).start()
        outq[chip] = (pairs[1, i, core].astype(F32) + prx[1, i].astype(F32)).astype(BF)

    for i in range(4):
        chip = lax.div(flip(blk, 2 * i), 2)
        if i == 0:
            nplane.arrive(-1)
        else:
            nplane.forward(i - 1)
            if i > 1:
                reduce(i - 1)
            nplane.arrive(i - 1)
        at = pl.ds(2 * chip, 2)
        rows = n2g[at].reshape(256, 1024)
        hidden = jnp.dot(rows, up[...].reshape(1024, 512), preferred_element_type=F32)
        grad_active = contract_cols(cots[at].reshape(256, 1024), down[...].reshape(512, 1024))
        cdf = 0.5 * (1.0 + lax.erf(hidden * math.sqrt(0.5)))
        active = (hidden * cdf).astype(BF)
        slope = cdf + hidden * jnp.exp(-0.5 * hidden * hidden) * (1.0 / math.sqrt(2 * math.pi))
        grad_hidden = (grad_active * slope).astype(BF)
        act[at] = active.reshape(2, 128, 512)
        gh[at] = grad_hidden.reshape(2, 128, 512)
        pairs[0, i] = (
            contract_cols(grad_hidden, up[...].reshape(1024, 512)).astype(BF).reshape(2, 128, 1024)
        )
        pairs[1, i] = (
            jnp.dot(active, down[...].reshape(512, 1024), preferred_element_type=F32)
            .astype(BF)
            .reshape(2, 128, 1024)
        )
        for copy in halves(i):
            copy.start()
    reduce(3)
    reduce(0)
    for group in range(4):
        lanes = slice(128 * group, 128 * group + 128)
        grad_down[group] = contract_rows(
            act[:, :, lanes].reshape(1024, 128), cots[...].reshape(1024, 1024)
        ).astype(BF)
    for group in range(4):
        lanes = slice(256 * group, 256 * group + 256)
        value = contract_rows(n2g[:, :, lanes].reshape(1024, 256), gh[...].reshape(1024, 512))
        grad_up[group] = value.astype(BF).reshape(8, 32, 512)
    uswap_r = Fold(head, blk, grad_up, uvia, ujoin, uin, usem_r)
    dfold = Fold(head, blk, grad_down, dvia, djoin, din, dsem_r)
    folds = (uswap_r, dfold)
    for fold in folds:
        fold.start_far()
        fold.start_one(3)

        @pl.when(fold.middle)
        def _():
            fold.copy(1).start()

    for i in range(1, 4):
        onward(i).wait_recv()
    sums[...] = jnp.zeros_like(sums)
    for seq in range(2):
        rows = slice(64 * seq, 64 * seq + 64)
        grad = gsend[0, rows, :].astype(F32)
        for i in range(1, 4):
            grad = grad + gin[i, rows, :].astype(F32)
        unit, spread = norm_stats(middle[rows, :])
        whole_grad = cots[blk, rows, :].astype(F32) + norm_back(
            unit, spread, grad, scales[2 + seq : 3 + seq, :]
        )
        grad_middle[rows, :] = whole_grad
        branch[rows, :] = whole_grad.astype(BF)
        sums[seq : seq + 1, :] = jnp.sum(grad * unit, axis=0, keepdims=True)

    def give(step, carry):
        group = flip_by(head, 3 - step)
        value = contract_cols(branch[...], out[group].reshape(256, 1024))
        for seq in range(2):
            for i in range(2):
                lanes = slice(128 * i, 128 * i + 128)
                top = value[64 * seq : 64 * seq + 32, lanes]
                bottom = value[64 * seq + 32 : 64 * seq + 64, lanes]
                for right in range(2):
                    tsend[group, 4 * seq + 2 * i + right] = join_halves(top, bottom, right).astype(BF)
        backward.start(3 - step)
        return carry

    lax.fori_loop(0, 4, give, 0)
    grad_rx[head, blk] = tsend[head, blk]
    for group in range(4):
        value = contract_rows(attended[group], branch[...])
        grad_out[group] = value.astype(BF).reshape(4, 2, 32, 1024)
    scatter = Scatter(head, blk, grad_out, near, joined, far, osem_r)
    scatter.start()
    outs = []
    for i in range(1, 4):
        peer = flip(blk, 2 * i)
        outs.append(
            send(outq.at[lax.div(peer, 2)], oin.at[i], qsem_r.at[0, i], qsem_r.at[1, i], head, peer)
        )
    vswap = Swap(head, blk, "blk", lambda i: usum.at[i], lambda i: up_own.at[i], vsem)
    xswap = Swap(head, blk, "head", lambda i: osum.at[i], lambda i: zin.at[i], xsem)
    left = half_lane((256, 128))
    keyt[...] = jnp.transpose(tiles[:, :, 0:64, :].reshape(2048, 128))[:64]

    def prepare(z, carry):
        flat = tiles[z, :, 64:96, :].reshape(256, 128).astype(F32)
        grad = grad_rx[z].reshape(256, 128).astype(F32)
        product = jnp.transpose(grad) * mixed[z]
        queries[2 * z] = jnp.where(left, flat, 0.0).astype(BF)
        queries[2 * z + 1] = jnp.where(left, pltpu.roll(flat, 64, 1), 0.0).astype(BF)
        turned = jnp.transpose(flat)
        slopes = jnp.transpose(grad)
        blank = jnp.zeros((64, 256), F32)
        for side in range(2):
            rows = slice(64 * side, 64 * side + 64)
            queries_t[2 * z + side] = jnp.concatenate([turned[rows], blank], axis=0).astype(BF)
            grads_t[2 * z + side] = jnp.concatenate([blank, slopes[rows]], axis=0).astype(BF)
        grads[2 * z] = jnp.where(left, 0.0, pltpu.roll(grad, 64, 1)).astype(BF)
        grads[2 * z + 1] = jnp.where(left, 0.0, grad).astype(BF)
        for side in range(2):
            delta = jnp.sum(product[64 * side : 64 * side + 64], axis=0, keepdims=True)
            shift = lse[z, side : side + 1, :] * math.log2(math.e)
            stats[2 * z + side] = jnp.concatenate([shift, delta, jnp.zeros((6, 256), F32)], axis=0)
        return carry

    def ready(kz, carry):
        backward.arrive(kz)
        return prepare(flip_by(head, kz), carry)

    scatter.join()
    lax.fori_loop(0, 4, ready, 0)
    dqt[...] = jnp.zeros_like(dqt)

    def kv_move(z):
        return Swap(
            head,
            blk,
            "blk",
            lambda i: bsend.at[i, z, pl.ds(0, 64)],
            lambda i: back.at[i, z, pl.ds(0, 64)],
            bsem_r.at[z],
        )

    def keys_step(z, carry):
        dkv[...] = jnp.zeros_like(dkv)

        def query_step(q, inner):
            query, grad = queries[q], grads[q]
            query_t, grad_t = queries_t[q], grads_t[q]
            shift, delta = stats[q, 0:1, :], stats[q, 1:2, :]
            dq = dqt[q]
            for c in range(2):
                keys = tiles[z, 4 * c : 4 * c + 4, 0:64, :].reshape(256, 128)
                probs = jnp.dot(keys, query_t, preferred_element_type=F32)
                probs = jnp.exp2(probs * EXP_SCALE - shift)
                slopes = jnp.dot(keys, grad_t, preferred_element_type=F32)
                slopes = (probs * (slopes - delta)).astype(BF)
                dkv[c] += jnp.dot(slopes, query, preferred_element_type=F32) + jnp.dot(
                    probs.astype(BF), grad, preferred_element_type=F32
                )
                at = pl.ds(pl.multiple_of(512 * z + 256 * c, 256), 256)
                dq = dq + jnp.dot(keyt[:, at], slopes, preferred_element_type=F32)
            dqt[q] = dq
            return inner

        lax.fori_loop(0, 8, query_step, 0)
        scale = jnp.where(left, SCORE_SCALE, 1.0)
        for c in range(2):
            bsend[4 * c : 4 * c + 4, pl.ds(z, 1), 0:64, :] = (
                (dkv[c] * scale).astype(BF).reshape(4, 1, 64, 128)
            )
        kv_move(z).start()

        @pl.when(z == 0)
        def _():
            for fold in folds:
                fold.start_one(2)

        @pl.when(z == 1)
        def _():
            for fold in folds:
                fold.relay()
            for copy in outs:
                copy.start()

        @pl.when(z == 2)
        def _():
            for fold in folds:

                @pl.when(jnp.logical_not(fold.middle))
                def _():
                    fold.copy(1).start()

            osum[...] = scatter.total().astype(BF)
            xswap.start()
            zin[head] = osum[head]

        return carry

    lax.fori_loop(0, 4, keys_step, 0)
    for z in range(4):
        both = jnp.concatenate([dqt[2 * z], dqt[2 * z + 1]], axis=0)
        both = (jnp.transpose(both) * SCORE_SCALE).astype(BF)
        bsend[:, z, 64:96, :] = both.reshape(8, 32, 128)
    qmove = Swap(
        head,
        blk,
        "blk",
        lambda i: bsend.at[i, :, pl.ds(64, 32)],
        lambda i: back.at[i, :, pl.ds(64, 32)],
        bsem_r.at[4],
    )
    qmove.start()
    back[blk] = bsend[blk]
    picked = turned[pl.ds(pl.multiple_of((head * 8 + blk) * 8, 8), 8), :]
    step_lane = lax.broadcasted_iota(jnp.int32, picked.shape, 1)
    columns = [
        jnp.sum(jnp.where(step_lane == tix[seq], picked, 0.0), axis=1, keepdims=True)
        for seq in range(2)
    ]
    for z in range(4):
        kv_move(z).arrive()
    qmove.arrive()
    gswap = Fold(head, blk, gnp, gvia, gjoin, gin_r, gsem_r)

    def unturn(step, carry):
        at = flip(head, step)
        for seq in range(2):
            table = tabg[at]
            if seq:
                table = pltpu.roll(table, 64, 1)
            both, keyed = turn_tables(table, -1.0)
            rows = slice(64 * seq, 64 * seq + 64)
            for j in range(4):
                kv = back[4 * seq + j, at, 0:64, :].astype(F32)
                kv = kv * keyed[0] + lane_swap(kv) * keyed[1]
                gp[at, rows, 128 * j : 128 * j + 128] = kv.astype(BF)
            for i in range(2):
                first = back[4 * seq + 2 * i, at, 64:96, :].astype(F32)
                second = back[4 * seq + 2 * i + 1, at, 64:96, :].astype(F32)
                query = jnp.concatenate(
                    [join_halves(first, second, 0), join_halves(first, second, 1)], axis=0
                )
                query = query * both[0] + lane_swap(query) * both[1]
                gp[at, rows, 512 + 128 * i : 640 + 128 * i] = query.astype(BF)
        gnp[at] = contract_cols(gp[at], wq[...].reshape(1024, 768)).astype(BF)
        return carry

    for step in (3, 2, 1, 0):
        unturn(step, 0)
        if step == 3:
            gswap.start_far()
            gswap.start_one(3)
    for group in range(4):
        lanes = slice(256 * group, 256 * group + 256)
        value = contract_rows(normed[:, :, lanes].reshape(512, 256), gp[...].reshape(512, 768))
        terms[group] = value.astype(BF).reshape(4, 2, 32, 768)
    scatter_q = Scatter(head, blk, terms, near_q, joined_q, far_q, osem_q)
    scatter_q.start()
    part_r[...] = jnp.concatenate(
        [jnp.zeros((2, 1024), F32), sums[0:2, :], jnp.zeros((4, 1024), F32)], axis=0
    )

    def gather_r(at, carry):
        for seq in range(2):
            unit, _ = norm_stats(tokg[at, seq].astype(F32))
            part_r[seq : seq + 1, :] += jnp.sum(
                gnp[at, pl.ds(64 * seq, 64), :].astype(F32) * unit, axis=0, keepdims=True
            )
        return carry

    lax.fori_loop(0, 4, gather_r, 0)
    one_r = Swap(head, blk, "blk", lambda i: part_r, lambda i: sums_in_r.at[i], asem_r)
    one_r.start()
    sums_in_r[blk] = part_r[...]
    gswap.start_one(2)
    gswap.relay()
    gswap.start_one(1)
    scatter_q.join()
    uswap_r.arrive()
    usum[...] = sum_four(uin).astype(BF)
    vswap.start()
    up_own[blk] = usum[blk]
    one_r.arrive()
    total = sums_in_r[0]
    for i in range(1, 8):
        total = total + sums_in_r[i]
    parts_r[head] = total
    two_r = Swap(head, blk, "head", lambda i: parts_r.at[head], lambda i: parts_r.at[i], csem_r)
    two_r.start()
    total = middle[...] + outq[lax.div(blk, 2)].astype(F32)
    for i in range(1, 4):
        outs[i - 1].wait_recv()
        total = total + oin[i].astype(F32)
    output[...] = total.astype(BF)
    dfold.arrive()
    g_down[...] = sum_four(din)
    osum_q[...] = scatter_q.total().astype(BF)
    xswap_q = Swap(head, blk, "head", lambda i: osum_q.at[i], lambda i: gq.at[i], xsem_q)
    xswap_q.start()
    gq[head] = osum_q[head]
    xswap.arrive()
    g_out[...] = sum_four(zin)
    two_r.arrive()
    total = (parts_r[0] + parts_r[1]) + (parts_r[2] + parts_r[3])
    grad_attn[...] = columns[0] * total[0:1] + columns[1] * total[1:2]
    grad_mlp[...] = columns[0] * total[2:3] + columns[1] * total[3:4]
    gswap.arrive()
    for seq in range(2):
        rows = slice(64 * seq, 64 * seq + 64)
        grad = sum_four([gin_r[i, rows, :] for i in range(4)])
        unit, spread = norm_stats(tokg[head, seq].astype(F32))
        grad_tokens[rows, :] = grad_middle[rows, :] + norm_back(
            unit, spread, grad, scales[seq : seq + 1, :]
        )
    vswap.arrive()
    for i in range(8):
        for group in range(4):
            at = 128 * (8 * group + i)
            g_up[:, at : at + 128] = up_own[i, :, 128 * group : 128 * group + 128].astype(F32)
    xswap_q.arrive()
    for group in range(4):
        for i in range(2):
            first = gq[group, :, 256 * i : 256 * i + 128].astype(F32)
            second = gq[group, :, 256 * i + 128 : 256 * i + 256].astype(F32)
            at = 256 * group + 128 * i
            for right in range(2):
                lanes = slice(1024 + 1024 * right + at, 1152 + 1024 * right + at)
                g_qkv[:, lanes] = join_halves(first, second, right)
        g_qkv[:, 256 * group : 256 * group + 256] = gq[group, :, 512:768].astype(F32)
    for z in range(4):
        kv_move(z).drain()
    for copy in outs:
        copy.wait_send()
    for copies in (
        scatter, uswap_r, dfold, vswap, xswap, qmove, gswap, scatter_q, xswap_q, one_r, two_r
    ):
        copies.drain()
    for at in range(4):
        move(at).drain()
    for i in range(4):
        for copy in halves(i):
            copy.wait_send()
        if i:
            onward(i).wait_send()
    for copies in (
        zswap, line, tline, plane, one, two, uswap, oline,
        uline, dline, oplane, cplane, everyone, nplane, backward,
    ):
        copies.drain()


def whole(count):
    return [pl.BlockSpec(memory_space=pltpu.VMEM)] * count


def layer(*operands):
    dma = pltpu.SemaphoreType.DMA
    shape = jax.ShapeDtypeStruct
    return pl.pallas_call(
        layer_kernel,
        out_shape=(
            shape((128, 1024), BF),
            shape((128, 1024), F32),
            shape((32, 3072), F32),
            shape((32, 1024), F32),
            shape((32, 4096), F32),
            shape((128, 1024), F32),
            shape((8, 1024), F32),
            shape((8, 1024), F32),
        ),
        in_specs=whole(11) + [pl.BlockSpec(memory_space=pltpu.SMEM)],
        out_specs=whole(8),
        scratch_shapes=[
            pltpu.VMEM((64, 128), F32),
            pltpu.VMEM((4, 32, 768), BF),
            pltpu.VMEM((8, 32, 512), BF),
            pltpu.VMEM((4, 32, 768), BF),
            pltpu.VMEM((8, 32, 512), BF),
            pltpu.VMEM((4, 8, 96, 128), BF),
            pltpu.VMEM((4, 128, 1024), BF),
            pltpu.VMEM((4, 8, 32, 768), BF),
            pltpu.VMEM((8, 1024), F32),
            pltpu.VMEM((4, 64, 128), F32),
            pltpu.VMEM((4, 2, 64, 1024), BF),
            pltpu.VMEM((4, 128, 256), F32),
            pltpu.VMEM((4, 8, 256), F32),
            pltpu.VMEM((4, 8, 32, 128), BF),
            pltpu.VMEM((128, 1024), F32),
            pltpu.VMEM((128, 1024), F32),
            pltpu.VMEM((4, 128, 1024), BF),
            pltpu.VMEM((4, 128, 1024), BF),
            pltpu.VMEM((4, 8, 32, 512), BF),
            pltpu.VMEM((4, 4, 2, 32, 1024), BF),
            pltpu.VMEM((8, 1024), F32),
            pltpu.VMEM((4, 32, 768), BF),
            pltpu.VMEM((256, 64), F32),
            pltpu.VMEM((8, 1024), F32),
            pltpu.VMEM((8, 8, 1024), F32),
            pltpu.VMEM((4, 8, 1024), F32),
            pltpu.VMEM((8, 4, 96, 128), BF),
            pltpu.VMEM((8, 32, 512), BF),
            pltpu.VMEM((4, 32, 1024), BF),
            pltpu.VMEM((4, 8, 32, 512), BF),
            pltpu.VMEM((4, 128, 1024), BF),
            pltpu.VMEM((4, 8, 32, 1024), BF),
            pltpu.VMEM((8, 128, 1024), BF),
            pltpu.VMEM((128, 2048), BF),
            pltpu.VMEM((2048 // KEYS, KEYS, 256), F32),
            pltpu.VMEM((4, 8, 32, 128), BF),
            pltpu.VMEM((4, 8, 32, 128), BF),
            pltpu.VMEM((4, 128, 256), BF),
            pltpu.VMEM((8, 128, 1024), BF),
            pltpu.VMEM((8, 128, 512), BF),
            pltpu.VMEM((8, 128, 512), BF),
            pltpu.VMEM((2, 4, 2, 128, 1024), BF),
            pltpu.VMEM((2, 4, 128, 1024), BF),
            pltpu.VMEM((4, 128, 1024), BF),
            pltpu.VMEM((4, 128, 1024), BF),
            pltpu.VMEM((4, 8, 32, 128), BF),
            pltpu.VMEM((128, 1024), BF),
            pltpu.VMEM((8, 256, 128), BF),
            pltpu.VMEM((8, 256, 128), BF),
            pltpu.VMEM((8, 128, 256), BF),
            pltpu.VMEM((8, 128, 256), BF),
            pltpu.VMEM((8, 8, 256), F32),
            pltpu.VMEM((64, 2048), BF),
            pltpu.VMEM((2, 256, 128), F32),
            pltpu.VMEM((8, 64, 256), F32),
            pltpu.VMEM((8, 4, 96, 128), BF),
            pltpu.VMEM((8, 4, 96, 128), BF),
            pltpu.VMEM((4, 128, 1024), BF),
            pltpu.VMEM((4, 128, 1024), BF),
            pltpu.VMEM((128, 1024), BF),
            pltpu.VMEM((128, 1024), BF),
            pltpu.VMEM((4, 8, 32, 512), BF),
            pltpu.VMEM((8, 32, 512), BF),
            pltpu.VMEM((8, 32, 512), BF),
            pltpu.VMEM((8, 32, 512), BF),
            pltpu.VMEM((4, 4, 32, 1024), BF),
            pltpu.VMEM((4, 4, 32, 1024), BF),
            pltpu.VMEM((4, 4, 32, 1024), BF),
            pltpu.VMEM((4, 32, 1024), BF),
            pltpu.VMEM((4, 32, 1024), BF),
            pltpu.VMEM((4, 128, 768), BF),
            pltpu.VMEM((4, 128, 1024), BF),
            pltpu.VMEM((128, 1024), BF),
            pltpu.VMEM((128, 1024), BF),
            pltpu.VMEM((4, 128, 1024), BF),
            pltpu.VMEM((4, 4, 2, 32, 768), BF),
            pltpu.VMEM((4, 4, 32, 768), BF),
            pltpu.VMEM((4, 4, 32, 768), BF),
            pltpu.VMEM((4, 4, 32, 768), BF),
            pltpu.VMEM((4, 32, 768), BF),
            pltpu.VMEM((8, 1024), F32),
            pltpu.VMEM((8, 8, 1024), F32),
            pltpu.VMEM((4, 8, 1024), F32),
            dma((2, 4)),
            dma((2, 2, 3)),
            dma((2, 2, 3)),
            dma((2, 7)),
            dma((2, 8)),
            dma((2, 4)),
            dma((4, 2, 8)),
            dma((2, 8)),
            dma((2, 4)),
            dma((2, 2, 3)),
            dma((2, 2, 3)),
            dma((2, 7)),
            dma((2, 7)),
            dma((2, 4, 8)),
            dma((2, 7)),
            dma((2, 2, 4)),
            dma((2, 4)),
            dma((2, 4, 8)),
            dma((2, 4)),
            dma((2, 4)),
            dma((2, 4)),
            dma((2, 8)),
            dma((2, 4)),
            dma((2, 4)),
            dma((5, 2, 8)),
            dma((2, 4)),
            dma((2, 4)),
            dma((2, 4)),
            dma((2, 8)),
            dma((2, 4)),
        ],
        compiler_params=pltpu.CompilerParams(
            collective_id=0, has_side_effects=True, vmem_limit_bytes=VMEM_LIMIT
        ),
        name="layer",
    )(*operands)


def finish_kernel(*refs):
    count = (len(refs) - 1) // 3
    sems = refs[-1]
    arrive = [
        pltpu.make_async_copy(refs[i], refs[2 * count + i], sems.at[0, i]) for i in range(count)
    ]
    leave = [
        pltpu.make_async_copy(refs[2 * count + i], refs[count + i], sems.at[1, i])
        for i in range(count)
    ]
    for copy in arrive:
        copy.start()
    for i in range(count):
        arrive[i].wait()
        leave[i].start()
    for copy in leave:
        copy.wait()


def finish(results):
    spec = [pl.BlockSpec(memory_space=pl.ANY)] * len(results)
    return pl.pallas_call(
        finish_kernel,
        out_shape=tuple(jax.ShapeDtypeStruct(x.shape, x.dtype) for x in results),
        in_specs=spec,
        out_specs=spec,
        scratch_shapes=[pltpu.VMEM(x.shape, x.dtype) for x in results]
        + [pltpu.SemaphoreType.DMA((2, len(results)))],
        name="finish",
    )(*results)


def blocked(
    tokens,
    positions,
    time_index,
    time_table,
    w_qkv,
    w_out,
    w_up,
    w_down,
    scale_attn,
    scale_mlp,
    cotangent,
):
    half_dim = HEAD_DIM // 2
    frequency = 10000.0 ** (-jnp.arange(half_dim, dtype=jnp.float32) / half_dim)
    results = layer(
        tokens,
        positions,
        jnp.broadcast_to(frequency[:, None], (half_dim, 128)),
        w_qkv,
        time_table,
        scale_attn,
        scale_mlp,
        w_up,
        w_out,
        w_down,
        cotangent.reshape(128, 1024),
        time_index,
    )
    output, grad_tokens, *others = finish(results)
    return (output.reshape(2, 64, 1024), grad_tokens.reshape(2, 64, 1024), *others)


def solution(mesh):
    fits = mesh.shape["head"] == 4 and mesh.shape["blk"] == 8
    placed = (
        P(None, ("head", "blk"), None),
        P(None, ("head", "blk")),
        P(),
        P(),
        P(("head", "blk"), None),
        P(("head", "blk"), None),
        P(("head", "blk"), None),
        P(("head", "blk"), None),
        P(("head", "blk"), None),
        P(("head", "blk"), None),
        P(None, ("head", "blk"), None),
    )
    return jax.shard_map(
        blocked if fits else general,
        mesh=mesh,
        in_specs=placed,
        out_specs=(
            P(None, ("head", "blk"), None),
            P(None, ("head", "blk"), None),
            P(("head", "blk"), None),
            P(("head", "blk"), None),
            P(("head", "blk"), None),
            P(("head", "blk"), None),
            P(("head", "blk"), None),
            P(("head", "blk"), None),
        ),
        check_vma=False,
    )
```

```python
import math

import jax
import jax.numpy as jnp
from jax import lax
from jax.experimental import pallas as pl
from jax.experimental.pallas import tpu as pltpu
from jax.sharding import PartitionSpec as P

HEADS = 16
HEAD_DIM = 64


NORM_EPSILON = 1e-05
PRECISE = lax.Precision.HIGHEST
START_TOP = -1e30
SCORE_SCALE = 0.125


def shifted(value, axis, steps):
    count = lax.axis_size(axis)
    pairs = [(source, (source + steps) % count) for source in range(count)]
    return lax.ppermute(value, axis, pairs)


def layer_norm(value, scale):
    centered = value - jnp.mean(value, axis=-1, keepdims=True)
    variance = jnp.mean(centered * centered, axis=-1, keepdims=True)
    return centered * lax.rsqrt(variance + NORM_EPSILON) * scale


def rotate(value, cosine_table, sine_table):
    half_dim = value.shape[-1] // 2
    first_half = value[..., :half_dim]
    second_half = value[..., half_dim:]
    return jnp.concatenate(
        [
            first_half * cosine_table - second_half * sine_table,
            second_half * cosine_table + first_half * sine_table,
        ],
        axis=-1,
    )


def rotary_tables(positions, head_dim):
    half_dim = head_dim // 2
    frequency = 10000.0 ** (-jnp.arange(half_dim, dtype=jnp.float32) / half_dim)
    turned = positions.astype(jnp.float32)[:, :, None, None] * frequency
    return (jnp.cos(turned), jnp.sin(turned))


def contract_rows(left, right):
    return lax.dot_general(
        left, right, (((0,), (0,)), ((), ())), preferred_element_type=jnp.float32
    )


def contract_cols(left, right):
    return lax.dot_general(
        left, right, (((1,), (1,)), ((), ())), preferred_element_type=jnp.float32
    )


def attend_step(running, query_block, key_block, value_block):
    row_top, row_sum, accum = running
    scores = (
        jnp.einsum("sqhd,skhd->sqhk", query_block, key_block, preferred_element_type=jnp.float32)
        * SCORE_SCALE
    )
    new_top = jnp.maximum(row_top, jnp.max(scores, axis=-1))
    shrink = jnp.exp(row_top - new_top)
    weights = jnp.exp(scores - new_top[..., None])
    row_sum = row_sum * shrink + jnp.sum(weights, axis=-1)
    accum = accum * shrink[..., None] + jnp.einsum(
        "sqhk,skhd->sqhd",
        weights.astype(jnp.bfloat16),
        value_block,
        preferred_element_type=jnp.float32,
    )
    return (new_top, row_sum, accum)


def back_step(query_block, key_block, value_block, grad_block, log_total, delta):
    scores = (
        jnp.einsum("sqhd,skhd->sqhk", query_block, key_block, preferred_element_type=jnp.float32)
        * SCORE_SCALE
    )
    probs = jnp.exp(scores - log_total[..., None])
    grad_values = jnp.einsum(
        "sqhk,sqhd->skhd",
        probs.astype(jnp.bfloat16),
        grad_block,
        preferred_element_type=jnp.float32,
    )
    grad_probs = jnp.einsum(
        "sqhd,skhd->sqhk", grad_block, value_block, preferred_element_type=jnp.float32
    )
    grad_scores = (probs * (grad_probs - delta[..., None])).astype(jnp.bfloat16)
    grad_query = jnp.einsum(
        "sqhk,skhd->sqhd", grad_scores, key_block, preferred_element_type=jnp.float32
    )
    grad_keys = jnp.einsum(
        "sqhk,sqhd->skhd", grad_scores, query_block, preferred_element_type=jnp.float32
    )
    return (grad_query, grad_keys, grad_values)


def general(
    tokens,
    positions,
    time_index,
    time_table,
    w_qkv,
    w_out,
    w_up,
    w_down,
    scale_attn,
    scale_mlp,
    cotangent,
):
    seq_count, row_count, model_width = tokens.shape
    group_count = lax.axis_size("head")
    local_heads = HEADS // group_count
    feature_width = local_heads * HEAD_DIM
    flat_rows = seq_count * row_count
    gathered = (
        lax.all_gather(w_qkv, ("head", "blk"), axis=0, tiled=True),
        lax.all_gather(w_out, ("head", "blk"), axis=0, tiled=True),
        lax.all_gather(w_up, ("head", "blk"), axis=0, tiled=True),
        lax.all_gather(w_down, ("head", "blk"), axis=0, tiled=True),
        lax.all_gather(scale_attn, ("head", "blk"), axis=0, tiled=True),
        lax.all_gather(scale_mlp, ("head", "blk"), axis=0, tiled=True),
    )
    full_qkv, full_out, full_up, full_down, full_scale_attn, full_scale_mlp = gathered
    step_count = time_table.shape[0]
    picker = (time_index[:, None] == jnp.arange(step_count, dtype=jnp.int32)[None, :]).astype(
        jnp.float32
    )
    time_embed = jnp.dot(picker, time_table, precision=PRECISE)
    scale_one = 1.0 + jnp.dot(time_embed, full_scale_attn.astype(jnp.float32), precision=PRECISE)
    scale_two = 1.0 + jnp.dot(time_embed, full_scale_mlp.astype(jnp.float32), precision=PRECISE)
    token_float = tokens.astype(jnp.float32)
    normed = (
        layer_norm(token_float, scale_one[:, None, :])
        .astype(jnp.bfloat16)
        .reshape(flat_rows, model_width)
    )
    projected = jnp.dot(normed, full_qkv, preferred_element_type=jnp.float32).reshape(
        seq_count, row_count, 3, HEADS, HEAD_DIM
    )
    cosine_table, sine_table = rotary_tables(positions, HEAD_DIM)
    query_tok = rotate(projected[:, :, 0], cosine_table, sine_table)
    keys_tok = rotate(projected[:, :, 1], cosine_table, sine_table)
    packed = (
        jnp.stack([query_tok, keys_tok, projected[:, :, 2]], axis=2)
        .reshape(seq_count, row_count, 3, model_width)
        .astype(jnp.bfloat16)
    )
    regrouped = lax.all_to_all(packed, "head", split_axis=3, concat_axis=1, tiled=True)
    block_len = regrouped.shape[1]
    local_query = regrouped[:, :, 0].reshape(seq_count, block_len, local_heads, HEAD_DIM)
    local_keys = regrouped[:, :, 1]
    local_values = regrouped[:, :, 2]
    start_state = (
        jnp.full((seq_count, block_len, local_heads), START_TOP, jnp.float32),
        jnp.zeros((seq_count, block_len, local_heads), jnp.float32),
        jnp.zeros((seq_count, block_len, local_heads, HEAD_DIM), jnp.float32),
    )
    key_piece = lax.all_gather(local_keys, "blk", axis=1, tiled=True)
    value_piece = lax.all_gather(local_values, "blk", axis=1, tiled=True)
    piece_len = key_piece.shape[1]
    step_len = math.gcd(piece_len, block_len)

    def one_block(index, state):
        key_block = lax.dynamic_slice_in_dim(key_piece, index * step_len, step_len, 1).reshape(
            seq_count, step_len, local_heads, HEAD_DIM
        )
        value_block = lax.dynamic_slice_in_dim(value_piece, index * step_len, step_len, 1).reshape(
            seq_count, step_len, local_heads, HEAD_DIM
        )
        return attend_step(state, local_query, key_block, value_block)

    row_top, row_sum, accum = lax.fori_loop(0, piece_len // step_len, one_block, start_state)
    mixed = accum / row_sum[..., None]
    log_total = row_top + jnp.log(row_sum)
    attended_heads = mixed.astype(jnp.bfloat16).reshape(seq_count, block_len, feature_width)
    attended = lax.all_to_all(
        attended_heads, "head", split_axis=1, concat_axis=2, tiled=True
    ).reshape(flat_rows, model_width)
    branch = jnp.dot(attended, full_out, preferred_element_type=jnp.float32)
    middle = token_float + branch.reshape(seq_count, row_count, model_width)
    normed_two = (
        layer_norm(middle, scale_two[:, None, :])
        .astype(jnp.bfloat16)
        .reshape(flat_rows, model_width)
    )
    hidden = jnp.dot(normed_two, full_up, preferred_element_type=jnp.float32)
    active = jax.nn.gelu(hidden, approximate=False).astype(jnp.bfloat16)
    result = middle.reshape(flat_rows, model_width) + jnp.dot(
        active, full_down, preferred_element_type=jnp.float32
    )
    output = result.astype(jnp.bfloat16).reshape(seq_count, row_count, model_width)
    back_qkv, back_out, back_up, back_down = (
        lax.all_gather(w_qkv, ("head", "blk"), axis=0, tiled=True),
        lax.all_gather(w_out, ("head", "blk"), axis=0, tiled=True),
        lax.all_gather(w_up, ("head", "blk"), axis=0, tiled=True),
        lax.all_gather(w_down, ("head", "blk"), axis=0, tiled=True),
    )
    grad_out = cotangent.reshape(flat_rows, model_width)
    grad_active = contract_cols(grad_out, back_down)
    grad_w_down = contract_rows(active, grad_out)
    gelu_value, gelu_pull = jax.vjp(lambda entry: jax.nn.gelu(entry, approximate=False), hidden)
    grad_hidden = gelu_pull(grad_active)[0].astype(jnp.bfloat16)
    grad_w_up = contract_rows(normed_two, grad_hidden)
    grad_normed_two = contract_cols(grad_hidden, back_up).reshape(seq_count, row_count, model_width)
    norm_value, norm_pull = jax.vjp(layer_norm, middle, scale_two[:, None, :])
    grad_middle_norm, grad_scale_two = norm_pull(grad_normed_two)
    grad_middle = cotangent.astype(jnp.float32) + grad_middle_norm
    grad_scale_mlp = jnp.dot(time_embed.T, grad_scale_two[:, 0, :], precision=PRECISE)
    grad_branch = grad_middle.reshape(flat_rows, model_width).astype(jnp.bfloat16)
    grad_w_out = contract_rows(attended, grad_branch)
    grad_attended = (
        contract_cols(grad_branch, back_out)
        .astype(jnp.bfloat16)
        .reshape(seq_count, row_count, model_width)
    )
    grad_heads = lax.all_to_all(
        grad_attended, "head", split_axis=2, concat_axis=1, tiled=True
    ).reshape(seq_count, block_len, local_heads, HEAD_DIM)
    delta = jnp.sum(grad_heads.astype(jnp.float32) * mixed, axis=-1)

    def turn(index, state):
        key_now, value_now, grad_keys_now, grad_values_now, grad_query_sum = state
        grad_query, grad_keys, grad_values = back_step(
            local_query,
            key_now.reshape(seq_count, block_len, local_heads, HEAD_DIM),
            value_now.reshape(seq_count, block_len, local_heads, HEAD_DIM),
            grad_heads,
            log_total,
            delta,
        )
        moved_keys, moved_values = shifted((key_now, value_now), "blk", 1)
        moved_grad_keys, moved_grad_values = (
            shifted(
                (grad_keys_now + grad_keys.reshape(seq_count, block_len, feature_width)).astype(
                    jnp.bfloat16
                ),
                "blk",
                1,
            ).astype(jnp.float32),
            shifted(
                (grad_values_now + grad_values.reshape(seq_count, block_len, feature_width)).astype(
                    jnp.bfloat16
                ),
                "blk",
                1,
            ).astype(jnp.float32),
        )
        return (
            moved_keys,
            moved_values,
            moved_grad_keys,
            moved_grad_values,
            grad_query_sum + grad_query,
        )

    zero_kv = jnp.zeros((seq_count, block_len, feature_width), jnp.float32)
    begin = (
        local_keys,
        local_values,
        zero_kv,
        zero_kv,
        jnp.zeros((seq_count, block_len, local_heads, HEAD_DIM), jnp.float32),
    )
    final_state = lax.fori_loop(0, lax.axis_size("blk"), turn, begin)
    grad_keys_own = final_state[2]
    grad_values_own = final_state[3]
    grad_query_all = final_state[4]
    stacked = jnp.stack(
        [
            grad_query_all.reshape(seq_count, block_len, feature_width) * SCORE_SCALE,
            grad_keys_own * SCORE_SCALE,
            grad_values_own,
        ],
        axis=2,
    ).astype(jnp.bfloat16)
    returned = lax.all_to_all(stacked, "head", split_axis=1, concat_axis=3, tiled=True)
    grad_query_tok = (
        returned[:, :, 0].astype(jnp.float32).reshape(seq_count, row_count, HEADS, HEAD_DIM)
    )
    grad_keys_tok = (
        returned[:, :, 1].astype(jnp.float32).reshape(seq_count, row_count, HEADS, HEAD_DIM)
    )
    grad_values_tok = (
        returned[:, :, 2].astype(jnp.float32).reshape(seq_count, row_count, HEADS, HEAD_DIM)
    )
    grad_projected = (
        jnp.stack(
            [
                rotate(grad_query_tok, cosine_table, -sine_table),
                rotate(grad_keys_tok, cosine_table, -sine_table),
                grad_values_tok,
            ],
            axis=2,
        )
        .reshape(flat_rows, 3 * model_width)
        .astype(jnp.bfloat16)
    )
    grad_w_qkv = contract_rows(normed, grad_projected)
    grad_normed = contract_cols(grad_projected, back_qkv).reshape(seq_count, row_count, model_width)
    first_value, first_pull = jax.vjp(layer_norm, token_float, scale_one[:, None, :])
    grad_token_norm, grad_scale_one = first_pull(grad_normed)
    grad_tokens = grad_middle + grad_token_norm
    grad_scale_attn = jnp.dot(time_embed.T, grad_scale_one[:, 0, :], precision=PRECISE)
    shards = (
        lax.psum_scatter(grad_w_qkv, ("head", "blk"), scatter_dimension=0, tiled=True),
        lax.psum_scatter(grad_w_out, ("head", "blk"), scatter_dimension=0, tiled=True),
        lax.psum_scatter(grad_w_up, ("head", "blk"), scatter_dimension=0, tiled=True),
        lax.psum_scatter(grad_w_down, ("head", "blk"), scatter_dimension=0, tiled=True),
        lax.psum_scatter(grad_scale_attn, ("head", "blk"), scatter_dimension=0, tiled=True),
        lax.psum_scatter(grad_scale_mlp, ("head", "blk"), scatter_dimension=0, tiled=True),
    )
    return (output, grad_tokens, shards[0], shards[1], shards[2], shards[3], shards[4], shards[5])


EPS = NORM_EPSILON
BF = jnp.bfloat16
F32 = jnp.float32


def norm_stats(value):
    centered = value - jnp.mean(value, axis=-1, keepdims=True)
    spread = lax.rsqrt(jnp.mean(centered * centered, axis=-1, keepdims=True) + EPS)
    return centered * spread, spread


def norm_back(unit, spread, grad, scale):
    scaled = grad * scale
    return spread * (
        scaled
        - jnp.mean(scaled, axis=-1, keepdims=True)
        - unit * jnp.mean(scaled * unit, axis=-1, keepdims=True)
    )


MESH = pl.DeviceIdType.MESH


def flip(value, bits):
    for bit in (1, 2, 4):
        if bits & bit:
            value = value + bit - 2 * bit * lax.rem(lax.div(value, bit), 2)
    return value


def greet(head, blk, heads, blks):
    barrier = pltpu.get_barrier_semaphore()
    for k in heads:
        pl.semaphore_signal(barrier, inc=1, device_id=(flip(head, k), blk), device_id_type=MESH)
    for k in blks:
        pl.semaphore_signal(barrier, inc=1, device_id=(head, flip(blk, k)), device_id_type=MESH)
    pl.semaphore_wait(barrier, len(heads) + len(blks))


def send(source, target, send_sem, recv_sem, head, blk):
    return pltpu.make_async_remote_copy(
        src_ref=source,
        dst_ref=target,
        send_sem=send_sem,
        recv_sem=recv_sem,
        device_id=(head, blk),
        device_id_type=MESH,
    )


class Swap:
    def __init__(self, head, blk, axis, source, target, sems):
        self.copies = []
        count = 4 if axis == "head" else 8
        me = head if axis == "head" else blk
        for k in range(1, count):
            peer = flip(me, k)
            where = (peer, blk) if axis == "head" else (head, peer)
            self.copies.append(
                send(source(peer), target(me), sems.at[0, k], sems.at[1, k], *where)
            )

    def start(self):
        for copy in self.copies:
            copy.start()

    def arrive(self):
        for copy in self.copies:
            copy.wait_recv()

    def drain(self):
        for copy in self.copies:
            copy.wait_send()


class Plane:
    def __init__(self, head, blk, own, slot, sems):
        sibling = flip(blk, 1)
        self.first = [send(own, slot(blk), sems.at[0, 0], sems.at[1, 0], head, sibling)]
        self.passed = []
        for i, k in enumerate((2, 4, 6)):
            peer = flip(blk, k)
            self.first.append(
                send(own, slot(blk), sems.at[0, i + 1], sems.at[1, i + 1], head, peer)
            )
            self.passed.append(
                send(slot(peer), slot(peer), sems.at[0, i + 4], sems.at[1, i + 4], head, sibling)
            )

    def start(self):
        for i in (3, 1, 2, 0):
            self.first[i].start()

    def forward(self, i):
        self.first[i + 1].wait_recv()
        self.passed[i].start()

    def arrive(self, i):
        if i < 0:
            self.first[0].wait_recv()
        else:
            self.passed[i].wait_recv()

    def finish(self):
        for i in range(3):
            self.forward(i)
        for i in range(-1, 3):
            self.arrive(i)

    def drain(self):
        for copy in self.first + self.passed:
            copy.wait_send()


class Split:
    def __init__(self, head, blk, own, slot, half, sems):
        sibling, across, along, far = (flip(blk, k) for k in (1, 2, 4, 6))

        def copy(source, target, i, peer):
            return send(source, target, sems.at[0, i], sems.at[1, i], head, peer)

        self.first = [
            copy(own, slot(blk), 0, sibling),
            copy(own, slot(blk), 1, across),
            copy(own, slot(blk), 2, along),
        ]
        self.cross = [
            copy(half(across, 1), half(across, 1), 3, along),
            copy(half(along, 0), half(along, 0), 4, across),
        ]
        self.passed = [
            copy(slot(peer), slot(peer), 5 + i, sibling)
            for i, peer in enumerate((across, along, far))
        ]

    def start(self):
        for i in (1, 2, 0):
            self.first[i].start()

    def forward(self, i):
        if i < 2:
            self.first[i + 1].wait_recv()
            self.cross[i].start()
        else:
            for copy in self.cross:
                copy.wait_recv()
        self.passed[i].start()

    def arrive(self, i):
        if i < 0:
            self.first[0].wait_recv()
        else:
            self.passed[i].wait_recv()

    def finish(self):
        for i in range(3):
            self.forward(i)
        for i in range(-1, 3):
            self.arrive(i)

    def drain(self):
        for copy in self.first + self.cross + self.passed:
            copy.wait_send()


def line_order(head, step):
    low = jnp.minimum(head, 3 - head)
    swap = low * ((step == 0).astype(jnp.int32) - (step == 1).astype(jnp.int32))
    at = step + swap
    return jnp.where(head < 2, at, 3 - at)


class Line:
    def __init__(self, head, blk, own, slot, sems):
        self.head, self.blk, self.own, self.slot, self.sems = head, blk, own, slot, sems

    def copy(self, source, at, up, k):
        head = self.head
        target = jnp.where(up, head + 1, head - 1)
        way = jnp.where(up, 0, 1)
        return send(
            source, self.slot(at), self.sems.at[0, way, k], self.sems.at[1, way, k], target, self.blk
        )

    def start(self):
        head = self.head

        @pl.when(head < 3)
        def _():
            self.copy(self.own, head, True, 0).start()

        @pl.when(head > 0)
        def _():
            self.copy(self.own, head, False, 0).start()

    def step(self, at):
        head = self.head
        up = at < head
        k = jnp.where(up, head - 1 - at, at - head - 1)
        self.copy(self.slot(at), at, up, k).wait_recv()

        @pl.when(jnp.where(up, head < 3, head > 0))
        def _():
            self.copy(self.slot(at), at, up, k + 1).start()

    def hop(self, k):
        head = self.head

        @pl.when(head >= k)
        def _():
            self.step(head - k)

        @pl.when(head + k <= 3)
        def _():
            self.step(head + k)

    def drain(self):
        head = self.head
        for k in range(3):

            @pl.when(jnp.logical_and(head < 3, head >= k))
            def _():
                self.copy(self.own, head, True, k).wait_send()

            @pl.when(jnp.logical_and(head > 0, head + k <= 3))
            def _():
                self.copy(self.own, head, False, k).wait_send()


class Reach:
    def __init__(self, head, blk, own, slot, sems):
        self.head, self.blk, self.own, self.slot, self.sems = head, blk, own, slot, sems
        self.middle = jnp.logical_and(head > 0, head < 3)

    def copy(self, k):
        peer = flip(self.head, k)
        return send(
            self.own, self.slot(self.head), self.sems.at[0, k], self.sems.at[1, k], peer, self.blk
        )

    def passed(self):
        at = self.slot(flip(self.head, 2))
        return send(at, at, self.sems.at[0, 0], self.sems.at[1, 3], flip(self.head, 1), self.blk)

    def start(self):
        self.copy(2).start()
        self.copy(1).start()

        @pl.when(self.middle)
        def _():
            self.copy(3).start()

    def forward(self):
        self.copy(2).wait_recv()

        @pl.when(self.middle)
        def _():
            self.passed().start()

    def arrive(self):
        self.copy(1).wait_recv()
        self.copy(3).wait_recv()

    def drain(self):
        self.copy(1).wait_send()
        self.copy(2).wait_send()

        @pl.when(self.middle)
        def _():
            self.copy(3).wait_send()
            self.passed().wait_send()


class Fold:
    def __init__(self, head, blk, terms, via, joined, into, sems):
        self.head, self.blk, self.sems = head, blk, sems
        self.terms, self.via, self.joined, self.into = terms, via, joined, into
        self.middle = jnp.logical_and(head > 0, head < 3)

    def copy(self, k):
        peer = flip(self.head, k)
        return send(
            self.terms.at[peer],
            self.into.at[k],
            self.sems.at[0, k],
            self.sems.at[1, k],
            peer,
            self.blk,
        )

    def handed(self):
        return send(
            self.terms.at[flip(self.head, 3)],
            self.via,
            self.sems.at[0, 0],
            self.sems.at[1, 0],
            flip(self.head, 1),
            self.blk,
        )

    def relayed(self):
        return send(
            self.joined,
            self.into.at[2],
            self.sems.at[0, 2],
            self.sems.at[1, 2],
            flip(self.head, 2),
            self.blk,
        )

    def start_far(self):
        @pl.when(jnp.logical_not(self.middle))
        def _():
            self.handed().start()

    def start_one(self, k):
        if k == 1:
            self.copy(1).start()
        elif k == 2:

            @pl.when(jnp.logical_not(self.middle))
            def _():
                self.copy(2).start()

        else:

            @pl.when(self.middle)
            def _():
                self.copy(3).start()

    def start(self):
        self.start_far()
        for k in (2, 3, 1):
            self.start_one(k)

    def relay(self):
        @pl.when(self.middle)
        def _():
            self.handed().wait_recv()
            mine = self.terms[flip(self.head, 2)].astype(F32)
            self.joined[...] = (mine + self.via[...].astype(F32)).astype(BF)
            self.relayed().start()

    def arrive(self):
        self.copy(1).wait_recv()
        self.copy(2).wait_recv()

        @pl.when(self.middle)
        def _():
            self.copy(3).wait_recv()

        @pl.when(jnp.logical_not(self.middle))
        def _():
            self.into[3] = jnp.zeros_like(self.into[3])

        self.into[0] = self.terms[self.head]

    def drain(self):
        self.copy(1).wait_send()

        @pl.when(self.middle)
        def _():
            self.copy(3).wait_send()
            self.relayed().wait_send()

        @pl.when(jnp.logical_not(self.middle))
        def _():
            self.copy(2).wait_send()
            self.handed().wait_send()


def half_lane(shape):
    return lax.broadcasted_iota(jnp.int32, shape, 1) < 64


def lane_swap(value):
    lane = lax.broadcasted_iota(jnp.int32, value.shape, 1)
    return jnp.where(
        lax.rem(lane, 64) < 32, pltpu.roll(value, 96, 1), pltpu.roll(value, 32, 1)
    )


def turn_tables(table, sign):
    lane = lax.broadcasted_iota(jnp.int32, table.shape, 1)
    cosine = jnp.where(lane < 32, table, 0.0)
    cosine = cosine + pltpu.roll(cosine, 32, 1)
    sine = jnp.where(jnp.logical_and(lane >= 32, lane < 64), table, 0.0) * sign
    sine = sine - pltpu.roll(sine, 96, 1)
    both = (cosine + pltpu.roll(cosine, 64, 1), sine + pltpu.roll(sine, 64, 1))
    return both, (jnp.where(lane < 64, cosine, 1.0), sine)


def join_halves(top, bottom, right):
    left = half_lane(top.shape)
    if right:
        return jnp.where(left, pltpu.roll(top, 64, 1), bottom)
    return jnp.where(left, top, pltpu.roll(bottom, 64, 1))


EXP_SCALE = SCORE_SCALE * math.log2(math.e)
KEYS = 256


def flip_by(head, k):
    low, high = lax.rem(k, 2), lax.div(k, 2)
    value = head + low - 2 * low * lax.rem(head, 2)
    return value + 2 * high - 4 * high * lax.div(head, 2)


class Everyone:
    def __init__(self, head, blk, source, target, sems):
        self.head, self.blk, self.source, self.target, self.sems = head, blk, source, target, sems
        self.peers = [flip(blk, k) for k in range(8)]

    def copy(self, kz, k):
        z = flip_by(self.head, jnp.int32(kz))
        return self.copy_to(z, kz, k)

    def copy_to(self, z, kz, k):
        b = self.peers[k]
        return send(
            self.source(z, b),
            self.target(self.head, self.blk),
            self.sems.at[0, kz, k],
            self.sems.at[1, kz, k],
            z,
            b,
        )

    def start(self, kz):
        z = flip_by(self.head, jnp.int32(kz))

        @pl.when(kz > 0)
        def _():
            self.copy_to(z, kz, 0).start()

        for k in range(1, 8):
            self.copy_to(z, kz, k).start()

    def arrive(self, kz):
        z = flip_by(self.head, jnp.int32(kz))

        @pl.when(kz > 0)
        def _():
            self.copy_to(z, kz, 0).wait_recv()

        for k in range(1, 8):
            self.copy_to(z, kz, k).wait_recv()

    def drain(self):
        for kz in range(4):
            for k in range(1 if kz == 0 else 0, 8):
                self.copy(kz, k).wait_send()


def greet_all(head, blk):
    barrier = pltpu.get_barrier_semaphore()
    for kz in range(4):
        for k in range(8):
            if kz or k:
                pl.semaphore_signal(
                    barrier, inc=1, device_id=(flip(head, kz), flip(blk, k)), device_id_type=MESH
                )
    pl.semaphore_wait(barrier, 31)


def group_rows(value):
    return jnp.sum(value.reshape(value.shape[0] // 8, 8, value.shape[1]), axis=0)


VMEM_LIMIT = 61 << 20


class Scatter:
    def __init__(self, head, blk, terms, near, joined, far, sems):
        self.head, self.blk, self.core = head, blk, lax.rem(blk, 2)
        self.terms, self.near, self.joined, self.far, self.sems = terms, near, joined, far, sems

    def halves(self):
        return send(
            self.terms.at[:, :, 1 - self.core],
            self.near,
            self.sems.at[0, 0],
            self.sems.at[1, 0],
            self.head,
            flip(self.blk, 1),
        )

    def chips(self, i):
        peer = flip(self.blk, 2 * i)
        return send(
            self.joined.at[lax.div(peer, 2)],
            self.far.at[i],
            self.sems.at[0, i],
            self.sems.at[1, i],
            self.head,
            peer,
        )

    def start(self):
        self.halves().start()

    def join(self):
        self.halves().wait_recv()
        for chip in range(4):
            mine = self.terms[:, chip, pl.ds(self.core, 1)].astype(F32)
            mine = mine.reshape(mine.shape[0], *mine.shape[2:])
            self.joined[chip] = (mine + self.near[:, chip].astype(F32)).astype(BF)
        for i in (3, 1, 2):
            self.chips(i).start()

    def total(self):
        value = self.joined[lax.div(self.blk, 2)].astype(F32)
        for i in range(1, 4):
            self.chips(i).wait_recv()
            value = value + self.far[i].astype(F32)
        return value

    def drain(self):
        self.halves().wait_send()
        for i in range(1, 4):
            self.chips(i).wait_send()


def sum_four(parts):
    return (parts[0].astype(F32) + parts[1].astype(F32)) + (
        parts[2].astype(F32) + parts[3].astype(F32)
    )


def layer_kernel(
    tok, pos, freq, w_qkv, ttab, sca, scm, w_up, out_own, down_own, cot_own, tix,
    output, grad_tokens, g_qkv, g_out, g_up, g_down, grad_attn, grad_mlp,
    tab, wqp, upp, gq, up_own,
    tiles, normed, wq, scales, tabg, tokg, mixed, lse, grad_rx, grad_middle, middle, outq, grad_down,
    grad_up, grad_out, sums, wqz, turned, part, sums_in, parts, out_tiles, upz, outz, up, down, out, cots,
    kvt, scores, att, received, attended, n2g, act, gh, pairs, prx, gsend, gin, tsend, branch, queries,
    grads, queries_t, grads_t, stats, keyt, dkv, dqt, bsend, back, oin, din, dvia, djoin, uin, uvia, ujoin,
    usum, near, joined, far, osum, zin, gp, gnp, gvia, gjoin, gin_r, terms, near_q, joined_q, far_q, osum_q,
    part_r, sums_in_r, parts_r, zsem, lsem, tsem, wsem, asem, bsem, psem, usem, osem, usem2, dsem, qsem,
    csem, esem, nsem, ssem, gsem, fsem, qsem_r, dsem_r, usem_r, vsem, osem_r, xsem, bsem_r, gsem_r, osem_q,
    xsem_q, asem_r, csem_r,
):
    head, blk = lax.axis_index("head"), lax.axis_index("blk")
    core = lax.rem(blk, 2)
    for group in range(4):
        for i in range(2):
            at = 256 * group + 128 * i
            keys = w_qkv[:, 1024 + at : 1152 + at].astype(F32)
            values = w_qkv[:, 2048 + at : 2176 + at].astype(F32)
            for right in range(2):
                lanes = slice(256 * i + 128 * right, 256 * i + 128 * right + 128)
                wqp[group, :, lanes] = join_halves(keys, values, right).astype(BF)
        wqp[group, :, 512:768] = w_qkv[:, 256 * group : 256 * group + 256]
    angles = [freq[:, 0:64] * pos[seq : seq + 1, :].astype(F32) for seq in range(2)]
    tab[...] = jnp.transpose(
        jnp.concatenate([turn(angle) for angle in angles for turn in (jnp.cos, jnp.sin)], axis=0)
    )
    for i in range(8):
        for group in range(4):
            at = 128 * (8 * group + i)
            upp[i, :, 128 * group : 128 * group + 128] = w_up[:, at : at + 128]
    greet_all(head, blk)
    zswap = Swap(head, blk, "head", lambda i: wqp.at[i], lambda i: wqz.at[i], zsem)
    zswap.start()
    line = Line(head, blk, tok, lambda i: tokg.at[i], lsem)
    tline = Line(head, blk, tab, lambda i: tabg.at[i], tsem)
    tline.start()
    line.start()
    uswap = Swap(head, blk, "blk", lambda i: upp.at[i], lambda i: upz.at[i], usem)
    oline = Reach(head, blk, out_own, lambda i: outz.at[i], osem)
    uline = Line(head, blk, upz, lambda i: up.at[i], usem2)
    dline = Line(head, blk, down_own, lambda i: down.at[i], dsem)
    oplane = Plane(head, blk, outz, lambda i: out.at[:, i], qsem)
    cplane = Plane(head, blk, cot_own, lambda i: cots.at[i], csem)
    everyone = Everyone(head, blk, lambda z, b: att.at[z, b], lambda z, b: received.at[z, b], esem)
    backward = Everyone(head, blk, lambda z, b: tsend.at[z, b], lambda z, b: grad_rx.at[z, b], fsem)
    turned[...] = jnp.transpose(ttab[...])
    rows = turned[pl.ds(pl.multiple_of((head * 8 + blk) * 8, 8), 8), :]
    step_lane = lax.broadcasted_iota(jnp.int32, rows.shape, 1)
    pieces = []
    for weight in (sca, scm):
        for seq in range(2):
            column = jnp.sum(jnp.where(step_lane == tix[seq], rows, 0.0), axis=1, keepdims=True)
            pieces.append(jnp.sum(column * weight[...].astype(F32), axis=0, keepdims=True))
    part[...] = jnp.concatenate(pieces + [jnp.zeros((4, 1024), F32)], axis=0)
    one = Swap(head, blk, "blk", lambda i: part, lambda i: sums_in.at[i], asem)
    one.start()
    uswap.start()
    sums_in[blk] = part[...]
    wqz[head] = wqp[head]
    tokg[head] = tok[...]
    tabg[head] = tab[...]
    upz[blk] = upp[blk]
    outz[head] = out_own[...]
    down[head] = down_own[...]
    cots[blk] = cot_own[...]
    one.arrive()
    total = sums_in[0]
    for i in range(1, 8):
        total = total + sums_in[i]
    parts[head] = total
    two = Swap(head, blk, "head", lambda i: parts.at[head], lambda i: parts.at[i], bsem)
    two.start()
    zswap.arrive()
    plane = Plane(head, blk, wqz, lambda i: wq.at[:, i], wsem)
    plane.start()
    wq[:, pl.ds(blk, 1)] = wqz[...].reshape(4, 1, 32, 768)
    two.arrive()
    total = 1.0 + ((parts[0] + parts[1]) + (parts[2] + parts[3]))
    scales[...] = total

    def gather(step, carry):
        at = line_order(head, step)

        @pl.when(step > 0)
        def _():
            tline.step(at)
            line.step(at)

        for seq in range(2):
            unit, _ = norm_stats(tokg[at, seq].astype(F32))
            normed[at, pl.ds(64 * seq, 64), :] = (unit * scales[seq : seq + 1, :]).astype(BF)
        return carry

    def project(step, carry):
        at = line_order(head, step)
        proj = jnp.dot(
            normed[at], wq[...].reshape(1024, 768), preferred_element_type=F32
        )
        for seq in range(2):
            table = tabg[at]
            if seq:
                table = pltpu.roll(table, 64, 1)
            both, keyed = turn_tables(table, 1.0)
            mine = proj[64 * seq : 64 * seq + 64]
            for j in range(4):
                kv = mine[:, 128 * j : 128 * j + 128]
                kv = kv * keyed[0] + lane_swap(kv) * keyed[1]
                out_tiles[4 * seq + j, at, 0:64, :] = kv.astype(BF)
            for i in range(2):
                query = mine[:, 512 + 128 * i : 640 + 128 * i]
                query = query * both[0] + lane_swap(query) * both[1]
                for right in range(2):
                    packed = join_halves(query[:32], query[32:], right)
                    out_tiles[4 * seq + 2 * i + right, at, 64:96, :] = packed.astype(BF)
        move(at).start()
        tiles[at, blk] = out_tiles[blk, at]
        return carry

    def move(at):
        return Swap(
            head, blk, "blk", lambda i: out_tiles.at[i, at], lambda i: tiles.at[at, i], psem.at[at]
        )

    lax.fori_loop(0, 3, gather, 0)
    oline.start()
    plane.finish()
    lax.fori_loop(0, 3, project, 0)

    def last(step, carry):
        gather(step, carry)
        return project(step, carry)

    lax.fori_loop(3, 4, last, 0)
    uswap.arrive()
    up[head] = upz[...]
    uline.start()
    oline.forward()
    oline.arrive()
    out[:, pl.ds(blk, 1)] = outz[...].reshape(4, 1, 32, 1024)
    for at in range(4):
        move(at).arrive()
    oplane.start()
    uline.hop(1)
    dline.start()
    kvt[...] = jnp.transpose(tiles[:, :, 0:64, :].reshape(2048, 128))

    def attend(step, carry):
        z = flip_by(head, 3 - step)
        flat = jnp.transpose(tiles[z, :, 64:96, :].reshape(256, 128).astype(F32))
        blank = jnp.zeros((64, 256), F32)
        results = []
        for side in range(2):
            query = jnp.concatenate([flat[64 * side : 64 * side + 64], blank], axis=0).astype(BF)
            top = None
            for c in range(2048 // KEYS):
                keys = tiles[c // 2, 4 * (c % 2) : 4 * (c % 2) + 4, 0:64, :].reshape(KEYS, 128)
                part = jnp.dot(keys, query, preferred_element_type=F32)
                scores[c] = part
                peak = jnp.max(part.reshape(KEYS // 8, 8, 256), axis=0)
                top = peak if top is None else jnp.maximum(top, peak)
            top = jnp.max(top, axis=0, keepdims=True)
            total = jnp.zeros((8, 256), F32)
            mix = jnp.zeros((64, 256), F32)
            for c in range(2048 // KEYS):
                weights = jnp.exp2((scores[c] - top) * EXP_SCALE)
                total = total + group_rows(weights)
                mix = mix + jnp.dot(
                    kvt[64:128, KEYS * c : KEYS * c + KEYS],
                    weights.astype(BF),
                    preferred_element_type=F32,
                )
            total = jnp.sum(total, axis=0, keepdims=True)
            mix = mix / total
            mixed[z, 64 * side : 64 * side + 64, :] = mix
            lse[z, side : side + 1, :] = top * SCORE_SCALE + jnp.log(total)
            results.append(mix)
        both = jnp.transpose(jnp.concatenate(results, axis=0))
        att[z] = both.astype(BF).reshape(8, 32, 128)
        everyone.start(3 - step)

        @pl.when(step == 1)
        def _():
            cplane.start()

        @pl.when(step == 2)
        def _():
            uline.hop(2)
            dline.hop(1)
            for i in range(3):
                oplane.forward(i)

        return carry

    lse[...] = jnp.zeros_like(lse)
    lax.fori_loop(0, 4, attend, 0)
    received[head, blk] = att[head, blk]
    for i in range(-1, 3):
        oplane.arrive(i)
    middle[...] = tok[...].astype(F32).reshape(128, 1024)
    for kz in range(4):
        group = flip(head, kz)
        everyone.arrive(kz)
        for seq in range(2):
            for i in range(2):
                first = received[group, 4 * seq + 2 * i].astype(F32)
                second = received[group, 4 * seq + 2 * i + 1].astype(F32)
                lanes = slice(128 * i, 128 * i + 128)
                for right in range(2):
                    at = slice(64 * seq + 32 * right, 64 * seq + 32 * right + 32)
                    attended[group, at, lanes] = join_halves(first, second, right).astype(BF)
        middle[...] += jnp.dot(
            attended[group], out[group].reshape(256, 1024), preferred_element_type=F32
        )
    for seq in range(2):
        rows = slice(64 * seq, 64 * seq + 64)
        unit, _ = norm_stats(middle[rows, :])
        n2g[blk, rows, :] = (unit * scales[2 + seq : 3 + seq, :]).astype(BF)
    nplane = Split(
        head, blk, n2g.at[blk], lambda i: n2g.at[i], lambda i, h: n2g.at[i, pl.ds(64 * h, 64)], nsem
    )
    for i in (1, 2, 0):
        nplane.first[i].start()
    uline.hop(3)
    dline.hop(2)
    cplane.finish()
    dline.hop(3)
    sibling = flip(blk, 1)

    def halves(i):
        return [
            send(pairs.at[w, i, 1 - core], prx.at[w, i], ssem.at[0, w, i], ssem.at[1, w, i], head, sibling)
            for w in range(2)
        ]

    def onward(i):
        peer = flip(blk, 2 * i)
        return send(gsend.at[i], gin.at[i], gsem.at[0, i], gsem.at[1, i], head, peer)

    def reduce(i):
        chip = lax.div(flip(blk, 2 * i), 2)
        for copy in halves(i):
            copy.wait_recv()
        gsend[i] = (pairs[0, i, core].astype(F32) + prx[0, i].astype(F32)).astype(BF)
        if i:
            onward(i).start()
        outq[chip] = (pairs[1, i, core].astype(F32) + prx[1, i].astype(F32)).astype(BF)

    for i in range(4):
        chip = lax.div(flip(blk, 2 * i), 2)
        if i == 0:
            nplane.arrive(-1)
        else:
            if i == 1:
                nplane.forward(0)
                nplane.forward(1)
            elif i == 3:
                nplane.forward(2)
            if i > 1:
                reduce(i - 1)
            nplane.arrive(i - 1)
        at = pl.ds(2 * chip, 2)
        rows = n2g[at].reshape(256, 1024)
        hidden = jnp.dot(rows, up[...].reshape(1024, 512), preferred_element_type=F32)
        grad_active = contract_cols(cots[at].reshape(256, 1024), down[...].reshape(512, 1024))
        cdf = 0.5 * (1.0 + lax.erf(hidden * math.sqrt(0.5)))
        active = (hidden * cdf).astype(BF)
        slope = cdf + hidden * jnp.exp(-0.5 * hidden * hidden) * (1.0 / math.sqrt(2 * math.pi))
        grad_hidden = (grad_active * slope).astype(BF)
        act[at] = active.reshape(2, 128, 512)
        gh[at] = grad_hidden.reshape(2, 128, 512)
        pairs[0, i] = (
            contract_cols(grad_hidden, up[...].reshape(1024, 512)).astype(BF).reshape(2, 128, 1024)
        )
        pairs[1, i] = (
            jnp.dot(active, down[...].reshape(512, 1024), preferred_element_type=F32)
            .astype(BF)
            .reshape(2, 128, 1024)
        )
        for copy in halves(i):
            copy.start()
    reduce(3)
    reduce(0)
    for group in range(4):
        lanes = slice(128 * group, 128 * group + 128)
        grad_down[group] = contract_rows(
            act[:, :, lanes].reshape(1024, 128), cots[...].reshape(1024, 1024)
        ).astype(BF)
    for group in range(4):
        lanes = slice(256 * group, 256 * group + 256)
        value = contract_rows(n2g[:, :, lanes].reshape(1024, 256), gh[...].reshape(1024, 512))
        grad_up[group] = value.astype(BF).reshape(8, 32, 512)
    uswap_r = Fold(head, blk, grad_up, uvia, ujoin, uin, usem_r)
    dfold = Fold(head, blk, grad_down, dvia, djoin, din, dsem_r)
    folds = (uswap_r, dfold)
    for fold in folds:
        fold.start_far()
        fold.start_one(3)

        @pl.when(fold.middle)
        def _():
            fold.copy(1).start()

    for i in range(1, 4):
        onward(i).wait_recv()
    sums[...] = jnp.zeros_like(sums)
    for seq in range(2):
        rows = slice(64 * seq, 64 * seq + 64)
        grad = gsend[0, rows, :].astype(F32)
        for i in range(1, 4):
            grad = grad + gin[i, rows, :].astype(F32)
        unit, spread = norm_stats(middle[rows, :])
        whole_grad = cots[blk, rows, :].astype(F32) + norm_back(
            unit, spread, grad, scales[2 + seq : 3 + seq, :]
        )
        grad_middle[rows, :] = whole_grad
        branch[rows, :] = whole_grad.astype(BF)
        sums[seq : seq + 1, :] = jnp.sum(grad * unit, axis=0, keepdims=True)

    def give(step, carry):
        group = flip_by(head, 3 - step)
        value = contract_cols(branch[...], out[group].reshape(256, 1024))
        for seq in range(2):
            for i in range(2):
                lanes = slice(128 * i, 128 * i + 128)
                top = value[64 * seq : 64 * seq + 32, lanes]
                bottom = value[64 * seq + 32 : 64 * seq + 64, lanes]
                for right in range(2):
                    tsend[group, 4 * seq + 2 * i + right] = join_halves(top, bottom, right).astype(BF)
        backward.start(3 - step)
        return carry

    lax.fori_loop(0, 4, give, 0)
    grad_rx[head, blk] = tsend[head, blk]
    for group in range(4):
        value = contract_rows(attended[group], branch[...])
        grad_out[group] = value.astype(BF).reshape(4, 2, 32, 1024)
    scatter = Scatter(head, blk, grad_out, near, joined, far, osem_r)
    scatter.start()
    outs = []
    for i in range(1, 4):
        peer = flip(blk, 2 * i)
        outs.append(
            send(outq.at[lax.div(peer, 2)], oin.at[i], qsem_r.at[0, i], qsem_r.at[1, i], head, peer)
        )
    vswap = Swap(head, blk, "blk", lambda i: usum.at[i], lambda i: up_own.at[i], vsem)
    xswap = Swap(head, blk, "head", lambda i: osum.at[i], lambda i: zin.at[i], xsem)
    left = half_lane((256, 128))
    keyt[...] = jnp.transpose(tiles[:, :, 0:64, :].reshape(2048, 128))[:64]

    def prepare(z, carry):
        flat = tiles[z, :, 64:96, :].reshape(256, 128).astype(F32)
        grad = grad_rx[z].reshape(256, 128).astype(F32)
        product = jnp.transpose(grad) * mixed[z]
        queries[2 * z] = jnp.where(left, flat, 0.0).astype(BF)
        queries[2 * z + 1] = jnp.where(left, pltpu.roll(flat, 64, 1), 0.0).astype(BF)
        turned = jnp.transpose(flat)
        slopes = jnp.transpose(grad)
        blank = jnp.zeros((64, 256), F32)
        for side in range(2):
            rows = slice(64 * side, 64 * side + 64)
            queries_t[2 * z + side] = jnp.concatenate([turned[rows], blank], axis=0).astype(BF)
            grads_t[2 * z + side] = jnp.concatenate([blank, slopes[rows]], axis=0).astype(BF)
        grads[2 * z] = jnp.where(left, 0.0, pltpu.roll(grad, 64, 1)).astype(BF)
        grads[2 * z + 1] = jnp.where(left, 0.0, grad).astype(BF)
        for side in range(2):
            delta = jnp.sum(product[64 * side : 64 * side + 64], axis=0, keepdims=True)
            shift = lse[z, side : side + 1, :] * math.log2(math.e)
            stats[2 * z + side] = jnp.concatenate([shift, delta, jnp.zeros((6, 256), F32)], axis=0)
        return carry

    def ready(kz, carry):
        backward.arrive(kz)
        return prepare(flip_by(head, kz), carry)

    scatter.join()
    lax.fori_loop(0, 4, ready, 0)
    dqt[...] = jnp.zeros_like(dqt)

    def kv_move(z):
        return Swap(
            head,
            blk,
            "blk",
            lambda i: bsend.at[i, z, pl.ds(0, 64)],
            lambda i: back.at[i, z, pl.ds(0, 64)],
            bsem_r.at[z],
        )

    def keys_step(z, carry):
        dkv[...] = jnp.zeros_like(dkv)

        def query_step(q, inner):
            query, grad = queries[q], grads[q]
            query_t, grad_t = queries_t[q], grads_t[q]
            shift, delta = stats[q, 0:1, :], stats[q, 1:2, :]
            dq = dqt[q]
            for c in range(2):
                keys = tiles[z, 4 * c : 4 * c + 4, 0:64, :].reshape(256, 128)
                probs = jnp.dot(keys, query_t, preferred_element_type=F32)
                probs = jnp.exp2(probs * EXP_SCALE - shift)
                slopes = jnp.dot(keys, grad_t, preferred_element_type=F32)
                slopes = (probs * (slopes - delta)).astype(BF)
                dkv[c] += jnp.dot(slopes, query, preferred_element_type=F32) + jnp.dot(
                    probs.astype(BF), grad, preferred_element_type=F32
                )
                at = pl.ds(pl.multiple_of(512 * z + 256 * c, 256), 256)
                dq = dq + jnp.dot(keyt[:, at], slopes, preferred_element_type=F32)
            dqt[q] = dq
            return inner

        lax.fori_loop(0, 8, query_step, 0, unroll=4)
        scale = jnp.where(left, SCORE_SCALE, 1.0)
        for c in range(2):
            bsend[4 * c : 4 * c + 4, pl.ds(z, 1), 0:64, :] = (
                (dkv[c] * scale).astype(BF).reshape(4, 1, 64, 128)
            )
        kv_move(z).start()

        @pl.when(z == 0)
        def _():
            for fold in folds:
                fold.start_one(2)

        @pl.when(z == 1)
        def _():
            for fold in folds:
                fold.relay()
            for copy in outs:
                copy.start()

        @pl.when(z == 2)
        def _():
            for fold in folds:

                @pl.when(jnp.logical_not(fold.middle))
                def _():
                    fold.copy(1).start()

            osum[...] = scatter.total().astype(BF)
            xswap.start()
            zin[head] = osum[head]

        return carry

    lax.fori_loop(0, 4, keys_step, 0)
    for z in range(4):
        both = jnp.concatenate([dqt[2 * z], dqt[2 * z + 1]], axis=0)
        both = (jnp.transpose(both) * SCORE_SCALE).astype(BF)
        bsend[:, z, 64:96, :] = both.reshape(8, 32, 128)
    qmove = Swap(
        head,
        blk,
        "blk",
        lambda i: bsend.at[i, :, pl.ds(64, 32)],
        lambda i: back.at[i, :, pl.ds(64, 32)],
        bsem_r.at[4],
    )
    qmove.start()
    back[blk] = bsend[blk]
    picked = turned[pl.ds(pl.multiple_of((head * 8 + blk) * 8, 8), 8), :]
    step_lane = lax.broadcasted_iota(jnp.int32, picked.shape, 1)
    columns = [
        jnp.sum(jnp.where(step_lane == tix[seq], picked, 0.0), axis=1, keepdims=True)
        for seq in range(2)
    ]
    for z in range(4):
        kv_move(z).arrive()
    qmove.arrive()
    gswap = Fold(head, blk, gnp, gvia, gjoin, gin_r, gsem_r)

    def unturn(step, carry):
        at = flip(head, step)
        for seq in range(2):
            table = tabg[at]
            if seq:
                table = pltpu.roll(table, 64, 1)
            both, keyed = turn_tables(table, -1.0)
            rows = slice(64 * seq, 64 * seq + 64)
            for j in range(4):
                kv = back[4 * seq + j, at, 0:64, :].astype(F32)
                kv = kv * keyed[0] + lane_swap(kv) * keyed[1]
                gp[at, rows, 128 * j : 128 * j + 128] = kv.astype(BF)
            for i in range(2):
                first = back[4 * seq + 2 * i, at, 64:96, :].astype(F32)
                second = back[4 * seq + 2 * i + 1, at, 64:96, :].astype(F32)
                query = jnp.concatenate(
                    [join_halves(first, second, 0), join_halves(first, second, 1)], axis=0
                )
                query = query * both[0] + lane_swap(query) * both[1]
                gp[at, rows, 512 + 128 * i : 640 + 128 * i] = query.astype(BF)
        return carry

    for step in (3, 2, 1, 0):
        unturn(step, 0)
    for group in range(4):
        lanes = slice(256 * group, 256 * group + 256)
        value = contract_rows(normed[:, :, lanes].reshape(512, 256), gp[...].reshape(512, 768))
        terms[group] = value.astype(BF).reshape(4, 2, 32, 768)
    scatter_q = Scatter(head, blk, terms, near_q, joined_q, far_q, osem_q)
    scatter_q.start()
    for step in (3, 2, 1, 0):
        at = flip(head, step)
        gnp[at] = contract_cols(gp[at], wq[...].reshape(1024, 768)).astype(BF)
        if step == 3:
            gswap.start_far()
            gswap.start_one(3)
    scatter_q.join()
    part_r[...] = jnp.concatenate(
        [jnp.zeros((2, 1024), F32), sums[0:2, :], jnp.zeros((4, 1024), F32)], axis=0
    )

    def gather_r(at, carry):
        for seq in range(2):
            unit, _ = norm_stats(tokg[at, seq].astype(F32))
            part_r[seq : seq + 1, :] += jnp.sum(
                gnp[at, pl.ds(64 * seq, 64), :].astype(F32) * unit, axis=0, keepdims=True
            )
        return carry

    lax.fori_loop(0, 4, gather_r, 0)
    one_r = Swap(head, blk, "blk", lambda i: part_r, lambda i: sums_in_r.at[i], asem_r)
    one_r.start()
    sums_in_r[blk] = part_r[...]
    gswap.start_one(2)
    gswap.relay()
    gswap.start_one(1)
    uswap_r.arrive()
    usum[...] = sum_four(uin).astype(BF)
    vswap.start()
    up_own[blk] = usum[blk]
    one_r.arrive()
    total = sums_in_r[0]
    for i in range(1, 8):
        total = total + sums_in_r[i]
    parts_r[head] = total
    two_r = Swap(head, blk, "head", lambda i: parts_r.at[head], lambda i: parts_r.at[i], csem_r)
    two_r.start()
    total = middle[...] + outq[lax.div(blk, 2)].astype(F32)
    for i in range(1, 4):
        outs[i - 1].wait_recv()
        total = total + oin[i].astype(F32)
    output[...] = total.astype(BF)
    dfold.arrive()
    g_down[...] = sum_four(din)
    osum_q[...] = scatter_q.total().astype(BF)
    xswap_q = Swap(head, blk, "head", lambda i: osum_q.at[i], lambda i: gq.at[i], xsem_q)
    xswap_q.start()
    gq[head] = osum_q[head]
    xswap.arrive()
    g_out[...] = sum_four(zin)
    two_r.arrive()
    total = (parts_r[0] + parts_r[1]) + (parts_r[2] + parts_r[3])
    grad_attn[...] = columns[0] * total[0:1] + columns[1] * total[1:2]
    grad_mlp[...] = columns[0] * total[2:3] + columns[1] * total[3:4]
    gswap.arrive()
    for seq in range(2):
        rows = slice(64 * seq, 64 * seq + 64)
        grad = sum_four([gin_r[i, rows, :] for i in range(4)])
        unit, spread = norm_stats(tokg[head, seq].astype(F32))
        grad_tokens[rows, :] = grad_middle[rows, :] + norm_back(
            unit, spread, grad, scales[seq : seq + 1, :]
        )
    vswap.arrive()
    for i in range(8):
        for group in range(4):
            at = 128 * (8 * group + i)
            g_up[:, at : at + 128] = up_own[i, :, 128 * group : 128 * group + 128].astype(F32)
    xswap_q.arrive()
    for group in range(4):
        for i in range(2):
            first = gq[group, :, 256 * i : 256 * i + 128].astype(F32)
            second = gq[group, :, 256 * i + 128 : 256 * i + 256].astype(F32)
            at = 256 * group + 128 * i
            for right in range(2):
                lanes = slice(1024 + 1024 * right + at, 1152 + 1024 * right + at)
                g_qkv[:, lanes] = join_halves(first, second, right)
        g_qkv[:, 256 * group : 256 * group + 256] = gq[group, :, 512:768].astype(F32)
    for z in range(4):
        kv_move(z).drain()
    for copy in outs:
        copy.wait_send()
    for copies in (
        scatter, uswap_r, dfold, vswap, xswap, qmove, gswap, scatter_q, xswap_q, one_r, two_r
    ):
        copies.drain()
    for at in range(4):
        move(at).drain()
    for i in range(4):
        for copy in halves(i):
            copy.wait_send()
        if i:
            onward(i).wait_send()
    for copies in (
        zswap, line, tline, plane, one, two, uswap, oline,
        uline, dline, oplane, cplane, everyone, nplane, backward,
    ):
        copies.drain()


def whole(count):
    return [pl.BlockSpec(memory_space=pltpu.VMEM)] * count


def layer(*operands):
    dma = pltpu.SemaphoreType.DMA
    shape = jax.ShapeDtypeStruct
    return pl.pallas_call(
        layer_kernel,
        out_shape=(
            shape((128, 1024), BF),
            shape((128, 1024), F32),
            shape((32, 3072), F32),
            shape((32, 1024), F32),
            shape((32, 4096), F32),
            shape((128, 1024), F32),
            shape((8, 1024), F32),
            shape((8, 1024), F32),
        ),
        in_specs=whole(11) + [pl.BlockSpec(memory_space=pltpu.SMEM)],
        out_specs=whole(8),
        scratch_shapes=[
            pltpu.VMEM((64, 128), F32),
            pltpu.VMEM((4, 32, 768), BF),
            pltpu.VMEM((8, 32, 512), BF),
            pltpu.VMEM((4, 32, 768), BF),
            pltpu.VMEM((8, 32, 512), BF),
            pltpu.VMEM((4, 8, 96, 128), BF),
            pltpu.VMEM((4, 128, 1024), BF),
            pltpu.VMEM((4, 8, 32, 768), BF),
            pltpu.VMEM((8, 1024), F32),
            pltpu.VMEM((4, 64, 128), F32),
            pltpu.VMEM((4, 2, 64, 1024), BF),
            pltpu.VMEM((4, 128, 256), F32),
            pltpu.VMEM((4, 8, 256), F32),
            pltpu.VMEM((4, 8, 32, 128), BF),
            pltpu.VMEM((128, 1024), F32),
            pltpu.VMEM((128, 1024), F32),
            pltpu.VMEM((4, 128, 1024), BF),
            pltpu.VMEM((4, 128, 1024), BF),
            pltpu.VMEM((4, 8, 32, 512), BF),
            pltpu.VMEM((4, 4, 2, 32, 1024), BF),
            pltpu.VMEM((8, 1024), F32),
            pltpu.VMEM((4, 32, 768), BF),
            pltpu.VMEM((256, 64), F32),
            pltpu.VMEM((8, 1024), F32),
            pltpu.VMEM((8, 8, 1024), F32),
            pltpu.VMEM((4, 8, 1024), F32),
            pltpu.VMEM((8, 4, 96, 128), BF),
            pltpu.VMEM((8, 32, 512), BF),
            pltpu.VMEM((4, 32, 1024), BF),
            pltpu.VMEM((4, 8, 32, 512), BF),
            pltpu.VMEM((4, 128, 1024), BF),
            pltpu.VMEM((4, 8, 32, 1024), BF),
            pltpu.VMEM((8, 128, 1024), BF),
            pltpu.VMEM((128, 2048), BF),
            pltpu.VMEM((2048 // KEYS, KEYS, 256), F32),
            pltpu.VMEM((4, 8, 32, 128), BF),
            pltpu.VMEM((4, 8, 32, 128), BF),
            pltpu.VMEM((4, 128, 256), BF),
            pltpu.VMEM((8, 128, 1024), BF),
            pltpu.VMEM((8, 128, 512), BF),
            pltpu.VMEM((8, 128, 512), BF),
            pltpu.VMEM((2, 4, 2, 128, 1024), BF),
            pltpu.VMEM((2, 4, 128, 1024), BF),
            pltpu.VMEM((4, 128, 1024), BF),
            pltpu.VMEM((4, 128, 1024), BF),
            pltpu.VMEM((4, 8, 32, 128), BF),
            pltpu.VMEM((128, 1024), BF),
            pltpu.VMEM((8, 256, 128), BF),
            pltpu.VMEM((8, 256, 128), BF),
            pltpu.VMEM((8, 128, 256), BF),
            pltpu.VMEM((8, 128, 256), BF),
            pltpu.VMEM((8, 8, 256), F32),
            pltpu.VMEM((64, 2048), BF),
            pltpu.VMEM((2, 256, 128), F32),
            pltpu.VMEM((8, 64, 256), F32),
            pltpu.VMEM((8, 4, 96, 128), BF),
            pltpu.VMEM((8, 4, 96, 128), BF),
            pltpu.VMEM((4, 128, 1024), BF),
            pltpu.VMEM((4, 128, 1024), BF),
            pltpu.VMEM((128, 1024), BF),
            pltpu.VMEM((128, 1024), BF),
            pltpu.VMEM((4, 8, 32, 512), BF),
            pltpu.VMEM((8, 32, 512), BF),
            pltpu.VMEM((8, 32, 512), BF),
            pltpu.VMEM((8, 32, 512), BF),
            pltpu.VMEM((4, 4, 32, 1024), BF),
            pltpu.VMEM((4, 4, 32, 1024), BF),
            pltpu.VMEM((4, 4, 32, 1024), BF),
            pltpu.VMEM((4, 32, 1024), BF),
            pltpu.VMEM((4, 32, 1024), BF),
            pltpu.VMEM((4, 128, 768), BF),
            pltpu.VMEM((4, 128, 1024), BF),
            pltpu.VMEM((128, 1024), BF),
            pltpu.VMEM((128, 1024), BF),
            pltpu.VMEM((4, 128, 1024), BF),
            pltpu.VMEM((4, 4, 2, 32, 768), BF),
            pltpu.VMEM((4, 4, 32, 768), BF),
            pltpu.VMEM((4, 4, 32, 768), BF),
            pltpu.VMEM((4, 4, 32, 768), BF),
            pltpu.VMEM((4, 32, 768), BF),
            pltpu.VMEM((8, 1024), F32),
            pltpu.VMEM((8, 8, 1024), F32),
            pltpu.VMEM((4, 8, 1024), F32),
            dma((2, 4)),
            dma((2, 2, 3)),
            dma((2, 2, 3)),
            dma((2, 8)),
            dma((2, 8)),
            dma((2, 4)),
            dma((4, 2, 8)),
            dma((2, 8)),
            dma((2, 4)),
            dma((2, 2, 3)),
            dma((2, 2, 3)),
            dma((2, 8)),
            dma((2, 8)),
            dma((2, 4, 8)),
            dma((2, 8)),
            dma((2, 2, 4)),
            dma((2, 4)),
            dma((2, 4, 8)),
            dma((2, 4)),
            dma((2, 4)),
            dma((2, 4)),
            dma((2, 8)),
            dma((2, 4)),
            dma((2, 4)),
            dma((5, 2, 8)),
            dma((2, 4)),
            dma((2, 4)),
            dma((2, 4)),
            dma((2, 8)),
            dma((2, 4)),
        ],
        compiler_params=pltpu.CompilerParams(
            collective_id=0, has_side_effects=True, vmem_limit_bytes=VMEM_LIMIT
        ),
        name="layer",
    )(*operands)


def finish_kernel(*refs):
    count = (len(refs) - 1) // 3
    sems = refs[-1]
    arrive = [
        pltpu.make_async_copy(refs[i], refs[2 * count + i], sems.at[0, i]) for i in range(count)
    ]
    leave = [
        pltpu.make_async_copy(refs[2 * count + i], refs[count + i], sems.at[1, i])
        for i in range(count)
    ]
    for copy in arrive:
        copy.start()
    for i in range(count):
        arrive[i].wait()
        leave[i].start()
    for copy in leave:
        copy.wait()


def finish(results):
    spec = [pl.BlockSpec(memory_space=pl.ANY)] * len(results)
    return pl.pallas_call(
        finish_kernel,
        out_shape=tuple(jax.ShapeDtypeStruct(x.shape, x.dtype) for x in results),
        in_specs=spec,
        out_specs=spec,
        scratch_shapes=[pltpu.VMEM(x.shape, x.dtype) for x in results]
        + [pltpu.SemaphoreType.DMA((2, len(results)))],
        name="finish",
    )(*results)


def blocked(
    tokens,
    positions,
    time_index,
    time_table,
    w_qkv,
    w_out,
    w_up,
    w_down,
    scale_attn,
    scale_mlp,
    cotangent,
):
    half_dim = HEAD_DIM // 2
    frequency = 10000.0 ** (-jnp.arange(half_dim, dtype=jnp.float32) / half_dim)
    results = layer(
        tokens,
        positions,
        jnp.broadcast_to(frequency[:, None], (half_dim, 128)),
        w_qkv,
        time_table,
        scale_attn,
        scale_mlp,
        w_up,
        w_out,
        w_down,
        cotangent.reshape(128, 1024),
        time_index,
    )
    output, grad_tokens, *others = finish(results)
    return (output.reshape(2, 64, 1024), grad_tokens.reshape(2, 64, 1024), *others)


def solution(mesh):
    fits = mesh.shape["head"] == 4 and mesh.shape["blk"] == 8
    placed = (
        P(None, ("head", "blk"), None),
        P(None, ("head", "blk")),
        P(),
        P(),
        P(("head", "blk"), None),
        P(("head", "blk"), None),
        P(("head", "blk"), None),
        P(("head", "blk"), None),
        P(("head", "blk"), None),
        P(("head", "blk"), None),
        P(None, ("head", "blk"), None),
    )
    return jax.shard_map(
        blocked if fits else general,
        mesh=mesh,
        in_specs=placed,
        out_specs=(
            P(None, ("head", "blk"), None),
            P(None, ("head", "blk"), None),
            P(("head", "blk"), None),
            P(("head", "blk"), None),
            P(("head", "blk"), None),
            P(("head", "blk"), None),
            P(("head", "blk"), None),
            P(("head", "blk"), None),
        ),
        check_vma=False,
    )
```

```python
import math

import jax
import jax.numpy as jnp
from jax import lax
from jax.experimental import pallas as pl
from jax.experimental.pallas import tpu as pltpu
from jax.sharding import PartitionSpec as P

HEADS = 16
HEAD_DIM = 64


NORM_EPSILON = 1e-05
PRECISE = lax.Precision.HIGHEST
START_TOP = -1e30
SCORE_SCALE = 0.125


def shifted(value, axis, steps):
    count = lax.axis_size(axis)
    pairs = [(source, (source + steps) % count) for source in range(count)]
    return lax.ppermute(value, axis, pairs)


def layer_norm(value, scale):
    centered = value - jnp.mean(value, axis=-1, keepdims=True)
    variance = jnp.mean(centered * centered, axis=-1, keepdims=True)
    return centered * lax.rsqrt(variance + NORM_EPSILON) * scale


def rotate(value, cosine_table, sine_table):
    half_dim = value.shape[-1] // 2
    first_half = value[..., :half_dim]
    second_half = value[..., half_dim:]
    return jnp.concatenate(
        [
            first_half * cosine_table - second_half * sine_table,
            second_half * cosine_table + first_half * sine_table,
        ],
        axis=-1,
    )


def rotary_tables(positions, head_dim):
    half_dim = head_dim // 2
    frequency = 10000.0 ** (-jnp.arange(half_dim, dtype=jnp.float32) / half_dim)
    turned = positions.astype(jnp.float32)[:, :, None, None] * frequency
    return (jnp.cos(turned), jnp.sin(turned))


def contract_rows(left, right):
    return lax.dot_general(
        left, right, (((0,), (0,)), ((), ())), preferred_element_type=jnp.float32
    )


def contract_cols(left, right):
    return lax.dot_general(
        left, right, (((1,), (1,)), ((), ())), preferred_element_type=jnp.float32
    )


def attend_step(running, query_block, key_block, value_block):
    row_top, row_sum, accum = running
    scores = (
        jnp.einsum("sqhd,skhd->sqhk", query_block, key_block, preferred_element_type=jnp.float32)
        * SCORE_SCALE
    )
    new_top = jnp.maximum(row_top, jnp.max(scores, axis=-1))
    shrink = jnp.exp(row_top - new_top)
    weights = jnp.exp(scores - new_top[..., None])
    row_sum = row_sum * shrink + jnp.sum(weights, axis=-1)
    accum = accum * shrink[..., None] + jnp.einsum(
        "sqhk,skhd->sqhd",
        weights.astype(jnp.bfloat16),
        value_block,
        preferred_element_type=jnp.float32,
    )
    return (new_top, row_sum, accum)


def back_step(query_block, key_block, value_block, grad_block, log_total, delta):
    scores = (
        jnp.einsum("sqhd,skhd->sqhk", query_block, key_block, preferred_element_type=jnp.float32)
        * SCORE_SCALE
    )
    probs = jnp.exp(scores - log_total[..., None])
    grad_values = jnp.einsum(
        "sqhk,sqhd->skhd",
        probs.astype(jnp.bfloat16),
        grad_block,
        preferred_element_type=jnp.float32,
    )
    grad_probs = jnp.einsum(
        "sqhd,skhd->sqhk", grad_block, value_block, preferred_element_type=jnp.float32
    )
    grad_scores = (probs * (grad_probs - delta[..., None])).astype(jnp.bfloat16)
    grad_query = jnp.einsum(
        "sqhk,skhd->sqhd", grad_scores, key_block, preferred_element_type=jnp.float32
    )
    grad_keys = jnp.einsum(
        "sqhk,sqhd->skhd", grad_scores, query_block, preferred_element_type=jnp.float32
    )
    return (grad_query, grad_keys, grad_values)


def general(
    tokens,
    positions,
    time_index,
    time_table,
    w_qkv,
    w_out,
    w_up,
    w_down,
    scale_attn,
    scale_mlp,
    cotangent,
):
    seq_count, row_count, model_width = tokens.shape
    group_count = lax.axis_size("head")
    local_heads = HEADS // group_count
    feature_width = local_heads * HEAD_DIM
    flat_rows = seq_count * row_count
    gathered = (
        lax.all_gather(w_qkv, ("head", "blk"), axis=0, tiled=True),
        lax.all_gather(w_out, ("head", "blk"), axis=0, tiled=True),
        lax.all_gather(w_up, ("head", "blk"), axis=0, tiled=True),
        lax.all_gather(w_down, ("head", "blk"), axis=0, tiled=True),
        lax.all_gather(scale_attn, ("head", "blk"), axis=0, tiled=True),
        lax.all_gather(scale_mlp, ("head", "blk"), axis=0, tiled=True),
    )
    full_qkv, full_out, full_up, full_down, full_scale_attn, full_scale_mlp = gathered
    step_count = time_table.shape[0]
    picker = (time_index[:, None] == jnp.arange(step_count, dtype=jnp.int32)[None, :]).astype(
        jnp.float32
    )
    time_embed = jnp.dot(picker, time_table, precision=PRECISE)
    scale_one = 1.0 + jnp.dot(time_embed, full_scale_attn.astype(jnp.float32), precision=PRECISE)
    scale_two = 1.0 + jnp.dot(time_embed, full_scale_mlp.astype(jnp.float32), precision=PRECISE)
    token_float = tokens.astype(jnp.float32)
    normed = (
        layer_norm(token_float, scale_one[:, None, :])
        .astype(jnp.bfloat16)
        .reshape(flat_rows, model_width)
    )
    projected = jnp.dot(normed, full_qkv, preferred_element_type=jnp.float32).reshape(
        seq_count, row_count, 3, HEADS, HEAD_DIM
    )
    cosine_table, sine_table = rotary_tables(positions, HEAD_DIM)
    query_tok = rotate(projected[:, :, 0], cosine_table, sine_table)
    keys_tok = rotate(projected[:, :, 1], cosine_table, sine_table)
    packed = (
        jnp.stack([query_tok, keys_tok, projected[:, :, 2]], axis=2)
        .reshape(seq_count, row_count, 3, model_width)
        .astype(jnp.bfloat16)
    )
    regrouped = lax.all_to_all(packed, "head", split_axis=3, concat_axis=1, tiled=True)
    block_len = regrouped.shape[1]
    local_query = regrouped[:, :, 0].reshape(seq_count, block_len, local_heads, HEAD_DIM)
    local_keys = regrouped[:, :, 1]
    local_values = regrouped[:, :, 2]
    start_state = (
        jnp.full((seq_count, block_len, local_heads), START_TOP, jnp.float32),
        jnp.zeros((seq_count, block_len, local_heads), jnp.float32),
        jnp.zeros((seq_count, block_len, local_heads, HEAD_DIM), jnp.float32),
    )
    key_piece = lax.all_gather(local_keys, "blk", axis=1, tiled=True)
    value_piece = lax.all_gather(local_values, "blk", axis=1, tiled=True)
    piece_len = key_piece.shape[1]
    step_len = math.gcd(piece_len, block_len)

    def one_block(index, state):
        key_block = lax.dynamic_slice_in_dim(key_piece, index * step_len, step_len, 1).reshape(
            seq_count, step_len, local_heads, HEAD_DIM
        )
        value_block = lax.dynamic_slice_in_dim(value_piece, index * step_len, step_len, 1).reshape(
            seq_count, step_len, local_heads, HEAD_DIM
        )
        return attend_step(state, local_query, key_block, value_block)

    row_top, row_sum, accum = lax.fori_loop(0, piece_len // step_len, one_block, start_state)
    mixed = accum / row_sum[..., None]
    log_total = row_top + jnp.log(row_sum)
    attended_heads = mixed.astype(jnp.bfloat16).reshape(seq_count, block_len, feature_width)
    attended = lax.all_to_all(
        attended_heads, "head", split_axis=1, concat_axis=2, tiled=True
    ).reshape(flat_rows, model_width)
    branch = jnp.dot(attended, full_out, preferred_element_type=jnp.float32)
    middle = token_float + branch.reshape(seq_count, row_count, model_width)
    normed_two = (
        layer_norm(middle, scale_two[:, None, :])
        .astype(jnp.bfloat16)
        .reshape(flat_rows, model_width)
    )
    hidden = jnp.dot(normed_two, full_up, preferred_element_type=jnp.float32)
    active = jax.nn.gelu(hidden, approximate=False).astype(jnp.bfloat16)
    result = middle.reshape(flat_rows, model_width) + jnp.dot(
        active, full_down, preferred_element_type=jnp.float32
    )
    output = result.astype(jnp.bfloat16).reshape(seq_count, row_count, model_width)
    back_qkv, back_out, back_up, back_down = (
        lax.all_gather(w_qkv, ("head", "blk"), axis=0, tiled=True),
        lax.all_gather(w_out, ("head", "blk"), axis=0, tiled=True),
        lax.all_gather(w_up, ("head", "blk"), axis=0, tiled=True),
        lax.all_gather(w_down, ("head", "blk"), axis=0, tiled=True),
    )
    grad_out = cotangent.reshape(flat_rows, model_width)
    grad_active = contract_cols(grad_out, back_down)
    grad_w_down = contract_rows(active, grad_out)
    gelu_value, gelu_pull = jax.vjp(lambda entry: jax.nn.gelu(entry, approximate=False), hidden)
    grad_hidden = gelu_pull(grad_active)[0].astype(jnp.bfloat16)
    grad_w_up = contract_rows(normed_two, grad_hidden)
    grad_normed_two = contract_cols(grad_hidden, back_up).reshape(seq_count, row_count, model_width)
    norm_value, norm_pull = jax.vjp(layer_norm, middle, scale_two[:, None, :])
    grad_middle_norm, grad_scale_two = norm_pull(grad_normed_two)
    grad_middle = cotangent.astype(jnp.float32) + grad_middle_norm
    grad_scale_mlp = jnp.dot(time_embed.T, grad_scale_two[:, 0, :], precision=PRECISE)
    grad_branch = grad_middle.reshape(flat_rows, model_width).astype(jnp.bfloat16)
    grad_w_out = contract_rows(attended, grad_branch)
    grad_attended = (
        contract_cols(grad_branch, back_out)
        .astype(jnp.bfloat16)
        .reshape(seq_count, row_count, model_width)
    )
    grad_heads = lax.all_to_all(
        grad_attended, "head", split_axis=2, concat_axis=1, tiled=True
    ).reshape(seq_count, block_len, local_heads, HEAD_DIM)
    delta = jnp.sum(grad_heads.astype(jnp.float32) * mixed, axis=-1)

    def turn(index, state):
        key_now, value_now, grad_keys_now, grad_values_now, grad_query_sum = state
        grad_query, grad_keys, grad_values = back_step(
            local_query,
            key_now.reshape(seq_count, block_len, local_heads, HEAD_DIM),
            value_now.reshape(seq_count, block_len, local_heads, HEAD_DIM),
            grad_heads,
            log_total,
            delta,
        )
        moved_keys, moved_values = shifted((key_now, value_now), "blk", 1)
        moved_grad_keys, moved_grad_values = (
            shifted(
                (grad_keys_now + grad_keys.reshape(seq_count, block_len, feature_width)).astype(
                    jnp.bfloat16
                ),
                "blk",
                1,
            ).astype(jnp.float32),
            shifted(
                (grad_values_now + grad_values.reshape(seq_count, block_len, feature_width)).astype(
                    jnp.bfloat16
                ),
                "blk",
                1,
            ).astype(jnp.float32),
        )
        return (
            moved_keys,
            moved_values,
            moved_grad_keys,
            moved_grad_values,
            grad_query_sum + grad_query,
        )

    zero_kv = jnp.zeros((seq_count, block_len, feature_width), jnp.float32)
    begin = (
        local_keys,
        local_values,
        zero_kv,
        zero_kv,
        jnp.zeros((seq_count, block_len, local_heads, HEAD_DIM), jnp.float32),
    )
    final_state = lax.fori_loop(0, lax.axis_size("blk"), turn, begin)
    grad_keys_own = final_state[2]
    grad_values_own = final_state[3]
    grad_query_all = final_state[4]
    stacked = jnp.stack(
        [
            grad_query_all.reshape(seq_count, block_len, feature_width) * SCORE_SCALE,
            grad_keys_own * SCORE_SCALE,
            grad_values_own,
        ],
        axis=2,
    ).astype(jnp.bfloat16)
    returned = lax.all_to_all(stacked, "head", split_axis=1, concat_axis=3, tiled=True)
    grad_query_tok = (
        returned[:, :, 0].astype(jnp.float32).reshape(seq_count, row_count, HEADS, HEAD_DIM)
    )
    grad_keys_tok = (
        returned[:, :, 1].astype(jnp.float32).reshape(seq_count, row_count, HEADS, HEAD_DIM)
    )
    grad_values_tok = (
        returned[:, :, 2].astype(jnp.float32).reshape(seq_count, row_count, HEADS, HEAD_DIM)
    )
    grad_projected = (
        jnp.stack(
            [
                rotate(grad_query_tok, cosine_table, -sine_table),
                rotate(grad_keys_tok, cosine_table, -sine_table),
                grad_values_tok,
            ],
            axis=2,
        )
        .reshape(flat_rows, 3 * model_width)
        .astype(jnp.bfloat16)
    )
    grad_w_qkv = contract_rows(normed, grad_projected)
    grad_normed = contract_cols(grad_projected, back_qkv).reshape(seq_count, row_count, model_width)
    first_value, first_pull = jax.vjp(layer_norm, token_float, scale_one[:, None, :])
    grad_token_norm, grad_scale_one = first_pull(grad_normed)
    grad_tokens = grad_middle + grad_token_norm
    grad_scale_attn = jnp.dot(time_embed.T, grad_scale_one[:, 0, :], precision=PRECISE)
    shards = (
        lax.psum_scatter(grad_w_qkv, ("head", "blk"), scatter_dimension=0, tiled=True),
        lax.psum_scatter(grad_w_out, ("head", "blk"), scatter_dimension=0, tiled=True),
        lax.psum_scatter(grad_w_up, ("head", "blk"), scatter_dimension=0, tiled=True),
        lax.psum_scatter(grad_w_down, ("head", "blk"), scatter_dimension=0, tiled=True),
        lax.psum_scatter(grad_scale_attn, ("head", "blk"), scatter_dimension=0, tiled=True),
        lax.psum_scatter(grad_scale_mlp, ("head", "blk"), scatter_dimension=0, tiled=True),
    )
    return (output, grad_tokens, shards[0], shards[1], shards[2], shards[3], shards[4], shards[5])


EPS = NORM_EPSILON
BF = jnp.bfloat16
F32 = jnp.float32


def norm_stats(value):
    centered = value - jnp.mean(value, axis=-1, keepdims=True)
    spread = lax.rsqrt(jnp.mean(centered * centered, axis=-1, keepdims=True) + EPS)
    return centered * spread, spread


def norm_back(unit, spread, grad, scale):
    scaled = grad * scale
    return spread * (
        scaled
        - jnp.mean(scaled, axis=-1, keepdims=True)
        - unit * jnp.mean(scaled * unit, axis=-1, keepdims=True)
    )


MESH = pl.DeviceIdType.MESH


def flip(value, bits):
    for bit in (1, 2, 4):
        if bits & bit:
            value = value + bit - 2 * bit * lax.rem(lax.div(value, bit), 2)
    return value


def greet(head, blk, heads, blks):
    barrier = pltpu.get_barrier_semaphore()
    for k in heads:
        pl.semaphore_signal(barrier, inc=1, device_id=(flip(head, k), blk), device_id_type=MESH)
    for k in blks:
        pl.semaphore_signal(barrier, inc=1, device_id=(head, flip(blk, k)), device_id_type=MESH)
    pl.semaphore_wait(barrier, len(heads) + len(blks))


def send(source, target, send_sem, recv_sem, head, blk):
    return pltpu.make_async_remote_copy(
        src_ref=source,
        dst_ref=target,
        send_sem=send_sem,
        recv_sem=recv_sem,
        device_id=(head, blk),
        device_id_type=MESH,
    )


class Swap:
    def __init__(self, head, blk, axis, source, target, sems):
        self.copies = []
        count = 4 if axis == "head" else 8
        me = head if axis == "head" else blk
        for k in range(1, count):
            peer = flip(me, k)
            where = (peer, blk) if axis == "head" else (head, peer)
            self.copies.append(
                send(source(peer), target(me), sems.at[0, k], sems.at[1, k], *where)
            )

    def start(self):
        for copy in self.copies:
            copy.start()

    def arrive(self):
        for copy in self.copies:
            copy.wait_recv()

    def drain(self):
        for copy in self.copies:
            copy.wait_send()


class Plane:
    def __init__(self, head, blk, own, slot, sems):
        sibling = flip(blk, 1)
        self.first = [send(own, slot(blk), sems.at[0, 0], sems.at[1, 0], head, sibling)]
        self.passed = []
        for i, k in enumerate((2, 4, 6)):
            peer = flip(blk, k)
            self.first.append(
                send(own, slot(blk), sems.at[0, i + 1], sems.at[1, i + 1], head, peer)
            )
            self.passed.append(
                send(slot(peer), slot(peer), sems.at[0, i + 4], sems.at[1, i + 4], head, sibling)
            )

    def start(self):
        for i in (3, 1, 2, 0):
            self.first[i].start()

    def forward(self, i):
        self.first[i + 1].wait_recv()
        self.passed[i].start()

    def arrive(self, i):
        if i < 0:
            self.first[0].wait_recv()
        else:
            self.passed[i].wait_recv()

    def finish(self):
        for i in range(3):
            self.forward(i)
        for i in range(-1, 3):
            self.arrive(i)

    def drain(self):
        for copy in self.first + self.passed:
            copy.wait_send()


class Split:
    def __init__(self, head, blk, own, slot, half, sems):
        sibling, across, along, far = (flip(blk, k) for k in (1, 2, 4, 6))

        def copy(source, target, i, peer):
            return send(source, target, sems.at[0, i], sems.at[1, i], head, peer)

        self.first = [
            copy(own, slot(blk), 0, sibling),
            copy(own, slot(blk), 1, across),
            copy(own, slot(blk), 2, along),
        ]
        self.cross = [
            copy(half(across, 1), half(across, 1), 3, along),
            copy(half(along, 0), half(along, 0), 4, across),
        ]
        self.passed = [
            copy(slot(peer), slot(peer), 5 + i, sibling)
            for i, peer in enumerate((across, along, far))
        ]

    def start(self):
        for i in (1, 2, 0):
            self.first[i].start()

    def forward(self, i):
        if i < 2:
            self.first[i + 1].wait_recv()
            self.cross[i].start()
        else:
            for copy in self.cross:
                copy.wait_recv()
        self.passed[i].start()

    def arrive(self, i):
        if i < 0:
            self.first[0].wait_recv()
        else:
            self.passed[i].wait_recv()

    def finish(self):
        for i in range(3):
            self.forward(i)
        for i in range(-1, 3):
            self.arrive(i)

    def drain(self):
        for copy in self.first + self.cross + self.passed:
            copy.wait_send()


def line_order(head, step):
    low = jnp.minimum(head, 3 - head)
    swap = low * ((step == 0).astype(jnp.int32) - (step == 1).astype(jnp.int32))
    at = step + swap
    return jnp.where(head < 2, at, 3 - at)


class Line:
    def __init__(self, head, blk, own, slot, sems):
        self.head, self.blk, self.own, self.slot, self.sems = head, blk, own, slot, sems

    def copy(self, source, at, up, k):
        head = self.head
        target = jnp.where(up, head + 1, head - 1)
        way = jnp.where(up, 0, 1)
        return send(
            source, self.slot(at), self.sems.at[0, way, k], self.sems.at[1, way, k], target, self.blk
        )

    def start(self):
        head = self.head

        @pl.when(head < 3)
        def _():
            self.copy(self.own, head, True, 0).start()

        @pl.when(head > 0)
        def _():
            self.copy(self.own, head, False, 0).start()

    def step(self, at):
        head = self.head
        up = at < head
        k = jnp.where(up, head - 1 - at, at - head - 1)
        self.copy(self.slot(at), at, up, k).wait_recv()

        @pl.when(jnp.where(up, head < 3, head > 0))
        def _():
            self.copy(self.slot(at), at, up, k + 1).start()

    def hop(self, k):
        head = self.head

        @pl.when(head >= k)
        def _():
            self.step(head - k)

        @pl.when(head + k <= 3)
        def _():
            self.step(head + k)

    def drain(self):
        head = self.head
        for k in range(3):

            @pl.when(jnp.logical_and(head < 3, head >= k))
            def _():
                self.copy(self.own, head, True, k).wait_send()

            @pl.when(jnp.logical_and(head > 0, head + k <= 3))
            def _():
                self.copy(self.own, head, False, k).wait_send()


class Reach:
    def __init__(self, head, blk, own, slot, sems):
        self.head, self.blk, self.own, self.slot, self.sems = head, blk, own, slot, sems
        self.middle = jnp.logical_and(head > 0, head < 3)

    def copy(self, k):
        peer = flip(self.head, k)
        return send(
            self.own, self.slot(self.head), self.sems.at[0, k], self.sems.at[1, k], peer, self.blk
        )

    def passed(self):
        at = self.slot(flip(self.head, 2))
        return send(at, at, self.sems.at[0, 0], self.sems.at[1, 3], flip(self.head, 1), self.blk)

    def start(self):
        self.copy(2).start()
        self.copy(1).start()

        @pl.when(self.middle)
        def _():
            self.copy(3).start()

    def forward(self):
        self.copy(2).wait_recv()

        @pl.when(self.middle)
        def _():
            self.passed().start()

    def arrive(self):
        self.copy(1).wait_recv()
        self.copy(3).wait_recv()

    def drain(self):
        self.copy(1).wait_send()
        self.copy(2).wait_send()

        @pl.when(self.middle)
        def _():
            self.copy(3).wait_send()
            self.passed().wait_send()


class Fold:
    def __init__(self, head, blk, terms, via, joined, into, sems):
        self.head, self.blk, self.sems = head, blk, sems
        self.terms, self.via, self.joined, self.into = terms, via, joined, into
        self.middle = jnp.logical_and(head > 0, head < 3)

    def copy(self, k):
        peer = flip(self.head, k)
        return send(
            self.terms.at[peer],
            self.into.at[k],
            self.sems.at[0, k],
            self.sems.at[1, k],
            peer,
            self.blk,
        )

    def handed(self):
        return send(
            self.terms.at[flip(self.head, 3)],
            self.via,
            self.sems.at[0, 0],
            self.sems.at[1, 0],
            flip(self.head, 1),
            self.blk,
        )

    def relayed(self):
        return send(
            self.joined,
            self.into.at[2],
            self.sems.at[0, 2],
            self.sems.at[1, 2],
            flip(self.head, 2),
            self.blk,
        )

    def start_far(self):
        @pl.when(jnp.logical_not(self.middle))
        def _():
            self.handed().start()

    def start_one(self, k):
        if k == 1:
            self.copy(1).start()
        elif k == 2:

            @pl.when(jnp.logical_not(self.middle))
            def _():
                self.copy(2).start()

        else:

            @pl.when(self.middle)
            def _():
                self.copy(3).start()

    def start(self):
        self.start_far()
        for k in (2, 3, 1):
            self.start_one(k)

    def relay(self):
        @pl.when(self.middle)
        def _():
            self.handed().wait_recv()
            mine = self.terms[flip(self.head, 2)].astype(F32)
            self.joined[...] = (mine + self.via[...].astype(F32)).astype(BF)
            self.relayed().start()

    def arrive(self):
        self.copy(1).wait_recv()
        self.copy(2).wait_recv()

        @pl.when(self.middle)
        def _():
            self.copy(3).wait_recv()

        @pl.when(jnp.logical_not(self.middle))
        def _():
            self.into[3] = jnp.zeros_like(self.into[3])

        self.into[0] = self.terms[self.head]

    def drain(self):
        self.copy(1).wait_send()

        @pl.when(self.middle)
        def _():
            self.copy(3).wait_send()
            self.relayed().wait_send()

        @pl.when(jnp.logical_not(self.middle))
        def _():
            self.copy(2).wait_send()
            self.handed().wait_send()


def half_lane(shape):
    return lax.broadcasted_iota(jnp.int32, shape, 1) < 64


def lane_swap(value):
    lane = lax.broadcasted_iota(jnp.int32, value.shape, 1)
    return jnp.where(
        lax.rem(lane, 64) < 32, pltpu.roll(value, 96, 1), pltpu.roll(value, 32, 1)
    )


def turn_tables(table, sign):
    lane = lax.broadcasted_iota(jnp.int32, table.shape, 1)
    cosine = jnp.where(lane < 32, table, 0.0)
    cosine = cosine + pltpu.roll(cosine, 32, 1)
    sine = jnp.where(jnp.logical_and(lane >= 32, lane < 64), table, 0.0) * sign
    sine = sine - pltpu.roll(sine, 96, 1)
    both = (cosine + pltpu.roll(cosine, 64, 1), sine + pltpu.roll(sine, 64, 1))
    return both, (jnp.where(lane < 64, cosine, 1.0), sine)


def join_halves(top, bottom, right):
    left = half_lane(top.shape)
    if right:
        return jnp.where(left, pltpu.roll(top, 64, 1), bottom)
    return jnp.where(left, top, pltpu.roll(bottom, 64, 1))


EXP_SCALE = SCORE_SCALE * math.log2(math.e)
KEYS = 256


def flip_by(head, k):
    low, high = lax.rem(k, 2), lax.div(k, 2)
    value = head + low - 2 * low * lax.rem(head, 2)
    return value + 2 * high - 4 * high * lax.div(head, 2)


class Everyone:
    def __init__(self, head, blk, source, target, sems):
        self.head, self.blk, self.source, self.target, self.sems = head, blk, source, target, sems
        self.peers = [flip(blk, k) for k in range(8)]

    def copy(self, kz, k):
        z = flip_by(self.head, jnp.int32(kz))
        return self.copy_to(z, kz, k)

    def copy_to(self, z, kz, k):
        b = self.peers[k]
        return send(
            self.source(z, b),
            self.target(self.head, self.blk),
            self.sems.at[0, kz, k],
            self.sems.at[1, kz, k],
            z,
            b,
        )

    def start(self, kz):
        z = flip_by(self.head, jnp.int32(kz))

        @pl.when(kz > 0)
        def _():
            self.copy_to(z, kz, 0).start()

        for k in range(1, 8):
            self.copy_to(z, kz, k).start()

    def arrive(self, kz):
        z = flip_by(self.head, jnp.int32(kz))

        @pl.when(kz > 0)
        def _():
            self.copy_to(z, kz, 0).wait_recv()

        for k in range(1, 8):
            self.copy_to(z, kz, k).wait_recv()

    def drain(self):
        for kz in range(4):
            for k in range(1 if kz == 0 else 0, 8):
                self.copy(kz, k).wait_send()


def greet_all(head, blk):
    barrier = pltpu.get_barrier_semaphore()
    for kz in range(4):
        for k in range(8):
            if kz or k:
                pl.semaphore_signal(
                    barrier, inc=1, device_id=(flip(head, kz), flip(blk, k)), device_id_type=MESH
                )


def all_here():
    pl.semaphore_wait(pltpu.get_barrier_semaphore(), 31)


def group_rows(value):
    return jnp.sum(value.reshape(value.shape[0] // 8, 8, value.shape[1]), axis=0)


VMEM_LIMIT = 61 << 20


class Scatter:
    def __init__(self, head, blk, terms, near, joined, far, sems):
        self.head, self.blk, self.core = head, blk, lax.rem(blk, 2)
        self.terms, self.near, self.joined, self.far, self.sems = terms, near, joined, far, sems

    def halves(self):
        return send(
            self.terms.at[:, :, 1 - self.core],
            self.near,
            self.sems.at[0, 0],
            self.sems.at[1, 0],
            self.head,
            flip(self.blk, 1),
        )

    def chips(self, i):
        peer = flip(self.blk, 2 * i)
        return send(
            self.joined.at[lax.div(peer, 2)],
            self.far.at[i],
            self.sems.at[0, i],
            self.sems.at[1, i],
            self.head,
            peer,
        )

    def start(self):
        self.halves().start()

    def join(self):
        self.halves().wait_recv()
        for chip in range(4):
            mine = self.terms[:, chip, pl.ds(self.core, 1)].astype(F32)
            mine = mine.reshape(mine.shape[0], *mine.shape[2:])
            self.joined[chip] = (mine + self.near[:, chip].astype(F32)).astype(BF)
        for i in (3, 1, 2):
            self.chips(i).start()

    def total(self):
        value = self.joined[lax.div(self.blk, 2)].astype(F32)
        for i in range(1, 4):
            self.chips(i).wait_recv()
            value = value + self.far[i].astype(F32)
        return value

    def drain(self):
        self.halves().wait_send()
        for i in range(1, 4):
            self.chips(i).wait_send()


def sum_four(parts):
    return (parts[0].astype(F32) + parts[1].astype(F32)) + (
        parts[2].astype(F32) + parts[3].astype(F32)
    )


def layer_kernel(
    tok, pos, freq, w_qkv, ttab, sca, scm, w_up, out_own, down_own, cot_own, tix,
    output, grad_tokens, g_qkv, g_out, g_up, g_down, grad_attn, grad_mlp,
    tab, wqp, upp, gq, up_own,
    tiles, normed, wq, scales, tabg, tokg, mixed, lse, grad_rx, grad_middle, middle, outq, grad_down,
    grad_up, grad_out, sums, wqz, turned, part, sums_in, parts, out_tiles, upz, outz, up, down, out, cots,
    kvt, scores, att, received, attended, n2g, act, gh, pairs, prx, gsend, gin, tsend, branch, queries,
    grads, queries_t, grads_t, stats, keyt, dkv, dqt, bsend, back, oin, din, dvia, djoin, uin, uvia, ujoin,
    usum, near, joined, far, osum, zin, gp, gnp, gvia, gjoin, gin_r, terms, near_q, joined_q, far_q, osum_q,
    part_r, sums_in_r, parts_r, zsem, lsem, tsem, wsem, asem, bsem, psem, usem, osem, usem2, dsem, qsem,
    csem, esem, nsem, ssem, gsem, fsem, qsem_r, dsem_r, usem_r, vsem, osem_r, xsem, bsem_r, gsem_r, osem_q,
    xsem_q, asem_r, csem_r,
):
    head, blk = lax.axis_index("head"), lax.axis_index("blk")
    core = lax.rem(blk, 2)
    greet_all(head, blk)
    for group in range(4):
        for i in range(2):
            at = 256 * group + 128 * i
            keys = w_qkv[:, 1024 + at : 1152 + at].astype(F32)
            values = w_qkv[:, 2048 + at : 2176 + at].astype(F32)
            for right in range(2):
                lanes = slice(256 * i + 128 * right, 256 * i + 128 * right + 128)
                wqp[group, :, lanes] = join_halves(keys, values, right).astype(BF)
        wqp[group, :, 512:768] = w_qkv[:, 256 * group : 256 * group + 256]
    angles = [freq[:, 0:64] * pos[seq : seq + 1, :].astype(F32) for seq in range(2)]
    tab[...] = jnp.transpose(
        jnp.concatenate([turn(angle) for angle in angles for turn in (jnp.cos, jnp.sin)], axis=0)
    )
    for i in range(8):
        for group in range(4):
            at = 128 * (8 * group + i)
            upp[i, :, 128 * group : 128 * group + 128] = w_up[:, at : at + 128]
    all_here()
    zswap = Swap(head, blk, "head", lambda i: wqp.at[i], lambda i: wqz.at[i], zsem)
    zswap.start()
    line = Line(head, blk, tok, lambda i: tokg.at[i], lsem)
    tline = Line(head, blk, tab, lambda i: tabg.at[i], tsem)
    line.start()
    tline.start()
    uswap = Swap(head, blk, "blk", lambda i: upp.at[i], lambda i: upz.at[i], usem)
    oline = Reach(head, blk, out_own, lambda i: outz.at[i], osem)
    uline = Line(head, blk, upz, lambda i: up.at[i], usem2)
    dline = Line(head, blk, down_own, lambda i: down.at[i], dsem)
    oplane = Plane(head, blk, outz, lambda i: out.at[:, i], qsem)
    cplane = Plane(head, blk, cot_own, lambda i: cots.at[i], csem)
    everyone = Everyone(head, blk, lambda z, b: att.at[z, b], lambda z, b: received.at[z, b], esem)
    backward = Everyone(head, blk, lambda z, b: tsend.at[z, b], lambda z, b: grad_rx.at[z, b], fsem)
    turned[...] = jnp.transpose(ttab[...])
    rows = turned[pl.ds(pl.multiple_of((head * 8 + blk) * 8, 8), 8), :]
    step_lane = lax.broadcasted_iota(jnp.int32, rows.shape, 1)
    pieces = []
    for weight in (sca, scm):
        for seq in range(2):
            column = jnp.sum(jnp.where(step_lane == tix[seq], rows, 0.0), axis=1, keepdims=True)
            pieces.append(jnp.sum(column * weight[...].astype(F32), axis=0, keepdims=True))
    part[...] = jnp.concatenate(pieces + [jnp.zeros((4, 1024), F32)], axis=0)
    one = Swap(head, blk, "blk", lambda i: part, lambda i: sums_in.at[i], asem)
    one.start()
    uswap.start()
    sums_in[blk] = part[...]
    wqz[head] = wqp[head]
    tokg[head] = tok[...]
    tabg[head] = tab[...]
    upz[blk] = upp[blk]
    outz[head] = out_own[...]
    down[head] = down_own[...]
    cots[blk] = cot_own[...]
    one.arrive()
    total = sums_in[0]
    for i in range(1, 8):
        total = total + sums_in[i]
    parts[head] = total
    two = Swap(head, blk, "head", lambda i: parts.at[head], lambda i: parts.at[i], bsem)
    two.start()
    zswap.arrive()
    plane = Plane(head, blk, wqz, lambda i: wq.at[:, i], wsem)
    plane.start()
    wq[:, pl.ds(blk, 1)] = wqz[...].reshape(4, 1, 32, 768)
    two.arrive()
    total = 1.0 + ((parts[0] + parts[1]) + (parts[2] + parts[3]))
    scales[...] = total

    def gather(step, carry):
        at = line_order(head, step)

        @pl.when(step > 0)
        def _():
            line.step(at)
            tline.step(at)

        for seq in range(2):
            unit, _ = norm_stats(tokg[at, seq].astype(F32))
            normed[at, pl.ds(64 * seq, 64), :] = (unit * scales[seq : seq + 1, :]).astype(BF)
        return carry

    def project(step, carry):
        at = line_order(head, step)
        proj = jnp.dot(
            normed[at], wq[...].reshape(1024, 768), preferred_element_type=F32
        )
        for seq in range(2):
            table = tabg[at]
            if seq:
                table = pltpu.roll(table, 64, 1)
            both, keyed = turn_tables(table, 1.0)
            mine = proj[64 * seq : 64 * seq + 64]
            for j in range(4):
                kv = mine[:, 128 * j : 128 * j + 128]
                kv = kv * keyed[0] + lane_swap(kv) * keyed[1]
                out_tiles[4 * seq + j, at, 0:64, :] = kv.astype(BF)
            for i in range(2):
                query = mine[:, 512 + 128 * i : 640 + 128 * i]
                query = query * both[0] + lane_swap(query) * both[1]
                for right in range(2):
                    packed = join_halves(query[:32], query[32:], right)
                    out_tiles[4 * seq + 2 * i + right, at, 64:96, :] = packed.astype(BF)
        move(at).start()
        tiles[at, blk] = out_tiles[blk, at]
        return carry

    def move(at):
        return Swap(
            head, blk, "blk", lambda i: out_tiles.at[i, at], lambda i: tiles.at[at, i], psem.at[at]
        )

    lax.fori_loop(0, 3, gather, 0)
    oline.start()
    plane.finish()
    lax.fori_loop(0, 3, project, 0)

    def last(step, carry):
        gather(step, carry)
        return project(step, carry)

    lax.fori_loop(3, 4, last, 0)
    uswap.arrive()
    up[head] = upz[...]
    uline.start()
    oline.forward()
    oline.arrive()
    out[:, pl.ds(blk, 1)] = outz[...].reshape(4, 1, 32, 1024)
    for at in range(4):
        move(at).arrive()
    oplane.start()
    uline.hop(1)
    dline.start()
    kvt[...] = jnp.transpose(tiles[:, :, 0:64, :].reshape(2048, 128))

    def attend(step, carry):
        z = flip_by(head, 3 - step)
        flat = jnp.transpose(tiles[z, :, 64:96, :].reshape(256, 128).astype(F32))
        blank = jnp.zeros((64, 256), F32)
        results = []
        for side in range(2):
            query = jnp.concatenate([flat[64 * side : 64 * side + 64], blank], axis=0).astype(BF)
            top = None
            for c in range(2048 // KEYS):
                keys = tiles[c // 2, 4 * (c % 2) : 4 * (c % 2) + 4, 0:64, :].reshape(KEYS, 128)
                part = jnp.dot(keys, query, preferred_element_type=F32)
                scores[c] = part
                peak = jnp.max(part.reshape(KEYS // 8, 8, 256), axis=0)
                top = peak if top is None else jnp.maximum(top, peak)
            top = jnp.max(top, axis=0, keepdims=True)
            total = jnp.zeros((8, 256), F32)
            mix = jnp.zeros((64, 256), F32)
            for c in range(2048 // KEYS):
                weights = jnp.exp2((scores[c] - top) * EXP_SCALE)
                total = total + group_rows(weights)
                mix = mix + jnp.dot(
                    kvt[64:128, KEYS * c : KEYS * c + KEYS],
                    weights.astype(BF),
                    preferred_element_type=F32,
                )
            total = jnp.sum(total, axis=0, keepdims=True)
            mix = mix / total
            mixed[z, 64 * side : 64 * side + 64, :] = mix
            lse[z, side : side + 1, :] = top * SCORE_SCALE + jnp.log(total)
            results.append(mix)
        both = jnp.transpose(jnp.concatenate(results, axis=0))
        att[z] = both.astype(BF).reshape(8, 32, 128)
        everyone.start(3 - step)

        @pl.when(step == 1)
        def _():
            cplane.start()

        @pl.when(step == 2)
        def _():
            uline.hop(2)
            dline.hop(1)
            for i in range(3):
                oplane.forward(i)

        return carry

    lse[...] = jnp.zeros_like(lse)
    lax.fori_loop(0, 4, attend, 0)
    received[head, blk] = att[head, blk]
    for i in range(-1, 3):
        oplane.arrive(i)
    middle[...] = tok[...].astype(F32).reshape(128, 1024)
    for kz in range(4):
        group = flip(head, kz)
        everyone.arrive(kz)
        for seq in range(2):
            for i in range(2):
                first = received[group, 4 * seq + 2 * i].astype(F32)
                second = received[group, 4 * seq + 2 * i + 1].astype(F32)
                lanes = slice(128 * i, 128 * i + 128)
                for right in range(2):
                    at = slice(64 * seq + 32 * right, 64 * seq + 32 * right + 32)
                    attended[group, at, lanes] = join_halves(first, second, right).astype(BF)
        middle[...] += jnp.dot(
            attended[group], out[group].reshape(256, 1024), preferred_element_type=F32
        )
    for seq in range(2):
        rows = slice(64 * seq, 64 * seq + 64)
        unit, _ = norm_stats(middle[rows, :])
        n2g[blk, rows, :] = (unit * scales[2 + seq : 3 + seq, :]).astype(BF)
    nplane = Split(
        head, blk, n2g.at[blk], lambda i: n2g.at[i], lambda i, h: n2g.at[i, pl.ds(64 * h, 64)], nsem
    )
    for i in (1, 2, 0):
        nplane.first[i].start()
    uline.hop(3)
    dline.hop(2)
    cplane.finish()
    dline.hop(3)
    sibling = flip(blk, 1)

    def halves(i):
        return [
            send(pairs.at[w, i, 1 - core], prx.at[w, i], ssem.at[0, w, i], ssem.at[1, w, i], head, sibling)
            for w in range(2)
        ]

    def onward(i):
        peer = flip(blk, 2 * i)
        return send(gsend.at[i], gin.at[i], gsem.at[0, i], gsem.at[1, i], head, peer)

    def reduce(i):
        chip = lax.div(flip(blk, 2 * i), 2)
        for copy in halves(i):
            copy.wait_recv()
        gsend[i] = (pairs[0, i, core].astype(F32) + prx[0, i].astype(F32)).astype(BF)
        if i:
            onward(i).start()
        outq[chip] = (pairs[1, i, core].astype(F32) + prx[1, i].astype(F32)).astype(BF)

    for i in range(4):
        chip = lax.div(flip(blk, 2 * i), 2)
        if i == 0:
            nplane.arrive(-1)
        else:
            if i == 1:
                nplane.forward(0)
                nplane.forward(1)
            elif i == 3:
                nplane.forward(2)
            if i > 1:
                reduce(i - 1)
            nplane.arrive(i - 1)
        at = pl.ds(2 * chip, 2)
        rows = n2g[at].reshape(256, 1024)
        hidden = jnp.dot(rows, up[...].reshape(1024, 512), preferred_element_type=F32)
        grad_active = contract_cols(cots[at].reshape(256, 1024), down[...].reshape(512, 1024))
        cdf = 0.5 * (1.0 + lax.erf(hidden * math.sqrt(0.5)))
        active = (hidden * cdf).astype(BF)
        slope = cdf + hidden * jnp.exp(-0.5 * hidden * hidden) * (1.0 / math.sqrt(2 * math.pi))
        grad_hidden = (grad_active * slope).astype(BF)
        act[at] = active.reshape(2, 128, 512)
        gh[at] = grad_hidden.reshape(2, 128, 512)
        pairs[0, i] = (
            contract_cols(grad_hidden, up[...].reshape(1024, 512)).astype(BF).reshape(2, 128, 1024)
        )
        pairs[1, i] = (
            jnp.dot(active, down[...].reshape(512, 1024), preferred_element_type=F32)
            .astype(BF)
            .reshape(2, 128, 1024)
        )
        for copy in halves(i):
            copy.start()
    reduce(3)
    reduce(0)
    for group in range(4):
        lanes = slice(128 * group, 128 * group + 128)
        grad_down[group] = contract_rows(
            act[:, :, lanes].reshape(1024, 128), cots[...].reshape(1024, 1024)
        ).astype(BF)
    for group in range(4):
        lanes = slice(256 * group, 256 * group + 256)
        value = contract_rows(n2g[:, :, lanes].reshape(1024, 256), gh[...].reshape(1024, 512))
        grad_up[group] = value.astype(BF).reshape(8, 32, 512)
    uswap_r = Fold(head, blk, grad_up, uvia, ujoin, uin, usem_r)
    dfold = Fold(head, blk, grad_down, dvia, djoin, din, dsem_r)
    folds = (uswap_r, dfold)
    for fold in folds:
        fold.start_far()
        fold.start_one(3)

        @pl.when(fold.middle)
        def _():
            fold.copy(1).start()

    for i in range(1, 4):
        onward(i).wait_recv()
    sums[...] = jnp.zeros_like(sums)
    for seq in range(2):
        rows = slice(64 * seq, 64 * seq + 64)
        grad = gsend[0, rows, :].astype(F32)
        for i in range(1, 4):
            grad = grad + gin[i, rows, :].astype(F32)
        unit, spread = norm_stats(middle[rows, :])
        whole_grad = cots[blk, rows, :].astype(F32) + norm_back(
            unit, spread, grad, scales[2 + seq : 3 + seq, :]
        )
        grad_middle[rows, :] = whole_grad
        branch[rows, :] = whole_grad.astype(BF)
        sums[seq : seq + 1, :] = jnp.sum(grad * unit, axis=0, keepdims=True)

    def give(step, carry):
        group = flip_by(head, 3 - step)
        value = contract_cols(branch[...], out[group].reshape(256, 1024))
        for seq in range(2):
            for i in range(2):
                lanes = slice(128 * i, 128 * i + 128)
                top = value[64 * seq : 64 * seq + 32, lanes]
                bottom = value[64 * seq + 32 : 64 * seq + 64, lanes]
                for right in range(2):
                    tsend[group, 4 * seq + 2 * i + right] = join_halves(top, bottom, right).astype(BF)
        backward.start(3 - step)
        return carry

    lax.fori_loop(0, 4, give, 0)
    grad_rx[head, blk] = tsend[head, blk]
    for group in range(4):
        value = contract_rows(attended[group], branch[...])
        grad_out[group] = value.astype(BF).reshape(4, 2, 32, 1024)
    scatter = Scatter(head, blk, grad_out, near, joined, far, osem_r)
    scatter.start()
    outs = []
    for i in range(1, 4):
        peer = flip(blk, 2 * i)
        outs.append(
            send(outq.at[lax.div(peer, 2)], oin.at[i], qsem_r.at[0, i], qsem_r.at[1, i], head, peer)
        )
    vswap = Swap(head, blk, "blk", lambda i: usum.at[i], lambda i: up_own.at[i], vsem)
    xswap = Swap(head, blk, "head", lambda i: osum.at[i], lambda i: zin.at[i], xsem)
    left = half_lane((256, 128))
    keyt[...] = jnp.transpose(tiles[:, :, 0:64, :].reshape(2048, 128))[:64]

    def prepare(z, carry):
        flat = tiles[z, :, 64:96, :].reshape(256, 128).astype(F32)
        grad = grad_rx[z].reshape(256, 128).astype(F32)
        product = jnp.transpose(grad) * mixed[z]
        queries[2 * z] = jnp.where(left, flat, 0.0).astype(BF)
        queries[2 * z + 1] = jnp.where(left, pltpu.roll(flat, 64, 1), 0.0).astype(BF)
        turned = jnp.transpose(flat)
        slopes = jnp.transpose(grad)
        blank = jnp.zeros((64, 256), F32)
        for side in range(2):
            rows = slice(64 * side, 64 * side + 64)
            queries_t[2 * z + side] = jnp.concatenate([turned[rows], blank], axis=0).astype(BF)
            grads_t[2 * z + side] = jnp.concatenate([blank, slopes[rows]], axis=0).astype(BF)
        grads[2 * z] = jnp.where(left, 0.0, pltpu.roll(grad, 64, 1)).astype(BF)
        grads[2 * z + 1] = jnp.where(left, 0.0, grad).astype(BF)
        for side in range(2):
            delta = jnp.sum(product[64 * side : 64 * side + 64], axis=0, keepdims=True)
            shift = lse[z, side : side + 1, :] * math.log2(math.e)
            stats[2 * z + side] = jnp.concatenate([shift, delta, jnp.zeros((6, 256), F32)], axis=0)
        return carry

    def ready(kz, carry):
        backward.arrive(kz)
        return prepare(flip_by(head, kz), carry)

    scatter.join()
    lax.fori_loop(0, 4, ready, 0)
    dqt[...] = jnp.zeros_like(dqt)

    def kv_move(z):
        return Swap(
            head,
            blk,
            "blk",
            lambda i: bsend.at[i, z, pl.ds(0, 64)],
            lambda i: back.at[i, z, pl.ds(0, 64)],
            bsem_r.at[z],
        )

    def keys_step(z, carry):
        dkv[...] = jnp.zeros_like(dkv)

        def query_step(q, inner):
            query, grad = queries[q], grads[q]
            query_t, grad_t = queries_t[q], grads_t[q]
            shift, delta = stats[q, 0:1, :], stats[q, 1:2, :]
            dq = dqt[q]
            for c in range(2):
                keys = tiles[z, 4 * c : 4 * c + 4, 0:64, :].reshape(256, 128)
                probs = jnp.dot(keys, query_t, preferred_element_type=F32)
                probs = jnp.exp2(probs * EXP_SCALE - shift)
                slopes = jnp.dot(keys, grad_t, preferred_element_type=F32)
                slopes = (probs * (slopes - delta)).astype(BF)
                dkv[c] += jnp.dot(slopes, query, preferred_element_type=F32) + jnp.dot(
                    probs.astype(BF), grad, preferred_element_type=F32
                )
                at = pl.ds(pl.multiple_of(512 * z + 256 * c, 256), 256)
                dq = dq + jnp.dot(keyt[:, at], slopes, preferred_element_type=F32)
            dqt[q] = dq
            return inner

        lax.fori_loop(0, 8, query_step, 0, unroll=4)
        scale = jnp.where(left, SCORE_SCALE, 1.0)
        for c in range(2):
            bsend[4 * c : 4 * c + 4, pl.ds(z, 1), 0:64, :] = (
                (dkv[c] * scale).astype(BF).reshape(4, 1, 64, 128)
            )
        kv_move(z).start()

        @pl.when(z == 0)
        def _():
            for fold in folds:
                fold.start_one(2)

        @pl.when(z == 1)
        def _():
            for fold in folds:
                fold.relay()
            for copy in outs:
                copy.start()

        @pl.when(z == 2)
        def _():
            for fold in folds:

                @pl.when(jnp.logical_not(fold.middle))
                def _():
                    fold.copy(1).start()

            osum[...] = scatter.total().astype(BF)
            xswap.start()
            zin[head] = osum[head]

        return carry

    lax.fori_loop(0, 4, keys_step, 0)
    for z in range(4):
        both = jnp.concatenate([dqt[2 * z], dqt[2 * z + 1]], axis=0)
        both = (jnp.transpose(both) * SCORE_SCALE).astype(BF)
        bsend[:, z, 64:96, :] = both.reshape(8, 32, 128)
    qmove = Swap(
        head,
        blk,
        "blk",
        lambda i: bsend.at[i, :, pl.ds(64, 32)],
        lambda i: back.at[i, :, pl.ds(64, 32)],
        bsem_r.at[4],
    )
    qmove.start()
    back[blk] = bsend[blk]
    picked = turned[pl.ds(pl.multiple_of((head * 8 + blk) * 8, 8), 8), :]
    step_lane = lax.broadcasted_iota(jnp.int32, picked.shape, 1)
    columns = [
        jnp.sum(jnp.where(step_lane == tix[seq], picked, 0.0), axis=1, keepdims=True)
        for seq in range(2)
    ]
    for z in range(4):
        kv_move(z).arrive()
    qmove.arrive()
    gswap = Fold(head, blk, gnp, gvia, gjoin, gin_r, gsem_r)

    def unturn(step, carry):
        at = flip(head, step)
        for seq in range(2):
            table = tabg[at]
            if seq:
                table = pltpu.roll(table, 64, 1)
            both, keyed = turn_tables(table, -1.0)
            rows = slice(64 * seq, 64 * seq + 64)
            for j in range(4):
                kv = back[4 * seq + j, at, 0:64, :].astype(F32)
                kv = kv * keyed[0] + lane_swap(kv) * keyed[1]
                gp[at, rows, 128 * j : 128 * j + 128] = kv.astype(BF)
            for i in range(2):
                first = back[4 * seq + 2 * i, at, 64:96, :].astype(F32)
                second = back[4 * seq + 2 * i + 1, at, 64:96, :].astype(F32)
                query = jnp.concatenate(
                    [join_halves(first, second, 0), join_halves(first, second, 1)], axis=0
                )
                query = query * both[0] + lane_swap(query) * both[1]
                gp[at, rows, 512 + 128 * i : 640 + 128 * i] = query.astype(BF)
        return carry

    for step in (3, 2, 1, 0):
        unturn(step, 0)
    for group in range(4):
        lanes = slice(256 * group, 256 * group + 256)
        value = contract_rows(normed[:, :, lanes].reshape(512, 256), gp[...].reshape(512, 768))
        terms[group] = value.astype(BF).reshape(4, 2, 32, 768)
    scatter_q = Scatter(head, blk, terms, near_q, joined_q, far_q, osem_q)
    scatter_q.start()
    for step in (3, 2, 1, 0):
        at = flip(head, step)
        gnp[at] = contract_cols(gp[at], wq[...].reshape(1024, 768)).astype(BF)
        if step == 3:
            gswap.start_far()
            gswap.start_one(3)
    scatter_q.join()
    part_r[...] = jnp.concatenate(
        [jnp.zeros((2, 1024), F32), sums[0:2, :], jnp.zeros((4, 1024), F32)], axis=0
    )

    def gather_r(at, carry):
        for seq in range(2):
            unit, _ = norm_stats(tokg[at, seq].astype(F32))
            part_r[seq : seq + 1, :] += jnp.sum(
                gnp[at, pl.ds(64 * seq, 64), :].astype(F32) * unit, axis=0, keepdims=True
            )
        return carry

    lax.fori_loop(0, 4, gather_r, 0)
    one_r = Swap(head, blk, "blk", lambda i: part_r, lambda i: sums_in_r.at[i], asem_r)
    one_r.start()
    sums_in_r[blk] = part_r[...]
    gswap.start_one(2)
    gswap.relay()
    gswap.start_one(1)
    uswap_r.arrive()
    usum[...] = sum_four(uin).astype(BF)
    vswap.start()
    up_own[blk] = usum[blk]
    one_r.arrive()
    total = sums_in_r[0]
    for i in range(1, 8):
        total = total + sums_in_r[i]
    parts_r[head] = total
    two_r = Swap(head, blk, "head", lambda i: parts_r.at[head], lambda i: parts_r.at[i], csem_r)
    two_r.start()
    total = middle[...] + outq[lax.div(blk, 2)].astype(F32)
    for i in range(1, 4):
        outs[i - 1].wait_recv()
        total = total + oin[i].astype(F32)
    output[...] = total.astype(BF)
    dfold.arrive()
    g_down[...] = sum_four(din)
    osum_q[...] = scatter_q.total().astype(BF)
    xswap_q = Swap(head, blk, "head", lambda i: osum_q.at[i], lambda i: gq.at[i], xsem_q)
    xswap_q.start()
    gq[head] = osum_q[head]
    xswap.arrive()
    g_out[...] = sum_four(zin)
    two_r.arrive()
    total = (parts_r[0] + parts_r[1]) + (parts_r[2] + parts_r[3])
    grad_attn[...] = columns[0] * total[0:1] + columns[1] * total[1:2]
    grad_mlp[...] = columns[0] * total[2:3] + columns[1] * total[3:4]
    gswap.arrive()
    for seq in range(2):
        rows = slice(64 * seq, 64 * seq + 64)
        grad = sum_four([gin_r[i, rows, :] for i in range(4)])
        unit, spread = norm_stats(tokg[head, seq].astype(F32))
        grad_tokens[rows, :] = grad_middle[rows, :] + norm_back(
            unit, spread, grad, scales[seq : seq + 1, :]
        )
    vswap.arrive()
    for i in range(8):
        for group in range(4):
            at = 128 * (8 * group + i)
            g_up[:, at : at + 128] = up_own[i, :, 128 * group : 128 * group + 128].astype(F32)
    xswap_q.arrive()
    for group in range(4):
        for i in range(2):
            first = gq[group, :, 256 * i : 256 * i + 128].astype(F32)
            second = gq[group, :, 256 * i + 128 : 256 * i + 256].astype(F32)
            at = 256 * group + 128 * i
            for right in range(2):
                lanes = slice(1024 + 1024 * right + at, 1152 + 1024 * right + at)
                g_qkv[:, lanes] = join_halves(first, second, right)
        g_qkv[:, 256 * group : 256 * group + 256] = gq[group, :, 512:768].astype(F32)
    for z in range(4):
        kv_move(z).drain()
    for copy in outs:
        copy.wait_send()
    for copies in (
        scatter, uswap_r, dfold, vswap, xswap, qmove, gswap, scatter_q, xswap_q, one_r, two_r
    ):
        copies.drain()
    for at in range(4):
        move(at).drain()
    for i in range(4):
        for copy in halves(i):
            copy.wait_send()
        if i:
            onward(i).wait_send()
    for copies in (
        zswap, line, tline, plane, one, two, uswap, oline,
        uline, dline, oplane, cplane, everyone, nplane, backward,
    ):
        copies.drain()


def whole(count):
    return [pl.BlockSpec(memory_space=pltpu.VMEM)] * count


def layer(*operands):
    dma = pltpu.SemaphoreType.DMA
    shape = jax.ShapeDtypeStruct
    return pl.pallas_call(
        layer_kernel,
        out_shape=(
            shape((128, 1024), BF),
            shape((128, 1024), F32),
            shape((32, 3072), F32),
            shape((32, 1024), F32),
            shape((32, 4096), F32),
            shape((128, 1024), F32),
            shape((8, 1024), F32),
            shape((8, 1024), F32),
        ),
        in_specs=whole(11) + [pl.BlockSpec(memory_space=pltpu.SMEM)],
        out_specs=whole(8),
        scratch_shapes=[
            pltpu.VMEM((64, 128), F32),
            pltpu.VMEM((4, 32, 768), BF),
            pltpu.VMEM((8, 32, 512), BF),
            pltpu.VMEM((4, 32, 768), BF),
            pltpu.VMEM((8, 32, 512), BF),
            pltpu.VMEM((4, 8, 96, 128), BF),
            pltpu.VMEM((4, 128, 1024), BF),
            pltpu.VMEM((4, 8, 32, 768), BF),
            pltpu.VMEM((8, 1024), F32),
            pltpu.VMEM((4, 64, 128), F32),
            pltpu.VMEM((4, 2, 64, 1024), BF),
            pltpu.VMEM((4, 128, 256), F32),
            pltpu.VMEM((4, 8, 256), F32),
            pltpu.VMEM((4, 8, 32, 128), BF),
            pltpu.VMEM((128, 1024), F32),
            pltpu.VMEM((128, 1024), F32),
            pltpu.VMEM((4, 128, 1024), BF),
            pltpu.VMEM((4, 128, 1024), BF),
            pltpu.VMEM((4, 8, 32, 512), BF),
            pltpu.VMEM((4, 4, 2, 32, 1024), BF),
            pltpu.VMEM((8, 1024), F32),
            pltpu.VMEM((4, 32, 768), BF),
            pltpu.VMEM((256, 64), F32),
            pltpu.VMEM((8, 1024), F32),
            pltpu.VMEM((8, 8, 1024), F32),
            pltpu.VMEM((4, 8, 1024), F32),
            pltpu.VMEM((8, 4, 96, 128), BF),
            pltpu.VMEM((8, 32, 512), BF),
            pltpu.VMEM((4, 32, 1024), BF),
            pltpu.VMEM((4, 8, 32, 512), BF),
            pltpu.VMEM((4, 128, 1024), BF),
            pltpu.VMEM((4, 8, 32, 1024), BF),
            pltpu.VMEM((8, 128, 1024), BF),
            pltpu.VMEM((128, 2048), BF),
            pltpu.VMEM((2048 // KEYS, KEYS, 256), F32),
            pltpu.VMEM((4, 8, 32, 128), BF),
            pltpu.VMEM((4, 8, 32, 128), BF),
            pltpu.VMEM((4, 128, 256), BF),
            pltpu.VMEM((8, 128, 1024), BF),
            pltpu.VMEM((8, 128, 512), BF),
            pltpu.VMEM((8, 128, 512), BF),
            pltpu.VMEM((2, 4, 2, 128, 1024), BF),
            pltpu.VMEM((2, 4, 128, 1024), BF),
            pltpu.VMEM((4, 128, 1024), BF),
            pltpu.VMEM((4, 128, 1024), BF),
            pltpu.VMEM((4, 8, 32, 128), BF),
            pltpu.VMEM((128, 1024), BF),
            pltpu.VMEM((8, 256, 128), BF),
            pltpu.VMEM((8, 256, 128), BF),
            pltpu.VMEM((8, 128, 256), BF),
            pltpu.VMEM((8, 128, 256), BF),
            pltpu.VMEM((8, 8, 256), F32),
            pltpu.VMEM((64, 2048), BF),
            pltpu.VMEM((2, 256, 128), F32),
            pltpu.VMEM((8, 64, 256), F32),
            pltpu.VMEM((8, 4, 96, 128), BF),
            pltpu.VMEM((8, 4, 96, 128), BF),
            pltpu.VMEM((4, 128, 1024), BF),
            pltpu.VMEM((4, 128, 1024), BF),
            pltpu.VMEM((128, 1024), BF),
            pltpu.VMEM((128, 1024), BF),
            pltpu.VMEM((4, 8, 32, 512), BF),
            pltpu.VMEM((8, 32, 512), BF),
            pltpu.VMEM((8, 32, 512), BF),
            pltpu.VMEM((8, 32, 512), BF),
            pltpu.VMEM((4, 4, 32, 1024), BF),
            pltpu.VMEM((4, 4, 32, 1024), BF),
            pltpu.VMEM((4, 4, 32, 1024), BF),
            pltpu.VMEM((4, 32, 1024), BF),
            pltpu.VMEM((4, 32, 1024), BF),
            pltpu.VMEM((4, 128, 768), BF),
            pltpu.VMEM((4, 128, 1024), BF),
            pltpu.VMEM((128, 1024), BF),
            pltpu.VMEM((128, 1024), BF),
            pltpu.VMEM((4, 128, 1024), BF),
            pltpu.VMEM((4, 4, 2, 32, 768), BF),
            pltpu.VMEM((4, 4, 32, 768), BF),
            pltpu.VMEM((4, 4, 32, 768), BF),
            pltpu.VMEM((4, 4, 32, 768), BF),
            pltpu.VMEM((4, 32, 768), BF),
            pltpu.VMEM((8, 1024), F32),
            pltpu.VMEM((8, 8, 1024), F32),
            pltpu.VMEM((4, 8, 1024), F32),
            dma((2, 4)),
            dma((2, 2, 3)),
            dma((2, 2, 3)),
            dma((2, 8)),
            dma((2, 8)),
            dma((2, 4)),
            dma((4, 2, 8)),
            dma((2, 8)),
            dma((2, 4)),
            dma((2, 2, 3)),
            dma((2, 2, 3)),
            dma((2, 8)),
            dma((2, 8)),
            dma((2, 4, 8)),
            dma((2, 8)),
            dma((2, 2, 4)),
            dma((2, 4)),
            dma((2, 4, 8)),
            dma((2, 4)),
            dma((2, 4)),
            dma((2, 4)),
            dma((2, 8)),
            dma((2, 4)),
            dma((2, 4)),
            dma((5, 2, 8)),
            dma((2, 4)),
            dma((2, 4)),
            dma((2, 4)),
            dma((2, 8)),
            dma((2, 4)),
        ],
        compiler_params=pltpu.CompilerParams(
            collective_id=0, has_side_effects=True, vmem_limit_bytes=VMEM_LIMIT
        ),
        name="layer",
    )(*operands)


def finish_kernel(*refs):
    count = (len(refs) - 1) // 3
    sems = refs[-1]
    arrive = [
        pltpu.make_async_copy(refs[i], refs[2 * count + i], sems.at[0, i]) for i in range(count)
    ]
    leave = [
        pltpu.make_async_copy(refs[2 * count + i], refs[count + i], sems.at[1, i])
        for i in range(count)
    ]
    for copy in arrive:
        copy.start()
    for i in range(count):
        arrive[i].wait()
        leave[i].start()
    for copy in leave:
        copy.wait()


def finish(results):
    spec = [pl.BlockSpec(memory_space=pl.ANY)] * len(results)
    return pl.pallas_call(
        finish_kernel,
        out_shape=tuple(jax.ShapeDtypeStruct(x.shape, x.dtype) for x in results),
        in_specs=spec,
        out_specs=spec,
        scratch_shapes=[pltpu.VMEM(x.shape, x.dtype) for x in results]
        + [pltpu.SemaphoreType.DMA((2, len(results)))],
        name="finish",
    )(*results)


def blocked(
    tokens,
    positions,
    time_index,
    time_table,
    w_qkv,
    w_out,
    w_up,
    w_down,
    scale_attn,
    scale_mlp,
    cotangent,
):
    half_dim = HEAD_DIM // 2
    frequency = 10000.0 ** (-jnp.arange(half_dim, dtype=jnp.float32) / half_dim)
    results = layer(
        tokens,
        positions,
        jnp.broadcast_to(frequency[:, None], (half_dim, 128)),
        w_qkv,
        time_table,
        scale_attn,
        scale_mlp,
        w_up,
        w_out,
        w_down,
        cotangent.reshape(128, 1024),
        time_index,
    )
    output, grad_tokens, *others = finish(results)
    return (output.reshape(2, 64, 1024), grad_tokens.reshape(2, 64, 1024), *others)


def solution(mesh):
    fits = mesh.shape["head"] == 4 and mesh.shape["blk"] == 8
    placed = (
        P(None, ("head", "blk"), None),
        P(None, ("head", "blk")),
        P(),
        P(),
        P(("head", "blk"), None),
        P(("head", "blk"), None),
        P(("head", "blk"), None),
        P(("head", "blk"), None),
        P(("head", "blk"), None),
        P(("head", "blk"), None),
        P(None, ("head", "blk"), None),
    )
    return jax.shard_map(
        blocked if fits else general,
        mesh=mesh,
        in_specs=placed,
        out_specs=(
            P(None, ("head", "blk"), None),
            P(None, ("head", "blk"), None),
            P(("head", "blk"), None),
            P(("head", "blk"), None),
            P(("head", "blk"), None),
            P(("head", "blk"), None),
            P(("head", "blk"), None),
            P(("head", "blk"), None),
        ),
        check_vma=False,
    )
```

```python
import math

import jax
import jax.numpy as jnp
from jax import lax
from jax.experimental import pallas as pl
from jax.experimental.pallas import tpu as pltpu
from jax.sharding import PartitionSpec as P

HEADS = 16
HEAD_DIM = 64


NORM_EPSILON = 1e-05
PRECISE = lax.Precision.HIGHEST
START_TOP = -1e30
SCORE_SCALE = 0.125


def shifted(value, axis, steps):
    count = lax.axis_size(axis)
    pairs = [(source, (source + steps) % count) for source in range(count)]
    return lax.ppermute(value, axis, pairs)


def layer_norm(value, scale):
    centered = value - jnp.mean(value, axis=-1, keepdims=True)
    variance = jnp.mean(centered * centered, axis=-1, keepdims=True)
    return centered * lax.rsqrt(variance + NORM_EPSILON) * scale


def rotate(value, cosine_table, sine_table):
    half_dim = value.shape[-1] // 2
    first_half = value[..., :half_dim]
    second_half = value[..., half_dim:]
    return jnp.concatenate(
        [
            first_half * cosine_table - second_half * sine_table,
            second_half * cosine_table + first_half * sine_table,
        ],
        axis=-1,
    )


def rotary_tables(positions, head_dim):
    half_dim = head_dim // 2
    frequency = 10000.0 ** (-jnp.arange(half_dim, dtype=jnp.float32) / half_dim)
    turned = positions.astype(jnp.float32)[:, :, None, None] * frequency
    return (jnp.cos(turned), jnp.sin(turned))


def contract_rows(left, right):
    return lax.dot_general(
        left, right, (((0,), (0,)), ((), ())), preferred_element_type=jnp.float32
    )


def contract_cols(left, right):
    return lax.dot_general(
        left, right, (((1,), (1,)), ((), ())), preferred_element_type=jnp.float32
    )


def attend_step(running, query_block, key_block, value_block):
    row_top, row_sum, accum = running
    scores = (
        jnp.einsum("sqhd,skhd->sqhk", query_block, key_block, preferred_element_type=jnp.float32)
        * SCORE_SCALE
    )
    new_top = jnp.maximum(row_top, jnp.max(scores, axis=-1))
    shrink = jnp.exp(row_top - new_top)
    weights = jnp.exp(scores - new_top[..., None])
    row_sum = row_sum * shrink + jnp.sum(weights, axis=-1)
    accum = accum * shrink[..., None] + jnp.einsum(
        "sqhk,skhd->sqhd",
        weights.astype(jnp.bfloat16),
        value_block,
        preferred_element_type=jnp.float32,
    )
    return (new_top, row_sum, accum)


def back_step(query_block, key_block, value_block, grad_block, log_total, delta):
    scores = (
        jnp.einsum("sqhd,skhd->sqhk", query_block, key_block, preferred_element_type=jnp.float32)
        * SCORE_SCALE
    )
    probs = jnp.exp(scores - log_total[..., None])
    grad_values = jnp.einsum(
        "sqhk,sqhd->skhd",
        probs.astype(jnp.bfloat16),
        grad_block,
        preferred_element_type=jnp.float32,
    )
    grad_probs = jnp.einsum(
        "sqhd,skhd->sqhk", grad_block, value_block, preferred_element_type=jnp.float32
    )
    grad_scores = (probs * (grad_probs - delta[..., None])).astype(jnp.bfloat16)
    grad_query = jnp.einsum(
        "sqhk,skhd->sqhd", grad_scores, key_block, preferred_element_type=jnp.float32
    )
    grad_keys = jnp.einsum(
        "sqhk,sqhd->skhd", grad_scores, query_block, preferred_element_type=jnp.float32
    )
    return (grad_query, grad_keys, grad_values)


def general(
    tokens,
    positions,
    time_index,
    time_table,
    w_qkv,
    w_out,
    w_up,
    w_down,
    scale_attn,
    scale_mlp,
    cotangent,
):
    seq_count, row_count, model_width = tokens.shape
    group_count = lax.axis_size("head")
    local_heads = HEADS // group_count
    feature_width = local_heads * HEAD_DIM
    flat_rows = seq_count * row_count
    gathered = (
        lax.all_gather(w_qkv, ("head", "blk"), axis=0, tiled=True),
        lax.all_gather(w_out, ("head", "blk"), axis=0, tiled=True),
        lax.all_gather(w_up, ("head", "blk"), axis=0, tiled=True),
        lax.all_gather(w_down, ("head", "blk"), axis=0, tiled=True),
        lax.all_gather(scale_attn, ("head", "blk"), axis=0, tiled=True),
        lax.all_gather(scale_mlp, ("head", "blk"), axis=0, tiled=True),
    )
    full_qkv, full_out, full_up, full_down, full_scale_attn, full_scale_mlp = gathered
    step_count = time_table.shape[0]
    picker = (time_index[:, None] == jnp.arange(step_count, dtype=jnp.int32)[None, :]).astype(
        jnp.float32
    )
    time_embed = jnp.dot(picker, time_table, precision=PRECISE)
    scale_one = 1.0 + jnp.dot(time_embed, full_scale_attn.astype(jnp.float32), precision=PRECISE)
    scale_two = 1.0 + jnp.dot(time_embed, full_scale_mlp.astype(jnp.float32), precision=PRECISE)
    token_float = tokens.astype(jnp.float32)
    normed = (
        layer_norm(token_float, scale_one[:, None, :])
        .astype(jnp.bfloat16)
        .reshape(flat_rows, model_width)
    )
    projected = jnp.dot(normed, full_qkv, preferred_element_type=jnp.float32).reshape(
        seq_count, row_count, 3, HEADS, HEAD_DIM
    )
    cosine_table, sine_table = rotary_tables(positions, HEAD_DIM)
    query_tok = rotate(projected[:, :, 0], cosine_table, sine_table)
    keys_tok = rotate(projected[:, :, 1], cosine_table, sine_table)
    packed = (
        jnp.stack([query_tok, keys_tok, projected[:, :, 2]], axis=2)
        .reshape(seq_count, row_count, 3, model_width)
        .astype(jnp.bfloat16)
    )
    regrouped = lax.all_to_all(packed, "head", split_axis=3, concat_axis=1, tiled=True)
    block_len = regrouped.shape[1]
    local_query = regrouped[:, :, 0].reshape(seq_count, block_len, local_heads, HEAD_DIM)
    local_keys = regrouped[:, :, 1]
    local_values = regrouped[:, :, 2]
    start_state = (
        jnp.full((seq_count, block_len, local_heads), START_TOP, jnp.float32),
        jnp.zeros((seq_count, block_len, local_heads), jnp.float32),
        jnp.zeros((seq_count, block_len, local_heads, HEAD_DIM), jnp.float32),
    )
    key_piece = lax.all_gather(local_keys, "blk", axis=1, tiled=True)
    value_piece = lax.all_gather(local_values, "blk", axis=1, tiled=True)
    piece_len = key_piece.shape[1]
    step_len = math.gcd(piece_len, block_len)

    def one_block(index, state):
        key_block = lax.dynamic_slice_in_dim(key_piece, index * step_len, step_len, 1).reshape(
            seq_count, step_len, local_heads, HEAD_DIM
        )
        value_block = lax.dynamic_slice_in_dim(value_piece, index * step_len, step_len, 1).reshape(
            seq_count, step_len, local_heads, HEAD_DIM
        )
        return attend_step(state, local_query, key_block, value_block)

    row_top, row_sum, accum = lax.fori_loop(0, piece_len // step_len, one_block, start_state)
    mixed = accum / row_sum[..., None]
    log_total = row_top + jnp.log(row_sum)
    attended_heads = mixed.astype(jnp.bfloat16).reshape(seq_count, block_len, feature_width)
    attended = lax.all_to_all(
        attended_heads, "head", split_axis=1, concat_axis=2, tiled=True
    ).reshape(flat_rows, model_width)
    branch = jnp.dot(attended, full_out, preferred_element_type=jnp.float32)
    middle = token_float + branch.reshape(seq_count, row_count, model_width)
    normed_two = (
        layer_norm(middle, scale_two[:, None, :])
        .astype(jnp.bfloat16)
        .reshape(flat_rows, model_width)
    )
    hidden = jnp.dot(normed_two, full_up, preferred_element_type=jnp.float32)
    active = jax.nn.gelu(hidden, approximate=False).astype(jnp.bfloat16)
    result = middle.reshape(flat_rows, model_width) + jnp.dot(
        active, full_down, preferred_element_type=jnp.float32
    )
    output = result.astype(jnp.bfloat16).reshape(seq_count, row_count, model_width)
    back_qkv, back_out, back_up, back_down = (
        lax.all_gather(w_qkv, ("head", "blk"), axis=0, tiled=True),
        lax.all_gather(w_out, ("head", "blk"), axis=0, tiled=True),
        lax.all_gather(w_up, ("head", "blk"), axis=0, tiled=True),
        lax.all_gather(w_down, ("head", "blk"), axis=0, tiled=True),
    )
    grad_out = cotangent.reshape(flat_rows, model_width)
    grad_active = contract_cols(grad_out, back_down)
    grad_w_down = contract_rows(active, grad_out)
    gelu_value, gelu_pull = jax.vjp(lambda entry: jax.nn.gelu(entry, approximate=False), hidden)
    grad_hidden = gelu_pull(grad_active)[0].astype(jnp.bfloat16)
    grad_w_up = contract_rows(normed_two, grad_hidden)
    grad_normed_two = contract_cols(grad_hidden, back_up).reshape(seq_count, row_count, model_width)
    norm_value, norm_pull = jax.vjp(layer_norm, middle, scale_two[:, None, :])
    grad_middle_norm, grad_scale_two = norm_pull(grad_normed_two)
    grad_middle = cotangent.astype(jnp.float32) + grad_middle_norm
    grad_scale_mlp = jnp.dot(time_embed.T, grad_scale_two[:, 0, :], precision=PRECISE)
    grad_branch = grad_middle.reshape(flat_rows, model_width).astype(jnp.bfloat16)
    grad_w_out = contract_rows(attended, grad_branch)
    grad_attended = (
        contract_cols(grad_branch, back_out)
        .astype(jnp.bfloat16)
        .reshape(seq_count, row_count, model_width)
    )
    grad_heads = lax.all_to_all(
        grad_attended, "head", split_axis=2, concat_axis=1, tiled=True
    ).reshape(seq_count, block_len, local_heads, HEAD_DIM)
    delta = jnp.sum(grad_heads.astype(jnp.float32) * mixed, axis=-1)

    def turn(index, state):
        key_now, value_now, grad_keys_now, grad_values_now, grad_query_sum = state
        grad_query, grad_keys, grad_values = back_step(
            local_query,
            key_now.reshape(seq_count, block_len, local_heads, HEAD_DIM),
            value_now.reshape(seq_count, block_len, local_heads, HEAD_DIM),
            grad_heads,
            log_total,
            delta,
        )
        moved_keys, moved_values = shifted((key_now, value_now), "blk", 1)
        moved_grad_keys, moved_grad_values = (
            shifted(
                (grad_keys_now + grad_keys.reshape(seq_count, block_len, feature_width)).astype(
                    jnp.bfloat16
                ),
                "blk",
                1,
            ).astype(jnp.float32),
            shifted(
                (grad_values_now + grad_values.reshape(seq_count, block_len, feature_width)).astype(
                    jnp.bfloat16
                ),
                "blk",
                1,
            ).astype(jnp.float32),
        )
        return (
            moved_keys,
            moved_values,
            moved_grad_keys,
            moved_grad_values,
            grad_query_sum + grad_query,
        )

    zero_kv = jnp.zeros((seq_count, block_len, feature_width), jnp.float32)
    begin = (
        local_keys,
        local_values,
        zero_kv,
        zero_kv,
        jnp.zeros((seq_count, block_len, local_heads, HEAD_DIM), jnp.float32),
    )
    final_state = lax.fori_loop(0, lax.axis_size("blk"), turn, begin)
    grad_keys_own = final_state[2]
    grad_values_own = final_state[3]
    grad_query_all = final_state[4]
    stacked = jnp.stack(
        [
            grad_query_all.reshape(seq_count, block_len, feature_width) * SCORE_SCALE,
            grad_keys_own * SCORE_SCALE,
            grad_values_own,
        ],
        axis=2,
    ).astype(jnp.bfloat16)
    returned = lax.all_to_all(stacked, "head", split_axis=1, concat_axis=3, tiled=True)
    grad_query_tok = (
        returned[:, :, 0].astype(jnp.float32).reshape(seq_count, row_count, HEADS, HEAD_DIM)
    )
    grad_keys_tok = (
        returned[:, :, 1].astype(jnp.float32).reshape(seq_count, row_count, HEADS, HEAD_DIM)
    )
    grad_values_tok = (
        returned[:, :, 2].astype(jnp.float32).reshape(seq_count, row_count, HEADS, HEAD_DIM)
    )
    grad_projected = (
        jnp.stack(
            [
                rotate(grad_query_tok, cosine_table, -sine_table),
                rotate(grad_keys_tok, cosine_table, -sine_table),
                grad_values_tok,
            ],
            axis=2,
        )
        .reshape(flat_rows, 3 * model_width)
        .astype(jnp.bfloat16)
    )
    grad_w_qkv = contract_rows(normed, grad_projected)
    grad_normed = contract_cols(grad_projected, back_qkv).reshape(seq_count, row_count, model_width)
    first_value, first_pull = jax.vjp(layer_norm, token_float, scale_one[:, None, :])
    grad_token_norm, grad_scale_one = first_pull(grad_normed)
    grad_tokens = grad_middle + grad_token_norm
    grad_scale_attn = jnp.dot(time_embed.T, grad_scale_one[:, 0, :], precision=PRECISE)
    shards = (
        lax.psum_scatter(grad_w_qkv, ("head", "blk"), scatter_dimension=0, tiled=True),
        lax.psum_scatter(grad_w_out, ("head", "blk"), scatter_dimension=0, tiled=True),
        lax.psum_scatter(grad_w_up, ("head", "blk"), scatter_dimension=0, tiled=True),
        lax.psum_scatter(grad_w_down, ("head", "blk"), scatter_dimension=0, tiled=True),
        lax.psum_scatter(grad_scale_attn, ("head", "blk"), scatter_dimension=0, tiled=True),
        lax.psum_scatter(grad_scale_mlp, ("head", "blk"), scatter_dimension=0, tiled=True),
    )
    return (output, grad_tokens, shards[0], shards[1], shards[2], shards[3], shards[4], shards[5])


EPS = NORM_EPSILON
BF = jnp.bfloat16
F32 = jnp.float32


def norm_stats(value):
    centered = value - jnp.mean(value, axis=-1, keepdims=True)
    spread = lax.rsqrt(jnp.mean(centered * centered, axis=-1, keepdims=True) + EPS)
    return centered * spread, spread


def norm_back(unit, spread, grad, scale):
    scaled = grad * scale
    return spread * (
        scaled
        - jnp.mean(scaled, axis=-1, keepdims=True)
        - unit * jnp.mean(scaled * unit, axis=-1, keepdims=True)
    )


MESH = pl.DeviceIdType.MESH


def flip(value, bits):
    for bit in (1, 2, 4):
        if bits & bit:
            value = value + bit - 2 * bit * lax.rem(lax.div(value, bit), 2)
    return value


def greet(head, blk, heads, blks):
    barrier = pltpu.get_barrier_semaphore()
    for k in heads:
        pl.semaphore_signal(barrier, inc=1, device_id=(flip(head, k), blk), device_id_type=MESH)
    for k in blks:
        pl.semaphore_signal(barrier, inc=1, device_id=(head, flip(blk, k)), device_id_type=MESH)
    pl.semaphore_wait(barrier, len(heads) + len(blks))


def send(source, target, send_sem, recv_sem, head, blk):
    return pltpu.make_async_remote_copy(
        src_ref=source,
        dst_ref=target,
        send_sem=send_sem,
        recv_sem=recv_sem,
        device_id=(head, blk),
        device_id_type=MESH,
    )


class Swap:
    def __init__(self, head, blk, axis, source, target, sems):
        self.copies = []
        count = 4 if axis == "head" else 8
        me = head if axis == "head" else blk
        for k in range(1, count):
            peer = flip(me, k)
            where = (peer, blk) if axis == "head" else (head, peer)
            self.copies.append(
                send(source(peer), target(me), sems.at[0, k], sems.at[1, k], *where)
            )

    def start(self):
        for copy in self.copies:
            copy.start()

    def arrive(self):
        for copy in self.copies:
            copy.wait_recv()

    def drain(self):
        for copy in self.copies:
            copy.wait_send()


class Plane:
    def __init__(self, head, blk, own, slot, sems):
        sibling = flip(blk, 1)
        self.first = [send(own, slot(blk), sems.at[0, 0], sems.at[1, 0], head, sibling)]
        self.passed = []
        for i, k in enumerate((2, 4, 6)):
            peer = flip(blk, k)
            self.first.append(
                send(own, slot(blk), sems.at[0, i + 1], sems.at[1, i + 1], head, peer)
            )
            self.passed.append(
                send(slot(peer), slot(peer), sems.at[0, i + 4], sems.at[1, i + 4], head, sibling)
            )

    def start(self):
        for i in (3, 1, 2, 0):
            self.first[i].start()

    def forward(self, i):
        self.first[i + 1].wait_recv()
        self.passed[i].start()

    def arrive(self, i):
        if i < 0:
            self.first[0].wait_recv()
        else:
            self.passed[i].wait_recv()

    def finish(self):
        for i in range(3):
            self.forward(i)
        for i in range(-1, 3):
            self.arrive(i)

    def drain(self):
        for copy in self.first + self.passed:
            copy.wait_send()


class Split:
    def __init__(self, head, blk, own, slot, half, sems):
        sibling, across, along, far = (flip(blk, k) for k in (1, 2, 4, 6))

        def copy(source, target, i, peer):
            return send(source, target, sems.at[0, i], sems.at[1, i], head, peer)

        self.first = [
            copy(own, slot(blk), 0, sibling),
            copy(own, slot(blk), 1, across),
            copy(own, slot(blk), 2, along),
        ]
        self.cross = [
            copy(half(across, 1), half(across, 1), 3, along),
            copy(half(along, 0), half(along, 0), 4, across),
        ]
        self.passed = [
            copy(slot(peer), slot(peer), 5 + i, sibling)
            for i, peer in enumerate((across, along, far))
        ]

    def start(self):
        for i in (1, 2, 0):
            self.first[i].start()

    def forward(self, i):
        if i < 2:
            self.first[i + 1].wait_recv()
            self.cross[i].start()
        else:
            for copy in self.cross:
                copy.wait_recv()
        self.passed[i].start()

    def arrive(self, i):
        if i < 0:
            self.first[0].wait_recv()
        else:
            self.passed[i].wait_recv()

    def finish(self):
        for i in range(3):
            self.forward(i)
        for i in range(-1, 3):
            self.arrive(i)

    def drain(self):
        for copy in self.first + self.cross + self.passed:
            copy.wait_send()


def line_order(head, step):
    low = jnp.minimum(head, 3 - head)
    swap = low * ((step == 0).astype(jnp.int32) - (step == 1).astype(jnp.int32))
    at = step + swap
    return jnp.where(head < 2, at, 3 - at)


class Line:
    def __init__(self, head, blk, own, slot, sems):
        self.head, self.blk, self.own, self.slot, self.sems = head, blk, own, slot, sems

    def copy(self, source, at, up, k):
        head = self.head
        target = jnp.where(up, head + 1, head - 1)
        way = jnp.where(up, 0, 1)
        return send(
            source, self.slot(at), self.sems.at[0, way, k], self.sems.at[1, way, k], target, self.blk
        )

    def start(self):
        head = self.head

        @pl.when(head < 3)
        def _():
            self.copy(self.own, head, True, 0).start()

        @pl.when(head > 0)
        def _():
            self.copy(self.own, head, False, 0).start()

    def step(self, at):
        head = self.head
        up = at < head
        k = jnp.where(up, head - 1 - at, at - head - 1)
        self.copy(self.slot(at), at, up, k).wait_recv()

        @pl.when(jnp.where(up, head < 3, head > 0))
        def _():
            self.copy(self.slot(at), at, up, k + 1).start()

    def hop(self, k):
        head = self.head

        @pl.when(head >= k)
        def _():
            self.step(head - k)

        @pl.when(head + k <= 3)
        def _():
            self.step(head + k)

    def drain(self):
        head = self.head
        for k in range(3):

            @pl.when(jnp.logical_and(head < 3, head >= k))
            def _():
                self.copy(self.own, head, True, k).wait_send()

            @pl.when(jnp.logical_and(head > 0, head + k <= 3))
            def _():
                self.copy(self.own, head, False, k).wait_send()


class Reach:
    def __init__(self, head, blk, own, slot, sems):
        self.head, self.blk, self.own, self.slot, self.sems = head, blk, own, slot, sems
        self.middle = jnp.logical_and(head > 0, head < 3)

    def copy(self, k):
        peer = flip(self.head, k)
        return send(
            self.own, self.slot(self.head), self.sems.at[0, k], self.sems.at[1, k], peer, self.blk
        )

    def passed(self):
        at = self.slot(flip(self.head, 2))
        return send(at, at, self.sems.at[0, 0], self.sems.at[1, 3], flip(self.head, 1), self.blk)

    def start(self):
        self.copy(2).start()
        self.copy(1).start()

        @pl.when(self.middle)
        def _():
            self.copy(3).start()

    def forward(self):
        self.copy(2).wait_recv()

        @pl.when(self.middle)
        def _():
            self.passed().start()

    def arrive(self):
        self.copy(1).wait_recv()
        self.copy(3).wait_recv()

    def drain(self):
        self.copy(1).wait_send()
        self.copy(2).wait_send()

        @pl.when(self.middle)
        def _():
            self.copy(3).wait_send()
            self.passed().wait_send()


class Fold:
    def __init__(self, head, blk, terms, via, joined, into, sems):
        self.head, self.blk, self.sems = head, blk, sems
        self.terms, self.via, self.joined, self.into = terms, via, joined, into
        self.middle = jnp.logical_and(head > 0, head < 3)

    def copy(self, k):
        peer = flip(self.head, k)
        return send(
            self.terms.at[peer],
            self.into.at[k],
            self.sems.at[0, k],
            self.sems.at[1, k],
            peer,
            self.blk,
        )

    def handed(self):
        return send(
            self.terms.at[flip(self.head, 3)],
            self.via,
            self.sems.at[0, 0],
            self.sems.at[1, 0],
            flip(self.head, 1),
            self.blk,
        )

    def relayed(self):
        return send(
            self.joined,
            self.into.at[2],
            self.sems.at[0, 2],
            self.sems.at[1, 2],
            flip(self.head, 2),
            self.blk,
        )

    def start_far(self):
        @pl.when(jnp.logical_not(self.middle))
        def _():
            self.handed().start()

    def start_one(self, k):
        if k == 1:
            self.copy(1).start()
        elif k == 2:

            @pl.when(jnp.logical_not(self.middle))
            def _():
                self.copy(2).start()

        else:

            @pl.when(self.middle)
            def _():
                self.copy(3).start()

    def start(self):
        self.start_far()
        for k in (2, 3, 1):
            self.start_one(k)

    def relay(self):
        @pl.when(self.middle)
        def _():
            self.handed().wait_recv()
            mine = self.terms[flip(self.head, 2)].astype(F32)
            self.joined[...] = (mine + self.via[...].astype(F32)).astype(BF)
            self.relayed().start()

    def arrive(self):
        self.copy(1).wait_recv()
        self.copy(2).wait_recv()

        @pl.when(self.middle)
        def _():
            self.copy(3).wait_recv()

        @pl.when(jnp.logical_not(self.middle))
        def _():
            self.into[3] = jnp.zeros_like(self.into[3])

        self.into[0] = self.terms[self.head]

    def drain(self):
        self.copy(1).wait_send()

        @pl.when(self.middle)
        def _():
            self.copy(3).wait_send()
            self.relayed().wait_send()

        @pl.when(jnp.logical_not(self.middle))
        def _():
            self.copy(2).wait_send()
            self.handed().wait_send()


def half_lane(shape):
    return lax.broadcasted_iota(jnp.int32, shape, 1) < 64


def lane_swap(value):
    lane = lax.broadcasted_iota(jnp.int32, value.shape, 1)
    return jnp.where(
        lax.rem(lane, 64) < 32, pltpu.roll(value, 96, 1), pltpu.roll(value, 32, 1)
    )


def turn_tables(table, sign):
    lane = lax.broadcasted_iota(jnp.int32, table.shape, 1)
    cosine = jnp.where(lane < 32, table, 0.0)
    cosine = cosine + pltpu.roll(cosine, 32, 1)
    sine = jnp.where(jnp.logical_and(lane >= 32, lane < 64), table, 0.0) * sign
    sine = sine - pltpu.roll(sine, 96, 1)
    both = (cosine + pltpu.roll(cosine, 64, 1), sine + pltpu.roll(sine, 64, 1))
    return both, (jnp.where(lane < 64, cosine, 1.0), sine)


def join_halves(top, bottom, right):
    left = half_lane(top.shape)
    if right:
        return jnp.where(left, pltpu.roll(top, 64, 1), bottom)
    return jnp.where(left, top, pltpu.roll(bottom, 64, 1))


EXP_SCALE = SCORE_SCALE * math.log2(math.e)
KEYS = 256


def flip_by(head, k):
    low, high = lax.rem(k, 2), lax.div(k, 2)
    value = head + low - 2 * low * lax.rem(head, 2)
    return value + 2 * high - 4 * high * lax.div(head, 2)


class Everyone:
    def __init__(self, head, blk, source, target, sems):
        self.head, self.blk, self.source, self.target, self.sems = head, blk, source, target, sems
        self.peers = [flip(blk, k) for k in range(8)]

    def copy(self, kz, k):
        z = flip_by(self.head, jnp.int32(kz))
        return self.copy_to(z, kz, k)

    def copy_to(self, z, kz, k):
        b = self.peers[k]
        return send(
            self.source(z, b),
            self.target(self.head, self.blk),
            self.sems.at[0, kz, k],
            self.sems.at[1, kz, k],
            z,
            b,
        )

    def start(self, kz):
        z = flip_by(self.head, jnp.int32(kz))

        @pl.when(kz > 0)
        def _():
            self.copy_to(z, kz, 0).start()

        for k in range(1, 8):
            self.copy_to(z, kz, k).start()

    def arrive(self, kz):
        z = flip_by(self.head, jnp.int32(kz))

        @pl.when(kz > 0)
        def _():
            self.copy_to(z, kz, 0).wait_recv()

        for k in range(1, 8):
            self.copy_to(z, kz, k).wait_recv()

    def drain(self):
        for kz in range(4):
            for k in range(1 if kz == 0 else 0, 8):
                self.copy(kz, k).wait_send()


def greet_all(head, blk):
    barrier = pltpu.get_barrier_semaphore()
    for kz in range(4):
        for k in range(8):
            if kz or k:
                pl.semaphore_signal(
                    barrier, inc=1, device_id=(flip(head, kz), flip(blk, k)), device_id_type=MESH
                )


def all_here():
    pl.semaphore_wait(pltpu.get_barrier_semaphore(), 31)


def group_rows(value):
    return jnp.sum(value.reshape(value.shape[0] // 8, 8, value.shape[1]), axis=0)


VMEM_LIMIT = 61 << 20


class Scatter:
    def __init__(self, head, blk, terms, near, joined, far, sems):
        self.head, self.blk, self.core = head, blk, lax.rem(blk, 2)
        self.terms, self.near, self.joined, self.far, self.sems = terms, near, joined, far, sems

    def halves(self):
        return send(
            self.terms.at[:, :, 1 - self.core],
            self.near,
            self.sems.at[0, 0],
            self.sems.at[1, 0],
            self.head,
            flip(self.blk, 1),
        )

    def chips(self, i):
        peer = flip(self.blk, 2 * i)
        return send(
            self.joined.at[lax.div(peer, 2)],
            self.far.at[i],
            self.sems.at[0, i],
            self.sems.at[1, i],
            self.head,
            peer,
        )

    def start(self):
        self.halves().start()

    def join(self):
        self.halves().wait_recv()
        for chip in range(4):
            mine = self.terms[:, chip, pl.ds(self.core, 1)].astype(F32)
            mine = mine.reshape(mine.shape[0], *mine.shape[2:])
            self.joined[chip] = (mine + self.near[:, chip].astype(F32)).astype(BF)
        for i in (3, 1, 2):
            self.chips(i).start()

    def total(self):
        value = self.joined[lax.div(self.blk, 2)].astype(F32)
        for i in range(1, 4):
            self.chips(i).wait_recv()
            value = value + self.far[i].astype(F32)
        return value

    def drain(self):
        self.halves().wait_send()
        for i in range(1, 4):
            self.chips(i).wait_send()


def sum_four(parts):
    return (parts[0].astype(F32) + parts[1].astype(F32)) + (
        parts[2].astype(F32) + parts[3].astype(F32)
    )


def layer_kernel(
    tok, pos, freq, w_qkv, ttab, sca, scm, w_up, out_own, down_own, cot_own, tix,
    output, grad_tokens, g_qkv, g_out, g_up, g_down, grad_attn, grad_mlp,
    tab, wqp, upp, gq, up_own,
    tiles, normed, wq, scales, tabg, tokg, mixed, lse, grad_rx, grad_middle, middle, outq, grad_down,
    grad_up, grad_out, sums, wqz, turned, part, sums_in, parts, out_tiles, upz, outz, up, down, out, cots,
    kvt, scores, att, received, attended, n2g, act, gh, pairs, prx, gsend, gin, tsend, branch, queries,
    grads, queries_t, grads_t, stats, keyt, dkv, dqt, bsend, back, oin, din, dvia, djoin, uin, uvia, ujoin,
    usum, near, joined, far, osum, zin, gp, gnp, gvia, gjoin, gin_r, terms, near_q, joined_q, far_q, osum_q,
    part_r, sums_in_r, parts_r, zsem, lsem, tsem, wsem, asem, bsem, psem, usem, osem, usem2, dsem, qsem,
    csem, esem, nsem, ssem, gsem, fsem, qsem_r, dsem_r, usem_r, vsem, osem_r, xsem, bsem_r, gsem_r, osem_q,
    xsem_q, asem_r, csem_r,
):
    head, blk = lax.axis_index("head"), lax.axis_index("blk")
    core = lax.rem(blk, 2)
    greet_all(head, blk)
    for group in range(4):
        for i in range(2):
            at = 256 * group + 128 * i
            keys = w_qkv[:, 1024 + at : 1152 + at].astype(F32)
            values = w_qkv[:, 2048 + at : 2176 + at].astype(F32)
            for right in range(2):
                lanes = slice(256 * i + 128 * right, 256 * i + 128 * right + 128)
                wqp[group, :, lanes] = join_halves(keys, values, right).astype(BF)
        wqp[group, :, 512:768] = w_qkv[:, 256 * group : 256 * group + 256]
    angles = [freq[:, 0:64] * pos[seq : seq + 1, :].astype(F32) for seq in range(2)]
    tab[...] = jnp.transpose(
        jnp.concatenate([turn(angle) for angle in angles for turn in (jnp.cos, jnp.sin)], axis=0)
    )
    for i in range(8):
        for group in range(4):
            at = 128 * (8 * group + i)
            upp[i, :, 128 * group : 128 * group + 128] = w_up[:, at : at + 128]
    all_here()
    zswap = Swap(head, blk, "head", lambda i: wqp.at[i], lambda i: wqz.at[i], zsem)
    zswap.start()
    line = Line(head, blk, tok, lambda i: tokg.at[i], lsem)
    tline = Line(head, blk, tab, lambda i: tabg.at[i], tsem)
    line.start()
    tline.start()
    uswap = Swap(head, blk, "blk", lambda i: upp.at[i], lambda i: upz.at[i], usem)
    oline = Reach(head, blk, out_own, lambda i: outz.at[i], osem)
    uline = Line(head, blk, upz, lambda i: up.at[i], usem2)
    dline = Line(head, blk, down_own, lambda i: down.at[i], dsem)
    oplane = Plane(head, blk, outz, lambda i: out.at[:, i], qsem)
    cplane = Plane(head, blk, cot_own, lambda i: cots.at[i], csem)
    everyone = Everyone(head, blk, lambda z, b: att.at[z, b], lambda z, b: received.at[z, b], esem)
    backward = Everyone(head, blk, lambda z, b: tsend.at[z, b], lambda z, b: grad_rx.at[z, b], fsem)
    turned[...] = jnp.transpose(ttab[...])
    rows = turned[pl.ds(pl.multiple_of((head * 8 + blk) * 8, 8), 8), :]
    step_lane = lax.broadcasted_iota(jnp.int32, rows.shape, 1)
    pieces = []
    for weight in (sca, scm):
        for seq in range(2):
            column = jnp.sum(jnp.where(step_lane == tix[seq], rows, 0.0), axis=1, keepdims=True)
            pieces.append(jnp.sum(column * weight[...].astype(F32), axis=0, keepdims=True))
    part[...] = jnp.concatenate(pieces + [jnp.zeros((4, 1024), F32)], axis=0)
    one = Swap(head, blk, "blk", lambda i: part, lambda i: sums_in.at[i], asem)
    one.start()
    uswap.start()
    sums_in[blk] = part[...]
    wqz[head] = wqp[head]
    tokg[head] = tok[...]
    tabg[head] = tab[...]
    upz[blk] = upp[blk]
    outz[head] = out_own[...]
    down[head] = down_own[...]
    cots[blk] = cot_own[...]
    one.arrive()
    total = sums_in[0]
    for i in range(1, 8):
        total = total + sums_in[i]
    parts[head] = total
    two = Swap(head, blk, "head", lambda i: parts.at[head], lambda i: parts.at[i], bsem)
    two.start()
    zswap.arrive()
    plane = Plane(head, blk, wqz, lambda i: wq.at[:, i], wsem)
    plane.start()
    wq[:, pl.ds(blk, 1)] = wqz[...].reshape(4, 1, 32, 768)
    two.arrive()
    total = 1.0 + ((parts[0] + parts[1]) + (parts[2] + parts[3]))
    scales[...] = total

    def gather(step, carry):
        at = line_order(head, step)

        @pl.when(step > 0)
        def _():
            line.step(at)
            tline.step(at)

        for seq in range(2):
            unit, _ = norm_stats(tokg[at, seq].astype(F32))
            normed[at, pl.ds(64 * seq, 64), :] = (unit * scales[seq : seq + 1, :]).astype(BF)
        return carry

    def project(step, carry):
        at = line_order(head, step)
        proj = jnp.dot(
            normed[at], wq[...].reshape(1024, 768), preferred_element_type=F32
        )
        for seq in range(2):
            table = tabg[at]
            if seq:
                table = pltpu.roll(table, 64, 1)
            both, keyed = turn_tables(table, 1.0)
            mine = proj[64 * seq : 64 * seq + 64]
            for j in range(4):
                kv = mine[:, 128 * j : 128 * j + 128]
                kv = kv * keyed[0] + lane_swap(kv) * keyed[1]
                out_tiles[4 * seq + j, at, 0:64, :] = kv.astype(BF)
            for i in range(2):
                query = mine[:, 512 + 128 * i : 640 + 128 * i]
                query = query * both[0] + lane_swap(query) * both[1]
                for right in range(2):
                    packed = join_halves(query[:32], query[32:], right)
                    out_tiles[4 * seq + 2 * i + right, at, 64:96, :] = packed.astype(BF)
        move(at).start()
        tiles[at, blk] = out_tiles[blk, at]
        return carry

    def move(at):
        return Swap(
            head, blk, "blk", lambda i: out_tiles.at[i, at], lambda i: tiles.at[at, i], psem.at[at]
        )

    lax.fori_loop(0, 3, gather, 0)
    oline.start()
    plane.finish()
    lax.fori_loop(0, 3, project, 0)

    def last(step, carry):
        gather(step, carry)
        return project(step, carry)

    lax.fori_loop(3, 4, last, 0)
    uswap.arrive()
    up[head] = upz[...]
    uline.start()
    oline.forward()
    oline.arrive()
    out[:, pl.ds(blk, 1)] = outz[...].reshape(4, 1, 32, 1024)
    for at in range(4):
        move(at).arrive()
    oplane.start()
    uline.hop(1)
    dline.start()
    kvt[...] = jnp.transpose(tiles[:, :, 0:64, :].reshape(2048, 128))

    def attend(step, carry):
        z = flip_by(head, 3 - step)
        flat = jnp.transpose(tiles[z, :, 64:96, :].reshape(256, 128).astype(F32))
        blank = jnp.zeros((64, 256), F32)
        results = []
        for side in range(2):
            query = jnp.concatenate([flat[64 * side : 64 * side + 64], blank], axis=0).astype(BF)
            top = None
            for c in range(2048 // KEYS):
                keys = tiles[c // 2, 4 * (c % 2) : 4 * (c % 2) + 4, 0:64, :].reshape(KEYS, 128)
                part = jnp.dot(keys, query, preferred_element_type=F32)
                scores[c] = part
                peak = jnp.max(part.reshape(KEYS // 8, 8, 256), axis=0)
                top = peak if top is None else jnp.maximum(top, peak)
            top = jnp.max(top, axis=0, keepdims=True)
            total = jnp.zeros((8, 256), F32)
            mix = jnp.zeros((64, 256), F32)
            for c in range(2048 // KEYS):
                weights = jnp.exp2((scores[c] - top) * EXP_SCALE)
                total = total + group_rows(weights)
                mix = mix + jnp.dot(
                    kvt[64:128, KEYS * c : KEYS * c + KEYS],
                    weights.astype(BF),
                    preferred_element_type=F32,
                )
            total = jnp.sum(total, axis=0, keepdims=True)
            mix = mix / total
            mixed[z, 64 * side : 64 * side + 64, :] = mix
            lse[z, side : side + 1, :] = top * SCORE_SCALE + jnp.log(total)
            results.append(mix)
        both = jnp.transpose(jnp.concatenate(results, axis=0))
        att[z] = both.astype(BF).reshape(8, 32, 128)
        everyone.start(3 - step)

        @pl.when(step == 1)
        def _():
            cplane.start()

        @pl.when(step == 2)
        def _():
            uline.hop(2)
            dline.hop(1)
            for i in range(3):
                oplane.forward(i)

        return carry

    lse[...] = jnp.zeros_like(lse)
    lax.fori_loop(0, 4, attend, 0)
    received[head, blk] = att[head, blk]
    for i in range(-1, 3):
        oplane.arrive(i)
    middle[...] = tok[...].astype(F32).reshape(128, 1024)
    for kz in range(4):
        group = flip(head, kz)
        everyone.arrive(kz)
        for seq in range(2):
            for i in range(2):
                first = received[group, 4 * seq + 2 * i].astype(F32)
                second = received[group, 4 * seq + 2 * i + 1].astype(F32)
                lanes = slice(128 * i, 128 * i + 128)
                for right in range(2):
                    at = slice(64 * seq + 32 * right, 64 * seq + 32 * right + 32)
                    attended[group, at, lanes] = join_halves(first, second, right).astype(BF)
        middle[...] += jnp.dot(
            attended[group], out[group].reshape(256, 1024), preferred_element_type=F32
        )
    for seq in range(2):
        rows = slice(64 * seq, 64 * seq + 64)
        unit, _ = norm_stats(middle[rows, :])
        n2g[blk, rows, :] = (unit * scales[2 + seq : 3 + seq, :]).astype(BF)
    nplane = Split(
        head, blk, n2g.at[blk], lambda i: n2g.at[i], lambda i, h: n2g.at[i, pl.ds(64 * h, 64)], nsem
    )
    for i in (1, 2, 0):
        nplane.first[i].start()
    uline.hop(3)
    dline.hop(2)
    cplane.finish()
    dline.hop(3)
    sibling = flip(blk, 1)

    def halves(i):
        return [
            send(pairs.at[w, i, 1 - core], prx.at[w, i], ssem.at[0, w, i], ssem.at[1, w, i], head, sibling)
            for w in range(2)
        ]

    def onward(i):
        peer = flip(blk, 2 * i)
        return send(gsend.at[i], gin.at[i], gsem.at[0, i], gsem.at[1, i], head, peer)

    def reduce(i):
        chip = lax.div(flip(blk, 2 * i), 2)
        for copy in halves(i):
            copy.wait_recv()
        gsend[i] = (pairs[0, i, core].astype(F32) + prx[0, i].astype(F32)).astype(BF)
        if i:
            onward(i).start()
        outq[chip] = (pairs[1, i, core].astype(F32) + prx[1, i].astype(F32)).astype(BF)

    for i in range(4):
        chip = lax.div(flip(blk, 2 * i), 2)
        if i == 0:
            nplane.arrive(-1)
        else:
            if i == 1:
                nplane.forward(0)
                nplane.forward(1)
            elif i == 3:
                nplane.forward(2)
            if i > 1:
                reduce(i - 1)
            nplane.arrive(i - 1)
        at = pl.ds(2 * chip, 2)
        rows = n2g[at].reshape(256, 1024)
        hidden = jnp.dot(rows, up[...].reshape(1024, 512), preferred_element_type=F32)
        grad_active = contract_cols(cots[at].reshape(256, 1024), down[...].reshape(512, 1024))
        cdf = 0.5 * (1.0 + lax.erf(hidden * math.sqrt(0.5)))
        active = (hidden * cdf).astype(BF)
        slope = cdf + hidden * jnp.exp(-0.5 * hidden * hidden) * (1.0 / math.sqrt(2 * math.pi))
        grad_hidden = (grad_active * slope).astype(BF)
        act[at] = active.reshape(2, 128, 512)
        gh[at] = grad_hidden.reshape(2, 128, 512)
        pairs[0, i] = (
            contract_cols(grad_hidden, up[...].reshape(1024, 512)).astype(BF).reshape(2, 128, 1024)
        )
        pairs[1, i] = (
            jnp.dot(active, down[...].reshape(512, 1024), preferred_element_type=F32)
            .astype(BF)
            .reshape(2, 128, 1024)
        )
        for copy in halves(i):
            copy.start()
    reduce(3)
    reduce(0)
    for group in range(4):
        lanes = slice(128 * group, 128 * group + 128)
        grad_down[group] = contract_rows(
            act[:, :, lanes].reshape(1024, 128), cots[...].reshape(1024, 1024)
        ).astype(BF)
    for group in range(4):
        lanes = slice(256 * group, 256 * group + 256)
        value = contract_rows(n2g[:, :, lanes].reshape(1024, 256), gh[...].reshape(1024, 512))
        grad_up[group] = value.astype(BF).reshape(8, 32, 512)
    uswap_r = Fold(head, blk, grad_up, uvia, ujoin, uin, usem_r)
    dfold = Fold(head, blk, grad_down, dvia, djoin, din, dsem_r)
    folds = (uswap_r, dfold)
    for fold in folds:
        fold.start_far()
        fold.start_one(3)

        @pl.when(fold.middle)
        def _():
            fold.copy(1).start()

    for i in range(1, 4):
        onward(i).wait_recv()
    sums[...] = jnp.zeros_like(sums)
    for seq in range(2):
        rows = slice(64 * seq, 64 * seq + 64)
        grad = gsend[0, rows, :].astype(F32)
        for i in range(1, 4):
            grad = grad + gin[i, rows, :].astype(F32)
        unit, spread = norm_stats(middle[rows, :])
        whole_grad = cots[blk, rows, :].astype(F32) + norm_back(
            unit, spread, grad, scales[2 + seq : 3 + seq, :]
        )
        grad_middle[rows, :] = whole_grad
        branch[rows, :] = whole_grad.astype(BF)
        sums[seq : seq + 1, :] = jnp.sum(grad * unit, axis=0, keepdims=True)

    def give(step, carry):
        group = flip_by(head, 3 - step)
        value = contract_cols(branch[...], out[group].reshape(256, 1024))
        for seq in range(2):
            for i in range(2):
                lanes = slice(128 * i, 128 * i + 128)
                top = value[64 * seq : 64 * seq + 32, lanes]
                bottom = value[64 * seq + 32 : 64 * seq + 64, lanes]
                for right in range(2):
                    tsend[group, 4 * seq + 2 * i + right] = join_halves(top, bottom, right).astype(BF)
        backward.start(3 - step)
        return carry

    lax.fori_loop(0, 4, give, 0)
    grad_rx[head, blk] = tsend[head, blk]
    for group in range(4):
        value = contract_rows(attended[group], branch[...])
        grad_out[group] = value.astype(BF).reshape(4, 2, 32, 1024)
    scatter = Scatter(head, blk, grad_out, near, joined, far, osem_r)
    scatter.start()
    outs = []
    for i in range(1, 4):
        peer = flip(blk, 2 * i)
        outs.append(
            send(outq.at[lax.div(peer, 2)], oin.at[i], qsem_r.at[0, i], qsem_r.at[1, i], head, peer)
        )
    vswap = Swap(head, blk, "blk", lambda i: usum.at[i], lambda i: up_own.at[i], vsem)
    xswap = Swap(head, blk, "head", lambda i: osum.at[i], lambda i: zin.at[i], xsem)
    left = half_lane((256, 128))
    keyt[...] = jnp.transpose(tiles[:, :, 0:64, :].reshape(2048, 128))[:64]

    def prepare(z, carry):
        flat = tiles[z, :, 64:96, :].reshape(256, 128).astype(F32)
        grad = grad_rx[z].reshape(256, 128).astype(F32)
        product = jnp.transpose(grad) * mixed[z]
        queries[2 * z] = jnp.where(left, flat, 0.0).astype(BF)
        queries[2 * z + 1] = jnp.where(left, pltpu.roll(flat, 64, 1), 0.0).astype(BF)
        turned = jnp.transpose(flat)
        slopes = jnp.transpose(grad)
        blank = jnp.zeros((64, 256), F32)
        for side in range(2):
            rows = slice(64 * side, 64 * side + 64)
            queries_t[2 * z + side] = jnp.concatenate([turned[rows], blank], axis=0).astype(BF)
            grads_t[2 * z + side] = jnp.concatenate([blank, slopes[rows]], axis=0).astype(BF)
        grads[2 * z] = jnp.where(left, 0.0, pltpu.roll(grad, 64, 1)).astype(BF)
        grads[2 * z + 1] = jnp.where(left, 0.0, grad).astype(BF)
        for side in range(2):
            delta = jnp.sum(product[64 * side : 64 * side + 64], axis=0, keepdims=True)
            shift = lse[z, side : side + 1, :] * math.log2(math.e)
            stats[2 * z + side] = jnp.concatenate([shift, delta, jnp.zeros((6, 256), F32)], axis=0)
        return carry

    def ready(kz, carry):
        backward.arrive(kz)
        return prepare(flip_by(head, kz), carry)

    scatter.join()
    lax.fori_loop(0, 4, ready, 0)
    dqt[...] = jnp.zeros_like(dqt)

    def kv_move(z):
        return Swap(
            head,
            blk,
            "blk",
            lambda i: bsend.at[i, z, pl.ds(0, 64)],
            lambda i: back.at[i, z, pl.ds(0, 64)],
            bsem_r.at[z],
        )

    def keys_step(z, carry):
        dkv[...] = jnp.zeros_like(dkv)

        def query_step(q, inner):
            query, grad = queries[q], grads[q]
            query_t, grad_t = queries_t[q], grads_t[q]
            shift, delta = stats[q, 0:1, :], stats[q, 1:2, :]
            dq = dqt[q]
            for c in range(2):
                keys = tiles[z, 4 * c : 4 * c + 4, 0:64, :].reshape(256, 128)
                probs = jnp.dot(keys, query_t, preferred_element_type=F32)
                probs = jnp.exp2(probs * EXP_SCALE - shift)
                slopes = jnp.dot(keys, grad_t, preferred_element_type=F32)
                slopes = (probs * (slopes - delta)).astype(BF)
                dkv[c] += jnp.dot(slopes, query, preferred_element_type=F32) + jnp.dot(
                    probs.astype(BF), grad, preferred_element_type=F32
                )
                at = pl.ds(pl.multiple_of(512 * z + 256 * c, 256), 256)
                dq = dq + jnp.dot(keyt[:, at], slopes, preferred_element_type=F32)
            dqt[q] = dq
            return inner

        lax.fori_loop(0, 8, query_step, 0, unroll=8)
        scale = jnp.where(left, SCORE_SCALE, 1.0)
        for c in range(2):
            bsend[4 * c : 4 * c + 4, pl.ds(z, 1), 0:64, :] = (
                (dkv[c] * scale).astype(BF).reshape(4, 1, 64, 128)
            )
        kv_move(z).start()

        @pl.when(z == 0)
        def _():
            for fold in folds:
                fold.start_one(2)

        @pl.when(z == 1)
        def _():
            for fold in folds:
                fold.relay()
            for copy in outs:
                copy.start()

        @pl.when(z == 2)
        def _():
            for fold in folds:

                @pl.when(jnp.logical_not(fold.middle))
                def _():
                    fold.copy(1).start()

            osum[...] = scatter.total().astype(BF)
            xswap.start()
            zin[head] = osum[head]

        return carry

    lax.fori_loop(0, 4, keys_step, 0)
    for z in range(4):
        both = jnp.concatenate([dqt[2 * z], dqt[2 * z + 1]], axis=0)
        both = (jnp.transpose(both) * SCORE_SCALE).astype(BF)
        bsend[:, z, 64:96, :] = both.reshape(8, 32, 128)
    qmove = Swap(
        head,
        blk,
        "blk",
        lambda i: bsend.at[i, :, pl.ds(64, 32)],
        lambda i: back.at[i, :, pl.ds(64, 32)],
        bsem_r.at[4],
    )
    qmove.start()
    back[blk] = bsend[blk]
    picked = turned[pl.ds(pl.multiple_of((head * 8 + blk) * 8, 8), 8), :]
    step_lane = lax.broadcasted_iota(jnp.int32, picked.shape, 1)
    columns = [
        jnp.sum(jnp.where(step_lane == tix[seq], picked, 0.0), axis=1, keepdims=True)
        for seq in range(2)
    ]
    for z in range(4):
        kv_move(z).arrive()
    qmove.arrive()
    gswap = Fold(head, blk, gnp, gvia, gjoin, gin_r, gsem_r)

    def unturn(step, carry):
        at = flip(head, step)
        for seq in range(2):
            table = tabg[at]
            if seq:
                table = pltpu.roll(table, 64, 1)
            both, keyed = turn_tables(table, -1.0)
            rows = slice(64 * seq, 64 * seq + 64)
            for j in range(4):
                kv = back[4 * seq + j, at, 0:64, :].astype(F32)
                kv = kv * keyed[0] + lane_swap(kv) * keyed[1]
                gp[at, rows, 128 * j : 128 * j + 128] = kv.astype(BF)
            for i in range(2):
                first = back[4 * seq + 2 * i, at, 64:96, :].astype(F32)
                second = back[4 * seq + 2 * i + 1, at, 64:96, :].astype(F32)
                query = jnp.concatenate(
                    [join_halves(first, second, 0), join_halves(first, second, 1)], axis=0
                )
                query = query * both[0] + lane_swap(query) * both[1]
                gp[at, rows, 512 + 128 * i : 640 + 128 * i] = query.astype(BF)
        return carry

    for step in (3, 2, 1, 0):
        unturn(step, 0)
    for group in range(4):
        lanes = slice(256 * group, 256 * group + 256)
        value = contract_rows(normed[:, :, lanes].reshape(512, 256), gp[...].reshape(512, 768))
        terms[group] = value.astype(BF).reshape(4, 2, 32, 768)
    scatter_q = Scatter(head, blk, terms, near_q, joined_q, far_q, osem_q)
    scatter_q.start()
    for step in (3, 2, 1, 0):
        at = flip(head, step)
        gnp[at] = contract_cols(gp[at], wq[...].reshape(1024, 768)).astype(BF)
        if step == 3:
            gswap.start_far()
            gswap.start_one(3)
    scatter_q.join()
    part_r[...] = jnp.concatenate(
        [jnp.zeros((2, 1024), F32), sums[0:2, :], jnp.zeros((4, 1024), F32)], axis=0
    )

    def gather_r(at, carry):
        for seq in range(2):
            unit, _ = norm_stats(tokg[at, seq].astype(F32))
            part_r[seq : seq + 1, :] += jnp.sum(
                gnp[at, pl.ds(64 * seq, 64), :].astype(F32) * unit, axis=0, keepdims=True
            )
        return carry

    lax.fori_loop(0, 4, gather_r, 0)
    one_r = Swap(head, blk, "blk", lambda i: part_r, lambda i: sums_in_r.at[i], asem_r)
    one_r.start()
    sums_in_r[blk] = part_r[...]
    gswap.start_one(2)
    gswap.relay()
    gswap.start_one(1)
    uswap_r.arrive()
    usum[...] = sum_four(uin).astype(BF)
    vswap.start()
    up_own[blk] = usum[blk]
    one_r.arrive()
    total = sums_in_r[0]
    for i in range(1, 8):
        total = total + sums_in_r[i]
    parts_r[head] = total
    two_r = Swap(head, blk, "head", lambda i: parts_r.at[head], lambda i: parts_r.at[i], csem_r)
    two_r.start()
    total = middle[...] + outq[lax.div(blk, 2)].astype(F32)
    for i in range(1, 4):
        outs[i - 1].wait_recv()
        total = total + oin[i].astype(F32)
    output[...] = total.astype(BF)
    dfold.arrive()
    g_down[...] = sum_four(din)
    osum_q[...] = scatter_q.total().astype(BF)
    xswap_q = Swap(head, blk, "head", lambda i: osum_q.at[i], lambda i: gq.at[i], xsem_q)
    xswap_q.start()
    gq[head] = osum_q[head]
    xswap.arrive()
    g_out[...] = sum_four(zin)
    two_r.arrive()
    total = (parts_r[0] + parts_r[1]) + (parts_r[2] + parts_r[3])
    grad_attn[...] = columns[0] * total[0:1] + columns[1] * total[1:2]
    grad_mlp[...] = columns[0] * total[2:3] + columns[1] * total[3:4]
    gswap.arrive()
    for seq in range(2):
        rows = slice(64 * seq, 64 * seq + 64)
        grad = sum_four([gin_r[i, rows, :] for i in range(4)])
        unit, spread = norm_stats(tokg[head, seq].astype(F32))
        grad_tokens[rows, :] = grad_middle[rows, :] + norm_back(
            unit, spread, grad, scales[seq : seq + 1, :]
        )
    vswap.arrive()
    for i in range(8):
        for group in range(4):
            at = 128 * (8 * group + i)
            g_up[:, at : at + 128] = up_own[i, :, 128 * group : 128 * group + 128].astype(F32)
    xswap_q.arrive()
    for group in range(4):
        for i in range(2):
            first = gq[group, :, 256 * i : 256 * i + 128].astype(F32)
            second = gq[group, :, 256 * i + 128 : 256 * i + 256].astype(F32)
            at = 256 * group + 128 * i
            for right in range(2):
                lanes = slice(1024 + 1024 * right + at, 1152 + 1024 * right + at)
                g_qkv[:, lanes] = join_halves(first, second, right)
        g_qkv[:, 256 * group : 256 * group + 256] = gq[group, :, 512:768].astype(F32)
    for z in range(4):
        kv_move(z).drain()
    for copy in outs:
        copy.wait_send()
    for copies in (
        scatter, uswap_r, dfold, vswap, xswap, qmove, gswap, scatter_q, xswap_q, one_r, two_r
    ):
        copies.drain()
    for at in range(4):
        move(at).drain()
    for i in range(4):
        for copy in halves(i):
            copy.wait_send()
        if i:
            onward(i).wait_send()
    for copies in (
        zswap, line, tline, plane, one, two, uswap, oline,
        uline, dline, oplane, cplane, everyone, nplane, backward,
    ):
        copies.drain()


def whole(count):
    return [pl.BlockSpec(memory_space=pltpu.VMEM)] * count


def layer(*operands):
    dma = pltpu.SemaphoreType.DMA
    shape = jax.ShapeDtypeStruct
    return pl.pallas_call(
        layer_kernel,
        out_shape=(
            shape((128, 1024), BF),
            shape((128, 1024), F32),
            shape((32, 3072), F32),
            shape((32, 1024), F32),
            shape((32, 4096), F32),
            shape((128, 1024), F32),
            shape((8, 1024), F32),
            shape((8, 1024), F32),
        ),
        in_specs=whole(11) + [pl.BlockSpec(memory_space=pltpu.SMEM)],
        out_specs=whole(8),
        scratch_shapes=[
            pltpu.VMEM((64, 128), F32),
            pltpu.VMEM((4, 32, 768), BF),
            pltpu.VMEM((8, 32, 512), BF),
            pltpu.VMEM((4, 32, 768), BF),
            pltpu.VMEM((8, 32, 512), BF),
            pltpu.VMEM((4, 8, 96, 128), BF),
            pltpu.VMEM((4, 128, 1024), BF),
            pltpu.VMEM((4, 8, 32, 768), BF),
            pltpu.VMEM((8, 1024), F32),
            pltpu.VMEM((4, 64, 128), F32),
            pltpu.VMEM((4, 2, 64, 1024), BF),
            pltpu.VMEM((4, 128, 256), F32),
            pltpu.VMEM((4, 8, 256), F32),
            pltpu.VMEM((4, 8, 32, 128), BF),
            pltpu.VMEM((128, 1024), F32),
            pltpu.VMEM((128, 1024), F32),
            pltpu.VMEM((4, 128, 1024), BF),
            pltpu.VMEM((4, 128, 1024), BF),
            pltpu.VMEM((4, 8, 32, 512), BF),
            pltpu.VMEM((4, 4, 2, 32, 1024), BF),
            pltpu.VMEM((8, 1024), F32),
            pltpu.VMEM((4, 32, 768), BF),
            pltpu.VMEM((256, 64), F32),
            pltpu.VMEM((8, 1024), F32),
            pltpu.VMEM((8, 8, 1024), F32),
            pltpu.VMEM((4, 8, 1024), F32),
            pltpu.VMEM((8, 4, 96, 128), BF),
            pltpu.VMEM((8, 32, 512), BF),
            pltpu.VMEM((4, 32, 1024), BF),
            pltpu.VMEM((4, 8, 32, 512), BF),
            pltpu.VMEM((4, 128, 1024), BF),
            pltpu.VMEM((4, 8, 32, 1024), BF),
            pltpu.VMEM((8, 128, 1024), BF),
            pltpu.VMEM((128, 2048), BF),
            pltpu.VMEM((2048 // KEYS, KEYS, 256), F32),
            pltpu.VMEM((4, 8, 32, 128), BF),
            pltpu.VMEM((4, 8, 32, 128), BF),
            pltpu.VMEM((4, 128, 256), BF),
            pltpu.VMEM((8, 128, 1024), BF),
            pltpu.VMEM((8, 128, 512), BF),
            pltpu.VMEM((8, 128, 512), BF),
            pltpu.VMEM((2, 4, 2, 128, 1024), BF),
            pltpu.VMEM((2, 4, 128, 1024), BF),
            pltpu.VMEM((4, 128, 1024), BF),
            pltpu.VMEM((4, 128, 1024), BF),
            pltpu.VMEM((4, 8, 32, 128), BF),
            pltpu.VMEM((128, 1024), BF),
            pltpu.VMEM((8, 256, 128), BF),
            pltpu.VMEM((8, 256, 128), BF),
            pltpu.VMEM((8, 128, 256), BF),
            pltpu.VMEM((8, 128, 256), BF),
            pltpu.VMEM((8, 8, 256), F32),
            pltpu.VMEM((64, 2048), BF),
            pltpu.VMEM((2, 256, 128), F32),
            pltpu.VMEM((8, 64, 256), F32),
            pltpu.VMEM((8, 4, 96, 128), BF),
            pltpu.VMEM((8, 4, 96, 128), BF),
            pltpu.VMEM((4, 128, 1024), BF),
            pltpu.VMEM((4, 128, 1024), BF),
            pltpu.VMEM((128, 1024), BF),
            pltpu.VMEM((128, 1024), BF),
            pltpu.VMEM((4, 8, 32, 512), BF),
            pltpu.VMEM((8, 32, 512), BF),
            pltpu.VMEM((8, 32, 512), BF),
            pltpu.VMEM((8, 32, 512), BF),
            pltpu.VMEM((4, 4, 32, 1024), BF),
            pltpu.VMEM((4, 4, 32, 1024), BF),
            pltpu.VMEM((4, 4, 32, 1024), BF),
            pltpu.VMEM((4, 32, 1024), BF),
            pltpu.VMEM((4, 32, 1024), BF),
            pltpu.VMEM((4, 128, 768), BF),
            pltpu.VMEM((4, 128, 1024), BF),
            pltpu.VMEM((128, 1024), BF),
            pltpu.VMEM((128, 1024), BF),
            pltpu.VMEM((4, 128, 1024), BF),
            pltpu.VMEM((4, 4, 2, 32, 768), BF),
            pltpu.VMEM((4, 4, 32, 768), BF),
            pltpu.VMEM((4, 4, 32, 768), BF),
            pltpu.VMEM((4, 4, 32, 768), BF),
            pltpu.VMEM((4, 32, 768), BF),
            pltpu.VMEM((8, 1024), F32),
            pltpu.VMEM((8, 8, 1024), F32),
            pltpu.VMEM((4, 8, 1024), F32),
            dma((2, 4)),
            dma((2, 2, 3)),
            dma((2, 2, 3)),
            dma((2, 8)),
            dma((2, 8)),
            dma((2, 4)),
            dma((4, 2, 8)),
            dma((2, 8)),
            dma((2, 4)),
            dma((2, 2, 3)),
            dma((2, 2, 3)),
            dma((2, 8)),
            dma((2, 8)),
            dma((2, 4, 8)),
            dma((2, 8)),
            dma((2, 2, 4)),
            dma((2, 4)),
            dma((2, 4, 8)),
            dma((2, 4)),
            dma((2, 4)),
            dma((2, 4)),
            dma((2, 8)),
            dma((2, 4)),
            dma((2, 4)),
            dma((5, 2, 8)),
            dma((2, 4)),
            dma((2, 4)),
            dma((2, 4)),
            dma((2, 8)),
            dma((2, 4)),
        ],
        compiler_params=pltpu.CompilerParams(
            collective_id=0, has_side_effects=True, vmem_limit_bytes=VMEM_LIMIT
        ),
        name="layer",
    )(*operands)


def finish_kernel(*refs):
    count = (len(refs) - 1) // 3
    sems = refs[-1]
    arrive = [
        pltpu.make_async_copy(refs[i], refs[2 * count + i], sems.at[0, i]) for i in range(count)
    ]
    leave = [
        pltpu.make_async_copy(refs[2 * count + i], refs[count + i], sems.at[1, i])
        for i in range(count)
    ]
    for copy in arrive:
        copy.start()
    for i in range(count):
        arrive[i].wait()
        leave[i].start()
    for copy in leave:
        copy.wait()


def finish(results):
    spec = [pl.BlockSpec(memory_space=pl.ANY)] * len(results)
    return pl.pallas_call(
        finish_kernel,
        out_shape=tuple(jax.ShapeDtypeStruct(x.shape, x.dtype) for x in results),
        in_specs=spec,
        out_specs=spec,
        scratch_shapes=[pltpu.VMEM(x.shape, x.dtype) for x in results]
        + [pltpu.SemaphoreType.DMA((2, len(results)))],
        name="finish",
    )(*results)


def blocked(
    tokens,
    positions,
    time_index,
    time_table,
    w_qkv,
    w_out,
    w_up,
    w_down,
    scale_attn,
    scale_mlp,
    cotangent,
):
    half_dim = HEAD_DIM // 2
    frequency = 10000.0 ** (-jnp.arange(half_dim, dtype=jnp.float32) / half_dim)
    results = layer(
        tokens,
        positions,
        jnp.broadcast_to(frequency[:, None], (half_dim, 128)),
        w_qkv,
        time_table,
        scale_attn,
        scale_mlp,
        w_up,
        w_out,
        w_down,
        cotangent.reshape(128, 1024),
        time_index,
    )
    output, grad_tokens, *others = finish(results)
    return (output.reshape(2, 64, 1024), grad_tokens.reshape(2, 64, 1024), *others)


def solution(mesh):
    fits = mesh.shape["head"] == 4 and mesh.shape["blk"] == 8
    placed = (
        P(None, ("head", "blk"), None),
        P(None, ("head", "blk")),
        P(),
        P(),
        P(("head", "blk"), None),
        P(("head", "blk"), None),
        P(("head", "blk"), None),
        P(("head", "blk"), None),
        P(("head", "blk"), None),
        P(("head", "blk"), None),
        P(None, ("head", "blk"), None),
    )
    return jax.shard_map(
        blocked if fits else general,
        mesh=mesh,
        in_specs=placed,
        out_specs=(
            P(None, ("head", "blk"), None),
            P(None, ("head", "blk"), None),
            P(("head", "blk"), None),
            P(("head", "blk"), None),
            P(("head", "blk"), None),
            P(("head", "blk"), None),
            P(("head", "blk"), None),
            P(("head", "blk"), None),
        ),
        check_vma=False,
    )
```
